32 devices in a mesh: dp: 4 (over y, core), vocab: 8 (over z, x).
Axes of the slice: x: 2, y: 2, z: 4, core: 2. Of those that a mesh axis runs over, the one named last changes fastest.
Arguments:
- token_ids: int32 [16384], P(('dp', 'vocab')), may hold values from 0 to 50303
- seq_lengths: int32 [32, 4], P(('dp', 'vocab')), may hold values from 0 to 512, as said below
- pick_rows: int32 [2048], P(('dp', 'vocab')), may hold values from 0 to 511
- targets: int32 [2048], P(('dp', 'vocab')), may hold values from 0 to 50303
- step_count: int32 [1], replicated, may hold values from 1 to 20
- block_order: int32 [48], replicated, may hold values from 0 to 47, each once
- slot_weights: float32 [48, 384, 384], P('dp'), may hold values from -0.21875 to 0.21875
- left_stats: float32 [48, 384, 384], P('dp'), as said below
- right_stats: float32 [48, 384, 384], P('dp'), as said below
- left_roots: float32 [48, 384, 384], P('dp'), as said below
- right_roots: float32 [48, 384, 384], P('dp'), as said below
- embedding: float32 [50304, 768], P('vocab', 'dp'), may hold values from -1 to 1
- embedding_first_moment: float32 [50304, 768], P('vocab', 'dp'), may hold values from -2.3841858e-06 to 2.3841858e-06
- emb_second: float32 [50304, 768], P('vocab', 'dp'), may hold values from 1.1566702e-13 to 4.583033e-13
- vectors: float32 [15, 768], replicated, may hold values from 0.5 to 1.5
- vec_first: float32 [15, 768], replicated, may hold values from -9.536743e-06 to 9.536743e-06
- vec_second: float32 [15, 768], replicated, may hold values from 1.8550372e-12 to 7.420149e-12
- feature_maps: float32 [2, 12, 64, 64], replicated, may hold values from -0.75 to 0.75
- map_first: float32 [2, 12, 64, 64], replicated, may hold values from -2.3841858e-06 to 2.3841858e-06
- map_second: float32 [2, 12, 64, 64], replicated, may hold values from 1.1566702e-13 to 4.583033e-13
Outputs:
- loss: float32 [], replicated
- grad_norm: float32 [], replicated
- slot_grads: float32 [48, 384, 384], P('dp')
- new_slot_weights: float32 [48, 384, 384], P('dp')
- new_left_stats: float32 [48, 384, 384], P('dp')
- new_right_stats: float32 [48, 384, 384], P('dp')
- new_embedding: float32 [50304, 768], P('vocab', 'dp')
- new_emb_first: float32 [50304, 768], P('vocab', 'dp')
- new_emb_second: float32 [50304, 768], P('vocab', 'dp')
- new_vectors: float32 [15, 768], replicated
- new_vec_first: float32 [15, 768], replicated
- new_vec_second: float32 [15, 768], replicated
- new_maps: float32 [2, 12, 64, 64], replicated
- new_map_first: float32 [2, 12, 64, 64], replicated
- new_map_second: float32 [2, 12, 64, 64], replicated
The draws below stay inside these ranges and needn't reach their ends.
Inputs may be any that keep to these rules, and one draw needn't show every extreme that they name: `seq_lengths`: row r holds the document lengths of packed row r in order; they sum to 512, the first is 128 or more, later ones may be 0, and row 0 is a single document. `left_stats`: each slot is symmetric. `right_stats`: each slot is symmetric. `left_roots`: each slot is symmetric. `right_roots`: each slot is symmetric.
All inputs are finite; a program needn't handle non-finite values.
Results may differ from the reference program's by a relative error of at most 0.0017.
The reference program's roundings to bfloat16 on the way count: a program that leaves them out, or rounds other values in their place, can miss the bound.
Values may be sent and summed in bfloat16 or wider, within the bound.
No kernel may reach another device: no remote copies, remote signals or barrier semaphores. Data moves between devices by JAX's collectives and lax.ppermute only.
A program may use at most 384 MiB of HBM per device.

```python
import math
import jax
import jax.numpy as jnp
import numpy as np
from jax import lax

D = 768
HEADS = 12
HD = 64
FF = 3072
VOCAB = 50304
BS = 384
TOK_DEV = 512
PICK = 64
DEV_ROWS = 32
TOKENS = 16384
PICKS = 2048
NBLK = 48
NPARAM = 45821184


SHAMPOO_BETA = 0.95


def noisy_identity(key, spread):
    noise = jax.random.normal(key, (NBLK, BS, BS), jnp.float32)
    symmetric = (noise + jnp.swapaxes(noise, 1, 2)) * (0.70710678 * spread / BS ** 0.5)
    return jnp.eye(BS, dtype=jnp.float32)[None] + symmetric


def stat_level():
    return (1.0 - SHAMPOO_BETA) / SHAMPOO_BETA * BS * 0.0001 / NPARAM


def slot_factor(key, low_end, high_end):
    return jnp.exp(jax.random.uniform(key, (NBLK, 1, 1), jnp.float32, jnp.log(low_end), jnp.log(high_end)))


def draw_stats(key, salt):
    base_key = jax.random.fold_in(key, salt)
    high_end = 4.0
    factor = slot_factor(jax.random.fold_in(base_key, 1), 1.0, high_end)
    return factor * stat_level() * noisy_identity(jax.random.fold_in(base_key, 2), 0.2)


def draw_roots(key, salt):
    base_key = jax.random.fold_in(key, salt)
    factor = slot_factor(jax.random.fold_in(base_key, 1), 0.7, 1.4)
    return factor * (2.0 * stat_level()) ** (-0.25) * noisy_identity(jax.random.fold_in(base_key, 2), 0.3)


def draw_left_stats(key, part):
    return draw_stats(key, 11)


def draw_right_stats(key, part):
    return draw_stats(key, 12)


def draw_left_roots(key, part):
    return draw_roots(key, 13)


def draw_right_roots(key, part):
    return draw_roots(key, 14)


def draw_seq_lengths(key, part):
    key_lead = jax.random.fold_in(key, 21)
    first_len = jax.random.randint(jax.random.fold_in(key_lead, 1), (DEV_ROWS,), TOK_DEV // 4, TOK_DEV + 1)
    first_len = jnp.where(jnp.arange(DEV_ROWS) == 0, TOK_DEV, first_len)
    rest_len = TOK_DEV - first_len
    second_len = jax.random.randint(jax.random.fold_in(key_lead, 2), (DEV_ROWS,), 0, TOK_DEV + 1) % (rest_len + 1)
    remain_len = rest_len - second_len
    third_len = jax.random.randint(jax.random.fold_in(key_lead, 3), (DEV_ROWS,), 0, TOK_DEV + 1) % (remain_len + 1)
    return jnp.stack([first_len, second_len, third_len, remain_len - third_len], 1).astype(jnp.int32)


def touch_ends(drawn, own_key, smallest, top_value):
    place = [jax.random.randint(jax.random.fold_in(own_key, axis), (), 0, length) for axis, length in enumerate(drawn.shape)]
    longest = drawn.shape.index(max(drawn.shape))
    beside = place[:longest] + [(place[longest] + 1) % drawn.shape[longest]] + place[longest + 1:]
    return drawn.at[tuple(place)].set(smallest).at[tuple(beside)].set(top_value)


def levels(stream_key, dims, shards, least, top_value):
    factor_of = 1.0
    for dim, shards_of in shards:
        heights = jax.random.uniform(jax.random.fold_in(jax.random.fold_in(stream_key, 6), dim), (shards_of,), jnp.float32, least / len(shards), top_value / len(shards))
        factor_of = factor_of * jnp.repeat(jnp.exp(heights), dims[dim] // shards_of).reshape((-1,) + (1,) * (len(dims) - 1 - dim))
    return factor_of


def rank_table(count, slope):
    loads = [(1 << 20) // math.isqrt(standing ** slope) + 1 for standing in range(1, count + 1)]
    scale = 1 + sum(loads) // (1 << 30)
    return np.cumsum(np.array([max(1, weight // scale) for weight in loads]))


def ranked(key, dims, number_of, lean):
    table = rank_table(number_of, lean)
    pick = jax.random.randint(jax.random.fold_in(key, 1), dims, 0, int(table[number_of - 1]))
    grade = jnp.searchsorted(jnp.asarray(table, jnp.int32), pick, side="right")
    return jax.random.permutation(jax.random.fold_in(key, 2), number_of)[grade].astype(jnp.int32)


def scatter_about(own_key, extent, deviation, limit, split=(), kind=jnp.bfloat16):
    level = levels(own_key, extent, split, -0.22, 0.18) if split else 1.0
    entries = jax.random.normal(own_key, extent, jnp.float32) * deviation * level
    return jnp.minimum(jnp.maximum(entries, -limit), limit).astype(kind)


def setup_inputs(seed: int = 0) -> dict:
    keys = jax.random.split(jax.random.key(seed), 21)
    token_ids = touch_ends(ranked(keys[0], (TOKENS,), VOCAB, 2), jax.random.fold_in(keys[0], 3), 0, VOCAB - 1).astype(jnp.int32)
    seq_lengths = draw_seq_lengths(jax.random.fold_in(keys[20], 71), 0)
    pick_rows = touch_ends(jax.random.randint(keys[2], (PICKS,), 0, TOK_DEV), jax.random.fold_in(keys[2], 1), 0, TOK_DEV - 1).astype(jnp.int32)
    targets = touch_ends(ranked(keys[3], (PICKS,), VOCAB, 2), jax.random.fold_in(keys[3], 3), 0, VOCAB - 1).astype(jnp.int32)
    step_count = jax.random.randint(keys[4], (1,), 1, 21).astype(jnp.int32)
    block_order = jax.random.permutation(keys[5], NBLK).astype(jnp.int32)
    slot_weights = scatter_about(keys[6], (NBLK, BS, BS), D ** -0.5, 0.21875, ((0, 4),), jnp.float32)
    left_stats = draw_left_stats(jax.random.fold_in(keys[20], 71), 0)
    right_stats = draw_right_stats(jax.random.fold_in(keys[20], 71), 0)
    left_roots = draw_left_roots(jax.random.fold_in(keys[20], 71), 0)
    right_roots = draw_right_roots(jax.random.fold_in(keys[20], 71), 0)
    embedding = scatter_about(keys[11], (VOCAB, D), (2 / D ** 0.5), 1.0, ((0, 8), (1, 4)), jnp.float32)
    embedding_first_moment = scatter_about(keys[12], (VOCAB, D), (0.11 * 0.01 / NPARAM ** 0.5), 2.384185791015625e-06, ((0, 8), (1, 4)), jnp.float32)
    emb_second = jnp.clip(jnp.exp(math.log(4.583033171717821e-13) - 1.37681564 * jax.random.uniform(keys[13], (VOCAB, D), jnp.float32) ** levels(keys[13], (VOCAB, D), ((0, 8), (1, 4)), -0.2, 0.2)), 1.1566702456944356e-13, 4.583033171717821e-13)
    vectors = jnp.clip(1.0 + 0.1 * jax.random.normal(keys[14], (15, D), jnp.float32), 0.5, 1.5)
    vec_first = scatter_about(keys[15], (15, D), (0.44 * 0.01 / NPARAM ** 0.5), 9.5367431640625e-06, (), jnp.float32)
    vec_second = jnp.clip(jnp.exp(jax.random.uniform(keys[16], (15, D), jnp.float32, math.log(1.855037174217089e-12), math.log(7.420148696868356e-12))), 1.855037174217089e-12, 7.420148696868356e-12)
    feature_maps = scatter_about(keys[17], (2, HEADS, HD, HD), HD ** -0.5, 0.75, (), jnp.float32)
    map_first = scatter_about(keys[18], (2, HEADS, HD, HD), (0.11 * 0.01 / NPARAM ** 0.5), 2.384185791015625e-06, (), jnp.float32)
    map_second = jnp.clip(jnp.exp(jax.random.uniform(keys[19], (2, HEADS, HD, HD), jnp.float32, math.log(1.1566702456944356e-13), math.log(4.583033171717821e-13))), 1.1566702456944356e-13, 4.583033171717821e-13)
    return {"token_ids": token_ids, "seq_lengths": seq_lengths, "pick_rows": pick_rows, "targets": targets, "step_count": step_count, "block_order": block_order, "slot_weights": slot_weights, "left_stats": left_stats, "right_stats": right_stats, "left_roots": left_roots, "right_roots": right_roots, "embedding": embedding, "embedding_first_moment": embedding_first_moment, "emb_second": emb_second, "vectors": vectors, "vec_first": vec_first, "vec_second": vec_second, "feature_maps": feature_maps, "map_first": map_first, "map_second": map_second}


@jax.custom_vjp
def low(v):
    return lax.optimization_barrier(v.astype(jnp.bfloat16)).astype(jnp.float32)

@jax.custom_vjp
def low_back(v):
    return v

def low_keep(v):
    return (low(v), None)

def low_pass(kept, grad):
    return (grad,)

def back_keep(v):
    return (v, None)

def back_low(kept, grad):
    return (low(grad),)
low.defvjp(low_keep, low_pass)
low_back.defvjp(back_keep, back_low)
NORM_EPSILON = 1e-05
CLIP_NORM = 0.01
DISTILL_WEIGHT = 0.5
BETA_FIRST = 0.9
BETA_SECOND = 0.95
ADAM_EPSILON = 1e-08
DECAY_RATE = 0.01
SHAMPOO_BETA = 0.95
RATE_BLOCKS = 0.1
RATE_TABLE = 0.05
RATE_VECTORS = 0.2
RATE_MAPS = 0.1
FULL_ACCURACY = lax.Precision.HIGHEST

def norm_layer(inputs, gain_row, bias_row):
    centered = inputs - lax.optimization_barrier(jnp.mean(inputs, -1, keepdims=True))
    variance = lax.optimization_barrier(jnp.mean(centered * centered, -1, keepdims=True))
    return centered * lax.rsqrt(variance + NORM_EPSILON) * gain_row + bias_row

def gelu_tanh(inputs):
    return 0.5 * inputs * (1.0 + jnp.tanh(0.7978845608 * (inputs + 0.044715 * inputs * inputs * inputs)))

def feature(inputs):
    return jnp.concatenate([jax.nn.softmax(inputs, -1), jax.nn.softmax(-inputs, -1)], -1)

def untile(tiles, height, width):
    return tiles.reshape(height // BS, width // BS, BS, BS).transpose(0, 2, 1, 3).reshape(height, width)

def retile(matrix):
    height, width = matrix.shape
    return matrix.reshape(height // BS, BS, width // BS, BS).transpose(0, 2, 1, 3).reshape(-1, BS, BS)

def split_tiles(tiles):
    first_end = 3 * D * D // (BS * BS)
    second_end = first_end + D * D // (BS * BS)
    third_end = second_end + D * FF // (BS * BS)
    return (untile(tiles[:first_end], D, 3 * D), untile(tiles[first_end:second_end], D, D), untile(tiles[second_end:third_end], D, FF), untile(tiles[third_end:], FF, D))

def segments(lengths, length_all):
    bounds = jnp.cumsum(lengths)[:-1].astype(jnp.int32)
    places = jnp.arange(length_all, dtype=jnp.int32)
    return lax.optimization_barrier(jnp.sum((places[:, None] >= bounds[None, :]).astype(jnp.int32), axis=1)).astype(jnp.int32)

def adam_update(weight, first, second, gradient, rate, step_value):
    first_new = BETA_FIRST * first + (1.0 - BETA_FIRST) * gradient
    second_new = BETA_SECOND * second + (1.0 - BETA_SECOND) * gradient * gradient
    first_hat = first_new / (1.0 - BETA_FIRST ** step_value)
    second_hat = second_new / (1.0 - BETA_SECOND ** step_value)
    return (weight - rate * (first_hat / (jnp.sqrt(second_hat) + ADAM_EPSILON) + DECAY_RATE * weight), first_new, second_new)

def shampoo_update(weights, grads, left_stats, right_stats, left_roots, right_roots):
    new_left = SHAMPOO_BETA * left_stats + (1.0 - SHAMPOO_BETA) * jnp.einsum('nij,nkj->nik', grads, grads, precision=FULL_ACCURACY)
    new_right = SHAMPOO_BETA * right_stats + (1.0 - SHAMPOO_BETA) * jnp.einsum('nji,njk->nik', grads, grads, precision=FULL_ACCURACY)
    turned = jnp.einsum('nij,njk->nik', grads, right_roots, precision=FULL_ACCURACY)
    direction = jnp.einsum('nij,njk->nik', left_roots, turned, precision=FULL_ACCURACY)
    return (weights - RATE_BLOCKS * (direction + DECAY_RATE * weights), new_left, new_right)

def project(params, token_row):
    table = low(params[0])
    embedded = low_back(jnp.take(table, token_row, axis=0))
    vectors = params[1]
    normed = low(norm_layer(embedded, vectors[0], vectors[1]))
    mixed = low(low_back(jnp.dot(normed, low(params[3]), precision=FULL_ACCURACY) + vectors[8:11].reshape(-1)))
    return (table, embedded, mixed)

def split_heads(flat):
    return flat.reshape(flat.shape[0], HEADS, HD)

def row_loss(params, frozen, row):
    token_row, length_row, pick_row, target_row = row
    table, embedded, mixed = project(params, token_row)
    teacher_mix = project(frozen, token_row)[2]
    vectors, maps = (params[1], params[2])
    segment = segments(length_row, TOK_DEV)
    places = jnp.arange(TOK_DEV, dtype=jnp.int32)
    causal_allowance = (places[None, :] <= places[:, None]) & (segment[None, :] == segment[:, None])
    queries = split_heads(mixed[:, :D])
    key_rows = split_heads(mixed[:, D:2 * D])
    value_rows = split_heads(mixed[:, 2 * D:])
    feat_query = low_back(jnp.einsum('thd,hde->the', queries, low(maps[0]), precision=FULL_ACCURACY))
    feat_key = low_back(jnp.einsum('thd,hde->the', key_rows, low(maps[1]), precision=FULL_ACCURACY))
    asking_side_lifted = low(feature(feat_query))
    lookup_side_lifted = low(feature(feat_key))
    teacher_scores = jnp.einsum('qhd,khd->hqk', split_heads(teacher_mix[:, :D]), split_heads(teacher_mix[:, D:2 * D]), precision=FULL_ACCURACY) * HD ** (-0.5)
    teacher_probs = jax.nn.softmax(jnp.where(causal_allowance, teacher_scores, -1e+30), -1)
    affinity_logits = low_back(jnp.einsum('dvh,uvh->vdu', asking_side_lifted, lookup_side_lifted, precision=FULL_ACCURACY) * causal_allowance)
    totals = lax.optimization_barrier(jnp.sum(affinity_logits, -1, keepdims=True))
    weights = low(affinity_logits / totals)
    attended = low(low_back(jnp.einsum('hqk,khd->qhd', weights, value_rows, precision=FULL_ACCURACY))).reshape(TOK_DEV, D)
    distill = jnp.sum(-teacher_probs * jnp.log(jnp.where(causal_allowance, affinity_logits, 1.0))) + jnp.sum(jnp.log(totals))
    residual_one = embedded + low_back(jnp.dot(attended, low(params[4]), precision=FULL_ACCURACY) + vectors[6])
    normed_two = low(norm_layer(residual_one, vectors[2], vectors[3]))
    upward = low_back(jnp.dot(normed_two, low(params[5]), precision=FULL_ACCURACY) + vectors[11:15].reshape(-1))
    branch = low_back(jnp.dot(low(gelu_tanh(upward)), low(params[6]), precision=FULL_ACCURACY) + vectors[7])
    residual_two = residual_one + branch
    final_norm = norm_layer(residual_two, vectors[4], vectors[5])
    picked = low(jnp.take(final_norm, pick_row, axis=0))
    logits = low_back(jnp.dot(picked, table.T, precision=FULL_ACCURACY))
    cross = jax.nn.logsumexp(logits, -1) - jnp.take_along_axis(logits, target_row[:, None], -1)[:, 0]
    return jnp.sum(cross) / PICKS + DISTILL_WEIGHT * distill / (TOKENS * HEADS)

def total_loss(params, frozen, rows):

    def one_row(row):
        return row_loss(params, frozen, row)
    return jnp.sum(lax.map(jax.checkpoint(one_row), rows))

def reference(token_ids, seq_lengths, pick_rows, targets, step_count, block_order, slot_weights, left_stats, right_stats, left_roots, right_roots, embedding, embedding_first_moment, emb_second, vectors, vec_first, vec_second, feature_maps, map_first, map_second):
    inverse = jnp.zeros((NBLK,), jnp.int32).at[block_order].set(jnp.arange(NBLK, dtype=jnp.int32))
    params = (embedding, vectors, feature_maps) + split_tiles(jnp.take(slot_weights, inverse, axis=0))
    rows = (token_ids.reshape(DEV_ROWS, TOK_DEV), seq_lengths, pick_rows.reshape(DEV_ROWS, PICK), targets.reshape(DEV_ROWS, PICK))
    loss, pull_back = jax.vjp(lambda current: total_loss(current, params, rows), params)
    grads = pull_back(jnp.ones_like(loss))[0]
    tile_grads = jnp.concatenate([retile(gradient) for gradient in grads[3:]], 0)
    slot_raw = jnp.take(tile_grads, block_order, axis=0)
    squares = jnp.sum(grads[0] * grads[0]) + jnp.sum(grads[1] * grads[1]) + jnp.sum(grads[2] * grads[2]) + jnp.sum(slot_raw * slot_raw)
    grad_norm = jnp.sqrt(squares)
    clip_scale = CLIP_NORM / jnp.maximum(grad_norm, CLIP_NORM)
    clipped = slot_raw * clip_scale
    new_slots, new_left, new_right = shampoo_update(slot_weights, clipped, left_stats, right_stats, left_roots, right_roots)
    step_value = step_count[0].astype(jnp.float32)
    emb_out = adam_update(embedding, embedding_first_moment, emb_second, grads[0] * clip_scale, RATE_TABLE, step_value)
    vec_out = adam_update(vectors, vec_first, vec_second, grads[1] * clip_scale, RATE_VECTORS, step_value)
    map_out = adam_update(feature_maps, map_first, map_second, grads[2] * clip_scale, RATE_MAPS, step_value)
    return (loss, grad_norm, clipped, new_slots, new_left, new_right, emb_out[0], emb_out[1], emb_out[2], vec_out[0], vec_out[1], vec_out[2], map_out[0], map_out[1], map_out[2])
```

```python
from functools import partial

import jax
import jax.numpy as jnp
import numpy as np
from jax import lax
from jax.experimental import pallas as pl
from jax.experimental.pallas import tpu as pltpu
from jax.sharding import PartitionSpec as P

D = 768
HEADS = 12
HD = 64
FF = 3072
BS = 384
PAIRS = HEADS // 2

NORM_EPSILON = 1e-05
CLIP_NORM = 0.01
DISTILL_WEIGHT = 0.5
BETA_FIRST = 0.9
BETA_SECOND = 0.95
ADAM_EPSILON = 1e-08
DECAY_RATE = 0.01
SHAMPOO_BETA = 0.95
RATE_BLOCKS = 0.1
RATE_TABLE = 0.05
RATE_VECTORS = 0.2
RATE_MAPS = 0.1

f32 = jnp.float32
bf16 = jnp.bfloat16
i32 = jnp.int32
SMEM = pltpu.SMEM
ANY = pl.ANY


def mm(left, right):
    return lax.dot_general(left, right, (((1,), (0,)), ((), ())), preferred_element_type=f32)


def mm_t(left, right):
    return lax.dot_general(left, right, (((1,), (1,)), ((), ())), preferred_element_type=f32)


def mm_l(left, right):
    return lax.dot_general(left, right, (((0,), (0,)), ((), ())), preferred_element_type=f32)


def split_two(values):
    high = values.astype(bf16)
    return high, (values - high.astype(f32)).astype(bf16)


def full(shape):
    return pl.BlockSpec(shape, lambda *_: (0,) * len(shape))


def cost(flops, bytes_moved, transcendentals=0):
    return pl.CostEstimate(
        flops=int(flops), bytes_accessed=int(bytes_moved), transcendentals=int(transcendentals)
    )


def place_kernel(piece_count, src_ref, off_ref, *refs):
    pieces = refs[:piece_count]
    outs = refs[piece_count : piece_count + 4]
    sems = refs[piece_count + 4]
    base = 0
    for out, rows, cols in zip(outs, (D, D, D, FF), (3 * D, D, FF, D)):
        wide = cols // BS
        count = (rows // BS) * wide

        def go(t, carry, out=out, wide=wide, base=base):
            k = base + t
            r0 = pl.multiple_of((t // wide) * BS, BS)
            c0 = pl.multiple_of((t % wide) * BS, BS)
            for p in range(piece_count):

                @pl.when(src_ref[k] == p)
                def _(p=p):
                    pltpu.make_async_copy(
                        pieces[p].at[off_ref[k]],
                        out.at[pl.ds(r0, BS), pl.ds(c0, BS)],
                        sems.at[k],
                    ).start()

            return carry

        lax.fori_loop(0, count, go, 0)
        base += count
    base = 0
    for out, rows, cols in zip(outs, (D, D, D, FF), (3 * D, D, FF, D)):
        count = (rows // BS) * (cols // BS)

        def done(t, carry, out=out, base=base):
            pltpu.make_async_copy(
                pieces[0].at[0], out.at[pl.ds(0, BS), pl.ds(0, BS)], sems.at[base + t]
            ).wait()
            return carry

        lax.fori_loop(0, count, done, 0)
        base += count


def place_blocks(src, off, pieces):
    count = len(pieces)
    return pl.pallas_call(
        partial(place_kernel, count),
        out_shape=[
            jax.ShapeDtypeStruct(shape, bf16)
            for shape in ((D, 3 * D), (D, D), (D, FF), (FF, D))
        ],
        in_specs=[pl.BlockSpec(memory_space=SMEM)] * 2 + [pl.BlockSpec(memory_space=ANY)] * count,
        out_specs=[pl.BlockSpec(memory_space=pltpu.VMEM)] * 4,
        scratch_shapes=[pltpu.SemaphoreType.DMA((48,))],
        name="place_blocks",
        cost_estimate=cost(0, 2 * 48 * BS * BS * 2),
    )(src, off, *pieces)


def hits_kernel(empty_row, packed_ref, list_ref, count_ref):
    total = packed_ref.shape[0]

    def go(i, n):
        for u in range(16):
            entry = packed_ref[i * 16 + u]
            list_ref[n] = entry
            n = n + 1 + (entry >> 31)
        return n

    n = lax.fori_loop(0, total // 16, go, jnp.int32(0))
    count_ref[0] = n
    for u in range(8):
        list_ref[n + u] = empty_row << 16


def find_hits(packed, empty_row):
    total = packed.shape[0]
    return pl.pallas_call(
        partial(hits_kernel, empty_row),
        out_shape=[
            jax.ShapeDtypeStruct((total + 16,), i32),
            jax.ShapeDtypeStruct((1,), i32),
        ],
        in_specs=[pl.BlockSpec(memory_space=SMEM)],
        out_specs=[pl.BlockSpec(memory_space=SMEM)] * 2,
        name="find_hits",
        cost_estimate=cost(1e10, total * 8),
    )(packed)


def lookup_kernel(rows_all, list_ref, count_ref, table_ref, out_ref, tab, acc):
    total = out_ref.shape[0]
    tab[pl.ds(0, rows_all), :] = table_ref[...].astype(f32)
    tab[pl.ds(rows_all, 8), :] = jnp.zeros((8, tab.shape[1]), f32)
    acc[...] = jnp.zeros(acc.shape, f32)

    def go(i, carry):
        for u in range(8):
            entry = list_ref[i * 8 + u]
            row = entry >> 16
            place = jnp.where(row < rows_all, entry & 0xFFFF, total)
            acc[pl.ds(place, 1), :] = tab[pl.ds(row, 1), :]
        return carry

    lax.fori_loop(0, (count_ref[0] + 7) // 8, go, 0)
    out_ref[...] = acc[pl.ds(0, total), :].astype(bf16)


def lookup(hit_list, hit_count, table, count):
    rows_all, width = table.shape
    return pl.pallas_call(
        partial(lookup_kernel, rows_all),
        out_shape=jax.ShapeDtypeStruct((count, width), bf16),
        in_specs=[pl.BlockSpec(memory_space=SMEM)] * 2 + [pl.BlockSpec(memory_space=pltpu.VMEM)],
        out_specs=pl.BlockSpec(memory_space=pltpu.VMEM),
        scratch_shapes=[
            pltpu.VMEM((rows_all + 8, width), f32),
            pltpu.VMEM((count + 8, width), f32),
        ],
        name="lookup",
        cost_estimate=cost(1e10, rows_all * width * 2),
    )(hit_list, hit_count, table)


def scatter_kernel(piece_count, half, rows_all, *refs):
    lists, counts = refs[0:4:2], refs[1:4:2]
    lex_ref = refs[4]
    pieces = refs[5 : 5 + piece_count]
    out_ref, square_ref, acc, tail, wide, pair = refs[5 + piece_count :]
    acc[...] = jnp.zeros(acc.shape, f32)
    tail[...] = jnp.zeros(tail.shape, f32)
    for k in range(piece_count):
        wide[pl.ds(k * 2 * half, 2 * half), :] = pieces[k][pl.ds(0, 2 * half), :].astype(f32)
        pair[pl.ds(k * half, half), :] = pieces[k][pl.ds(2 * half, half), :].astype(f32)
    upper = lax.broadcasted_iota(i32, (1, 128), 1) >= 64
    for side in range(2):
        own = upper if side else ~upper

        def go(i, carry, side=side, own=own):
            for u in range(8):
                entry = lists[side][i * 8 + u]
                row = entry >> 16
                p = entry & 0xFFFF
                q = (p // half) * half + p + side * half
                acc[pl.ds(row, 1), :] += wide[pl.ds(q, 1), :]
                tail[pl.ds(row, 1), :] += jnp.where(own, pair[pl.ds(p, 1), :], 0.0)
            return carry

        lax.fori_loop(0, (counts[side][0] + 7) // 8, go, 0)
    chunks = rows_all // 128
    rest = rows_all - chunks * 128

    def turn(start, width):
        upright = acc[pl.ds(start, 128), :].T
        lower = tail[pl.ds(start, 128), :].T
        lower = lower[:64] + lower[64:]
        lanes = pl.ds(start, width)
        left = lex_ref[pl.ds(0, 128), lanes] + upright[:, :width]
        right = lex_ref[pl.ds(128, 64), lanes] + lower[:, :width]
        out_ref[pl.ds(0, 128), lanes] = left
        out_ref[pl.ds(128, 64), lanes] = right
        return jnp.sum(left * left, 0, keepdims=True), jnp.sum(right * right, 0, keepdims=True)

    def step(i, carry):
        left, right = turn(pl.multiple_of(i * 128, 128), 128)
        return carry + left + right

    squares = lax.fori_loop(0, chunks, step, jnp.zeros((1, 128), f32))
    total = jnp.sum(squares)
    if rest:
        left, right = turn(chunks * 128, rest)
        total = total + jnp.sum(left) + jnp.sum(right)
    square_ref[0, 0] = total


def scatter_rows(lists, lex, pieces):
    width, rows_all = lex.shape
    half = pieces[0].shape[0] // 3
    count = len(pieces)
    padded = (rows_all // 128 + 1) * 128
    return pl.pallas_call(
        partial(scatter_kernel, count, half, rows_all),
        out_shape=[
            jax.ShapeDtypeStruct((width, rows_all), f32),
            jax.ShapeDtypeStruct((1, 1), f32),
        ],
        in_specs=[pl.BlockSpec(memory_space=SMEM)] * 4
        + [pl.BlockSpec(memory_space=pltpu.VMEM)] * (count + 1),
        out_specs=[
            pl.BlockSpec(memory_space=pltpu.VMEM),
            pl.BlockSpec(memory_space=SMEM),
        ],
        scratch_shapes=[
            pltpu.VMEM((padded, 128), f32),
            pltpu.VMEM((padded, 128), f32),
            pltpu.VMEM((count * 2 * half, 128), f32),
            pltpu.VMEM((count * half, 128), f32),
        ],
        name="scatter_rows",
        cost_estimate=cost(1.5e10, rows_all * width * 8),
    )(*lists, lex, *pieces)


def norm_parts(inputs):
    centered = inputs - jnp.mean(inputs, -1, keepdims=True)
    scale = lax.rsqrt(jnp.mean(centered * centered, -1, keepdims=True) + NORM_EPSILON)
    return centered, scale


def norm_pull(inputs, gain_row, grads):
    centered, scale = norm_parts(inputs)
    unit = centered * scale
    pulled = grads * gain_row
    lead = jnp.mean(pulled, -1, keepdims=True)
    along = jnp.mean(pulled * unit, -1, keepdims=True)
    grad_in = scale * (pulled - lead - unit * along)
    return (
        grad_in,
        jnp.sum(grads * unit, 0, keepdims=True),
        jnp.sum(grads, 0, keepdims=True),
    )


def qkv_kernel(x_ref, w_ref, vec_ref, h_ref, mixed_ref):
    j = pl.program_id(0)

    @pl.when(j == 0)
    def _():
        centered, scale = norm_parts(x_ref[...].astype(f32))
        h_ref[...] = (centered * scale * vec_ref[0:1, :] + vec_ref[1:2, :]).astype(bf16)

    mixed_ref[...] = (mm(h_ref[...], w_ref[...]) + vec_ref[pl.ds(8 + j, 1), :]).astype(bf16)


def qkv_forward(x0, wqkv, vectors):
    tokens = x0.shape[0]
    return pl.pallas_call(
        qkv_kernel,
        grid=(3,),
        out_shape=[
            jax.ShapeDtypeStruct((tokens, D), bf16),
            jax.ShapeDtypeStruct((tokens, 3 * D), bf16),
        ],
        in_specs=[
            full((tokens, D)),
            pl.BlockSpec((D, D), lambda j: (0, j)),
            full(vectors.shape),
        ],
        out_specs=[full((tokens, D)), pl.BlockSpec((tokens, D), lambda j: (0, j))],
        name="qkv_forward",
        cost_estimate=cost(2 * tokens * D * 3 * D, 8e6),
    )(x0, wqkv, vectors)


def feature_parts(values, lift, low_half):
    raw = mm(values, lift)
    top_a = jnp.max(jnp.where(low_half, raw, -jnp.inf), -1, keepdims=True)
    top_b = jnp.max(jnp.where(low_half, -jnp.inf, raw), -1, keepdims=True)
    grown = jnp.exp(raw - jnp.where(low_half, top_a, top_b))
    sum_a = jnp.sum(jnp.where(low_half, grown, 0.0), -1, keepdims=True)
    sum_b = jnp.sum(jnp.where(low_half, 0.0, grown), -1, keepdims=True)
    return grown / jnp.where(low_half, sum_a, sum_b)


def feature_pull(soft, grads, low_half):
    weighed = soft * grads
    sum_a = jnp.sum(jnp.where(low_half, weighed, 0.0), -1, keepdims=True)
    sum_b = jnp.sum(jnp.where(low_half, 0.0, weighed), -1, keepdims=True)
    pulled = soft * (grads - jnp.where(low_half, sum_a, sum_b))
    return (pulled - pltpu.roll(pulled, HD, 1)).astype(bf16)


def fill_allowed(len_ref, allow_ref):
    tokens = allow_ref.shape[0]
    first = len_ref[0, 0]
    second = first + len_ref[0, 1]
    third = second + len_ref[0, 2]

    def document(places):
        return (
            (places >= first).astype(i32)
            + (places >= second).astype(i32)
            + (places >= third).astype(i32)
        )

    rows = lax.broadcasted_iota(i32, (tokens, tokens), 0)
    cols = lax.broadcasted_iota(i32, (tokens, tokens), 1)
    allow_ref[...] = ((cols <= rows) & (document(rows) == document(cols))).astype(f32)


ROWS = 256


def attend_kernel(
    len_ref, q_ref, k_ref, v_ref, fq_ref, fk_ref, y_ref, distill_ref, allow_ref, lift_q, lift_k
):
    tokens = q_ref.shape[0]

    @pl.when(pl.program_id(0) == 0)
    def _():
        fill_allowed(len_ref, allow_ref)
        distill_ref[...] = jnp.zeros_like(distill_ref)

    low_half = lax.broadcasted_iota(i32, (1, 2 * HD), 1) < HD
    low_rows = lax.broadcasted_iota(i32, (ROWS, 2 * HD), 1) < HD
    total = jnp.zeros((1, 1), f32)
    for h in range(2):
        lift_q[h] = feature_parts(q_ref[...], fq_ref[h], low_half).astype(bf16)
        lift_k[h] = feature_parts(k_ref[...], fk_ref[h], low_half).astype(bf16)
    for begin in range(0, tokens, ROWS):
        width = begin + ROWS
        ok = allow_ref[pl.ds(begin, ROWS), pl.ds(0, width)] > 0.5
        queries = q_ref[pl.ds(begin, ROWS), :] * jnp.asarray(HD**-0.5, bf16)
        keys = k_ref[pl.ds(0, width), :]
        values = v_ref[pl.ds(0, width), :]
        parts = []
        for h in range(2):
            own = low_rows if h == 0 else ~low_rows
            scores = mm_t(jnp.where(own, queries, jnp.zeros_like(queries)), keys)
            scores = jnp.where(ok, scores, -1e30)
            grown = jnp.exp(scores - jnp.max(scores, -1, keepdims=True))
            inverse = 1.0 / jnp.sum(grown, -1, keepdims=True)
            similar = mm_t(lift_q[h, pl.ds(begin, ROWS), :], lift_k[h, pl.ds(0, width), :])
            kept = jnp.where(ok, similar, 0.0)
            sums = jnp.sum(kept, -1, keepdims=True)
            weights = (kept * (1.0 / sums)).astype(bf16)
            parts.append(mm(weights, values))
            logs = jnp.log(jnp.where(ok, similar, 1.0))
            row_terms = jnp.log(sums) - jnp.sum(grown * logs, -1, keepdims=True) * inverse
            total = total + jnp.sum(row_terms, 0, keepdims=True)
        y_ref[pl.ds(begin, ROWS), :] = jnp.where(low_rows, parts[0], parts[1]).astype(bf16)
    distill_ref[...] += jnp.broadcast_to(total, distill_ref.shape)


def attend(lengths, mixed, lift_maps):
    tokens = mixed.shape[0]
    column = lambda base: pl.BlockSpec((tokens, 2 * HD), lambda g: (0, base + g))
    maps = pl.BlockSpec((2, 2 * HD, 2 * HD), lambda g: (g, 0, 0))
    return pl.pallas_call(
        attend_kernel,
        grid=(PAIRS,),
        out_shape=[
            jax.ShapeDtypeStruct((tokens, D), bf16),
            jax.ShapeDtypeStruct((8, 128), f32),
        ],
        in_specs=[
            pl.BlockSpec(memory_space=SMEM),
            column(0),
            column(PAIRS),
            column(2 * PAIRS),
            maps,
            maps,
        ],
        out_specs=[column(0), full((8, 128))],
        scratch_shapes=[
            pltpu.VMEM((tokens, tokens), f32),
            pltpu.VMEM((2, tokens, 2 * HD), bf16),
            pltpu.VMEM((2, tokens, 2 * HD), bf16),
        ],
        name="attend",
        cost_estimate=cost(1.2e10, 4e6, 6e6),
    )(lengths, mixed, mixed, mixed, lift_maps[0], lift_maps[1])


def attend_back_kernel(
    coefficient,
    later,
    len_ref,
    q_ref,
    k_ref,
    v_ref,
    gy_ref,
    fq_ref,
    fk_ref,
    *refs,
):
    g_ref, gq_map_ref, gk_map_ref, allow_ref, soft_q, soft_k, grad_q, grad_k, grad_v = refs[later:]
    tokens = q_ref.shape[0]

    @pl.when(pl.program_id(0) == 0)
    def _():
        fill_allowed(len_ref, allow_ref)

    low_half = lax.broadcasted_iota(i32, (1, 2 * HD), 1) < HD
    low_rows = lax.broadcasted_iota(i32, (ROWS, 2 * HD), 1) < HD
    for h in range(2):
        soft_q[h] = feature_parts(q_ref[...], fq_ref[h], low_half)
        soft_k[h] = feature_parts(k_ref[...], fk_ref[h], low_half)
    for step, begin in enumerate(reversed(range(0, tokens, ROWS))):
        width = begin + ROWS
        ok = allow_ref[pl.ds(begin, ROWS), pl.ds(0, width)] > 0.5
        queries = q_ref[pl.ds(begin, ROWS), :] * jnp.asarray(HD**-0.5, bf16)
        keys = k_ref[pl.ds(0, width), :]
        values = v_ref[pl.ds(0, width), :]
        grads = gy_ref[pl.ds(begin, ROWS), :]
        value_sum = None
        for h in range(2):
            own = low_rows if h == 0 else ~low_rows
            scores = mm_t(jnp.where(own, queries, jnp.zeros_like(queries)), keys)
            scores = jnp.where(ok, scores, -1e30)
            grown = jnp.exp(scores - jnp.max(scores, -1, keepdims=True))
            teach = grown * (coefficient / jnp.sum(grown, -1, keepdims=True))
            phi_q = soft_q[h, pl.ds(begin, ROWS), :].astype(bf16)
            phi_k = soft_k[h, pl.ds(0, width), :].astype(bf16)
            similar = mm_t(phi_q, phi_k)
            kept = jnp.where(ok, similar, 0.0)
            inverse = 1.0 / jnp.sum(kept, -1, keepdims=True)
            weights = kept * inverse
            own_grads = jnp.where(own, grads, jnp.zeros_like(grads))
            grad_w = mm_t(own_grads, values)
            row_sum = jnp.sum(grad_w * weights, -1, keepdims=True)
            grad_sums = (coefficient - row_sum) * inverse
            grad_sim = jnp.where(
                ok,
                grad_w * inverse - teach / jnp.where(ok, similar, 1.0) + grad_sums,
                0.0,
            ).astype(bf16)
            grad_q[h, pl.ds(begin, ROWS), :] = mm(grad_sim, phi_k)
            part_k = mm_l(grad_sim, phi_q)
            part_v = mm_l(weights.astype(bf16), own_grads)
            value_sum = part_v if value_sum is None else value_sum + part_v
            if step == 0:
                grad_k[h] = part_k
            else:
                grad_k[h, pl.ds(0, width), :] += part_k
        if step == 0:
            grad_v[...] = value_sum
        else:
            grad_v[pl.ds(0, width), :] += value_sum
    for slot, own_ref, map_ref, soft, grad, out in (
        (0, q_ref, fq_ref, soft_q, grad_q, gq_map_ref),
        (1, k_ref, fk_ref, soft_k, grad_k, gk_map_ref),
    ):
        result = None
        for h in range(2):
            pulled = feature_pull(soft[h], grad[h], low_half)
            back = mm_t(pulled, map_ref[h]) * 0.5
            result = back if result is None else result + back
            out[h] = mm_l(own_ref[...], pulled)[h * HD : (h + 1) * HD, :HD]
        g_ref[slot] = result.astype(bf16)
    g_ref[2] = grad_v[...].astype(bf16)


def attend_back(lengths, mixed, grad_y, lift_maps, coefficient, start, pairs, before):
    tokens = mixed.shape[0]
    column = lambda base: pl.BlockSpec((tokens, 2 * HD), lambda g: (0, base + start + g))
    maps = pl.BlockSpec((2, 2 * HD, 2 * HD), lambda g: (start + g, 0, 0))
    small = pl.BlockSpec((2, HD, HD), lambda g: (g, 0, 0))
    wide = (2, tokens, 2 * HD)
    later = before is not None
    return pl.pallas_call(
        partial(attend_back_kernel, coefficient, int(later)),
        grid=(pairs,),
        out_shape=[
            jax.ShapeDtypeStruct((3, tokens, D), bf16),
            jax.ShapeDtypeStruct((2 * pairs, HD, HD), f32),
            jax.ShapeDtypeStruct((2 * pairs, HD, HD), f32),
        ],
        in_specs=[
            pl.BlockSpec(memory_space=SMEM),
            column(0),
            column(PAIRS),
            column(2 * PAIRS),
            column(0),
            maps,
            maps,
        ]
        + [pl.BlockSpec(memory_space=ANY)] * later,
        out_specs=[
            pl.BlockSpec((3, tokens, 2 * HD), lambda g: (0, 0, start + g)),
            small,
            small,
        ],
        scratch_shapes=[
            pltpu.VMEM((tokens, tokens), f32),
            pltpu.VMEM(wide, f32),
            pltpu.VMEM(wide, f32),
            pltpu.VMEM(wide, f32),
            pltpu.VMEM(wide, f32),
            pltpu.VMEM((tokens, 2 * HD), f32),
        ],
        input_output_aliases={7: 0} if later else {},
        name="attend_back",
        cost_estimate=cost(1.2e10, 4e6, 3e6),
    )(lengths, mixed, mixed, mixed, grad_y, lift_maps[0], lift_maps[1], *([before] * later))


FSTEPS = FF // D


def mlp_kernel(
    x_ref,
    y_ref,
    wo_ref,
    wup_ref,
    wdown_ref,
    vec_ref,
    pick_ref,
    x1_ref,
    h_ref,
    up_ref,
    act_ref,
    x2_ref,
    hp_ref,
):
    j = pl.program_id(0)

    @pl.when(j == 0)
    def _():
        x1 = x_ref[...].astype(f32) + mm(y_ref[...], wo_ref[...]) + vec_ref[6:7, :]
        x1_ref[...] = x1
        centered, scale = norm_parts(x1)
        h_ref[...] = (centered * scale * vec_ref[2:3, :] + vec_ref[3:4, :]).astype(bf16)
        x2_ref[...] = x1 + vec_ref[7:8, :]

    up = mm(h_ref[...], wup_ref[...]) + vec_ref[pl.ds(11 + j, 1), :]
    up_ref[...] = up
    act = (0.5 * up * (1.0 + jnp.tanh(0.7978845608 * (up + 0.044715 * up * up * up)))).astype(bf16)
    act_ref[...] = act
    x2_ref[...] += mm(act, wdown_ref[...])

    @pl.when(j == FSTEPS - 1)
    def _():
        centered, scale = norm_parts(x2_ref[...])
        last = (centered * scale * vec_ref[4:5, :] + vec_ref[5:6, :]).astype(bf16)
        tokens = last.shape[0]
        places = lax.broadcasted_iota(i32, (pick_ref.shape[0], tokens), 1)
        chosen = (places == pick_ref[...]).astype(bf16)
        hp_ref[...] = mm(chosen, last).astype(bf16)


def mlp_forward(x0, y, wo, wup, wdown, vectors, picks):
    tokens = x0.shape[0]
    count = picks.shape[0]
    wide = pl.BlockSpec((tokens, D), lambda j: (0, j))
    shape = lambda cols, kind: jax.ShapeDtypeStruct((tokens, cols), kind)
    return pl.pallas_call(
        mlp_kernel,
        grid=(FSTEPS,),
        out_shape=[
            shape(D, f32),
            shape(D, bf16),
            shape(FF, f32),
            shape(FF, bf16),
            shape(D, f32),
            jax.ShapeDtypeStruct((count, D), bf16),
        ],
        in_specs=[
            full((tokens, D)),
            full((tokens, D)),
            full((D, D)),
            pl.BlockSpec((D, D), lambda j: (0, j)),
            pl.BlockSpec((D, D), lambda j: (j, 0)),
            full(vectors.shape),
            full((count, 1)),
        ],
        out_specs=[
            full((tokens, D)),
            full((tokens, D)),
            wide,
            wide,
            full((tokens, D)),
            full((count, D)),
        ],
        name="mlp_forward",
        cost_estimate=cost(2 * tokens * D * (2 * FF + D), 3e7, tokens * FF),
    )(x0, y, wo, wup, wdown, vectors, picks.reshape(count, 1))


def halve(core, tile, outs, slot, row, col):
    half = BS // 2
    near = pl.multiple_of(row * BS + core * half, half)
    far = pl.multiple_of(row * BS + (1 - core) * half, half)
    for start, out, top in ((near, outs[0], outs[2]), (far, outs[1], outs[3])):
        values = tile[pl.ds(start, half), pl.ds(col * BS, BS)]
        out[slot] = values
        top[slot] = jnp.max(jnp.abs(values), 0, keepdims=True)


def mlp_back_kernel(
    core_ref,
    ghp_ref,
    pick_ref,
    x2_ref,
    act_ref,
    up_ref,
    h_ref,
    x1_ref,
    wdown_ref,
    wup_ref,
    wo_ref,
    vec_ref,
    mine_ref,
    theirs_ref,
    mine_top_ref,
    theirs_top_ref,
    gx1_ref,
    ga_ref,
    gy_ref,
    vg_ref,
    gx2,
    gm,
    gh,
    tile_a,
    tile_b,
):
    j = pl.program_id(0)
    core = core_ref[0]
    tokens = x2_ref.shape[0]
    outs = (mine_ref, theirs_ref, mine_top_ref, theirs_top_ref)

    @pl.when(j == 0)
    def _():
        vg_ref[...] = jnp.zeros_like(vg_ref)
        places = lax.broadcasted_iota(i32, (tokens, pick_ref.shape[1]), 0)
        chosen = (places == pick_ref[...]).astype(bf16)
        rest = ghp_ref[...]
        spread = jnp.zeros((tokens, D), f32)
        for _ in range(3):
            part = rest.astype(bf16)
            rest = rest - part.astype(f32)
            spread = spread + mm(chosen, part)
        grad, gain, bias = norm_pull(x2_ref[...], vec_ref[4:5, :], spread)
        gx2[...] = grad
        low = grad.astype(bf16)
        gm[...] = low
        vg_ref[4:5, :] = gain
        vg_ref[5:6, :] = bias
        vg_ref[7:8, :] = jnp.sum(low.astype(f32), 0, keepdims=True)

    grad_act = mm_t(gm[...], wdown_ref[...])
    up = up_ref[...]
    turn = jnp.tanh(0.7978845608 * (up + 0.044715 * up * up * up))
    slope = 0.5 * (1.0 + turn) + 0.5 * up * (1.0 - turn * turn) * (
        0.7978845608 * (1.0 + 3.0 * 0.044715 * up * up)
    )
    gup = (grad_act * slope).astype(bf16)
    vg_ref[pl.ds(11 + j, 1), :] = jnp.sum(gup.astype(f32), 0, keepdims=True)
    part = mm_t(gup, wup_ref[...])

    @pl.when(j == 0)
    def _():
        gh[...] = part

    @pl.when(j > 0)
    def _():
        gh[...] += part

    tile_a[...] = mm_l(h_ref[...], gup)
    tile_b[...] = mm_l(act_ref[...], gm[...])
    for r in range(2):
        for c in range(2):
            halve(core, tile_a, outs, 2 * r + c, r, c)
            halve(core, tile_b, outs, 4 + 2 * r + c, r, c)

    @pl.when(j == FSTEPS - 1)
    def _():
        grad, gain, bias = norm_pull(x1_ref[...], vec_ref[2:3, :], gh[...])
        vg_ref[2:3, :] = gain
        vg_ref[3:4, :] = bias
        grad = grad + gx2[...]
        gx1_ref[...] = grad
        low = grad.astype(bf16)
        ga_ref[...] = low
        vg_ref[6:7, :] = jnp.sum(low.astype(f32), 0, keepdims=True)
        gy_ref[...] = mm_t(low, wo_ref[...]).astype(bf16)


def mlp_back(core, ghp, picks, x2, act, up, h2, x1, wdown, wup, wo, vectors):
    tokens = x2.shape[0]
    count = picks.shape[0]
    wide = pl.BlockSpec((tokens, D), lambda j: (0, j))
    flat = full((tokens, D))
    tiles = pl.BlockSpec((8, BS // 2, BS), lambda j: (j, 0, 0))
    tops = pl.BlockSpec((8, 1, BS), lambda j: (j, 0, 0))
    halves = jax.ShapeDtypeStruct((8 * FSTEPS, BS // 2, BS), f32)
    highs = jax.ShapeDtypeStruct((8 * FSTEPS, 1, BS), f32)
    return pl.pallas_call(
        mlp_back_kernel,
        grid=(FSTEPS,),
        out_shape=[
            halves,
            halves,
            highs,
            highs,
            jax.ShapeDtypeStruct((tokens, D), f32),
            jax.ShapeDtypeStruct((tokens, D), bf16),
            jax.ShapeDtypeStruct((tokens, D), bf16),
            jax.ShapeDtypeStruct((16, D), f32),
        ],
        in_specs=[
            pl.BlockSpec(memory_space=SMEM),
            full((count, D)),
            full((1, count)),
            flat,
            wide,
            wide,
            flat,
            flat,
            pl.BlockSpec((D, D), lambda j: (j, 0)),
            pl.BlockSpec((D, D), lambda j: (0, j)),
            full((D, D)),
            full(vectors.shape),
        ],
        out_specs=[tiles, tiles, tops, tops, flat, flat, flat, full((16, D))],
        scratch_shapes=[
            pltpu.VMEM((tokens, D), f32),
            pltpu.VMEM((tokens, D), bf16),
            pltpu.VMEM((tokens, D), f32),
            pltpu.VMEM((D, D), f32),
            pltpu.VMEM((D, D), f32),
        ],
        name="mlp_back",
        cost_estimate=cost(8 * tokens * D * FF, 5e7, tokens * FF),
    )(core, ghp, picks.reshape(1, count), x2, act, up, h2, x1, wdown, wup, wo, vectors)


def qkv_back_kernel(g_ref, w_ref, x_ref, gx1_ref, vec_ref, gx0_ref, vg_ref, gh):
    j = pl.program_id(0)
    part = mm_t(g_ref[0], w_ref[...])

    @pl.when(j == 0)
    def _():
        vg_ref[...] = jnp.zeros_like(vg_ref)
        gh[...] = part

    @pl.when(j > 0)
    def _():
        gh[...] += part

    vg_ref[pl.ds(8 + j, 1), :] = jnp.sum(g_ref[0].astype(f32), 0, keepdims=True)

    @pl.when(j == 2)
    def _():
        grad, gain, bias = norm_pull(x_ref[...].astype(f32), vec_ref[0:1, :], gh[...])
        vg_ref[0:1, :] = gain
        vg_ref[1:2, :] = bias
        gx0_ref[...] = (gx1_ref[...] + grad).astype(bf16)


def qkv_back(grads, wqkv, x0, gx1, vectors):
    tokens = x0.shape[0]
    flat = full((tokens, D))
    return pl.pallas_call(
        qkv_back_kernel,
        grid=(3,),
        out_shape=[
            jax.ShapeDtypeStruct((tokens, D), bf16),
            jax.ShapeDtypeStruct((16, D), f32),
        ],
        in_specs=[
            pl.BlockSpec((1, tokens, D), lambda j: (j, 0, 0)),
            pl.BlockSpec((D, D), lambda j: (0, j)),
            flat,
            flat,
            full(vectors.shape),
        ],
        out_specs=[flat, full((16, D))],
        scratch_shapes=[pltpu.VMEM((tokens, D), f32)],
        name="qkv_back",
        cost_estimate=cost(2 * tokens * D * 3 * D, 1e7),
    )(grads, wqkv, x0, gx1, vectors)


def qkv_weights_kernel(
    core_ref, h_ref, g_ref, y_ref, ga_ref, small_ref, mine_ref, theirs_ref, mtop_ref, ttop_ref, tile
):
    j = pl.program_id(0)
    core = core_ref[0]
    outs = (mine_ref, theirs_ref, mtop_ref, ttop_ref)

    @pl.when(j < 3)
    def _():
        tile[...] = mm_l(h_ref[...], g_ref[0])

    @pl.when(j == 3)
    def _():
        tile[...] = mm_l(y_ref[...], ga_ref[...])

    @pl.when(j < 4)
    def _():
        for r in range(2):
            for c in range(2):
                halve(core, tile, outs, 4 * j + 2 * r + c, r, c)

    @pl.when(j == 4)
    def _():
        halve(core, small_ref, outs, 16, 0, 0)


def qkv_weights(core, h1, grads, y, ga, small):
    tokens = h1.shape[0]
    flat = full((tokens, D))
    halves = (17, BS // 2, BS)
    highs = (17, 1, BS)
    shapes = (halves, halves, highs, highs)
    return pl.pallas_call(
        qkv_weights_kernel,
        grid=(5,),
        out_shape=[jax.ShapeDtypeStruct(shape, f32) for shape in shapes],
        in_specs=[
            pl.BlockSpec(memory_space=SMEM),
            flat,
            pl.BlockSpec((1, tokens, D), lambda j: (jnp.minimum(j, 2), 0, 0)),
            flat,
            flat,
            full((BS, BS)),
        ],
        out_specs=[full(shape) for shape in shapes],
        scratch_shapes=[pltpu.VMEM((D, D), f32)],
        name="qkv_weights",
        cost_estimate=cost(2 * tokens * D * 4 * D, 2e7),
    )(core, h1, grads, y, ga, small)


def comm_positions():
    order = []
    for j in range(FSTEPS):
        order += [16 + r * 8 + 2 * j + c for r in range(2) for c in range(2)]
        order += [32 + (2 * j + r) * 2 + c for r in range(2) for c in range(2)]
    for j in range(3):
        order += [r * 6 + 2 * j + c for r in range(2) for c in range(2)]
    order += [12 + r * 2 + c for r in range(2) for c in range(2)]
    positions = np.zeros(48, np.int32)
    positions[np.array(order)] = np.arange(48)
    return positions


def three(left, right, product):
    left_high, left_low = left
    right_high, right_low = right
    return (
        product(left_high, right_high)
        + product(left_high, right_low)
        + product(left_low, right_high)
    )


def shampoo_kernel(count, strip, places_ref, clip_ref, *refs):
    pieces = refs[:count]
    w_ref, ls_ref, rs_ref, lr_ref, rr_ref = refs[count : count + 5]
    g_ref, nw_ref, nl_ref, nr_ref = refs[count + 5 :]
    clip = clip_ref[0]
    for k in range(count):
        for half in range(2):
            place = pl.multiple_of(places_ref[2 * k + half], strip)
            g_ref[0, pl.ds(place, strip), :] = pieces[k][0, half] * clip
    grads = split_two(g_ref[0])
    nl_ref[0] = SHAMPOO_BETA * ls_ref[0] + (1.0 - SHAMPOO_BETA) * three(grads, grads, mm_t)
    nr_ref[0] = SHAMPOO_BETA * rs_ref[0] + (1.0 - SHAMPOO_BETA) * three(grads, grads, mm_l)
    turned = split_two(three(grads, split_two(rr_ref[0]), mm))
    direction = three(split_two(lr_ref[0]), turned, mm)
    weights = w_ref[0]
    nw_ref[0] = weights - RATE_BLOCKS * (direction + DECAY_RATE * weights)


def shampoo(places, clip, pieces, weights, left_stats, right_stats, left_roots, right_roots):
    slots = weights.shape[0]
    count = len(pieces)
    strip = pieces[0].shape[2]
    block = pl.BlockSpec((1, BS, BS), lambda s: (s, 0, 0))
    shape = jax.ShapeDtypeStruct((slots, BS, BS), f32)
    return pl.pallas_call(
        partial(shampoo_kernel, count, strip),
        grid=(slots,),
        out_shape=[shape] * 4,
        in_specs=[pl.BlockSpec(memory_space=SMEM)] * 2
        + [pl.BlockSpec((1, 2, strip, BS), lambda s: (s, 0, 0, 0))] * count
        + [block] * 5,
        out_specs=[block] * 4,
        name="shampoo",
        cost_estimate=cost(slots * 24 * BS**3, slots * BS * BS * 40),
    )(places, clip, *pieces, weights, left_stats, right_stats, left_roots, right_roots)


def adam_update(weight, first, second, gradient, rate, step_value):
    first_new = BETA_FIRST * first + (1.0 - BETA_FIRST) * gradient
    second_new = BETA_SECOND * second + (1.0 - BETA_SECOND) * gradient * gradient
    first_hat = first_new / (1.0 - BETA_FIRST**step_value)
    second_hat = second_new / (1.0 - BETA_SECOND**step_value)
    return (
        weight - rate * (first_hat / (jnp.sqrt(second_hat) + ADAM_EPSILON) + DECAY_RATE * weight),
        first_new,
        second_new,
    )


def tie(values, *others):
    return lax.optimization_barrier((values,) + others)[0]


LEVEL = 32768.0


def encode(values, bound):
    return (values * (LEVEL / jnp.maximum(bound, 1e-30))).astype(jnp.float16)


def decode(coded, bound):
    return coded.astype(f32) * (jnp.maximum(bound, 1e-30) * (1.0 / LEVEL))


def per_device(
    sizes,
    token_ids,
    seq_lengths,
    pick_rows,
    targets,
    step_count,
    block_order,
    slot_weights,
    left_stats,
    right_stats,
    left_roots,
    right_roots,
    embedding,
    embedding_first_moment,
    emb_second,
    vectors,
    vec_first,
    vec_second,
    feature_maps,
    map_first,
    map_second,
):
    ny, nc, n1, n0 = sizes
    n_dp, n_voc = ny * nc, n1 * n0
    dp_index, voc_index = lax.axis_index("dp"), lax.axis_index("vocab")
    y_at, c_at = dp_index // nc, dp_index % nc
    i1, i0 = voc_index // n0, voc_index % n0

    def over_dp(values, dy, dc):
        pairs = [
            (a * nc + b, ((a + dy) % ny) * nc + (b + dc) % nc) for a in range(ny) for b in range(nc)
        ]
        return lax.ppermute(values, "dp", pairs)

    def over_voc(values, d1, d0):
        pairs = [
            (a * n0 + b, ((a + d1) % n1) * n0 + (b + d0) % n0) for a in range(n1) for b in range(n0)
        ]
        return lax.ppermute(values, "vocab", pairs)

    def gather_voc(values):
        near = [values] + [over_voc(values, k, 0) for k in range(1, n1)]
        return [[part] + [over_voc(part, 0, k) for k in range(1, n0)] for part in near]

    def flat_gather(values):
        return [part for line in gather_voc(values) for part in line]

    def gather_y(values):
        return [values] + [over_dp(values, k, 0) for k in range(1, ny)]

    def line_up(parts, at):
        size = len(parts)
        return jnp.take(jnp.stack(parts), (at - jnp.arange(size)) % size, axis=0)

    tokens = token_ids.shape[0]
    picks_own = pick_rows.shape[0]
    devices_all = n_dp * n_voc
    total_picks = picks_own * devices_all
    coefficient = DISTILL_WEIGHT / (tokens * devices_all * HEADS)
    shard_rows, cols_own = embedding.shape
    cols_y = cols_own * nc
    vocab_start = (voc_index * shard_rows).astype(i32)
    per_owner = slot_weights.shape[0]
    block_count = block_order.shape[0]
    table_own = embedding.T
    relative = [((y_at - ky) % ny) * nc + (c_at + kc) % nc for kc in range(nc) for ky in range(ny)]
    relative = jnp.stack(relative)
    canonical = jnp.stack(
        [
            ((j % nc - c_at) % nc) * ny + (y_at - j // nc) % ny
            for j in range(n_dp)
        ]
    )

    ids_y = jnp.stack(gather_y(token_ids))
    ids_rows = jnp.concatenate(flat_gather(ids_y), 0).reshape(-1)
    targets_all = jnp.concatenate(flat_gather(targets), 0)
    local_ids = ids_rows - vocab_start
    packed_ids = jnp.where(
        (local_ids >= 0) & (local_ids < shard_rows),
        (local_ids << 16) | jnp.arange(ids_rows.shape[0], dtype=i32),
        -1,
    )
    hit_list, hit_count = find_hits(packed_ids, shard_rows)

    low_own = table_own.astype(bf16)
    low_other = over_dp(low_own, 0, 1)
    first_core = c_at == 0
    upright = jnp.concatenate(
        [jnp.where(first_core, low_own, low_other), jnp.where(first_core, low_other, low_own)], 0
    ).T

    slots_y = gather_y(slot_weights.astype(bf16))

    found = lookup(hit_list, hit_count, upright, ids_rows.shape[0])
    found = found.reshape(n1, n0, ny, tokens, cols_y)
    by_one = []
    for a in list(range(1, n1)) + [0]:
        part = found[a, 0]
        for b in range(1, n0):
            part = part + over_voc(found[a, b], 0, -b)
        by_one.append(part)
    mine = by_one[-1]
    for a in range(1, n1):
        mine = mine + over_voc(by_one[a - 1], -a, 0)

    slots_y = [slots_y[0]] + [tie(part, *by_one[:-1]) for part in slots_y[1:]]
    slots_core = [over_dp(part, 0, 1) for part in slots_y]
    inverse = (
        jnp.zeros((block_count,), i32).at[block_order].set(jnp.arange(block_count, dtype=i32))
    )
    owner = inverse // per_owner
    src = ((c_at - owner % nc) % nc) * ny + (y_at - owner // nc) % ny
    wqkv, wo, wup, wdown = place_blocks(
        src.astype(i32), inverse % per_owner, slots_y + slots_core
    )

    low_sent = tie(low_own, *slots_y[1:])
    low_y = [over_dp(low_sent, k, 0) for k in range(1, ny)]

    row_parts = [mine[0]] + [over_dp(mine[k], -k, 0) for k in range(1, ny)]
    if ny == 2:
        first = y_at == 0
        x0 = jnp.concatenate(
            [
                jnp.where(first, row_parts[0], row_parts[1]),
                jnp.where(first, row_parts[1], row_parts[0]),
            ],
            1,
        )
    else:
        stacked = jnp.stack(row_parts)
        x0 = jnp.concatenate(
            [jnp.take(stacked, (j - y_at) % ny, axis=0) for j in range(ny)], axis=1
        )

    maps_low = feature_maps.astype(bf16)
    both = jnp.concatenate([maps_low, -maps_low], -1).reshape(2, PAIRS, 2, HD, 2 * HD)
    empty = jnp.zeros_like(both[:, :, 0])
    lift_maps = jnp.stack(
        [
            jnp.concatenate([both[:, :, 0], empty], -2),
            jnp.concatenate([empty, both[:, :, 1]], -2),
        ],
        2,
    ).reshape(2, HEADS, 2 * HD, 2 * HD)
    h1, mixed = qkv_forward(x0, wqkv, vectors)
    y, distill = attend(seq_lengths, mixed, lift_maps)
    x1, h2, up, act, x2, picked = mlp_forward(x0, y, wo, wup, wdown, vectors, pick_rows)

    low_y = [tie(part, picked) for part in low_y]
    low_y_other = [over_dp(part, 0, 1) for part in low_y]
    table = jnp.concatenate([low_own] + low_y + [low_other] + low_y_other, 0)
    picked = jnp.take(picked.reshape(picks_own, n_dp, cols_own), relative, axis=1)
    picked = picked.reshape(picks_own, D)
    group = jnp.concatenate(flat_gather(picked), 0)
    local_targets = targets_all - vocab_start
    logits = mm(group, table)
    hit = jnp.arange(shard_rows, dtype=i32)[None, :] == local_targets[:, None]
    top = jnp.max(logits, 1)
    exp_sum = jnp.sum(jnp.exp(logits - top[:, None]), 1)
    chosen = jnp.sum(jnp.where(hit, logits, 0.0), 1)
    stats = jnp.stack([top, exp_sum, chosen]).reshape(3, n1, n0, picks_own)
    stats_all = gather_voc(stats)
    lined = jnp.stack(
        [jnp.roll(stats_all[a][b], (a, b), (1, 2)) for a in range(n1) for b in range(n0)]
    ).reshape(n_voc, 3, n_voc * picks_own)
    top_all = jnp.max(lined[:, 0], 0)
    sum_all = jnp.sum(lined[:, 1] * jnp.exp(lined[:, 0] - top_all[None]), 0)
    losses = top_all + jnp.log(sum_all) - jnp.sum(lined[:, 2], 0)
    loss_part = jnp.sum(losses[:picks_own]) / total_picks + coefficient * distill[0, 0]
    grad_logits = (
        (jnp.exp(logits - top_all[:, None]) * (1.0 / sum_all)[:, None] - hit) / total_picks
    ).astype(bf16)
    grad_group = mm_t(grad_logits, table).reshape(n1, n0, picks_own, D)
    by_one = []
    for a in list(range(1, n1)) + [0]:
        part = grad_group[a, 0]
        for b in range(1, n0):
            part = part + over_voc(grad_group[a, b], 0, -b)
        by_one.append(part)
    near_parts = [over_voc(by_one[a - 1], -a, 0) for a in range(1, n1)]

    lex_theirs = mm_l(group[:, D // nc :], grad_logits)
    lex_arrived = over_dp(lex_theirs, 0, 1)
    near_parts = [tie(part, lex_theirs) for part in near_parts]
    ghp = by_one[-1]
    for part in near_parts:
        ghp = ghp + part
    ghp = jnp.take(ghp.reshape(picks_own, n_dp, cols_own), canonical, axis=1)
    ghp = ghp.reshape(picks_own, D)
    lex_sums = mm_l(group[:, : D // nc], grad_logits) + lex_arrived
    lex = lex_sums[:cols_own]
    for k in range(1, ny):
        lex = lex + over_dp(lex_sums[k * cols_own : (k + 1) * cols_own], -k, 0)

    core = c_at.astype(i32).reshape(1)

    def reduce_blocks(mine_half, their_half, mine_top, their_top):
        part = mine_half + over_dp(their_half, 0, 1)
        bound = mine_top + over_dp(their_top, 0, 1)
        for size, at, far in ((n0, i0, 0), (n1, i1, 1)):
            rows = part.shape[1] // size
            total = lax.dynamic_slice_in_dim(part, at * rows, rows, 1)
            bound_next = bound
            for k in range(1, size):
                d1, d0 = (k, 0) if far else (0, k)
                piece = lax.dynamic_slice_in_dim(part, ((at + k) % size) * rows, rows, 1)
                coded = over_voc(encode(piece, bound), d1, d0)
                theirs = over_voc(bound, d1, d0)
                total = total + decode(coded, theirs)
                bound_next = bound_next + theirs
            part, bound = total, bound_next
        return part

    *halves_a, gx1, ga, gy, vg_a = mlp_back(
        core, ghp, pick_rows, x2, act, up, h2, x1, wdown, wup, wo, vectors
    )
    blocks_a = reduce_blocks(*halves_a)
    half_pairs = PAIRS // 2
    gqkv, map_q_a, map_k_a = attend_back(
        seq_lengths, mixed, gy, lift_maps, coefficient, 0, half_pairs, None
    )
    gqkv, map_q_b, map_k_b = attend_back(
        seq_lengths, mixed, gy, lift_maps, coefficient, half_pairs, half_pairs, gqkv
    )
    gx0, vg_b = qkv_back(gqkv, wqkv, x0, gx1, vectors)

    map_grads = jnp.concatenate([map_q_a, map_q_b, map_k_a, map_k_b], 0)
    vec_grads = (vg_a + vg_b)[:15]
    small_count = map_grads.size + vec_grads.size
    small = jnp.concatenate(
        [
            map_grads.reshape(-1),
            vec_grads.reshape(-1),
            jnp.zeros((BS * BS - small_count,), f32),
        ]
    ).reshape(BS, BS)
    blocks_b = reduce_blocks(*qkv_weights(core, h1, gqkv, y, ga, small))

    gx0_cols = gx0.reshape(tokens, ny, cols_y)
    arrived = [jnp.take(gx0_cols, y_at, axis=1)] + [
        over_dp(jnp.take(gx0_cols, (y_at + k) % ny, axis=1), k, 0) for k in range(1, ny)
    ]
    arrived = jnp.concatenate(arrived, 0).reshape(ny * tokens, nc, cols_own)
    rows_mine = jnp.take(arrived, c_at, axis=1)
    rows_other = over_dp(jnp.take(arrived, (c_at + 1) % nc, axis=1), 0, 1)
    if cols_own == 192:
        packed = jnp.concatenate(
            [
                rows_mine[:, :128],
                rows_other[:, :128],
                jnp.concatenate([rows_mine[:, 128:], rows_other[:, 128:]], 1),
            ],
            0,
        )
        pieces = flat_gather(packed)
        lists = (hit_list, hit_count, over_dp(hit_list, 0, 1), over_dp(hit_count, 0, 1))
        emb_grads, emb_square = scatter_rows(lists, lex, pieces)
        emb_square = emb_square[0, 0]
    else:
        packed = jnp.stack([rows_mine, rows_other])
        pieces = jnp.stack(flat_gather(packed), 1).reshape(-1, cols_own)
        local = jnp.concatenate([ids_rows, over_dp(ids_rows, 0, 1)]) - vocab_start
        local = jnp.where((local >= 0) & (local < shard_rows), local, shard_rows)
        emb_grads = lex.T.at[local].add(pieces.astype(f32), mode="drop").T
        emb_square = jnp.sum(emb_grads * emb_grads)

    blocks = jnp.concatenate([blocks_a, blocks_b], 0)
    slot_places = jnp.take(jnp.asarray(comm_positions()), block_order).reshape(
        ny, nc * per_owner
    )

    def slots_of(k):
        places = jnp.take(slot_places, (y_at + k) % ny, axis=0)
        return jnp.take(blocks, places, axis=0)

    strips = slots_of(0)
    small_parts = [blocks[block_count:]]
    for k in range(1, ny):
        moved = over_dp(jnp.concatenate([slots_of(k), blocks[block_count:]], 0), k, 0)
        strips = strips + moved[:-1]
        small_parts.append(moved[-1:])
    if ny == 2:
        small_sum = small_parts[0] + small_parts[1]
    else:
        small_sum = jnp.sum(line_up(small_parts, y_at), 0)
    strip_rows = strips.shape[1]
    strips = strips.reshape(nc, per_owner, strip_rows, BS)

    def with_small(k):
        return jnp.concatenate([jnp.take(strips, (c_at + k) % nc, axis=0), small_sum], 0)

    own_strips = jnp.stack([with_small(0), over_dp(with_small(1), 0, 1)], 1)
    strip_bound = jnp.max(jnp.abs(own_strips), 2, keepdims=True)
    coded_all = flat_gather(encode(own_strips, strip_bound))
    bound_all = flat_gather(strip_bound)
    strip_pieces = [decode(part, bound) for part, bound in zip(coded_all, bound_all)]

    square = emb_square + jnp.sum(strips * strips)
    square = square + jnp.where(y_at == 0, jnp.sum(small_sum * small_sum), 0.0)
    sums = jnp.pad(jnp.stack([square, loss_part]).reshape(1, 2), ((0, 7), (0, 126)))
    sums = sums + over_dp(sums, 0, 1)
    sums = jnp.sum(line_up(gather_y(sums), y_at), 0)
    sums = jnp.sum(line_up([sums] + [over_voc(sums, 0, k) for k in range(1, n0)], i0), 0)
    sums = jnp.sum(line_up([sums] + [over_voc(sums, k, 0) for k in range(1, n1)], i1), 0)
    grad_norm = jnp.sqrt(sums[0, 0])
    loss_total = sums[0, 1]
    clip_scale = CLIP_NORM / jnp.maximum(grad_norm, CLIP_NORM)

    small_all = jnp.stack([part[per_owner] for part in strip_pieces])
    small_all = small_all.reshape(n1, n0, nc, strip_rows, BS)
    small_all = jnp.take(small_all, (i1 - jnp.arange(n1)) % n1, axis=0)
    small_all = jnp.take(small_all, (i0 - jnp.arange(n0)) % n0, axis=1)
    small_all = jnp.take(small_all, (c_at - jnp.arange(nc)) % nc, axis=2)
    small_all = small_all.transpose(2, 1, 0, 3, 4).reshape(-1)
    map_sum = small_all[: map_grads.size].reshape(feature_maps.shape)
    vec_sum = small_all[map_grads.size : small_count].reshape(vectors.shape)

    strip_half = BS // nc
    if strip_rows % 8:
        whole = jnp.stack(strip_pieces).reshape(n1, n0, per_owner + 1, nc, strip_rows, BS)
        whole = jnp.take(whole, (i1 - jnp.arange(n1)) % n1, axis=0)
        whole = jnp.take(whole, (i0 - jnp.arange(n0)) % n0, axis=1)
        strip_pieces = [
            whole.transpose(2, 3, 1, 0, 4, 5).reshape(per_owner + 1, nc, strip_half, BS)
        ]
        bases = [0]
    else:
        bases = [
            ((i0 - b) % n0) * (strip_half // n0) + ((i1 - a) % n1) * strip_rows
            for a in range(n1)
            for b in range(n0)
        ]
    places = []
    for base in bases:
        places += [c_at * strip_half + base, ((c_at + 1) % nc) * strip_half + base]
    places = jnp.stack(places).astype(i32)
    clipped, new_slots, new_left, new_right = shampoo(
        places,
        clip_scale.reshape(1),
        strip_pieces,
        slot_weights,
        left_stats,
        right_stats,
        left_roots,
        right_roots,
    )
    step_value = step_count[0].astype(f32)
    emb_out = adam_update(
        table_own,
        embedding_first_moment.T,
        emb_second.T,
        emb_grads * clip_scale,
        RATE_TABLE,
        step_value,
    )
    vec_out = adam_update(
        vectors, vec_first, vec_second, vec_sum * clip_scale, RATE_VECTORS, step_value
    )
    map_out = adam_update(
        feature_maps, map_first, map_second, map_sum * clip_scale, RATE_MAPS, step_value
    )
    return (
        loss_total,
        grad_norm,
        clipped,
        new_slots,
        new_left,
        new_right,
        emb_out[0].T,
        emb_out[1].T,
        emb_out[2].T,
        vec_out[0],
        vec_out[1],
        vec_out[2],
        map_out[0],
        map_out[1],
        map_out[2],
    )


def solution(mesh):
    n_dp, n_voc = mesh.shape["dp"], mesh.shape["vocab"]
    sizes = (n_dp // 2, 2, 4, n_voc // 4)
    rows = P(("dp", "vocab"))
    blocks = P("dp", None, None)
    table = P("vocab", "dp")
    placed = (
        (rows, P(("dp", "vocab"), None), rows, rows, P(), P())
        + (blocks,) * 5
        + (table,) * 3
        + (P(),) * 6
    )
    return jax.shard_map(
        partial(per_device, sizes),
        mesh=mesh,
        in_specs=placed,
        out_specs=(P(), P()) + (blocks,) * 4 + (table,) * 3 + (P(),) * 6,
        check_vma=False,
    )
```

```python
from functools import partial

import jax
import jax.numpy as jnp
import numpy as np
from jax import lax
from jax.experimental import pallas as pl
from jax.experimental.pallas import tpu as pltpu
from jax.sharding import PartitionSpec as P

D = 768
HEADS = 12
HD = 64
FF = 3072
BS = 384
PAIRS = HEADS // 2

NORM_EPSILON = 1e-05
CLIP_NORM = 0.01
DISTILL_WEIGHT = 0.5
BETA_FIRST = 0.9
BETA_SECOND = 0.95
ADAM_EPSILON = 1e-08
DECAY_RATE = 0.01
SHAMPOO_BETA = 0.95
RATE_BLOCKS = 0.1
RATE_TABLE = 0.05
RATE_VECTORS = 0.2
RATE_MAPS = 0.1

f32 = jnp.float32
bf16 = jnp.bfloat16
i32 = jnp.int32
SMEM = pltpu.SMEM
ANY = pl.ANY


def mm(left, right):
    return lax.dot_general(left, right, (((1,), (0,)), ((), ())), preferred_element_type=f32)


def mm_t(left, right):
    return lax.dot_general(left, right, (((1,), (1,)), ((), ())), preferred_element_type=f32)


def mm_l(left, right):
    return lax.dot_general(left, right, (((0,), (0,)), ((), ())), preferred_element_type=f32)


def split_two(values):
    high = values.astype(bf16)
    return high, (values - high.astype(f32)).astype(bf16)


def full(shape):
    return pl.BlockSpec(shape, lambda *_: (0,) * len(shape))


def cost(flops, bytes_moved, transcendentals=0):
    return pl.CostEstimate(
        flops=int(flops * 0.02),
        bytes_accessed=int(bytes_moved * 0.02),
        transcendentals=int(transcendentals * 0.02),
    )


def place_kernel(piece_count, src_ref, off_ref, *refs):
    pieces = refs[:piece_count]
    outs = refs[piece_count : piece_count + 4]
    sems = refs[piece_count + 4]
    base = 0
    for out, rows, cols in zip(outs, (D, D, D, FF), (3 * D, D, FF, D)):
        wide = cols // BS
        count = (rows // BS) * wide

        def go(t, carry, out=out, wide=wide, base=base):
            k = base + t
            r0 = pl.multiple_of((t // wide) * BS, BS)
            c0 = pl.multiple_of((t % wide) * BS, BS)
            for p in range(piece_count):

                @pl.when(src_ref[k] == p)
                def _(p=p):
                    pltpu.make_async_copy(
                        pieces[p].at[off_ref[k]],
                        out.at[pl.ds(r0, BS), pl.ds(c0, BS)],
                        sems.at[k],
                    ).start()

            return carry

        lax.fori_loop(0, count, go, 0)
        base += count
    base = 0
    for out, rows, cols in zip(outs, (D, D, D, FF), (3 * D, D, FF, D)):
        count = (rows // BS) * (cols // BS)

        def done(t, carry, out=out, base=base):
            pltpu.make_async_copy(
                pieces[0].at[0], out.at[pl.ds(0, BS), pl.ds(0, BS)], sems.at[base + t]
            ).wait()
            return carry

        lax.fori_loop(0, count, done, 0)
        base += count


def place_blocks(src, off, pieces):
    count = len(pieces)
    return pl.pallas_call(
        partial(place_kernel, count),
        out_shape=[
            jax.ShapeDtypeStruct(shape, bf16)
            for shape in ((D, 3 * D), (D, D), (D, FF), (FF, D))
        ],
        in_specs=[pl.BlockSpec(memory_space=SMEM)] * 2 + [pl.BlockSpec(memory_space=ANY)] * count,
        out_specs=[pl.BlockSpec(memory_space=pltpu.VMEM)] * 4,
        scratch_shapes=[pltpu.SemaphoreType.DMA((48,))],
        name="place_blocks",
        cost_estimate=cost(0, 2 * 48 * BS * BS * 2),
    )(src, off, *pieces)


def hits_kernel(empty_row, packed_ref, list_ref):
    total = packed_ref.shape[0]

    def go(i, n):
        for u in range(16):
            entry = packed_ref[i * 16 + u]
            list_ref[n] = entry
            n = n + 1 + (entry >> 31)
        return n

    n = lax.fori_loop(0, total // 16, go, jnp.int32(0))
    list_ref[total + 8] = n
    for u in range(8):
        list_ref[n + u] = empty_row << 16


def find_hits(packed, empty_row):
    total = packed.shape[0]
    return pl.pallas_call(
        partial(hits_kernel, empty_row),
        out_shape=jax.ShapeDtypeStruct((total + 16,), i32),
        in_specs=[pl.BlockSpec(memory_space=SMEM)],
        out_specs=pl.BlockSpec(memory_space=SMEM),
        name="find_hits",
        cost_estimate=cost(1e10, total * 8),
    )(packed)


def turn_kernel(core_ref, own_ref, other_ref, out_ref):
    first = core_ref[0] == 0
    own, other = own_ref[...].astype(f32), other_ref[...].astype(f32)
    depth = own.shape[0]
    both = jnp.concatenate([jnp.where(first, own, other), jnp.where(first, other, own)], 0)
    out_ref[...] = both.T[:, : 2 * depth].astype(bf16)


def turn_table(core, own, other):
    depth, rows_all = own.shape
    wide = lane_block(rows_all)
    block = pl.BlockSpec((depth, wide), lambda j: (0, j))
    return pl.pallas_call(
        turn_kernel,
        grid=(pl.cdiv(rows_all, wide),),
        out_shape=jax.ShapeDtypeStruct((rows_all, 2 * depth), bf16),
        in_specs=[pl.BlockSpec(memory_space=SMEM), block, block],
        out_specs=pl.BlockSpec((wide, 2 * depth), lambda j: (j, 0)),
        name="turn_table",
        cost_estimate=cost(1e7, 1e7),
    )(core, own, other)


def lookup_kernel(rows_all, list_ref, table_ref, *refs):
    outs, (tab, acc) = refs[:-2], refs[-2:]
    total = acc.shape[0] - 8
    tab[pl.ds(0, rows_all), :] = table_ref[...].astype(f32)
    tab[pl.ds(rows_all, 8), :] = jnp.zeros((8, tab.shape[1]), f32)
    acc[...] = jnp.zeros(acc.shape, f32)

    def go(i, carry):
        for u in range(8):
            entry = list_ref[i * 8 + u]
            row = entry >> 16
            place = jnp.where(row < rows_all, entry & 0xFFFF, total)
            acc[pl.ds(place, 1), :] = tab[pl.ds(row, 1), :]
        return carry

    lax.fori_loop(0, (list_ref[total + 8] + 7) // 8, go, 0)
    each = outs[0].shape[0]
    for part, out in enumerate(outs):
        out[...] = acc[pl.ds(part * each, each), :].astype(bf16)


def lookup(hit_list, table, count, parts):
    rows_all, width = table.shape
    return pl.pallas_call(
        partial(lookup_kernel, rows_all),
        out_shape=[jax.ShapeDtypeStruct((count // parts, width), bf16)] * parts,
        in_specs=[
            pl.BlockSpec(memory_space=SMEM),
            pl.BlockSpec(memory_space=pltpu.VMEM),
        ],
        out_specs=[pl.BlockSpec(memory_space=pltpu.VMEM)] * parts,
        scratch_shapes=[
            pltpu.VMEM((rows_all + 8, width), f32),
            pltpu.VMEM((count + 8, width), f32),
        ],
        name="lookup",
        cost_estimate=cost(1e10, rows_all * width * 2),
    )(hit_list, table)


def scatter_kernel(piece_count, half, rows_all, starts, *refs):
    used = len(starts)
    lists = refs[:used]
    lex_ref = refs[used]
    pieces = refs[used + 1 : used + 1 + piece_count]
    out_ref, square_ref, acc, tail, wide, pair = refs[used + 1 + piece_count :]
    acc[...] = jnp.zeros(acc.shape, f32)
    tail[...] = jnp.zeros(tail.shape, f32)
    for k in range(piece_count):
        wide[pl.ds(k * 2 * half, 2 * half), :] = pieces[k][pl.ds(0, 2 * half), :].astype(f32)
        pair[pl.ds(k * half, half), :] = pieces[k][pl.ds(2 * half, half), :].astype(f32)
    upper = lax.broadcasted_iota(i32, (1, 128), 1) >= 64
    for which, (side, start) in enumerate(starts):
        own = upper if side else ~upper

        def go(i, carry, which=which, side=side, start=start, own=own):
            for u in range(8):
                entry = lists[which][i * 8 + u]
                row = entry >> 16
                p = (entry & 0xFFFF) + start
                q = (p // half) * half + p + side * half
                acc[pl.ds(row, 1), :] += wide[pl.ds(q, 1), :]
                tail[pl.ds(row, 1), :] += jnp.where(own, pair[pl.ds(p, 1), :], 0.0)
            return carry

        held = lists[which].shape[0] - 8
        lax.fori_loop(0, (lists[which][held] + 7) // 8, go, 0)
    chunks = rows_all // 128
    rest = rows_all - chunks * 128

    def turn(start, width):
        upright = acc[pl.ds(start, 128), :].T
        lower = tail[pl.ds(start, 128), :].T
        lower = lower[:64] + lower[64:]
        lanes = pl.ds(start, width)
        left = lex_ref[pl.ds(0, 128), lanes] + upright[:, :width]
        right = lex_ref[pl.ds(128, 64), lanes] + lower[:, :width]
        out_ref[pl.ds(0, 128), lanes] = left
        out_ref[pl.ds(128, 64), lanes] = right
        return jnp.sum(left * left, 0, keepdims=True), jnp.sum(right * right, 0, keepdims=True)

    def step(i, carry):
        left, right = turn(pl.multiple_of(i * 128, 128), 128)
        return carry + left + right

    squares = lax.fori_loop(0, chunks, step, jnp.zeros((1, 128), f32))
    total = jnp.sum(squares)
    if rest:
        left, right = turn(chunks * 128, rest)
        total = total + jnp.sum(left) + jnp.sum(right)
    square_ref[0, 0] = total


def scatter_rows(hits, lex, pieces, rows_all):
    lists, starts, start = [], [], 0
    for own_list, other_list in hits:
        lists += [own_list, other_list]
        starts += [(0, start), (1, start)]
        start += own_list.shape[0] - 16
    width = lex.shape[0]
    half = pieces[0].shape[0] // 3
    count = len(pieces)
    padded = (rows_all // 128 + 1) * 128
    return pl.pallas_call(
        partial(scatter_kernel, count, half, rows_all, tuple(starts)),
        out_shape=[
            jax.ShapeDtypeStruct((width, rows_all), f32),
            jax.ShapeDtypeStruct((1, 1), f32),
        ],
        in_specs=[pl.BlockSpec(memory_space=SMEM)] * len(lists)
        + [pl.BlockSpec(memory_space=pltpu.VMEM)] * (count + 1),
        out_specs=[
            pl.BlockSpec(memory_space=pltpu.VMEM),
            pl.BlockSpec(memory_space=SMEM),
        ],
        scratch_shapes=[
            pltpu.VMEM((padded, 128), f32),
            pltpu.VMEM((padded, 128), f32),
            pltpu.VMEM((count * 2 * half, 128), f32),
            pltpu.VMEM((count * half, 128), f32),
        ],
        name="scatter_rows",
        cost_estimate=cost(1.5e10, rows_all * width * 8),
    )(*lists, lex, *pieces)


def norm_parts(inputs):
    centered = inputs - jnp.mean(inputs, -1, keepdims=True)
    scale = lax.rsqrt(jnp.mean(centered * centered, -1, keepdims=True) + NORM_EPSILON)
    return centered, scale


def norm_pull(inputs, gain_row, grads):
    centered, scale = norm_parts(inputs)
    unit = centered * scale
    pulled = grads * gain_row
    lead = jnp.mean(pulled, -1, keepdims=True)
    along = jnp.mean(pulled * unit, -1, keepdims=True)
    grad_in = scale * (pulled - lead - unit * along)
    return (
        grad_in,
        jnp.sum(grads * unit, 0, keepdims=True),
        jnp.sum(grads, 0, keepdims=True),
    )


def qkv_kernel(x_ref, w_ref, vec_ref, h_ref, mixed_ref):
    j = pl.program_id(0)

    @pl.when(j == 0)
    def _():
        centered, scale = norm_parts(x_ref[...].astype(f32))
        h_ref[...] = (centered * scale * vec_ref[0:1, :] + vec_ref[1:2, :]).astype(bf16)

    mixed_ref[...] = (mm(h_ref[...], w_ref[...]) + vec_ref[pl.ds(8 + j, 1), :]).astype(bf16)


def qkv_forward(x0, wqkv, vectors):
    tokens = x0.shape[0]
    return pl.pallas_call(
        qkv_kernel,
        grid=(3,),
        out_shape=[
            jax.ShapeDtypeStruct((tokens, D), bf16),
            jax.ShapeDtypeStruct((tokens, 3 * D), bf16),
        ],
        in_specs=[
            full((tokens, D)),
            pl.BlockSpec((D, D), lambda j: (0, j)),
            full(vectors.shape),
        ],
        out_specs=[full((tokens, D)), pl.BlockSpec((tokens, D), lambda j: (0, j))],
        name="qkv_forward",
        cost_estimate=cost(2 * tokens * D * 3 * D, 8e6),
    )(x0, wqkv, vectors)


def feature_parts(values, lift, low_half):
    raw = mm(values, lift)
    top_a = jnp.max(jnp.where(low_half, raw, -jnp.inf), -1, keepdims=True)
    top_b = jnp.max(jnp.where(low_half, -jnp.inf, raw), -1, keepdims=True)
    grown = jnp.exp(raw - jnp.where(low_half, top_a, top_b))
    sum_a = jnp.sum(jnp.where(low_half, grown, 0.0), -1, keepdims=True)
    sum_b = jnp.sum(jnp.where(low_half, 0.0, grown), -1, keepdims=True)
    return grown / jnp.where(low_half, sum_a, sum_b)


def feature_pull(soft, grads, low_half):
    weighed = soft * grads
    sum_a = jnp.sum(jnp.where(low_half, weighed, 0.0), -1, keepdims=True)
    sum_b = jnp.sum(jnp.where(low_half, 0.0, weighed), -1, keepdims=True)
    pulled = soft * (grads - jnp.where(low_half, sum_a, sum_b))
    return (pulled - pltpu.roll(pulled, HD, 1)).astype(bf16)


def fill_allowed(len_ref, allow_ref):
    tokens = allow_ref.shape[0]
    first = len_ref[0, 0]
    second = first + len_ref[0, 1]
    third = second + len_ref[0, 2]

    def document(places):
        return (
            (places >= first).astype(i32)
            + (places >= second).astype(i32)
            + (places >= third).astype(i32)
        )

    rows = lax.broadcasted_iota(i32, (tokens, tokens), 0)
    cols = lax.broadcasted_iota(i32, (tokens, tokens), 1)
    allow_ref[...] = ((cols <= rows) & (document(rows) == document(cols))).astype(f32)


ROWS = 256


def attend_kernel(
    len_ref, q_ref, k_ref, v_ref, fq_ref, fk_ref, y_ref, distill_ref, allow_ref, lift_q, lift_k
):
    tokens = q_ref.shape[0]

    @pl.when(pl.program_id(0) == 0)
    def _():
        fill_allowed(len_ref, allow_ref)
        distill_ref[...] = jnp.zeros_like(distill_ref)

    low_half = lax.broadcasted_iota(i32, (1, 2 * HD), 1) < HD
    low_rows = lax.broadcasted_iota(i32, (ROWS, 2 * HD), 1) < HD
    total = jnp.zeros((1, 1), f32)
    for h in range(2):
        lift_q[h] = feature_parts(q_ref[...], fq_ref[h], low_half).astype(bf16)
        lift_k[h] = feature_parts(k_ref[...], fk_ref[h], low_half).astype(bf16)
    for begin in range(0, tokens, ROWS):
        width = begin + ROWS
        ok = allow_ref[pl.ds(begin, ROWS), pl.ds(0, width)] > 0.5
        queries = q_ref[pl.ds(begin, ROWS), :] * jnp.asarray(HD**-0.5, bf16)
        keys = k_ref[pl.ds(0, width), :]
        values = v_ref[pl.ds(0, width), :]
        parts = []
        for h in range(2):
            own = low_rows if h == 0 else ~low_rows
            scores = mm_t(jnp.where(own, queries, jnp.zeros_like(queries)), keys)
            scores = jnp.where(ok, scores, -1e30)
            grown = jnp.exp(scores - jnp.max(scores, -1, keepdims=True))
            inverse = 1.0 / jnp.sum(grown, -1, keepdims=True)
            similar = mm_t(lift_q[h, pl.ds(begin, ROWS), :], lift_k[h, pl.ds(0, width), :])
            kept = jnp.where(ok, similar, 0.0)
            sums = jnp.sum(kept, -1, keepdims=True)
            weights = (kept * (1.0 / sums)).astype(bf16)
            parts.append(mm(weights, values))
            logs = jnp.log(jnp.where(ok, similar, 1.0))
            row_terms = jnp.log(sums) - jnp.sum(grown * logs, -1, keepdims=True) * inverse
            total = total + jnp.sum(row_terms, 0, keepdims=True)
        y_ref[pl.ds(begin, ROWS), :] = jnp.where(low_rows, parts[0], parts[1]).astype(bf16)
    distill_ref[...] += jnp.broadcast_to(total, distill_ref.shape)


def attend(lengths, mixed, lift_maps):
    tokens = mixed.shape[0]
    column = lambda base: pl.BlockSpec((tokens, 2 * HD), lambda g: (0, base + g))
    maps = pl.BlockSpec((2, 2 * HD, 2 * HD), lambda g: (g, 0, 0))
    return pl.pallas_call(
        attend_kernel,
        grid=(PAIRS,),
        out_shape=[
            jax.ShapeDtypeStruct((tokens, D), bf16),
            jax.ShapeDtypeStruct((8, 128), f32),
        ],
        in_specs=[
            pl.BlockSpec(memory_space=SMEM),
            column(0),
            column(PAIRS),
            column(2 * PAIRS),
            maps,
            maps,
        ],
        out_specs=[column(0), full((8, 128))],
        scratch_shapes=[
            pltpu.VMEM((tokens, tokens), f32),
            pltpu.VMEM((2, tokens, 2 * HD), bf16),
            pltpu.VMEM((2, tokens, 2 * HD), bf16),
        ],
        name="attend",
        cost_estimate=cost(1.2e10, 4e6, 6e6),
    )(lengths, mixed, mixed, mixed, lift_maps[0], lift_maps[1])


def attend_back_kernel(
    coefficient,
    later,
    len_ref,
    q_ref,
    k_ref,
    v_ref,
    gy_ref,
    fq_ref,
    fk_ref,
    *refs,
):
    g_ref, gq_map_ref, gk_map_ref, allow_ref, soft_q, soft_k, grad_q, grad_k, grad_v = refs[later:]
    tokens = q_ref.shape[0]

    @pl.when(pl.program_id(0) == 0)
    def _():
        fill_allowed(len_ref, allow_ref)

    low_half = lax.broadcasted_iota(i32, (1, 2 * HD), 1) < HD
    low_rows = lax.broadcasted_iota(i32, (ROWS, 2 * HD), 1) < HD
    for h in range(2):
        soft_q[h] = feature_parts(q_ref[...], fq_ref[h], low_half)
        soft_k[h] = feature_parts(k_ref[...], fk_ref[h], low_half)
    for step, begin in enumerate(reversed(range(0, tokens, ROWS))):
        width = begin + ROWS
        ok = allow_ref[pl.ds(begin, ROWS), pl.ds(0, width)] > 0.5
        queries = q_ref[pl.ds(begin, ROWS), :] * jnp.asarray(HD**-0.5, bf16)
        keys = k_ref[pl.ds(0, width), :]
        values = v_ref[pl.ds(0, width), :]
        grads = gy_ref[pl.ds(begin, ROWS), :]
        value_sum = None
        for h in range(2):
            own = low_rows if h == 0 else ~low_rows
            scores = mm_t(jnp.where(own, queries, jnp.zeros_like(queries)), keys)
            scores = jnp.where(ok, scores, -1e30)
            grown = jnp.exp(scores - jnp.max(scores, -1, keepdims=True))
            teach = grown * (coefficient / jnp.sum(grown, -1, keepdims=True))
            phi_q = soft_q[h, pl.ds(begin, ROWS), :].astype(bf16)
            phi_k = soft_k[h, pl.ds(0, width), :].astype(bf16)
            similar = mm_t(phi_q, phi_k)
            kept = jnp.where(ok, similar, 0.0)
            inverse = 1.0 / jnp.sum(kept, -1, keepdims=True)
            weights = kept * inverse
            own_grads = jnp.where(own, grads, jnp.zeros_like(grads))
            grad_w = mm_t(own_grads, values)
            row_sum = jnp.sum(grad_w * weights, -1, keepdims=True)
            grad_sums = (coefficient - row_sum) * inverse
            grad_sim = jnp.where(
                ok,
                grad_w * inverse - teach / jnp.where(ok, similar, 1.0) + grad_sums,
                0.0,
            ).astype(bf16)
            grad_q[h, pl.ds(begin, ROWS), :] = mm(grad_sim, phi_k)
            part_k = mm_l(grad_sim, phi_q)
            part_v = mm_l(weights.astype(bf16), own_grads)
            value_sum = part_v if value_sum is None else value_sum + part_v
            if step == 0:
                grad_k[h] = part_k
            else:
                grad_k[h, pl.ds(0, width), :] += part_k
        if step == 0:
            grad_v[...] = value_sum
        else:
            grad_v[pl.ds(0, width), :] += value_sum
    for slot, own_ref, map_ref, soft, grad, out in (
        (0, q_ref, fq_ref, soft_q, grad_q, gq_map_ref),
        (1, k_ref, fk_ref, soft_k, grad_k, gk_map_ref),
    ):
        result = None
        for h in range(2):
            pulled = feature_pull(soft[h], grad[h], low_half)
            back = mm_t(pulled, map_ref[h]) * 0.5
            result = back if result is None else result + back
            out[h] = mm_l(own_ref[...], pulled)[h * HD : (h + 1) * HD, :HD]
        g_ref[slot] = result.astype(bf16)
    g_ref[2] = grad_v[...].astype(bf16)


def attend_back(lengths, mixed, grad_y, lift_maps, coefficient, start, pairs, before):
    tokens = mixed.shape[0]
    column = lambda base: pl.BlockSpec((tokens, 2 * HD), lambda g: (0, base + start + g))
    maps = pl.BlockSpec((2, 2 * HD, 2 * HD), lambda g: (start + g, 0, 0))
    small = pl.BlockSpec((2, HD, HD), lambda g: (g, 0, 0))
    wide = (2, tokens, 2 * HD)
    later = before is not None
    return pl.pallas_call(
        partial(attend_back_kernel, coefficient, int(later)),
        grid=(pairs,),
        out_shape=[
            jax.ShapeDtypeStruct((3, tokens, D), bf16),
            jax.ShapeDtypeStruct((2 * pairs, HD, HD), f32),
            jax.ShapeDtypeStruct((2 * pairs, HD, HD), f32),
        ],
        in_specs=[
            pl.BlockSpec(memory_space=SMEM),
            column(0),
            column(PAIRS),
            column(2 * PAIRS),
            column(0),
            maps,
            maps,
        ]
        + [pl.BlockSpec(memory_space=ANY)] * later,
        out_specs=[
            pl.BlockSpec((3, tokens, 2 * HD), lambda g: (0, 0, start + g)),
            small,
            small,
        ],
        scratch_shapes=[
            pltpu.VMEM((tokens, tokens), f32),
            pltpu.VMEM(wide, f32),
            pltpu.VMEM(wide, f32),
            pltpu.VMEM(wide, f32),
            pltpu.VMEM(wide, f32),
            pltpu.VMEM((tokens, 2 * HD), f32),
        ],
        input_output_aliases={7: 0} if later else {},
        name="attend_back",
        cost_estimate=cost(1.2e10, 4e6, 3e6),
    )(lengths, mixed, mixed, mixed, grad_y, lift_maps[0], lift_maps[1], *([before] * later))


FSTEPS = FF // D


def mlp_kernel(
    x_ref,
    y_ref,
    wo_ref,
    wup_ref,
    wdown_ref,
    vec_ref,
    pick_ref,
    x1_ref,
    h_ref,
    up_ref,
    act_ref,
    x2_ref,
    hp_ref,
):
    j = pl.program_id(0)

    @pl.when(j == 0)
    def _():
        x1 = x_ref[...].astype(f32) + mm(y_ref[...], wo_ref[...]) + vec_ref[6:7, :]
        x1_ref[...] = x1
        centered, scale = norm_parts(x1)
        h_ref[...] = (centered * scale * vec_ref[2:3, :] + vec_ref[3:4, :]).astype(bf16)
        x2_ref[...] = x1 + vec_ref[7:8, :]

    up = mm(h_ref[...], wup_ref[...]) + vec_ref[pl.ds(11 + j, 1), :]
    up_ref[...] = up
    act = (0.5 * up * (1.0 + jnp.tanh(0.7978845608 * (up + 0.044715 * up * up * up)))).astype(bf16)
    act_ref[...] = act
    x2_ref[...] += mm(act, wdown_ref[...])

    @pl.when(j == FSTEPS - 1)
    def _():
        centered, scale = norm_parts(x2_ref[...])
        last = (centered * scale * vec_ref[4:5, :] + vec_ref[5:6, :]).astype(bf16)
        tokens = last.shape[0]
        places = lax.broadcasted_iota(i32, (pick_ref.shape[0], tokens), 1)
        chosen = (places == pick_ref[...]).astype(bf16)
        hp_ref[...] = mm(chosen, last).astype(bf16)


def mlp_forward(x0, y, wo, wup, wdown, vectors, picks):
    tokens = x0.shape[0]
    count = picks.shape[0]
    wide = pl.BlockSpec((tokens, D), lambda j: (0, j))
    shape = lambda cols, kind: jax.ShapeDtypeStruct((tokens, cols), kind)
    return pl.pallas_call(
        mlp_kernel,
        grid=(FSTEPS,),
        out_shape=[
            shape(D, f32),
            shape(D, bf16),
            shape(FF, f32),
            shape(FF, bf16),
            shape(D, f32),
            jax.ShapeDtypeStruct((count, D), bf16),
        ],
        in_specs=[
            full((tokens, D)),
            full((tokens, D)),
            full((D, D)),
            pl.BlockSpec((D, D), lambda j: (0, j)),
            pl.BlockSpec((D, D), lambda j: (j, 0)),
            full(vectors.shape),
            full((count, 1)),
        ],
        out_specs=[
            full((tokens, D)),
            full((tokens, D)),
            wide,
            wide,
            full((tokens, D)),
            full((count, D)),
        ],
        name="mlp_forward",
        cost_estimate=cost(2 * tokens * D * (2 * FF + D), 3e7, tokens * FF),
    )(x0, y, wo, wup, wdown, vectors, picks.reshape(count, 1))


def keep_tiles(values, out, top, slot):
    for c in range(2):
        out[slot + c] = values[:, c * BS : (c + 1) * BS]
    high = jnp.max(jnp.abs(values), 0, keepdims=True)
    top[...] = jnp.maximum(top[...], jnp.maximum(high[:, :BS], high[:, BS:]))


def near_far(core):
    return pl.ds(pl.multiple_of(core * BS, BS), BS), pl.ds(pl.multiple_of((1 - core) * BS, BS), BS)


def mlp_back_kernel(
    core_ref,
    ghp_ref,
    pick_ref,
    x2_ref,
    act_ref,
    up_ref,
    h_ref,
    x1_ref,
    wdown_ref,
    wup_ref,
    wo_ref,
    vec_ref,
    mine_ref,
    theirs_ref,
    mine_top_ref,
    theirs_top_ref,
    gx1_ref,
    ga_ref,
    gy_ref,
    vg_ref,
    gx2,
    gm,
    gh,
):
    j = pl.program_id(0)
    core = core_ref[0]
    tokens = x2_ref.shape[0]

    @pl.when(j == 0)
    def _():
        mine_top_ref[...] = jnp.zeros_like(mine_top_ref)
        theirs_top_ref[...] = jnp.zeros_like(theirs_top_ref)
        vg_ref[...] = jnp.zeros_like(vg_ref)
        places = lax.broadcasted_iota(i32, (tokens, pick_ref.shape[1]), 0)
        chosen = (places == pick_ref[...]).astype(bf16)
        rest = ghp_ref[...]
        spread = jnp.zeros((tokens, D), f32)
        for _ in range(3):
            part = rest.astype(bf16)
            rest = rest - part.astype(f32)
            spread = spread + mm(chosen, part)
        grad, gain, bias = norm_pull(x2_ref[...], vec_ref[4:5, :], spread)
        gx2[...] = grad
        low = grad.astype(bf16)
        gm[...] = low
        vg_ref[4:5, :] = gain
        vg_ref[5:6, :] = bias
        vg_ref[7:8, :] = jnp.sum(low.astype(f32), 0, keepdims=True)

    grad_act = mm_t(gm[...], wdown_ref[...])
    up = up_ref[...]
    turn = jnp.tanh(0.7978845608 * (up + 0.044715 * up * up * up))
    slope = 0.5 * (1.0 + turn) + 0.5 * up * (1.0 - turn * turn) * (
        0.7978845608 * (1.0 + 3.0 * 0.044715 * up * up)
    )
    gup = (grad_act * slope).astype(bf16)
    vg_ref[pl.ds(11 + j, 1), :] = jnp.sum(gup.astype(f32), 0, keepdims=True)
    part = mm_t(gup, wup_ref[...])

    @pl.when(j == 0)
    def _():
        gh[...] = part

    @pl.when(j > 0)
    def _():
        gh[...] += part

    for cols, out, top in zip(
        near_far(core), (mine_ref, theirs_ref), (mine_top_ref, theirs_top_ref)
    ):
        keep_tiles(mm_l(h_ref[:, cols], gup), out, top, 0)
        keep_tiles(mm_l(act_ref[:, cols], gm[...]), out, top, 2)

    @pl.when(j == FSTEPS - 1)
    def _():
        grad, gain, bias = norm_pull(x1_ref[...], vec_ref[2:3, :], gh[...])
        vg_ref[2:3, :] = gain
        vg_ref[3:4, :] = bias
        grad = grad + gx2[...]
        gx1_ref[...] = grad
        low = grad.astype(bf16)
        ga_ref[...] = low
        vg_ref[6:7, :] = jnp.sum(low.astype(f32), 0, keepdims=True)
        gy_ref[...] = mm_t(low, wo_ref[...]).astype(bf16)


def mlp_back(core, ghp, picks, x2, act, up, h2, x1, wdown, wup, wo, vectors):
    tokens = x2.shape[0]
    count = picks.shape[0]
    wide = pl.BlockSpec((tokens, D), lambda j: (0, j))
    flat = full((tokens, D))
    tiles = pl.BlockSpec((4, BS, BS), lambda j: (j, 0, 0))
    tops = full((1, BS))
    halves = jax.ShapeDtypeStruct((4 * FSTEPS, BS, BS), f32)
    highs = jax.ShapeDtypeStruct((1, BS), f32)
    return pl.pallas_call(
        mlp_back_kernel,
        grid=(FSTEPS,),
        out_shape=[
            halves,
            halves,
            highs,
            highs,
            jax.ShapeDtypeStruct((tokens, D), f32),
            jax.ShapeDtypeStruct((tokens, D), bf16),
            jax.ShapeDtypeStruct((tokens, D), bf16),
            jax.ShapeDtypeStruct((16, D), f32),
        ],
        in_specs=[
            pl.BlockSpec(memory_space=SMEM),
            full((count, D)),
            full((1, count)),
            flat,
            wide,
            wide,
            flat,
            flat,
            pl.BlockSpec((D, D), lambda j: (j, 0)),
            pl.BlockSpec((D, D), lambda j: (0, j)),
            full((D, D)),
            full(vectors.shape),
        ],
        out_specs=[tiles, tiles, tops, tops, flat, flat, flat, full((16, D))],
        scratch_shapes=[
            pltpu.VMEM((tokens, D), f32),
            pltpu.VMEM((tokens, D), bf16),
            pltpu.VMEM((tokens, D), f32),
        ],
        name="mlp_back",
        cost_estimate=cost(8 * tokens * D * FF, 5e7, tokens * FF),
    )(core, ghp, picks.reshape(1, count), x2, act, up, h2, x1, wdown, wup, wo, vectors)


def qkv_back_kernel(g_ref, w_ref, x_ref, gx1_ref, vec_ref, gx0_ref, vg_ref, gh):
    j = pl.program_id(0)
    part = mm_t(g_ref[0], w_ref[...])

    @pl.when(j == 0)
    def _():
        vg_ref[...] = jnp.zeros_like(vg_ref)
        gh[...] = part

    @pl.when(j > 0)
    def _():
        gh[...] += part

    vg_ref[pl.ds(8 + j, 1), :] = jnp.sum(g_ref[0].astype(f32), 0, keepdims=True)

    @pl.when(j == 2)
    def _():
        grad, gain, bias = norm_pull(x_ref[...].astype(f32), vec_ref[0:1, :], gh[...])
        vg_ref[0:1, :] = gain
        vg_ref[1:2, :] = bias
        gx0_ref[...] = (gx1_ref[...] + grad).astype(bf16)


def qkv_back(grads, wqkv, x0, gx1, vectors):
    tokens = x0.shape[0]
    flat = full((tokens, D))
    return pl.pallas_call(
        qkv_back_kernel,
        grid=(3,),
        out_shape=[
            jax.ShapeDtypeStruct((tokens, D), bf16),
            jax.ShapeDtypeStruct((16, D), f32),
        ],
        in_specs=[
            pl.BlockSpec((1, tokens, D), lambda j: (j, 0, 0)),
            pl.BlockSpec((D, D), lambda j: (0, j)),
            flat,
            flat,
            full(vectors.shape),
        ],
        out_specs=[flat, full((16, D))],
        scratch_shapes=[pltpu.VMEM((tokens, D), f32)],
        name="qkv_back",
        cost_estimate=cost(2 * tokens * D * 3 * D, 1e7),
    )(grads, wqkv, x0, gx1, vectors)


def qkv_weights_kernel(
    core_ref, h_ref, g_ref, y_ref, ga_ref, small_ref, mine_ref, theirs_ref, mtop_ref, ttop_ref
):
    j = pl.program_id(0)
    core = core_ref[0]
    both = tuple(zip(near_far(core), (mine_ref, theirs_ref), (mtop_ref, ttop_ref)))

    @pl.when(j == 0)
    def _():
        for turn, (_, out, top) in enumerate(both):
            values = small_ref[core if turn == 0 else 1 - core]
            out[8] = values
            top[...] = jnp.max(jnp.abs(values), 0, keepdims=True)

    @pl.when(j < 3)
    def _():
        for cols, out, top in both:
            keep_tiles(mm_l(h_ref[:, cols], g_ref[0]), out, top, 2 * j)

    @pl.when(j == 3)
    def _():
        for cols, out, top in both:
            keep_tiles(mm_l(y_ref[:, cols], ga_ref[...]), out, top, 6)


def qkv_weights(core, h1, grads, y, ga, small):
    tokens = h1.shape[0]
    flat = full((tokens, D))
    halves = (9, BS, BS)
    highs = (1, BS)
    shapes = (halves, halves, highs, highs)
    return pl.pallas_call(
        qkv_weights_kernel,
        grid=(4,),
        out_shape=[jax.ShapeDtypeStruct(shape, f32) for shape in shapes],
        in_specs=[
            pl.BlockSpec(memory_space=SMEM),
            flat,
            pl.BlockSpec((1, tokens, D), lambda j: (jnp.minimum(j, 2), 0, 0)),
            flat,
            flat,
            full((2, BS, BS)),
        ],
        out_specs=[full(shape) for shape in shapes],
        name="qkv_weights",
        cost_estimate=cost(2 * tokens * D * 4 * D, 2e7),
    )(core, h1, grads, y, ga, small)


def comm_positions():
    side = np.zeros(48, np.int32)
    place = np.zeros(48, np.int32)
    for r in range(2):
        for c in range(2):
            for j in range(FSTEPS):
                place[16 + r * 8 + 2 * j + c] = 4 * j + c
                place[32 + (2 * j + r) * 2 + c] = 4 * j + 2 + c
                side[16 + r * 8 + 2 * j + c] = side[32 + (2 * j + r) * 2 + c] = r
            for j in range(3):
                place[r * 6 + 2 * j + c] = 16 + 2 * j + c
                side[r * 6 + 2 * j + c] = r
            place[12 + r * 2 + c] = 22 + c
            side[12 + r * 2 + c] = r
    return side, place


def lane_block(rows_all):
    return min(1280, (rows_all // 128 + 1) * 128)


def fill_table(places_ref, pieces, tab, valid):
    depth = pieces[0].shape[0]
    for p, piece in enumerate(pieces):
        start = pl.multiple_of(places_ref[p], depth)
        tab[pl.ds(start, depth), :] = jnp.where(valid, piece[...], jnp.zeros((), bf16))


def logits_kernel(rows_all, count, places_ref, group_ref, target_ref, *refs):
    pieces = refs[:count]
    logit_ref, stat_ref, tab, top, total, chosen = refs[count:]
    j = pl.program_id(0)
    wide = tab.shape[1]
    lane = lax.broadcasted_iota(i32, (1, wide), 1) + j * wide
    valid = lane < rows_all
    fill_table(places_ref, pieces, tab, valid)

    @pl.when(j == 0)
    def _():
        top[...] = jnp.full(top.shape, -jnp.inf, f32)
        total[...] = jnp.zeros(total.shape, f32)
        chosen[...] = jnp.zeros(chosen.shape, f32)

    logits = mm(group_ref[...], tab[...])
    logit_ref[...] = logits
    kept = jnp.where(valid, logits, -jnp.inf)
    before = top[...]
    after = jnp.maximum(before, jnp.max(kept, -1, keepdims=True))
    top[...] = after
    total[...] = total[...] * jnp.exp(before - after) + jnp.sum(
        jnp.exp(kept - after), -1, keepdims=True
    )
    hit = (lane == target_ref[...]) & valid
    chosen[...] += jnp.sum(jnp.where(hit, logits, 0.0), -1, keepdims=True)

    @pl.when(j == pl.num_programs(0) - 1)
    def _():
        spot = lax.broadcasted_iota(i32, (1, 128), 1)
        merged = jnp.where(
            spot == 0, top[...], jnp.where(spot == 1, total[...], chosen[...])
        )
        stat_ref[...] = merged.T[:8]


def table_specs(pieces, wide):
    return [pl.BlockSpec((pieces[0].shape[0], wide), lambda j: (0, j))] * len(pieces)


def vocabulary_logits(places, group, local_targets, pieces):
    count, rows_all = group.shape[0], pieces[0].shape[1]
    wide = lane_block(rows_all)
    return pl.pallas_call(
        partial(logits_kernel, rows_all, len(pieces)),
        grid=(pl.cdiv(rows_all, wide),),
        out_shape=[
            jax.ShapeDtypeStruct((count, rows_all), f32),
            jax.ShapeDtypeStruct((8, count), f32),
        ],
        in_specs=[pl.BlockSpec(memory_space=SMEM), full((count, D)), full((count, 1))]
        + table_specs(pieces, wide),
        out_specs=[pl.BlockSpec((count, wide), lambda j: (0, j)), full((8, count))],
        scratch_shapes=[pltpu.VMEM((D, wide), bf16)] + [pltpu.VMEM((count, 1), f32)] * 3,
        name="vocabulary_logits",
        cost_estimate=cost(2 * count * D * rows_all, 2e7, count * rows_all),
    )(places, group, local_targets.reshape(count, 1), *pieces)


def vocabulary_back_kernel(
    rows_all, count, scale, places_ref, logit_ref, stat_ref, target_ref, *refs
):
    pieces = refs[:count]
    grad_ref, ghp_ref, tab, stat = refs[count:]
    j = pl.program_id(0)
    wide = tab.shape[1]
    lane = lax.broadcasted_iota(i32, (1, wide), 1) + j * wide
    valid = lane < rows_all
    fill_table(places_ref, pieces, tab, valid)

    @pl.when(j == 0)
    def _():
        stat[...] = stat_ref[...].T
        ghp_ref[...] = jnp.zeros_like(ghp_ref)

    hit = (lane == target_ref[...]).astype(f32)
    soft = jnp.exp(logit_ref[...] - stat[:, 0:1]) * stat[:, 1:2]
    grads = jnp.where(valid, (soft - hit) * scale, 0.0).astype(bf16)
    grad_ref[...] = grads
    ghp_ref[...] += mm_t(grads, tab[...])


def vocabulary_back(places, logits, stats, local_targets, pieces, scale):
    count, rows_all = logits.shape
    wide = lane_block(rows_all)
    block = pl.BlockSpec((count, wide), lambda j: (0, j))
    return pl.pallas_call(
        partial(vocabulary_back_kernel, rows_all, len(pieces), scale),
        grid=(pl.cdiv(rows_all, wide),),
        out_shape=[
            jax.ShapeDtypeStruct((count, pl.cdiv(rows_all, wide) * wide), bf16),
            jax.ShapeDtypeStruct((count, D), f32),
        ],
        in_specs=[
            pl.BlockSpec(memory_space=SMEM),
            block,
            full(stats.shape),
            full((count, 1)),
        ]
        + table_specs(pieces, wide),
        out_specs=[block, full((count, D))],
        scratch_shapes=[pltpu.VMEM((D, wide), bf16), pltpu.VMEM((count, stats.shape[0]), f32)],
        name="vocabulary_back",
        cost_estimate=cost(2 * count * D * rows_all, 3e7, count * rows_all),
    )(places, logits, stats, local_targets.reshape(count, 1), *pieces)


def lexicon_kernel(
    depth, places_ref, turned_ref, grad_ref, mine_ref, theirs_ref, mtop_ref, ttop_ref, sel
):
    j = pl.program_id(0)
    half = mine_ref.shape[0]

    @pl.when(j == 0)
    def _():
        for p in range(sel.shape[0] // depth):
            start = pl.multiple_of(places_ref[p], depth)
            sel[pl.ds(p * depth, depth), :] = turned_ref[pl.ds(start, depth), :]
        mtop_ref[...] = jnp.zeros_like(mtop_ref)
        ttop_ref[...] = jnp.zeros_like(ttop_ref)

    for start, out, top in ((0, mine_ref, mtop_ref), (half, theirs_ref, ttop_ref)):
        part = mm(sel[pl.ds(start, half), :], grad_ref[...])
        out[...] = part
        top[...] = jnp.maximum(top[...], jnp.max(jnp.abs(part), 0, keepdims=True))


def lexicon(places, turned, grads, depth, rows_all):
    count, padded = grads.shape
    wide = lane_block(rows_all)
    half = D // 2
    block = pl.BlockSpec((half, wide), lambda j: (0, j))
    return pl.pallas_call(
        partial(lexicon_kernel, depth),
        grid=(padded // wide,),
        out_shape=[jax.ShapeDtypeStruct((half, padded), f32)] * 2
        + [jax.ShapeDtypeStruct((1, wide), f32)] * 2,
        in_specs=[
            pl.BlockSpec(memory_space=SMEM),
            full((D, count)),
            pl.BlockSpec((count, wide), lambda j: (0, j)),
        ],
        out_specs=[block, block, full((1, wide)), full((1, wide))],
        scratch_shapes=[pltpu.VMEM((D, count), bf16)],
        name="lexicon",
        cost_estimate=cost(2 * count * D * padded, 3e7),
    )(places, turned, grads)


def three(left, right, product):
    left_high, left_low = left
    right_high, right_low = right
    return (
        product(left_high, right_high)
        + product(left_high, right_low)
        + product(left_low, right_high)
    )


def shampoo_kernel(count, strip, places_ref, clip_ref, *refs):
    pieces = refs[:count]
    w_ref, ls_ref, rs_ref, lr_ref, rr_ref = refs[count : count + 5]
    g_ref, nw_ref, nl_ref, nr_ref = refs[count + 5 :]
    clip = clip_ref[0]
    for k in range(count):
        place = pl.multiple_of(places_ref[k], strip)
        g_ref[0, pl.ds(place, strip), :] = pieces[k][0] * clip
    grads = split_two(g_ref[0])
    for old, new, product in ((ls_ref, nl_ref, mm_t), (rs_ref, nr_ref, mm_l)):
        cross = product(grads[0], grads[1])
        outer = product(grads[0], grads[0]) + (cross + cross.T)
        new[0] = SHAMPOO_BETA * old[0] + (1.0 - SHAMPOO_BETA) * outer
    turned = split_two(three(grads, split_two(rr_ref[0]), mm))
    direction = three(split_two(lr_ref[0]), turned, mm)
    weights = w_ref[0]
    nw_ref[0] = weights - RATE_BLOCKS * (direction + DECAY_RATE * weights)


def shampoo(places, clip, pieces, weights, left_stats, right_stats, left_roots, right_roots):
    slots = weights.shape[0]
    count = len(pieces)
    strip = pieces[0].shape[1]
    block = pl.BlockSpec((1, BS, BS), lambda s: (s, 0, 0))
    shape = jax.ShapeDtypeStruct((slots, BS, BS), f32)
    return pl.pallas_call(
        partial(shampoo_kernel, count, strip),
        grid=(slots,),
        out_shape=[shape] * 4,
        in_specs=[pl.BlockSpec(memory_space=SMEM)] * 2
        + [pl.BlockSpec((1, strip, BS), lambda s: (s, 0, 0))] * count
        + [block] * 5,
        out_specs=[block] * 4,
        name="shampoo",
        cost_estimate=cost(slots * 24 * BS**3, slots * BS * BS * 40),
    )(places, clip, *pieces, weights, left_stats, right_stats, left_roots, right_roots)


def adam_update(weight, first, second, gradient, rate, step_value):
    first_new = BETA_FIRST * first + (1.0 - BETA_FIRST) * gradient
    second_new = BETA_SECOND * second + (1.0 - BETA_SECOND) * gradient * gradient
    first_hat = first_new / (1.0 - BETA_FIRST**step_value)
    second_hat = second_new / (1.0 - BETA_SECOND**step_value)
    return (
        weight - rate * (first_hat / (jnp.sqrt(second_hat) + ADAM_EPSILON) + DECAY_RATE * weight),
        first_new,
        second_new,
    )


def tie(values, *others):
    return lax.optimization_barrier((values,) + others)[0]


def exponent(bound):
    return jnp.floor(jnp.log2(jnp.maximum(bound, 1e-30))) + 1.0


def encode(values, bound):
    level = exponent(bound)
    coded = (values * jnp.exp2(15.0 - level)).astype(jnp.float16)
    return coded.reshape(-1, values.shape[-1]), level.astype(jnp.float16)


def pack(values, bound):
    coded, level = encode(values, bound)
    return jnp.concatenate([coded, jnp.broadcast_to(level, (16, coded.shape[1]))], 0)


def unpack(payload, shape):
    level = payload[-1, 0].astype(f32)
    values = payload[:-16].reshape(shape).astype(f32) * jnp.exp2(level - 15.0)
    return values, jnp.exp2(level)


def pack_lanes(values, bound):
    coded, level = encode(values, bound)
    lane = lax.broadcasted_iota(i32, coded.shape, 1)
    return jnp.where(lane == coded.shape[1] - 1, level, coded)


def unpack_lanes(payload):
    level = payload[0, -1].astype(f32)
    return payload.astype(f32) * jnp.exp2(level - 15.0)


def per_device(
    sizes,
    token_ids,
    seq_lengths,
    pick_rows,
    targets,
    step_count,
    block_order,
    slot_weights,
    left_stats,
    right_stats,
    left_roots,
    right_roots,
    embedding,
    embedding_first_moment,
    emb_second,
    vectors,
    vec_first,
    vec_second,
    feature_maps,
    map_first,
    map_second,
):
    ny, nc, n1, n0 = sizes
    n_dp, n_voc = ny * nc, n1 * n0
    dp_index, voc_index = lax.axis_index("dp"), lax.axis_index("vocab")
    y_at, c_at = dp_index // nc, dp_index % nc
    i1, i0 = voc_index // n0, voc_index % n0

    def over_dp(values, dy, dc):
        pairs = [
            (a * nc + b, ((a + dy) % ny) * nc + (b + dc) % nc) for a in range(ny) for b in range(nc)
        ]
        return lax.ppermute(values, "dp", pairs)

    def over_voc(values, d1, d0):
        pairs = [
            (a * n0 + b, ((a + d1) % n1) * n0 + (b + d0) % n0) for a in range(n1) for b in range(n0)
        ]
        return lax.ppermute(values, "vocab", pairs)

    def gather_voc(values):
        near = [values] + [over_voc(values, k, 0) for k in range(1, n1)]
        return [[part] + [over_voc(part, 0, k) for k in range(1, n0)] for part in near]

    def gather_stacked(values):
        near = jnp.stack([values] + [over_voc(values, 0, k) for k in range(1, n0)])
        return jnp.stack([near] + [over_voc(near, k, 0) for k in range(1, n1)])

    def flat_gather(values):
        return [part for line in gather_voc(values) for part in line]

    def gather_y(values):
        return [values] + [over_dp(values, k, 0) for k in range(1, ny)]

    def line_up(parts, at):
        size = len(parts)
        return jnp.take(jnp.stack(parts), (at - jnp.arange(size)) % size, axis=0)

    tokens = token_ids.shape[0]
    picks_own = pick_rows.shape[0]
    devices_all = n_dp * n_voc
    total_picks = picks_own * devices_all
    coefficient = DISTILL_WEIGHT / (tokens * devices_all * HEADS)
    shard_rows, cols_own = embedding.shape
    cols_y = cols_own * nc
    vocab_start = (voc_index * shard_rows).astype(i32)
    per_owner = slot_weights.shape[0]
    block_count = block_order.shape[0]
    table_own = embedding.T
    core = c_at.astype(i32).reshape(1)
    piece_places = jnp.stack(
        [
            (((y_at - ky) % ny) * nc + (c_at + kc) % nc) * cols_own
            for kc in range(nc)
            for ky in range(ny)
        ]
    ).astype(i32)

    low_own = table_own.astype(bf16)
    low_other = over_dp(low_own, 0, 1)
    upright = turn_table(core, low_own, low_other)

    ids_y = gather_y(token_ids)
    numbers = jnp.concatenate(ids_y + [targets])

    slots_y = gather_y(tie(slot_weights.astype(bf16), numbers))
    numbers = gather_stacked(numbers)
    targets_all = numbers[:, :, ny * tokens :].reshape(-1)
    piece_order = [(a, b) for b in list(range(1, n0)) + [0] for a in list(range(1, n1)) + [0]]
    early = (n0 - 1) * n1
    ids_order = [numbers[a, b, : ny * tokens] for a, b in piece_order]
    halves, hits = [], []
    for first, last in ((0, early), (early, n0 * n1)):
        ids_rows = jnp.concatenate(ids_order[first:last])
        local_ids = ids_rows - vocab_start
        packed_ids = jnp.where(
            (local_ids >= 0) & (local_ids < shard_rows),
            (local_ids << 16) | jnp.arange(ids_rows.shape[0], dtype=i32),
            -1,
        )
        hits.append(find_hits(tie(packed_ids, upright), shard_rows))
        halves += lookup(hits[-1], upright, ids_rows.shape[0], 2 * (last - first) // n1)

    def near_half(h, *before):
        part = halves[2 * (n0 - 1) + h]
        for b in range(1, n0):
            moved = over_voc(tie(halves[2 * (b - 1) + h], *before[:1]), 0, -b)
            part = part + tie(moved, *before)
        return [line for line in part.reshape(n1 // 2, ny, tokens, cols_y)]

    by_one = near_half(0)
    slots_y = [tie(part, by_one[0]) for part in slots_y]
    slots_core = [over_dp(part, 0, 1) for part in slots_y]
    inverse = (
        jnp.zeros((block_count,), i32).at[block_order].set(jnp.arange(block_count, dtype=i32))
    )
    owner = inverse // per_owner
    src = ((c_at - owner % nc) % nc) * ny + (y_at - owner // nc) % ny
    wqkv, wo, wup, wdown = place_blocks(
        src.astype(i32), inverse % per_owner, slots_y + slots_core
    )

    by_one = by_one + near_half(1, by_one[0], wup)
    far_parts = [over_voc(by_one[a - 1], -a, 0) for a in range(1, n1)]
    mine = by_one[-1]
    for part in far_parts:
        mine = mine + part
    row_parts = [mine[0]] + [over_dp(mine[k], -k, 0) for k in range(1, ny)]
    if ny == 2:
        first = y_at == 0
        x0 = jnp.concatenate(
            [
                jnp.where(first, row_parts[0], row_parts[1]),
                jnp.where(first, row_parts[1], row_parts[0]),
            ],
            1,
        )
    else:
        stacked = jnp.stack(row_parts)
        x0 = jnp.concatenate(
            [jnp.take(stacked, (j - y_at) % ny, axis=0) for j in range(ny)], axis=1
        )

    low_sent = tie(low_own, x0)
    low_y = [over_dp(low_sent, k, 0) for k in range(1, ny)]

    maps_low = feature_maps.astype(bf16)
    both = jnp.concatenate([maps_low, -maps_low], -1).reshape(2, PAIRS, 2, HD, 2 * HD)
    empty = jnp.zeros_like(both[:, :, 0])
    lift_maps = jnp.stack(
        [
            jnp.concatenate([both[:, :, 0], empty], -2),
            jnp.concatenate([empty, both[:, :, 1]], -2),
        ],
        2,
    ).reshape(2, HEADS, 2 * HD, 2 * HD)
    their_hits = [over_dp(own, 0, 1) for own in hits]
    h1, mixed = qkv_forward(tie(x0, *their_hits), wqkv, vectors)
    y, distill = attend(seq_lengths, mixed, lift_maps)
    x1, h2, up, act, x2, picked = mlp_forward(x0, y, wo, wup, wdown, vectors, pick_rows)

    low_y = [tie(part, picked) for part in low_y]
    low_y_other = [over_dp(part, 0, 1) for part in low_y]
    pieces = [low_own] + low_y + [low_other] + low_y_other
    group = jnp.concatenate(flat_gather(picked), 0)
    local_targets = targets_all - vocab_start
    logits, stats = vocabulary_logits(piece_places, group, local_targets, pieces)
    stats_all = gather_stacked(stats)
    lined = jnp.stack(
        [
            jnp.roll(stats_all[a, b, :3].reshape(3, n1, n0, picks_own), (a, b), (1, 2))
            for a in range(n1)
            for b in range(n0)
        ]
    ).reshape(n_voc, 3, n_voc * picks_own)
    top_all = jnp.max(lined[:, 0], 0)
    sum_all = jnp.sum(lined[:, 1] * jnp.exp(lined[:, 0] - top_all[None]), 0)
    losses = top_all + jnp.log(sum_all) - jnp.sum(lined[:, 2], 0)
    loss_part = jnp.sum(losses[:picks_own]) / total_picks + coefficient * distill[0, 0]
    shares = jnp.pad(jnp.stack([top_all, 1.0 / sum_all]), ((0, 126), (0, 0)))
    grad_logits, grad_group = vocabulary_back(
        piece_places, logits, shares, local_targets, pieces, 1.0 / total_picks
    )
    grad_group = grad_group.reshape(n1, n0, picks_own, D)
    by_one = []
    for a in list(range(1, n1)) + [0]:
        part = grad_group[a, 0]
        for b in range(1, n0):
            part = part + over_voc(grad_group[a, b], 0, -b)
        by_one.append(part)
    near_parts = [over_voc(by_one[a - 1], -a, 0) for a in range(1, n1)]

    lex_mine, lex_theirs, mine_high, theirs_high = lexicon(
        piece_places, group.T, tie(grad_logits, *by_one[:-1]), cols_own, shard_rows
    )
    lex_arrived = over_dp(lex_theirs, 0, 1)
    lex_high = jnp.max(mine_high) + jnp.max(over_dp(theirs_high, 0, 1))
    ghp = by_one[-1]
    for part in near_parts:
        ghp = ghp + tie(part, lex_theirs)

    def lex_lines(k):
        lines = slice(k * cols_own, (k + 1) * cols_own)
        return lex_mine[lines] + lex_arrived[lines]

    lex_sent = [pack_lanes(lex_lines(k), lex_high) for k in range(1, ny)]


    def core_parts(mine_part, their_part, mine_top, their_top, *later):
        arrived = tie(over_dp(their_part, 0, 1), *later)
        bound = jnp.max(mine_top) + jnp.max(over_dp(their_top, 0, 1))
        return coded_parts((mine_part, arrived), bound, False) + (bound,)

    def coded_parts(parts, bound, far):
        size, at = (n1, i1) if far else (n0, i0)
        rows = parts[0].shape[1] // size

        def lines(k):
            cut = [
                lax.dynamic_slice_in_dim(part, ((at + k) % size) * rows, rows, 1) for part in parts
            ]
            return sum(cut[1:], cut[0])

        return lines(0), [pack(lines(k), bound) for k in range(1, size)]

    def exchange(own, sent, bound, far, *later):
        total, high = own, bound
        for k, coded in enumerate(sent, 1):
            d1, d0 = (k, 0) if far else (0, k)
            values, top = unpack(tie(over_voc(coded, d1, d0), *later), own.shape)
            total = total + values
            high = high + top
        return total, high

    *halves_a, gx1, ga, gy, vg_a = mlp_back(
        core, ghp, pick_rows, x2, act, up, h2, x1, wdown, wup, wo, vectors
    )
    half_pairs = PAIRS // 2
    gy = tie(gy, *lex_sent)
    gqkv, map_q_a, map_k_a = attend_back(
        seq_lengths, mixed, gy, lift_maps, coefficient, 0, half_pairs, None
    )
    own_a, sent_a, bound_a = core_parts(*halves_a, gqkv)
    gy = tie(gy, own_a, *sent_a)
    gqkv, map_q_b, map_k_b = attend_back(
        seq_lengths, mixed, gy, lift_maps, coefficient, half_pairs, half_pairs, gqkv
    )
    lex_parts = [over_dp(part, -k, 0) for k, part in enumerate(lex_sent, 1)]
    gx0, vg_b = qkv_back(gqkv, wqkv, x0, gx1, vectors)

    map_grads = jnp.concatenate([map_q_a, map_q_b, map_k_a, map_k_b], 0)
    vec_grads = (vg_a + vg_b)[:15]
    small_count = map_grads.size + vec_grads.size
    small = jnp.concatenate(
        [
            map_grads.reshape(-1),
            vec_grads.reshape(-1),
            jnp.zeros((2 * BS * BS - small_count,), f32),
        ]
    ).reshape(2, BS, BS)
    gx0_cols = gx0.reshape(tokens, ny, cols_y)
    cols_sent = [jnp.take(gx0_cols, (y_at + k) % ny, axis=1) for k in range(1, ny)]
    arrived = [jnp.take(gx0_cols, y_at, axis=1)] + [
        over_dp(part, k, 0) for k, part in enumerate(cols_sent, 1)
    ]
    arrived = jnp.concatenate(arrived, 0).reshape(ny * tokens, nc, cols_own)
    rows_mine = jnp.take(arrived, c_at, axis=1)
    moved_a = [over_voc(part, 0, k) for k, part in enumerate(sent_a, 1)]
    rows_other = over_dp(jnp.take(arrived, (c_at + 1) % nc, axis=1), 0, 1)
    if cols_own == 192:
        packed = jnp.concatenate(
            [
                rows_mine[:, :128],
                rows_other[:, :128],
                jnp.concatenate([rows_mine[:, 128:], rows_other[:, 128:]], 1),
            ],
            0,
        )
    else:
        packed = jnp.stack([rows_mine, rows_other])
    halves_b = qkv_weights(core, tie(h1, packed, *moved_a, *lex_parts), gqkv, y, ga, small)
    total_a, high_a = own_a, bound_a
    for part in moved_a:
        values, top = unpack(tie(part, halves_b[0]), own_a.shape)
        total_a, high_a = total_a + values, high_a + top
    own_b, sent_b, bound_b = core_parts(*halves_b, packed)
    total_b, high_b = exchange(own_b, sent_b, bound_b, False)
    total = jnp.concatenate([total_a, total_b], 0)
    high = jnp.maximum(high_a, high_b)
    own, sent = coded_parts((total,), high, True)
    near_rows = [packed] + [tie(over_voc(packed, k, 0), *sent) for k in range(1, n1)]
    gathered = [[packed] + [over_voc(packed, 0, k) for k in range(1, n0)]]
    sent = [tie(part, *near_rows, *gathered[0]) for part in sent]
    gathered += [[part] + [over_voc(part, 0, k) for k in range(1, n0)] for part in near_rows[1:]]
    blocks = exchange(own, sent, high, True, *(line[-1] for line in gathered))[0]

    per_side = blocks.shape[0]
    both = jnp.concatenate([blocks, over_dp(blocks, 0, 1)], 0)
    side, place = comm_positions()
    side = jnp.concatenate([jnp.take(jnp.asarray(side), block_order), jnp.arange(2, dtype=i32)])
    place = jnp.concatenate(
        [jnp.take(jnp.asarray(place), block_order), jnp.full((2,), per_side - 1, i32)]
    )
    at_place = ((side - c_at) % nc) * per_side + place
    smalls = at_place[block_count:]
    at_place = at_place[:block_count].reshape(ny, nc, per_owner)

    def slots_of(k):
        mine = jnp.take(jnp.take(at_place, c_at, axis=1), (y_at + k) % ny, axis=0)
        return jnp.take(both, jnp.concatenate([mine, smalls]), axis=0)

    own_slots = slots_of(0)
    strips, small_parts = own_slots[:per_owner], []
    strip_rows = own_slots.shape[1]
    tail = own_slots[per_owner:]
    values, _ = unpack(pack(tail, jnp.max(jnp.abs(own_slots))), tail.shape)
    small_parts.append(values)
    slots_sent = []
    for k in range(1, ny):
        moved = slots_of(k)
        high = jnp.maximum(jnp.max(jnp.abs(moved)), jnp.max(jnp.abs(own_slots)))
        slots_sent.append(pack(moved, high))
    lex = lex_lines(0)
    for part in lex_parts:
        lex = lex + unpack_lanes(part)
    lex = tie(lex, *slots_sent)
    if cols_own == 192:
        pieces = [gathered[a][b] for a, b in piece_order]
        emb_grads, emb_square = scatter_rows(
            list(zip(hits, their_hits)), lex, pieces, shard_rows
        )
        emb_square = emb_square[0, 0]
    else:
        pieces = jnp.stack([gathered[a][b] for a, b in piece_order], 1).reshape(-1, cols_own)
        ids_rows = jnp.concatenate(ids_order)
        local = jnp.concatenate([ids_rows, over_dp(ids_rows, 0, 1)]) - vocab_start
        local = jnp.where((local >= 0) & (local < shard_rows), local, shard_rows)
        emb_grads = lex[:, :shard_rows].T.at[local].add(pieces.astype(f32), mode="drop").T
        emb_square = jnp.sum(emb_grads * emb_grads)

    for k, sent in enumerate(slots_sent, 1):
        moved, _ = unpack(over_dp(sent, k, 0), own_slots.shape)
        strips = strips + moved[:per_owner]
        small_parts.append(moved[per_owner:])
    if ny == 2:
        small_sum = small_parts[0] + small_parts[1]
    else:
        small_sum = jnp.sum(line_up(small_parts, y_at), 0)
    own_strips = jnp.concatenate([strips, small_sum], 0)
    coded_all = flat_gather(pack(own_strips, jnp.max(jnp.abs(own_strips))))
    strip_pieces = [unpack(part, own_strips.shape)[0] for part in coded_all]

    square = emb_square + jnp.sum(strips * strips)
    square = square + jnp.where(dp_index == 0, jnp.sum(small_sum * small_sum), 0.0)
    sums = jnp.pad(jnp.stack([square, loss_part]).reshape(1, 2), ((0, 7), (0, 126)))
    sums = sums + over_dp(sums, 0, 1)
    sums = jnp.sum(line_up(gather_y(sums), y_at), 0)
    sums = jnp.sum(line_up([sums] + [over_voc(sums, 0, k) for k in range(1, n0)], i0), 0)
    sums = jnp.sum(line_up([sums] + [over_voc(sums, k, 0) for k in range(1, n1)], i1), 0)
    grad_norm = jnp.sqrt(sums[0, 0])
    loss_total = sums[0, 1]
    clip_scale = CLIP_NORM / jnp.maximum(grad_norm, CLIP_NORM)

    small_all = jnp.stack([part[per_owner:] for part in strip_pieces])
    small_all = small_all.reshape(n1, n0, 2, strip_rows, BS)
    small_all = jnp.take(small_all, (i1 - jnp.arange(n1)) % n1, axis=0)
    small_all = jnp.take(small_all, (i0 - jnp.arange(n0)) % n0, axis=1)
    small_all = small_all.transpose(2, 1, 0, 3, 4).reshape(-1)
    map_sum = small_all[: map_grads.size].reshape(feature_maps.shape)
    vec_sum = small_all[map_grads.size : small_count].reshape(vectors.shape)

    places = [
        ((i0 - b) % n0) * (BS // n0) + ((i1 - a) % n1) * strip_rows
        for a in range(n1)
        for b in range(n0)
    ]
    places = jnp.stack(places).astype(i32)
    clipped, new_slots, new_left, new_right = shampoo(
        places,
        clip_scale.reshape(1),
        strip_pieces,
        slot_weights,
        left_stats,
        right_stats,
        left_roots,
        right_roots,
    )
    step_value = step_count[0].astype(f32)
    emb_out = adam_update(
        table_own,
        embedding_first_moment.T,
        emb_second.T,
        emb_grads * clip_scale,
        RATE_TABLE,
        step_value,
    )
    vec_out = adam_update(
        vectors, vec_first, vec_second, vec_sum * clip_scale, RATE_VECTORS, step_value
    )
    map_out = adam_update(
        feature_maps, map_first, map_second, map_sum * clip_scale, RATE_MAPS, step_value
    )
    return (
        loss_total,
        grad_norm,
        clipped,
        new_slots,
        new_left,
        new_right,
        emb_out[0].T,
        emb_out[1].T,
        emb_out[2].T,
        vec_out[0],
        vec_out[1],
        vec_out[2],
        map_out[0],
        map_out[1],
        map_out[2],
    )


def solution(mesh):
    n_dp, n_voc = mesh.shape["dp"], mesh.shape["vocab"]
    sizes = (n_dp // 2, 2, 4, n_voc // 4)
    rows = P(("dp", "vocab"))
    blocks = P("dp", None, None)
    table = P("vocab", "dp")
    placed = (
        (rows, P(("dp", "vocab"), None), rows, rows, P(), P())
        + (blocks,) * 5
        + (table,) * 3
        + (P(),) * 6
    )
    return jax.shard_map(
        partial(per_device, sizes),
        mesh=mesh,
        in_specs=placed,
        out_specs=(P(), P()) + (blocks,) * 4 + (table,) * 3 + (P(),) * 6,
        check_vma=False,
    )
```

```python
from functools import partial

import jax
import jax.numpy as jnp
import numpy as np
from jax import lax
from jax.experimental import pallas as pl
from jax.experimental.pallas import tpu as pltpu
from jax.sharding import PartitionSpec as P

D = 768
HEADS = 12
HD = 64
FF = 3072
BS = 384
PAIRS = HEADS // 2

NORM_EPSILON = 1e-05
CLIP_NORM = 0.01
DISTILL_WEIGHT = 0.5
BETA_FIRST = 0.9
BETA_SECOND = 0.95
ADAM_EPSILON = 1e-08
DECAY_RATE = 0.01
SHAMPOO_BETA = 0.95
RATE_BLOCKS = 0.1
RATE_TABLE = 0.05
RATE_VECTORS = 0.2
RATE_MAPS = 0.1

f32 = jnp.float32
bf16 = jnp.bfloat16
i32 = jnp.int32
SMEM = pltpu.SMEM
ANY = pl.ANY


def mm(left, right):
    return lax.dot_general(left, right, (((1,), (0,)), ((), ())), preferred_element_type=f32)


def mm_t(left, right):
    return lax.dot_general(left, right, (((1,), (1,)), ((), ())), preferred_element_type=f32)


def mm_l(left, right):
    return lax.dot_general(left, right, (((0,), (0,)), ((), ())), preferred_element_type=f32)


def split_two(values):
    high = values.astype(bf16)
    return high, (values - high.astype(f32)).astype(bf16)


def full(shape):
    return pl.BlockSpec(shape, lambda *_: (0,) * len(shape))


def cost(flops, bytes_moved, transcendentals=0):
    return pl.CostEstimate(
        flops=int(flops * 0.02),
        bytes_accessed=int(bytes_moved * 0.02),
        transcendentals=int(transcendentals * 0.02),
    )


def place_kernel(piece_count, src_ref, off_ref, *refs):
    pieces = refs[:piece_count]
    outs = refs[piece_count : piece_count + 4]
    sems = refs[piece_count + 4]
    base = 0
    for out, rows, cols in zip(outs, (D, D, D, FF), (3 * D, D, FF, D)):
        wide = cols // BS
        count = (rows // BS) * wide

        def go(t, carry, out=out, wide=wide, base=base):
            k = base + t
            r0 = pl.multiple_of((t // wide) * BS, BS)
            c0 = pl.multiple_of((t % wide) * BS, BS)
            for p in range(piece_count):

                @pl.when(src_ref[k] == p)
                def _(p=p):
                    pltpu.make_async_copy(
                        pieces[p].at[off_ref[k]],
                        out.at[pl.ds(r0, BS), pl.ds(c0, BS)],
                        sems.at[k],
                    ).start()

            return carry

        lax.fori_loop(0, count, go, 0)
        base += count
    base = 0
    for out, rows, cols in zip(outs, (D, D, D, FF), (3 * D, D, FF, D)):
        count = (rows // BS) * (cols // BS)

        def done(t, carry, out=out, base=base):
            pltpu.make_async_copy(
                pieces[0].at[0], out.at[pl.ds(0, BS), pl.ds(0, BS)], sems.at[base + t]
            ).wait()
            return carry

        lax.fori_loop(0, count, done, 0)
        base += count


def place_blocks(src, off, pieces):
    count = len(pieces)
    return pl.pallas_call(
        partial(place_kernel, count),
        out_shape=[
            jax.ShapeDtypeStruct(shape, bf16)
            for shape in ((D, 3 * D), (D, D), (D, FF), (FF, D))
        ],
        in_specs=[pl.BlockSpec(memory_space=SMEM)] * 2 + [pl.BlockSpec(memory_space=ANY)] * count,
        out_specs=[pl.BlockSpec(memory_space=pltpu.VMEM)] * 4,
        scratch_shapes=[pltpu.SemaphoreType.DMA((48,))],
        name="place_blocks",
        cost_estimate=cost(0, 2 * 48 * BS * BS * 2),
    )(src, off, *pieces)


def hits_kernel(empty_row, packed_ref, list_ref):
    total = packed_ref.shape[0]

    def go(i, n):
        for u in range(16):
            entry = packed_ref[i * 16 + u]
            list_ref[n] = entry
            n = n + 1 + (entry >> 31)
        return n

    n = lax.fori_loop(0, total // 16, go, jnp.int32(0))
    list_ref[total + 8] = n
    for u in range(8):
        list_ref[n + u] = empty_row << 16


def find_hits(packed, empty_row):
    total = packed.shape[0]
    return pl.pallas_call(
        partial(hits_kernel, empty_row),
        out_shape=jax.ShapeDtypeStruct((total + 16,), i32),
        in_specs=[pl.BlockSpec(memory_space=SMEM)],
        out_specs=pl.BlockSpec(memory_space=SMEM),
        name="find_hits",
        cost_estimate=cost(1e10, total * 8),
    )(packed)


def turn_kernel(core_ref, own_ref, other_ref, out_ref):
    first = core_ref[0] == 0
    own, other = own_ref[...].astype(f32), other_ref[...].astype(f32)
    depth = own.shape[0]
    both = jnp.concatenate([jnp.where(first, own, other), jnp.where(first, other, own)], 0)
    out_ref[...] = both.T


def turn_table(core, own, other):
    depth, rows_all = own.shape
    wide = lane_block(rows_all)
    block = pl.BlockSpec((depth, wide), lambda j: (0, j))
    return pl.pallas_call(
        turn_kernel,
        grid=(pl.cdiv(rows_all, wide),),
        out_shape=jax.ShapeDtypeStruct((rows_all, 2 * depth), f32),
        in_specs=[pl.BlockSpec(memory_space=SMEM), block, block],
        out_specs=pl.BlockSpec((wide, 2 * depth), lambda j: (j, 0)),
        name="turn_table",
        cost_estimate=cost(1e7, 1e7),
    )(core, own, other)


def in_chunks(count, size, body):
    def go(i, carry):
        body(pl.multiple_of(i * size, size))
        return carry

    lax.fori_loop(0, count // size, go, 0)


def lookup_kernel(rows_all, list_ref, table_ref, *refs):
    outs, acc = refs[:-1], refs[-1]
    total = acc.shape[0] - 8
    chunk = 128

    def clear(start):
        acc[pl.ds(start, chunk), :] = jnp.zeros((chunk, acc.shape[1]), f32)

    in_chunks(total, chunk, clear)

    def go(i, carry):
        for u in range(8):
            entry = list_ref[i * 8 + u]
            row = entry >> 16
            place = jnp.where(row < rows_all, entry & 0xFFFF, total)
            row = jnp.minimum(row, rows_all - 1)
            acc[pl.ds(place, 1), :] = table_ref[pl.ds(row, 1), :]
        return carry

    lax.fori_loop(0, (list_ref[total + 8] + 7) // 8, go, 0)
    each = outs[0].shape[0]
    for part, out in enumerate(outs):

        def keep(start, part=part, out=out):
            out[pl.ds(start, chunk), :] = acc[pl.ds(part * each + start, chunk), :].astype(bf16)

        in_chunks(each, chunk, keep)


def lookup(hit_list, table, count, parts):
    rows_all, width = table.shape
    return pl.pallas_call(
        partial(lookup_kernel, rows_all),
        out_shape=[jax.ShapeDtypeStruct((count // parts, width), bf16)] * parts,
        in_specs=[
            pl.BlockSpec(memory_space=SMEM),
            pl.BlockSpec(memory_space=pltpu.VMEM),
        ],
        out_specs=[pl.BlockSpec(memory_space=pltpu.VMEM)] * parts,
        scratch_shapes=[pltpu.VMEM((count + 8, width), f32)],
        name="lookup",
        cost_estimate=cost(1e10, rows_all * width * 2),
    )(hit_list, table)


def scatter_kernel(piece_count, half, rows_all, starts, *refs):
    used = len(starts)
    lists = refs[:used]
    lex_ref = refs[used]
    pieces = refs[used + 1 : used + 1 + piece_count]
    out_ref, square_ref, acc, tail, wide, pair = refs[used + 1 + piece_count :]
    chunk = 128

    def clear(start):
        acc[pl.ds(start, chunk), :] = jnp.zeros((chunk, 128), f32)
        tail[pl.ds(start, chunk), :] = jnp.zeros((chunk, 128), f32)

    in_chunks(acc.shape[0], chunk, clear)
    for k in range(piece_count):

        def widen(start, k=k):
            values = pieces[k][pl.ds(start, chunk), :].astype(f32)
            wide[pl.ds(k * 2 * half + start, chunk), :] = values

        def widen_pair(start, k=k):
            values = pieces[k][pl.ds(2 * half + start, chunk), :].astype(f32)
            pair[pl.ds(k * half + start, chunk), :] = values

        in_chunks(2 * half, chunk, widen)
        in_chunks(half, chunk, widen_pair)
    upper = lax.broadcasted_iota(i32, (1, 128), 1) >= 64
    for which, (side, start) in enumerate(starts):
        own = upper if side else ~upper

        def go(i, carry, which=which, side=side, start=start, own=own):
            for u in range(8):
                entry = lists[which][i * 8 + u]
                row = entry >> 16
                p = (entry & 0xFFFF) + start
                q = (p // half) * half + p + side * half
                acc[pl.ds(row, 1), :] += wide[pl.ds(q, 1), :]
                tail[pl.ds(row, 1), :] += jnp.where(own, pair[pl.ds(p, 1), :], 0.0)
            return carry

        held = lists[which].shape[0] - 8
        lax.fori_loop(0, (lists[which][held] + 7) // 8, go, 0)
    chunks = rows_all // 128
    rest = rows_all - chunks * 128

    def turn(start, width):
        upright = acc[pl.ds(start, 128), :].T
        lower = tail[pl.ds(start, 128), :].T
        lower = lower[:64] + lower[64:]
        lanes = pl.ds(start, width)
        left = lex_ref[pl.ds(0, 128), lanes] + upright[:, :width]
        right = lex_ref[pl.ds(128, 64), lanes] + lower[:, :width]
        out_ref[pl.ds(0, 128), lanes] = left
        out_ref[pl.ds(128, 64), lanes] = right
        return jnp.sum(left * left, 0, keepdims=True), jnp.sum(right * right, 0, keepdims=True)

    def step(i, carry):
        left, right = turn(pl.multiple_of(i * 128, 128), 128)
        return carry + left + right

    squares = lax.fori_loop(0, chunks, step, jnp.zeros((1, 128), f32))
    total = jnp.sum(squares)
    if rest:
        left, right = turn(chunks * 128, rest)
        total = total + jnp.sum(left) + jnp.sum(right)
    square_ref[0, 0] = total


def scatter_rows(hits, lex, pieces, rows_all):
    lists, starts, start = [], [], 0
    for own_list, other_list in hits:
        lists += [own_list, other_list]
        starts += [(0, start), (1, start)]
        start += own_list.shape[0] - 16
    width = lex.shape[0]
    half = pieces[0].shape[0] // 3
    count = len(pieces)
    padded = (rows_all // 128 + 1) * 128
    return pl.pallas_call(
        partial(scatter_kernel, count, half, rows_all, tuple(starts)),
        out_shape=[
            jax.ShapeDtypeStruct((width, rows_all), f32),
            jax.ShapeDtypeStruct((1, 1), f32),
        ],
        in_specs=[pl.BlockSpec(memory_space=SMEM)] * len(lists)
        + [pl.BlockSpec(memory_space=pltpu.VMEM)] * (count + 1),
        out_specs=[
            pl.BlockSpec(memory_space=pltpu.VMEM),
            pl.BlockSpec(memory_space=SMEM),
        ],
        scratch_shapes=[
            pltpu.VMEM((padded, 128), f32),
            pltpu.VMEM((padded, 128), f32),
            pltpu.VMEM((count * 2 * half, 128), f32),
            pltpu.VMEM((count * half, 128), f32),
        ],
        name="scatter_rows",
        cost_estimate=cost(1.5e10, rows_all * width * 8),
    )(*lists, lex, *pieces)


def norm_parts(inputs):
    centered = inputs - jnp.mean(inputs, -1, keepdims=True)
    scale = lax.rsqrt(jnp.mean(centered * centered, -1, keepdims=True) + NORM_EPSILON)
    return centered, scale


def norm_pull(inputs, gain_row, grads):
    centered, scale = norm_parts(inputs)
    unit = centered * scale
    pulled = grads * gain_row
    lead = jnp.mean(pulled, -1, keepdims=True)
    along = jnp.mean(pulled * unit, -1, keepdims=True)
    grad_in = scale * (pulled - lead - unit * along)
    return (
        grad_in,
        jnp.sum(grads * unit, 0, keepdims=True),
        jnp.sum(grads, 0, keepdims=True),
    )


def qkv_kernel(x_ref, w_ref, vec_ref, h_ref, mixed_ref):
    j = pl.program_id(0)

    @pl.when(j == 0)
    def _():
        centered, scale = norm_parts(x_ref[...].astype(f32))
        h_ref[...] = (centered * scale * vec_ref[0:1, :] + vec_ref[1:2, :]).astype(bf16)

    mixed_ref[...] = (mm(h_ref[...], w_ref[...]) + vec_ref[pl.ds(8 + j, 1), :]).astype(bf16)


def qkv_forward(x0, wqkv, vectors):
    tokens = x0.shape[0]
    return pl.pallas_call(
        qkv_kernel,
        grid=(3,),
        out_shape=[
            jax.ShapeDtypeStruct((tokens, D), bf16),
            jax.ShapeDtypeStruct((tokens, 3 * D), bf16),
        ],
        in_specs=[
            full((tokens, D)),
            pl.BlockSpec((D, D), lambda j: (0, j)),
            full(vectors.shape),
        ],
        out_specs=[full((tokens, D)), pl.BlockSpec((tokens, D), lambda j: (0, j))],
        name="qkv_forward",
        cost_estimate=cost(2 * tokens * D * 3 * D, 8e6),
    )(x0, wqkv, vectors)


def feature_parts(values, lift, low_half):
    raw = mm(values, lift)
    top_a = jnp.max(jnp.where(low_half, raw, -jnp.inf), -1, keepdims=True)
    top_b = jnp.max(jnp.where(low_half, -jnp.inf, raw), -1, keepdims=True)
    grown = jnp.exp(raw - jnp.where(low_half, top_a, top_b))
    sum_a = jnp.sum(jnp.where(low_half, grown, 0.0), -1, keepdims=True)
    sum_b = jnp.sum(jnp.where(low_half, 0.0, grown), -1, keepdims=True)
    return grown / jnp.where(low_half, sum_a, sum_b)


def feature_pull(soft, grads, low_half):
    weighed = soft * grads
    sum_a = jnp.sum(jnp.where(low_half, weighed, 0.0), -1, keepdims=True)
    sum_b = jnp.sum(jnp.where(low_half, 0.0, weighed), -1, keepdims=True)
    pulled = soft * (grads - jnp.where(low_half, sum_a, sum_b))
    return (pulled - pltpu.roll(pulled, HD, 1)).astype(bf16)


def fill_allowed(len_ref, allow_ref):
    tokens = allow_ref.shape[0]
    first = len_ref[0, 0]
    second = first + len_ref[0, 1]
    third = second + len_ref[0, 2]

    def document(places):
        return (
            (places >= first).astype(i32)
            + (places >= second).astype(i32)
            + (places >= third).astype(i32)
        )

    rows = lax.broadcasted_iota(i32, (tokens, tokens), 0)
    cols = lax.broadcasted_iota(i32, (tokens, tokens), 1)
    allow_ref[...] = ((cols <= rows) & (document(rows) == document(cols))).astype(f32)


ROWS = 256


def attend_kernel(
    len_ref, q_ref, k_ref, v_ref, fq_ref, fk_ref, y_ref, distill_ref, allow_ref, lift_q, lift_k
):
    tokens = q_ref.shape[0]

    @pl.when(pl.program_id(0) == 0)
    def _():
        fill_allowed(len_ref, allow_ref)
        distill_ref[...] = jnp.zeros_like(distill_ref)

    low_half = lax.broadcasted_iota(i32, (1, 2 * HD), 1) < HD
    low_rows = lax.broadcasted_iota(i32, (ROWS, 2 * HD), 1) < HD
    total = jnp.zeros((1, 1), f32)
    for h in range(2):
        lift_q[h] = feature_parts(q_ref[...], fq_ref[h], low_half).astype(bf16)
        lift_k[h] = feature_parts(k_ref[...], fk_ref[h], low_half).astype(bf16)
    for begin in range(0, tokens, ROWS):
        width = begin + ROWS
        ok = allow_ref[pl.ds(begin, ROWS), pl.ds(0, width)] > 0.5
        queries = q_ref[pl.ds(begin, ROWS), :] * jnp.asarray(HD**-0.5, bf16)
        keys = k_ref[pl.ds(0, width), :]
        values = v_ref[pl.ds(0, width), :]
        parts = []
        for h in range(2):
            own = low_rows if h == 0 else ~low_rows
            scores = mm_t(jnp.where(own, queries, jnp.zeros_like(queries)), keys)
            scores = jnp.where(ok, scores, -1e30)
            grown = jnp.exp(scores - jnp.max(scores, -1, keepdims=True))
            inverse = 1.0 / jnp.sum(grown, -1, keepdims=True)
            similar = mm_t(lift_q[h, pl.ds(begin, ROWS), :], lift_k[h, pl.ds(0, width), :])
            kept = jnp.where(ok, similar, 0.0)
            sums = jnp.sum(kept, -1, keepdims=True)
            weights = (kept * (1.0 / sums)).astype(bf16)
            parts.append(mm(weights, values))
            logs = jnp.log(jnp.where(ok, similar, 1.0))
            row_terms = jnp.log(sums) - jnp.sum(grown * logs, -1, keepdims=True) * inverse
            total = total + jnp.sum(row_terms, 0, keepdims=True)
        y_ref[pl.ds(begin, ROWS), :] = jnp.where(low_rows, parts[0], parts[1]).astype(bf16)
    distill_ref[...] += jnp.broadcast_to(total, distill_ref.shape)


def attend(lengths, mixed, lift_maps):
    tokens = mixed.shape[0]
    column = lambda base: pl.BlockSpec((tokens, 2 * HD), lambda g: (0, base + g))
    maps = pl.BlockSpec((2, 2 * HD, 2 * HD), lambda g: (g, 0, 0))
    return pl.pallas_call(
        attend_kernel,
        grid=(PAIRS,),
        out_shape=[
            jax.ShapeDtypeStruct((tokens, D), bf16),
            jax.ShapeDtypeStruct((8, 128), f32),
        ],
        in_specs=[
            pl.BlockSpec(memory_space=SMEM),
            column(0),
            column(PAIRS),
            column(2 * PAIRS),
            maps,
            maps,
        ],
        out_specs=[column(0), full((8, 128))],
        scratch_shapes=[
            pltpu.VMEM((tokens, tokens), f32),
            pltpu.VMEM((2, tokens, 2 * HD), bf16),
            pltpu.VMEM((2, tokens, 2 * HD), bf16),
        ],
        name="attend",
        cost_estimate=cost(1.2e10, 4e6, 6e6),
    )(lengths, mixed, mixed, mixed, lift_maps[0], lift_maps[1])


def attend_back_kernel(
    coefficient,
    later,
    len_ref,
    q_ref,
    k_ref,
    v_ref,
    gy_ref,
    fq_ref,
    fk_ref,
    *refs,
):
    g_ref, gq_map_ref, gk_map_ref, allow_ref, soft_q, soft_k, grad_q, grad_k, grad_v = refs[later:]
    tokens = q_ref.shape[0]

    @pl.when(pl.program_id(0) == 0)
    def _():
        fill_allowed(len_ref, allow_ref)

    low_half = lax.broadcasted_iota(i32, (1, 2 * HD), 1) < HD
    low_rows = lax.broadcasted_iota(i32, (ROWS, 2 * HD), 1) < HD
    for h in range(2):
        soft_q[h] = feature_parts(q_ref[...], fq_ref[h], low_half)
        soft_k[h] = feature_parts(k_ref[...], fk_ref[h], low_half)
    for step, begin in enumerate(reversed(range(0, tokens, ROWS))):
        width = begin + ROWS
        ok = allow_ref[pl.ds(begin, ROWS), pl.ds(0, width)] > 0.5
        queries = q_ref[pl.ds(begin, ROWS), :] * jnp.asarray(HD**-0.5, bf16)
        keys = k_ref[pl.ds(0, width), :]
        values = v_ref[pl.ds(0, width), :]
        grads = gy_ref[pl.ds(begin, ROWS), :]
        value_sum = None
        for h in range(2):
            own = low_rows if h == 0 else ~low_rows
            scores = mm_t(jnp.where(own, queries, jnp.zeros_like(queries)), keys)
            scores = jnp.where(ok, scores, -1e30)
            grown = jnp.exp(scores - jnp.max(scores, -1, keepdims=True))
            teach = grown * (coefficient / jnp.sum(grown, -1, keepdims=True))
            phi_q = soft_q[h, pl.ds(begin, ROWS), :].astype(bf16)
            phi_k = soft_k[h, pl.ds(0, width), :].astype(bf16)
            similar = mm_t(phi_q, phi_k)
            kept = jnp.where(ok, similar, 0.0)
            inverse = 1.0 / jnp.sum(kept, -1, keepdims=True)
            weights = kept * inverse
            own_grads = jnp.where(own, grads, jnp.zeros_like(grads))
            grad_w = mm_t(own_grads, values)
            row_sum = jnp.sum(grad_w * weights, -1, keepdims=True)
            grad_sums = (coefficient - row_sum) * inverse
            grad_sim = jnp.where(
                ok,
                grad_w * inverse - teach / jnp.where(ok, similar, 1.0) + grad_sums,
                0.0,
            ).astype(bf16)
            grad_q[h, pl.ds(begin, ROWS), :] = mm(grad_sim, phi_k)
            part_k = mm_l(grad_sim, phi_q)
            part_v = mm_l(weights.astype(bf16), own_grads)
            value_sum = part_v if value_sum is None else value_sum + part_v
            if step == 0:
                grad_k[h] = part_k
            else:
                grad_k[h, pl.ds(0, width), :] += part_k
        if step == 0:
            grad_v[...] = value_sum
        else:
            grad_v[pl.ds(0, width), :] += value_sum
    for slot, own_ref, map_ref, soft, grad, out in (
        (0, q_ref, fq_ref, soft_q, grad_q, gq_map_ref),
        (1, k_ref, fk_ref, soft_k, grad_k, gk_map_ref),
    ):
        result = None
        for h in range(2):
            pulled = feature_pull(soft[h], grad[h], low_half)
            back = mm_t(pulled, map_ref[h]) * 0.5
            result = back if result is None else result + back
            out[h] = mm_l(own_ref[...], pulled)[h * HD : (h + 1) * HD, :HD]
        g_ref[slot] = result.astype(bf16)
    g_ref[2] = grad_v[...].astype(bf16)


def attend_back(lengths, mixed, grad_y, lift_maps, coefficient, start, pairs, before):
    tokens = mixed.shape[0]
    column = lambda base: pl.BlockSpec((tokens, 2 * HD), lambda g: (0, base + start + g))
    maps = pl.BlockSpec((2, 2 * HD, 2 * HD), lambda g: (start + g, 0, 0))
    small = pl.BlockSpec((2, HD, HD), lambda g: (g, 0, 0))
    wide = (2, tokens, 2 * HD)
    later = before is not None
    return pl.pallas_call(
        partial(attend_back_kernel, coefficient, int(later)),
        grid=(pairs,),
        out_shape=[
            jax.ShapeDtypeStruct((3, tokens, D), bf16),
            jax.ShapeDtypeStruct((2 * pairs, HD, HD), f32),
            jax.ShapeDtypeStruct((2 * pairs, HD, HD), f32),
        ],
        in_specs=[
            pl.BlockSpec(memory_space=SMEM),
            column(0),
            column(PAIRS),
            column(2 * PAIRS),
            column(0),
            maps,
            maps,
        ]
        + [pl.BlockSpec(memory_space=ANY)] * later,
        out_specs=[
            pl.BlockSpec((3, tokens, 2 * HD), lambda g: (0, 0, start + g)),
            small,
            small,
        ],
        scratch_shapes=[
            pltpu.VMEM((tokens, tokens), f32),
            pltpu.VMEM(wide, f32),
            pltpu.VMEM(wide, f32),
            pltpu.VMEM(wide, f32),
            pltpu.VMEM(wide, f32),
            pltpu.VMEM((tokens, 2 * HD), f32),
        ],
        input_output_aliases={7: 0} if later else {},
        name="attend_back",
        cost_estimate=cost(1.2e10, 4e6, 3e6),
    )(lengths, mixed, mixed, mixed, grad_y, lift_maps[0], lift_maps[1], *([before] * later))


FSTEPS = FF // D


def mlp_kernel(
    x_ref,
    y_ref,
    wo_ref,
    wup_ref,
    wdown_ref,
    vec_ref,
    pick_ref,
    x1_ref,
    h_ref,
    up_ref,
    act_ref,
    x2_ref,
    hp_ref,
):
    j = pl.program_id(0)

    @pl.when(j == 0)
    def _():
        x1 = x_ref[...].astype(f32) + mm(y_ref[...], wo_ref[...]) + vec_ref[6:7, :]
        x1_ref[...] = x1
        centered, scale = norm_parts(x1)
        h_ref[...] = (centered * scale * vec_ref[2:3, :] + vec_ref[3:4, :]).astype(bf16)
        x2_ref[...] = x1 + vec_ref[7:8, :]

    up = mm(h_ref[...], wup_ref[...]) + vec_ref[pl.ds(11 + j, 1), :]
    up_ref[...] = up
    act = (0.5 * up * (1.0 + jnp.tanh(0.7978845608 * (up + 0.044715 * up * up * up)))).astype(bf16)
    act_ref[...] = act
    x2_ref[...] += mm(act, wdown_ref[...])

    @pl.when(j == FSTEPS - 1)
    def _():
        centered, scale = norm_parts(x2_ref[...])
        last = (centered * scale * vec_ref[4:5, :] + vec_ref[5:6, :]).astype(bf16)
        tokens = last.shape[0]
        places = lax.broadcasted_iota(i32, (pick_ref.shape[0], tokens), 1)
        chosen = (places == pick_ref[...]).astype(bf16)
        hp_ref[...] = mm(chosen, last).astype(bf16)


def mlp_forward(x0, y, wo, wup, wdown, vectors, picks):
    tokens = x0.shape[0]
    count = picks.shape[0]
    wide = pl.BlockSpec((tokens, D), lambda j: (0, j))
    shape = lambda cols, kind: jax.ShapeDtypeStruct((tokens, cols), kind)
    return pl.pallas_call(
        mlp_kernel,
        grid=(FSTEPS,),
        out_shape=[
            shape(D, f32),
            shape(D, bf16),
            shape(FF, f32),
            shape(FF, bf16),
            shape(D, f32),
            jax.ShapeDtypeStruct((count, D), bf16),
        ],
        in_specs=[
            full((tokens, D)),
            full((tokens, D)),
            full((D, D)),
            pl.BlockSpec((D, D), lambda j: (0, j)),
            pl.BlockSpec((D, D), lambda j: (j, 0)),
            full(vectors.shape),
            full((count, 1)),
        ],
        out_specs=[
            full((tokens, D)),
            full((tokens, D)),
            wide,
            wide,
            full((tokens, D)),
            full((count, D)),
        ],
        name="mlp_forward",
        cost_estimate=cost(2 * tokens * D * (2 * FF + D), 3e7, tokens * FF),
    )(x0, y, wo, wup, wdown, vectors, picks.reshape(count, 1))


def keep_tiles(values, out, top, slot):
    for c in range(2):
        out[slot + c] = values[:, c * BS : (c + 1) * BS]
    high = jnp.max(jnp.abs(values), 0, keepdims=True)
    top[...] = jnp.maximum(top[...], jnp.maximum(high[:, :BS], high[:, BS:]))


def near_far(core):
    return pl.ds(pl.multiple_of(core * BS, BS), BS), pl.ds(pl.multiple_of((1 - core) * BS, BS), BS)


def mlp_back_kernel(
    core_ref,
    ghp_ref,
    pick_ref,
    x2_ref,
    act_ref,
    up_ref,
    h_ref,
    x1_ref,
    wdown_ref,
    wup_ref,
    wo_ref,
    vec_ref,
    mine_ref,
    theirs_ref,
    mine_top_ref,
    theirs_top_ref,
    gx1_ref,
    ga_ref,
    gy_ref,
    vg_ref,
    gx2,
    gm,
    gh,
):
    j = pl.program_id(0)
    core = core_ref[0]
    tokens = x2_ref.shape[0]

    @pl.when(j == 0)
    def _():
        mine_top_ref[...] = jnp.zeros_like(mine_top_ref)
        theirs_top_ref[...] = jnp.zeros_like(theirs_top_ref)
        vg_ref[...] = jnp.zeros_like(vg_ref)
        places = lax.broadcasted_iota(i32, (tokens, pick_ref.shape[1]), 0)
        chosen = (places == pick_ref[...]).astype(bf16)
        rest = ghp_ref[...]
        spread = jnp.zeros((tokens, D), f32)
        for _ in range(3):
            part = rest.astype(bf16)
            rest = rest - part.astype(f32)
            spread = spread + mm(chosen, part)
        grad, gain, bias = norm_pull(x2_ref[...], vec_ref[4:5, :], spread)
        gx2[...] = grad
        low = grad.astype(bf16)
        gm[...] = low
        vg_ref[4:5, :] = gain
        vg_ref[5:6, :] = bias
        vg_ref[7:8, :] = jnp.sum(low.astype(f32), 0, keepdims=True)

    grad_act = mm_t(gm[...], wdown_ref[...])
    up = up_ref[...]
    turn = jnp.tanh(0.7978845608 * (up + 0.044715 * up * up * up))
    slope = 0.5 * (1.0 + turn) + 0.5 * up * (1.0 - turn * turn) * (
        0.7978845608 * (1.0 + 3.0 * 0.044715 * up * up)
    )
    gup = (grad_act * slope).astype(bf16)
    vg_ref[pl.ds(11 + j, 1), :] = jnp.sum(gup.astype(f32), 0, keepdims=True)
    part = mm_t(gup, wup_ref[...])

    @pl.when(j == 0)
    def _():
        gh[...] = part

    @pl.when(j > 0)
    def _():
        gh[...] += part

    for cols, out, top in zip(
        near_far(core), (mine_ref, theirs_ref), (mine_top_ref, theirs_top_ref)
    ):
        keep_tiles(mm_l(h_ref[:, cols], gup), out, top, 0)
        keep_tiles(mm_l(act_ref[:, cols], gm[...]), out, top, 2)

    @pl.when(j == FSTEPS - 1)
    def _():
        grad, gain, bias = norm_pull(x1_ref[...], vec_ref[2:3, :], gh[...])
        vg_ref[2:3, :] = gain
        vg_ref[3:4, :] = bias
        grad = grad + gx2[...]
        gx1_ref[...] = grad
        low = grad.astype(bf16)
        ga_ref[...] = low
        vg_ref[6:7, :] = jnp.sum(low.astype(f32), 0, keepdims=True)
        gy_ref[...] = mm_t(low, wo_ref[...]).astype(bf16)


def mlp_back(core, ghp, picks, x2, act, up, h2, x1, wdown, wup, wo, vectors):
    tokens = x2.shape[0]
    count = picks.shape[0]
    wide = pl.BlockSpec((tokens, D), lambda j: (0, j))
    flat = full((tokens, D))
    tiles = pl.BlockSpec((4, BS, BS), lambda j: (j, 0, 0))
    tops = full((1, BS))
    halves = jax.ShapeDtypeStruct((4 * FSTEPS, BS, BS), f32)
    highs = jax.ShapeDtypeStruct((1, BS), f32)
    return pl.pallas_call(
        mlp_back_kernel,
        grid=(FSTEPS,),
        out_shape=[
            halves,
            halves,
            highs,
            highs,
            jax.ShapeDtypeStruct((tokens, D), f32),
            jax.ShapeDtypeStruct((tokens, D), bf16),
            jax.ShapeDtypeStruct((tokens, D), bf16),
            jax.ShapeDtypeStruct((16, D), f32),
        ],
        in_specs=[
            pl.BlockSpec(memory_space=SMEM),
            full((count, D)),
            full((1, count)),
            flat,
            wide,
            wide,
            flat,
            flat,
            pl.BlockSpec((D, D), lambda j: (j, 0)),
            pl.BlockSpec((D, D), lambda j: (0, j)),
            full((D, D)),
            full(vectors.shape),
        ],
        out_specs=[tiles, tiles, tops, tops, flat, flat, flat, full((16, D))],
        scratch_shapes=[
            pltpu.VMEM((tokens, D), f32),
            pltpu.VMEM((tokens, D), bf16),
            pltpu.VMEM((tokens, D), f32),
        ],
        name="mlp_back",
        cost_estimate=cost(8 * tokens * D * FF, 5e7, tokens * FF),
    )(core, ghp, picks.reshape(1, count), x2, act, up, h2, x1, wdown, wup, wo, vectors)


def qkv_back_kernel(g_ref, w_ref, x_ref, gx1_ref, vec_ref, gx0_ref, vg_ref, gh):
    j = pl.program_id(0)
    part = mm_t(g_ref[0], w_ref[...])

    @pl.when(j == 0)
    def _():
        vg_ref[...] = jnp.zeros_like(vg_ref)
        gh[...] = part

    @pl.when(j > 0)
    def _():
        gh[...] += part

    vg_ref[pl.ds(8 + j, 1), :] = jnp.sum(g_ref[0].astype(f32), 0, keepdims=True)

    @pl.when(j == 2)
    def _():
        grad, gain, bias = norm_pull(x_ref[...].astype(f32), vec_ref[0:1, :], gh[...])
        vg_ref[0:1, :] = gain
        vg_ref[1:2, :] = bias
        gx0_ref[...] = (gx1_ref[...] + grad).astype(bf16)


def qkv_back(grads, wqkv, x0, gx1, vectors):
    tokens = x0.shape[0]
    flat = full((tokens, D))
    return pl.pallas_call(
        qkv_back_kernel,
        grid=(3,),
        out_shape=[
            jax.ShapeDtypeStruct((tokens, D), bf16),
            jax.ShapeDtypeStruct((16, D), f32),
        ],
        in_specs=[
            pl.BlockSpec((1, tokens, D), lambda j: (j, 0, 0)),
            pl.BlockSpec((D, D), lambda j: (0, j)),
            flat,
            flat,
            full(vectors.shape),
        ],
        out_specs=[flat, full((16, D))],
        scratch_shapes=[pltpu.VMEM((tokens, D), f32)],
        name="qkv_back",
        cost_estimate=cost(2 * tokens * D * 3 * D, 1e7),
    )(grads, wqkv, x0, gx1, vectors)


def qkv_weights_kernel(
    core_ref, h_ref, g_ref, y_ref, ga_ref, small_ref, mine_ref, theirs_ref, mtop_ref, ttop_ref
):
    j = pl.program_id(0)
    core = core_ref[0]
    both = tuple(zip(near_far(core), (mine_ref, theirs_ref), (mtop_ref, ttop_ref)))

    @pl.when(j == 0)
    def _():
        for turn, (_, out, top) in enumerate(both):
            values = small_ref[core if turn == 0 else 1 - core]
            out[8] = values
            top[...] = jnp.max(jnp.abs(values), 0, keepdims=True)

    @pl.when(j < 3)
    def _():
        for cols, out, top in both:
            keep_tiles(mm_l(h_ref[:, cols], g_ref[0]), out, top, 2 * j)

    @pl.when(j == 3)
    def _():
        for cols, out, top in both:
            keep_tiles(mm_l(y_ref[:, cols], ga_ref[...]), out, top, 6)


def qkv_weights(core, h1, grads, y, ga, small):
    tokens = h1.shape[0]
    flat = full((tokens, D))
    halves = (9, BS, BS)
    highs = (1, BS)
    shapes = (halves, halves, highs, highs)
    return pl.pallas_call(
        qkv_weights_kernel,
        grid=(4,),
        out_shape=[jax.ShapeDtypeStruct(shape, f32) for shape in shapes],
        in_specs=[
            pl.BlockSpec(memory_space=SMEM),
            flat,
            pl.BlockSpec((1, tokens, D), lambda j: (jnp.minimum(j, 2), 0, 0)),
            flat,
            flat,
            full((2, BS, BS)),
        ],
        out_specs=[full(shape) for shape in shapes],
        name="qkv_weights",
        cost_estimate=cost(2 * tokens * D * 4 * D, 2e7),
    )(core, h1, grads, y, ga, small)


def comm_positions():
    side = np.zeros(48, np.int32)
    place = np.zeros(48, np.int32)
    for r in range(2):
        for c in range(2):
            for j in range(FSTEPS):
                place[16 + r * 8 + 2 * j + c] = 4 * j + c
                place[32 + (2 * j + r) * 2 + c] = 4 * j + 2 + c
                side[16 + r * 8 + 2 * j + c] = side[32 + (2 * j + r) * 2 + c] = r
            for j in range(3):
                place[r * 6 + 2 * j + c] = 16 + 2 * j + c
                side[r * 6 + 2 * j + c] = r
            place[12 + r * 2 + c] = 22 + c
            side[12 + r * 2 + c] = r
    return side, place


def lane_block(rows_all):
    return min(1280, (rows_all // 128 + 1) * 128)


def fill_table(places_ref, pieces, tab, valid):
    depth = pieces[0].shape[0]
    for p, piece in enumerate(pieces):
        start = pl.multiple_of(places_ref[p], depth)
        tab[pl.ds(start, depth), :] = jnp.where(valid, piece[...], jnp.zeros((), bf16))


def logits_kernel(rows_all, count, places_ref, group_ref, target_ref, *refs):
    pieces = refs[:count]
    logit_ref, stat_ref, tab, top, total, chosen = refs[count:]
    j = pl.program_id(0)
    wide = tab.shape[1]
    lane = lax.broadcasted_iota(i32, (1, wide), 1) + j * wide
    valid = lane < rows_all
    fill_table(places_ref, pieces, tab, valid)

    @pl.when(j == 0)
    def _():
        top[...] = jnp.full(top.shape, -jnp.inf, f32)
        total[...] = jnp.zeros(total.shape, f32)
        chosen[...] = jnp.zeros(chosen.shape, f32)

    logits = mm(group_ref[...], tab[...])
    logit_ref[...] = logits
    kept = jnp.where(valid, logits, -jnp.inf)
    before = top[...]
    after = jnp.maximum(before, jnp.max(kept, -1, keepdims=True))
    top[...] = after
    total[...] = total[...] * jnp.exp(before - after) + jnp.sum(
        jnp.exp(kept - after), -1, keepdims=True
    )
    hit = (lane == target_ref[...]) & valid
    chosen[...] += jnp.sum(jnp.where(hit, logits, 0.0), -1, keepdims=True)

    @pl.when(j == pl.num_programs(0) - 1)
    def _():
        spot = lax.broadcasted_iota(i32, (1, 128), 1)
        merged = jnp.where(
            spot == 0, top[...], jnp.where(spot == 1, total[...], chosen[...])
        )
        stat_ref[...] = merged.T[:8]


def table_specs(pieces, wide):
    return [pl.BlockSpec((pieces[0].shape[0], wide), lambda j: (0, j))] * len(pieces)


def vocabulary_logits(places, group, local_targets, pieces):
    count, rows_all = group.shape[0], pieces[0].shape[1]
    wide = lane_block(rows_all)
    return pl.pallas_call(
        partial(logits_kernel, rows_all, len(pieces)),
        grid=(pl.cdiv(rows_all, wide),),
        out_shape=[
            jax.ShapeDtypeStruct((count, rows_all), f32),
            jax.ShapeDtypeStruct((8, count), f32),
        ],
        in_specs=[pl.BlockSpec(memory_space=SMEM), full((count, D)), full((count, 1))]
        + table_specs(pieces, wide),
        out_specs=[pl.BlockSpec((count, wide), lambda j: (0, j)), full((8, count))],
        scratch_shapes=[pltpu.VMEM((D, wide), bf16)] + [pltpu.VMEM((count, 1), f32)] * 3,
        name="vocabulary_logits",
        cost_estimate=cost(2 * count * D * rows_all, 2e7, count * rows_all),
    )(places, group, local_targets.reshape(count, 1), *pieces)


def vocabulary_back_kernel(
    rows_all, count, scale, places_ref, logit_ref, stat_ref, target_ref, *refs
):
    pieces = refs[:count]
    grad_ref, ghp_ref, tab, stat = refs[count:]
    j = pl.program_id(0)
    wide = tab.shape[1]
    lane = lax.broadcasted_iota(i32, (1, wide), 1) + j * wide
    valid = lane < rows_all
    fill_table(places_ref, pieces, tab, valid)

    @pl.when(j == 0)
    def _():
        stat[...] = stat_ref[...].T
        ghp_ref[...] = jnp.zeros_like(ghp_ref)

    hit = (lane == target_ref[...]).astype(f32)
    soft = jnp.exp(logit_ref[...] - stat[:, 0:1]) * stat[:, 1:2]
    grads = jnp.where(valid, (soft - hit) * scale, 0.0).astype(bf16)
    grad_ref[...] = grads
    ghp_ref[...] += mm_t(grads, tab[...])


def vocabulary_back(places, logits, stats, local_targets, pieces, scale):
    count, rows_all = logits.shape
    wide = lane_block(rows_all)
    block = pl.BlockSpec((count, wide), lambda j: (0, j))
    return pl.pallas_call(
        partial(vocabulary_back_kernel, rows_all, len(pieces), scale),
        grid=(pl.cdiv(rows_all, wide),),
        out_shape=[
            jax.ShapeDtypeStruct((count, pl.cdiv(rows_all, wide) * wide), bf16),
            jax.ShapeDtypeStruct((count, D), f32),
        ],
        in_specs=[
            pl.BlockSpec(memory_space=SMEM),
            block,
            full(stats.shape),
            full((count, 1)),
        ]
        + table_specs(pieces, wide),
        out_specs=[block, full((count, D))],
        scratch_shapes=[pltpu.VMEM((D, wide), bf16), pltpu.VMEM((count, stats.shape[0]), f32)],
        name="vocabulary_back",
        cost_estimate=cost(2 * count * D * rows_all, 3e7, count * rows_all),
    )(places, logits, stats, local_targets.reshape(count, 1), *pieces)


def lexicon_kernel(
    depth, places_ref, turned_ref, grad_ref, mine_ref, theirs_ref, mtop_ref, ttop_ref, sel
):
    j = pl.program_id(0)
    half = mine_ref.shape[0]

    @pl.when(j == 0)
    def _():
        for p in range(sel.shape[0] // depth):
            start = pl.multiple_of(places_ref[p], depth)
            sel[pl.ds(p * depth, depth), :] = turned_ref[pl.ds(start, depth), :]
        mtop_ref[...] = jnp.zeros_like(mtop_ref)
        ttop_ref[...] = jnp.zeros_like(ttop_ref)

    for start, out, top in ((0, mine_ref, mtop_ref), (half, theirs_ref, ttop_ref)):
        part = mm(sel[pl.ds(start, half), :], grad_ref[...])
        out[...] = part
        top[...] = jnp.maximum(top[...], jnp.max(jnp.abs(part), 0, keepdims=True))


def lexicon(places, turned, grads, depth, rows_all):
    count, padded = grads.shape
    wide = lane_block(rows_all)
    half = D // 2
    block = pl.BlockSpec((half, wide), lambda j: (0, j))
    return pl.pallas_call(
        partial(lexicon_kernel, depth),
        grid=(padded // wide,),
        out_shape=[jax.ShapeDtypeStruct((half, padded), f32)] * 2
        + [jax.ShapeDtypeStruct((1, wide), f32)] * 2,
        in_specs=[
            pl.BlockSpec(memory_space=SMEM),
            full((D, count)),
            pl.BlockSpec((count, wide), lambda j: (0, j)),
        ],
        out_specs=[block, block, full((1, wide)), full((1, wide))],
        scratch_shapes=[pltpu.VMEM((D, count), bf16)],
        name="lexicon",
        cost_estimate=cost(2 * count * D * padded, 3e7),
    )(places, turned, grads)


def three(left, right, product):
    left_high, left_low = left
    right_high, right_low = right
    return (
        product(left_high, right_high)
        + product(left_high, right_low)
        + product(left_low, right_high)
    )


def shampoo_kernel(count, strip, places_ref, clip_ref, *refs):
    pieces, smalls, tails = refs[:count], refs[count : 2 * count], refs[2 * count : 3 * count]
    w_ref, ls_ref, rs_ref, lr_ref, rr_ref = refs[3 * count : 3 * count + 5]
    g_ref, nw_ref, nl_ref, nr_ref, small_ref = refs[3 * count + 5 :]
    clip = clip_ref[0]
    for k in range(count):
        place = pl.multiple_of(places_ref[k], strip)
        scale = jnp.exp2(tails[k][0:1, :] - 15.0) * clip
        g_ref[0, pl.ds(place, strip), :] = pieces[k][...] * scale

        @pl.when(pl.program_id(0) == 0)
        def _(k=k, place=place, scale=scale):
            for side in range(2):
                values = smalls[k][pl.ds(side * strip, strip), :] * scale
                small_ref[side, pl.ds(place, strip), :] = values

    grads = split_two(g_ref[0])
    for old, new, product in ((ls_ref, nl_ref, mm_t), (rs_ref, nr_ref, mm_l)):
        cross = product(grads[0], grads[1])
        outer = product(grads[0], grads[0]) + (cross + cross.T)
        new[0] = SHAMPOO_BETA * old[0] + (1.0 - SHAMPOO_BETA) * outer
    turned = split_two(three(grads, split_two(rr_ref[0]), mm))
    direction = three(split_two(lr_ref[0]), turned, mm)
    weights = w_ref[0]
    nw_ref[0] = weights - RATE_BLOCKS * (direction + DECAY_RATE * weights)


def shampoo(places, clip, pieces, strip, kept):
    slots = kept[0].shape[0]
    count = len(pieces)
    block = pl.BlockSpec((1, BS, BS), lambda s: (s, 0, 0))
    shape = jax.ShapeDtypeStruct((slots, BS, BS), f32)
    small_at, tail_at = slots // 2, (slots + 2) * strip // 16
    return pl.pallas_call(
        partial(shampoo_kernel, count, strip),
        grid=(slots,),
        out_shape=[shape] * 4 + [jax.ShapeDtypeStruct((2, BS, BS), f32)],
        in_specs=[pl.BlockSpec(memory_space=SMEM)] * 2
        + [pl.BlockSpec((strip, BS), lambda s: (s, 0))] * count
        + [pl.BlockSpec((2 * strip, BS), lambda s: (small_at, 0))] * count
        + [pl.BlockSpec((16, BS), lambda s: (tail_at, 0))] * count
        + [block] * 5,
        out_specs=[block] * 4 + [full((2, BS, BS))],
        name="shampoo",
        cost_estimate=cost(slots * 24 * BS**3, slots * BS * BS * 40),
    )(places, clip, *pieces, *pieces, *pieces, *kept)


def adam_update(weight, first, second, gradient, rate, step_value):
    first_new = BETA_FIRST * first + (1.0 - BETA_FIRST) * gradient
    second_new = BETA_SECOND * second + (1.0 - BETA_SECOND) * gradient * gradient
    first_hat = first_new / (1.0 - BETA_FIRST**step_value)
    second_hat = second_new / (1.0 - BETA_SECOND**step_value)
    return (
        weight - rate * (first_hat / (jnp.sqrt(second_hat) + ADAM_EPSILON) + DECAY_RATE * weight),
        first_new,
        second_new,
    )


def tie(values, *others):
    return lax.optimization_barrier((values,) + others)[0]


def exponent(bound):
    return jnp.floor(jnp.log2(jnp.maximum(bound, 1e-30))) + 1.0


def encode(values, bound):
    level = exponent(bound)
    coded = (values * jnp.exp2(15.0 - level)).astype(jnp.float16)
    return coded.reshape(-1, values.shape[-1]), level.astype(jnp.float16)


def pack(values, bound):
    coded, level = encode(values, bound)
    return jnp.concatenate([coded, jnp.broadcast_to(level, (16, coded.shape[1]))], 0)


def unpack(payload, shape):
    count = payload.shape[0] - 16
    wide = payload.astype(f32)
    level = wide[count : count + 1]
    values = wide[:count] * jnp.exp2(level - 15.0)
    return values.reshape(shape), jnp.exp2(payload[-1, 0].astype(f32))


def pack_lanes(values, bound):
    coded, level = encode(values, bound)
    lane = lax.broadcasted_iota(i32, coded.shape, 1)
    return jnp.where(lane == coded.shape[1] - 1, level, coded)


def unpack_lanes(payload):
    level = payload[0, -1].astype(f32)
    return payload.astype(f32) * jnp.exp2(level - 15.0)


def per_device(
    sizes,
    token_ids,
    seq_lengths,
    pick_rows,
    targets,
    step_count,
    block_order,
    slot_weights,
    left_stats,
    right_stats,
    left_roots,
    right_roots,
    embedding,
    embedding_first_moment,
    emb_second,
    vectors,
    vec_first,
    vec_second,
    feature_maps,
    map_first,
    map_second,
):
    ny, nc, n1, n0 = sizes
    n_dp, n_voc = ny * nc, n1 * n0
    dp_index, voc_index = lax.axis_index("dp"), lax.axis_index("vocab")
    y_at, c_at = dp_index // nc, dp_index % nc
    i1, i0 = voc_index // n0, voc_index % n0

    def over_dp(values, dy, dc):
        pairs = [
            (a * nc + b, ((a + dy) % ny) * nc + (b + dc) % nc) for a in range(ny) for b in range(nc)
        ]
        return lax.ppermute(values, "dp", pairs)

    def over_voc(values, d1, d0):
        pairs = [
            (a * n0 + b, ((a + d1) % n1) * n0 + (b + d0) % n0) for a in range(n1) for b in range(n0)
        ]
        return lax.ppermute(values, "vocab", pairs)

    def gather_voc(values):
        near = [values] + [over_voc(values, k, 0) for k in range(1, n1)]
        return [[part] + [over_voc(part, 0, k) for k in range(1, n0)] for part in near]

    def gather_stacked(values):
        near = jnp.stack([values] + [over_voc(values, 0, k) for k in range(1, n0)])
        return jnp.stack([near] + [over_voc(near, k, 0) for k in range(1, n1)])

    def flat_gather(values):
        return [part for line in gather_voc(values) for part in line]

    def gather_y(values):
        return [values] + [over_dp(values, k, 0) for k in range(1, ny)]

    def line_up(parts, at):
        size = len(parts)
        return jnp.take(jnp.stack(parts), (at - jnp.arange(size)) % size, axis=0)

    tokens = token_ids.shape[0]
    picks_own = pick_rows.shape[0]
    devices_all = n_dp * n_voc
    total_picks = picks_own * devices_all
    coefficient = DISTILL_WEIGHT / (tokens * devices_all * HEADS)
    shard_rows, cols_own = embedding.shape
    cols_y = cols_own * nc
    vocab_start = (voc_index * shard_rows).astype(i32)
    per_owner = slot_weights.shape[0]
    block_count = block_order.shape[0]
    table_own = embedding.T
    core = c_at.astype(i32).reshape(1)
    piece_places = jnp.stack(
        [
            (((y_at - ky) % ny) * nc + (c_at + kc) % nc) * cols_own
            for kc in range(nc)
            for ky in range(ny)
        ]
    ).astype(i32)

    low_own = table_own.astype(bf16)
    low_other = over_dp(low_own, 0, 1)
    upright = turn_table(core, low_own, low_other)

    ids_y = gather_y(token_ids)
    numbers = jnp.concatenate(ids_y + [targets])

    slots_y = gather_y(tie(slot_weights.astype(bf16), numbers))
    numbers = gather_stacked(numbers)
    targets_all = numbers[:, :, ny * tokens :].reshape(-1)
    lines = sorted(range(1, n1), key=lambda a: -min(a, n1 - a)) + [0]
    piece_order = [(a, b) for b in list(range(1, n0)) + [0] for a in lines]
    early = (n0 - 1) * n1
    ids_order = [numbers[a, b, : ny * tokens] for a, b in piece_order]
    looked, hits = [], []
    for first, last in ((0, early), (early, n0 * n1)):
        ids_rows = jnp.concatenate(ids_order[first:last])
        local_ids = ids_rows - vocab_start
        packed_ids = jnp.where(
            (local_ids >= 0) & (local_ids < shard_rows),
            (local_ids << 16) | jnp.arange(ids_rows.shape[0], dtype=i32),
            -1,
        )
        hits.append(find_hits(tie(packed_ids, upright), shard_rows))
        looked += lookup(hits[-1], upright, ids_rows.shape[0], last - first)

    def near_piece(h, sums, *before):
        part = looked[n1 * (n0 - 1) + h]
        for b in range(1, n0):
            moved = over_voc(tie(looked[(b - 1) * n1 + h], *sums[: max(h - 1, 0)]), 0, -b)
            part = part + tie(moved, *sums, *before)
        return part.reshape(ny, tokens, cols_y)

    by_one = []
    for h in range(n1 - 1):
        by_one.append(near_piece(h, by_one))
    slots_y = [tie(part, by_one[1]) for part in slots_y]
    slots_core = [over_dp(part, 0, 1) for part in slots_y]
    inverse = (
        jnp.zeros((block_count,), i32).at[block_order].set(jnp.arange(block_count, dtype=i32))
    )
    owner = inverse // per_owner
    src = ((c_at - owner % nc) % nc) * ny + (y_at - owner // nc) % ny
    wqkv, wo, wup, wdown = place_blocks(
        src.astype(i32), inverse % per_owner, slots_y + slots_core
    )

    far_parts = [over_voc(by_one[h], -lines[h], 0) for h in range(n1 - 1)]
    by_one.append(near_piece(n1 - 1, by_one, wup, far_parts[0]))
    mine = by_one[-1]
    for part in far_parts:
        mine = mine + part

    row_parts = [mine[0]] + [over_dp(mine[k], -k, 0) for k in range(1, ny)]
    if ny == 2:
        first = y_at == 0
        x0 = jnp.concatenate(
            [
                jnp.where(first, row_parts[0], row_parts[1]),
                jnp.where(first, row_parts[1], row_parts[0]),
            ],
            1,
        )
    else:
        stacked = jnp.stack(row_parts)
        x0 = jnp.concatenate(
            [jnp.take(stacked, (j - y_at) % ny, axis=0) for j in range(ny)], axis=1
        )

    low_sent = tie(low_own, x0)
    low_y = [over_dp(low_sent, k, 0) for k in range(1, ny)]

    maps_low = feature_maps.astype(bf16)
    both = jnp.concatenate([maps_low, -maps_low], -1).reshape(2, PAIRS, 2, HD, 2 * HD)
    empty = jnp.zeros_like(both[:, :, 0])
    lift_maps = jnp.stack(
        [
            jnp.concatenate([both[:, :, 0], empty], -2),
            jnp.concatenate([empty, both[:, :, 1]], -2),
        ],
        2,
    ).reshape(2, HEADS, 2 * HD, 2 * HD)
    their_hits = [over_dp(own, 0, 1) for own in hits]
    h1, mixed = qkv_forward(tie(x0, *their_hits), wqkv, vectors)
    y, distill = attend(seq_lengths, mixed, lift_maps)
    x1, h2, up, act, x2, picked = mlp_forward(x0, y, wo, wup, wdown, vectors, pick_rows)

    near_picked = [picked] + [over_voc(picked, 0, k) for k in range(1, n0)]
    low_y = [tie(part, *near_picked) for part in low_y]
    low_y_other = [over_dp(part, 0, 1) for part in low_y]
    pieces = [low_own] + low_y + [low_other] + low_y_other
    near_picked = jnp.concatenate(near_picked, 0)
    group = [near_picked] + [over_voc(near_picked, k, 0) for k in range(1, n1)]
    group = jnp.concatenate(group, 0)
    local_targets = targets_all - vocab_start
    logits, stats = vocabulary_logits(piece_places, group, local_targets, pieces)
    stats_all = gather_stacked(stats)
    lined = jnp.stack(
        [
            jnp.roll(stats_all[a, b, :3].reshape(3, n1, n0, picks_own), (a, b), (1, 2))
            for a in range(n1)
            for b in range(n0)
        ]
    ).reshape(n_voc, 3, n_voc * picks_own)
    top_all = jnp.max(lined[:, 0], 0)
    sum_all = jnp.sum(lined[:, 1] * jnp.exp(lined[:, 0] - top_all[None]), 0)
    losses = top_all + jnp.log(sum_all) - jnp.sum(lined[:, 2], 0)
    loss_part = jnp.sum(losses[:picks_own]) / total_picks + coefficient * distill[0, 0]
    shares = jnp.pad(jnp.stack([top_all, 1.0 / sum_all]), ((0, 126), (0, 0)))
    grad_logits, grad_group = vocabulary_back(
        piece_places, logits, shares, local_targets, pieces, 1.0 / total_picks
    )
    grad_group = grad_group.reshape(n1, n0, picks_own, D)
    by_one = []
    for a in list(range(1, n1)) + [0]:
        part = grad_group[a, 0]
        for b in range(1, n0):
            part = part + over_voc(grad_group[a, b], 0, -b)
        by_one.append(part)
    near_parts = [over_voc(by_one[a - 1], -a, 0) for a in range(1, n1)]

    lex_mine, lex_theirs, mine_high, theirs_high = lexicon(
        piece_places, group.T, tie(grad_logits, *by_one[:-1]), cols_own, shard_rows
    )
    lex_arrived = over_dp(lex_theirs, 0, 1)
    lex_high = jnp.max(mine_high) + jnp.max(over_dp(theirs_high, 0, 1))
    ghp = by_one[-1]
    for part in near_parts:
        ghp = ghp + tie(part, lex_theirs)

    def lex_lines(k):
        lines = slice(k * cols_own, (k + 1) * cols_own)
        return lex_mine[lines] + lex_arrived[lines]

    lex_sent = [pack_lanes(lex_lines(k), lex_high) for k in range(1, ny)]


    def core_parts(mine_part, their_part, mine_top, their_top, *later):
        arrived = tie(over_dp(their_part, 0, 1), *later)
        bound = jnp.max(mine_top) + jnp.max(over_dp(their_top, 0, 1))
        return coded_parts((mine_part, arrived), bound, 0) + (bound,)

    def coded_parts(parts, bound, axis):
        size = (n0, ny, n1)[axis]

        def lines(part, k):
            count = part.shape[0]
            if axis == 1:
                rows = part.reshape(count, n1, ny, -1, BS)
                rows = lax.dynamic_index_in_dim(rows, (y_at + k) % ny, 2, False)
                return rows.reshape(count, -1, BS)
            rows = part.shape[1] // size
            at = (i0 if axis == 0 else i1) + k
            return lax.dynamic_slice_in_dim(part, (at % size) * rows, rows, 1)

        def summed(k):
            cut = [lines(part, k) for part in parts]
            return sum(cut[1:], cut[0])

        return summed(0), [pack(summed(k), bound) for k in range(1, size)]

    def moved_parts(sent, axis):
        if axis == 1:
            return [over_dp(part, k, 0) for k, part in enumerate(sent, 1)]
        return [
            over_voc(part, k, 0) if axis == 2 else over_voc(part, 0, k)
            for k, part in enumerate(sent, 1)
        ]

    def collect(own, arrived, bound, *later):
        total, high = own, bound
        for part in arrived:
            values, top = unpack(tie(part, *later), own.shape)
            total = total + values
            high = high + top
        return total, high

    *halves_a, gx1, ga, gy, vg_a = mlp_back(
        core, ghp, pick_rows, x2, act, up, h2, x1, wdown, wup, wo, vectors
    )
    own_a, sent_a, bound_a = core_parts(*halves_a, *lex_sent)
    gy = tie(gy, *lex_sent, own_a, *sent_a)
    gqkv, map_q, map_k = attend_back(
        seq_lengths, mixed, gy, lift_maps, coefficient, 0, PAIRS, None
    )
    lex_parts = [over_dp(part, -k, 0) for k, part in enumerate(lex_sent, 1)]
    gx0, vg_b = qkv_back(gqkv, wqkv, x0, gx1, vectors)

    map_grads = jnp.concatenate([map_q, map_k], 0)
    vec_grads = (vg_a + vg_b)[:15]
    small_count = map_grads.size + vec_grads.size
    small = jnp.concatenate(
        [
            map_grads.reshape(-1),
            vec_grads.reshape(-1),
            jnp.zeros((2 * BS * BS - small_count,), f32),
        ]
    ).reshape(2, BS, BS)
    gx0_cols = gx0.reshape(tokens, ny, cols_y)
    cols_sent = [jnp.take(gx0_cols, (y_at + k) % ny, axis=1) for k in range(1, ny)]
    lex = lex_lines(0)
    for part in lex_parts:
        lex = lex + unpack_lanes(part)
    arrived = [jnp.take(gx0_cols, y_at, axis=1)] + [
        tie(over_dp(part, k, 0), lex) for k, part in enumerate(cols_sent, 1)
    ]
    arrived = jnp.concatenate(arrived, 0).reshape(ny * tokens, nc, cols_own)
    rows_mine = jnp.take(arrived, c_at, axis=1)
    moved_a = moved_parts(sent_a, 0)
    rows_sent = jnp.take(arrived, (c_at + 1) % nc, axis=1)
    rows_other = over_dp(rows_sent, 0, 1)
    if cols_own == 192:
        packed = jnp.concatenate(
            [
                rows_mine[:, :128],
                rows_other[:, :128],
                jnp.concatenate([rows_mine[:, 128:], rows_other[:, 128:]], 1),
            ],
            0,
        )
    else:
        packed = jnp.stack([rows_mine, rows_other])
    halves_b = qkv_weights(core, tie(h1, rows_sent, *moved_a), gqkv, y, ga, small)
    total_a, high_a = collect(own_a, moved_a, bound_a, halves_b[0])
    own_b, sent_b, bound_b = core_parts(*halves_b, packed)
    near_raw = [over_voc(packed, k, 0) for k in range(1, n1)]
    total_b, high_b = collect(own_b, moved_parts(sent_b, 0), bound_b, near_raw[0])
    total = jnp.concatenate([total_a, total_b], 0)
    high = jnp.maximum(high_a, high_b)
    own, sent = coded_parts((total,), high, 1)
    near_rows = [packed] + [tie(part, *sent) for part in near_raw]
    total, high = collect(own, moved_parts(sent, 1), high)
    own, sent = coded_parts((total,), high, 2)
    gathered = [[packed] + [over_voc(packed, 0, k) for k in range(1, n0)]]
    sent = [tie(part, *near_rows, *gathered[0]) for part in sent]
    gathered += [[part] + [over_voc(part, 0, k) for k in range(1, n0)] for part in near_rows[1:]]
    moved_ab = moved_parts(sent, 2)
    lex = tie(lex, moved_ab[0])
    if cols_own == 192:
        pieces = [gathered[a][b] for a, b in piece_order]
        emb_grads, emb_square = scatter_rows(
            list(zip(hits, their_hits)), lex, pieces, shard_rows
        )
        emb_square = emb_square[0, 0]
    else:
        pieces = jnp.stack([gathered[a][b] for a, b in piece_order], 1).reshape(-1, cols_own)
        ids_rows = jnp.concatenate(ids_order)
        local = jnp.concatenate([ids_rows, over_dp(ids_rows, 0, 1)]) - vocab_start
        local = jnp.where((local >= 0) & (local < shard_rows), local, shard_rows)
        emb_grads = lex[:, :shard_rows].T.at[local].add(pieces.astype(f32), mode="drop").T
        emb_square = jnp.sum(emb_grads * emb_grads)
    blocks = collect(own, moved_ab, high, emb_grads)[0]

    square = emb_square + jnp.sum(blocks * blocks)
    sums = jnp.pad(jnp.stack([square, loss_part]).reshape(1, 2), ((0, 7), (0, 126)))
    sums = sums + over_dp(sums, 0, 1)
    sums = jnp.sum(line_up(gather_y(sums), y_at), 0)
    per_side = blocks.shape[0]
    both = jnp.concatenate([blocks, over_dp(blocks, 0, 1)], 0)
    side, place = comm_positions()
    side = jnp.concatenate([jnp.take(jnp.asarray(side), block_order), jnp.arange(2, dtype=i32)])
    place = jnp.concatenate(
        [jnp.take(jnp.asarray(place), block_order), jnp.full((2,), per_side - 1, i32)]
    )
    at_place = ((side - c_at) % nc) * per_side + place
    smalls = at_place[block_count:]
    at_place = at_place[:block_count].reshape(ny, nc, per_owner)

    def slots_of(k):
        mine = jnp.take(jnp.take(at_place, c_at, axis=1), (y_at + k) % ny, axis=0)
        return jnp.take(both, jnp.concatenate([mine, smalls]), axis=0)

    moved = [slots_of(k) for k in range(1, ny)]
    slots_sent = [pack(part, jnp.max(jnp.abs(both))) for part in moved]
    sums = tie(sums, *slots_sent)
    sums = jnp.sum(line_up([sums] + [over_voc(sums, 0, k) for k in range(1, n0)], i0), 0)

    small_own = unpack(slots_sent[0], moved[0].shape)[0][per_owner:]
    strip_parts = [jnp.concatenate([slots_of(0)[:per_owner], small_own], 0)]
    slots_moved = moved_parts(slots_sent, 1)
    sums = tie(sums, *slots_moved)
    for part in slots_moved:
        strip_parts.append(unpack(part, moved[0].shape)[0])
    sums = jnp.sum(line_up([sums] + [over_voc(sums, k, 0) for k in range(1, n1)], i1), 0)
    grad_norm = jnp.sqrt(sums[0, 0])
    loss_total = sums[0, 1]
    clip_scale = CLIP_NORM / jnp.maximum(grad_norm, CLIP_NORM)
    own_strips = line_up(strip_parts, y_at).transpose(1, 0, 2, 3)
    own_strips = own_strips.reshape(per_owner + 2, -1, BS)
    strip_rows = own_strips.shape[1]
    strip_half = BS // n0
    places = [
        ((i0 - b) % n0) * strip_half + ((i1 - a) % n1) * strip_rows
        for a in range(n1)
        for b in range(n0)
    ]
    places = jnp.stack(places).astype(i32)
    strip_sent = tie(pack(own_strips, jnp.max(jnp.abs(own_strips))), sums)
    strip_pieces = [part.astype(f32) for part in flat_gather(strip_sent)]
    clipped, new_slots, new_left, new_right, small_all = shampoo(
        places,
        clip_scale.reshape(1),
        strip_pieces,
        strip_rows,
        (slot_weights, left_stats, right_stats, left_roots, right_roots),
    )
    clip_late = tie(clip_scale, strip_sent)
    small_all = small_all.reshape(-1)
    map_grad = small_all[: map_grads.size].reshape(feature_maps.shape)
    vec_grad = small_all[map_grads.size : small_count].reshape(vectors.shape)

    step_value = step_count[0].astype(f32)
    emb_out = adam_update(
        table_own,
        embedding_first_moment.T,
        emb_second.T,
        emb_grads * clip_late,
        RATE_TABLE,
        step_value,
    )
    vec_out = adam_update(
        vectors, vec_first, vec_second, vec_grad, RATE_VECTORS, step_value
    )
    map_out = adam_update(
        feature_maps, map_first, map_second, map_grad, RATE_MAPS, step_value
    )
    return (
        loss_total,
        grad_norm,
        clipped,
        new_slots,
        new_left,
        new_right,
        emb_out[0].T,
        emb_out[1].T,
        emb_out[2].T,
        vec_out[0],
        vec_out[1],
        vec_out[2],
        map_out[0],
        map_out[1],
        map_out[2],
    )


def solution(mesh):
    n_dp, n_voc = mesh.shape["dp"], mesh.shape["vocab"]
    sizes = (n_dp // 2, 2, 4, n_voc // 4)
    rows = P(("dp", "vocab"))
    blocks = P("dp", None, None)
    table = P("vocab", "dp")
    placed = (
        (rows, P(("dp", "vocab"), None), rows, rows, P(), P())
        + (blocks,) * 5
        + (table,) * 3
        + (P(),) * 6
    )
    return jax.shard_map(
        partial(per_device, sizes),
        mesh=mesh,
        in_specs=placed,
        out_specs=(P(), P()) + (blocks,) * 4 + (table,) * 3 + (P(),) * 6,
        check_vma=False,
    )
```

```python
from functools import partial

import jax
import jax.numpy as jnp
import numpy as np
from jax import lax
from jax.experimental import pallas as pl
from jax.experimental.pallas import tpu as pltpu
from jax.sharding import PartitionSpec as P

D = 768
HEADS = 12
HD = 64
FF = 3072
BS = 384
PAIRS = HEADS // 2

NORM_EPSILON = 1e-05
CLIP_NORM = 0.01
DISTILL_WEIGHT = 0.5
BETA_FIRST = 0.9
BETA_SECOND = 0.95
ADAM_EPSILON = 1e-08
DECAY_RATE = 0.01
SHAMPOO_BETA = 0.95
RATE_BLOCKS = 0.1
RATE_TABLE = 0.05
RATE_VECTORS = 0.2
RATE_MAPS = 0.1

f32 = jnp.float32
bf16 = jnp.bfloat16
i32 = jnp.int32
SMEM = pltpu.SMEM
ANY = pl.ANY


def mm(left, right):
    return lax.dot_general(left, right, (((1,), (0,)), ((), ())), preferred_element_type=f32)


def mm_t(left, right):
    return lax.dot_general(left, right, (((1,), (1,)), ((), ())), preferred_element_type=f32)


def mm_l(left, right):
    return lax.dot_general(left, right, (((0,), (0,)), ((), ())), preferred_element_type=f32)


def split_two(values):
    high = values.astype(bf16)
    return high, (values - high.astype(f32)).astype(bf16)


def full(shape):
    return pl.BlockSpec(shape, lambda *_: (0,) * len(shape))


def cost(flops, bytes_moved, transcendentals=0):
    return pl.CostEstimate(
        flops=int(flops * 0.02),
        bytes_accessed=int(bytes_moved * 0.02),
        transcendentals=int(transcendentals * 0.02),
    )


def place_kernel(piece_count, src_ref, off_ref, *refs):
    pieces = refs[:piece_count]
    outs = refs[piece_count : piece_count + 4]
    sems = refs[piece_count + 4]
    base = 0
    for out, rows, cols in zip(outs, (D, D, D, FF), (3 * D, D, FF, D)):
        wide = cols // BS
        count = (rows // BS) * wide

        def go(t, carry, out=out, wide=wide, base=base):
            k = base + t
            r0 = pl.multiple_of((t // wide) * BS, BS)
            c0 = pl.multiple_of((t % wide) * BS, BS)
            for p in range(piece_count):

                @pl.when(src_ref[k] == p)
                def _(p=p):
                    pltpu.make_async_copy(
                        pieces[p].at[off_ref[k]],
                        out.at[pl.ds(r0, BS), pl.ds(c0, BS)],
                        sems.at[k],
                    ).start()

            return carry

        lax.fori_loop(0, count, go, 0)
        base += count
    base = 0
    for out, rows, cols in zip(outs, (D, D, D, FF), (3 * D, D, FF, D)):
        count = (rows // BS) * (cols // BS)

        def done(t, carry, out=out, base=base):
            pltpu.make_async_copy(
                pieces[0].at[0], out.at[pl.ds(0, BS), pl.ds(0, BS)], sems.at[base + t]
            ).wait()
            return carry

        lax.fori_loop(0, count, done, 0)
        base += count


def place_blocks(src, off, pieces):
    count = len(pieces)
    return pl.pallas_call(
        partial(place_kernel, count),
        out_shape=[
            jax.ShapeDtypeStruct(shape, bf16)
            for shape in ((D, 3 * D), (D, D), (D, FF), (FF, D))
        ],
        in_specs=[pl.BlockSpec(memory_space=SMEM)] * 2 + [pl.BlockSpec(memory_space=ANY)] * count,
        out_specs=[pl.BlockSpec(memory_space=pltpu.VMEM)] * 4,
        scratch_shapes=[pltpu.SemaphoreType.DMA((48,))],
        name="place_blocks",
        cost_estimate=cost(0, 2 * 48 * BS * BS * 2),
    )(src, off, *pieces)


def hits_kernel(empty_row, packed_ref, list_ref):
    total = packed_ref.shape[0]

    def go(i, n):
        for u in range(16):
            entry = packed_ref[i * 16 + u]
            list_ref[n] = entry
            n = n + 1 + (entry >> 31)
        return n

    n = lax.fori_loop(0, total // 16, go, jnp.int32(0))
    list_ref[total + 8] = n
    for u in range(8):
        list_ref[n + u] = empty_row << 16


def find_hits(packed, empty_row):
    total = packed.shape[0]
    return pl.pallas_call(
        partial(hits_kernel, empty_row),
        out_shape=jax.ShapeDtypeStruct((total + 16,), i32),
        in_specs=[pl.BlockSpec(memory_space=SMEM)],
        out_specs=pl.BlockSpec(memory_space=SMEM),
        name="find_hits",
        cost_estimate=cost(1e10, total * 8),
    )(packed)


def turn_kernel(core_ref, own_ref, other_ref, out_ref):
    first = core_ref[0] == 0
    own, other = own_ref[...].astype(f32), other_ref[...].astype(f32)
    depth = own.shape[0]
    both = jnp.concatenate([jnp.where(first, own, other), jnp.where(first, other, own)], 0)
    out_ref[...] = both.T


def turn_table(core, own, other):
    depth, rows_all = own.shape
    wide = lane_block(rows_all)
    block = pl.BlockSpec((depth, wide), lambda j: (0, j))
    return pl.pallas_call(
        turn_kernel,
        grid=(pl.cdiv(rows_all, wide),),
        out_shape=jax.ShapeDtypeStruct((rows_all, 2 * depth), f32),
        in_specs=[pl.BlockSpec(memory_space=SMEM), block, block],
        out_specs=pl.BlockSpec((wide, 2 * depth), lambda j: (j, 0)),
        name="turn_table",
        cost_estimate=cost(1e7, 1e7),
    )(core, own, other)


def in_chunks(count, size, body):
    def go(i, carry):
        body(pl.multiple_of(i * size, size))
        return carry

    lax.fori_loop(0, count // size, go, 0)


def lookup_kernel(rows_all, list_ref, table_ref, *refs):
    outs, acc = refs[:-1], refs[-1]
    total = acc.shape[0] - 8
    chunk = 128

    def clear(start):
        acc[pl.ds(start, chunk), :] = jnp.zeros((chunk, acc.shape[1]), f32)

    in_chunks(total, chunk, clear)

    def go(i, carry):
        for u in range(8):
            entry = list_ref[i * 8 + u]
            row = entry >> 16
            place = jnp.where(row < rows_all, entry & 0xFFFF, total)
            row = jnp.minimum(row, rows_all - 1)
            acc[pl.ds(place, 1), :] = table_ref[pl.ds(row, 1), :]
        return carry

    lax.fori_loop(0, (list_ref[total + 8] + 7) // 8, go, 0)
    each = outs[0].shape[0]
    for part, out in enumerate(outs):

        def keep(start, part=part, out=out):
            out[pl.ds(start, chunk), :] = acc[pl.ds(part * each + start, chunk), :].astype(bf16)

        in_chunks(each, chunk, keep)


def lookup(hit_list, table, count, parts):
    rows_all, width = table.shape
    return pl.pallas_call(
        partial(lookup_kernel, rows_all),
        out_shape=[jax.ShapeDtypeStruct((count // parts, width), bf16)] * parts,
        in_specs=[
            pl.BlockSpec(memory_space=SMEM),
            pl.BlockSpec(memory_space=pltpu.VMEM),
        ],
        out_specs=[pl.BlockSpec(memory_space=pltpu.VMEM)] * parts,
        scratch_shapes=[pltpu.VMEM((count + 8, width), f32)],
        name="lookup",
        cost_estimate=cost(1e10, rows_all * width * 2),
    )(hit_list, table)


def add_rows(own_ref, their_ref, groups, pieces, acc, tail, wide, pair):
    half = pieces[0].shape[0] // 3
    chunk = 128
    for k, piece in enumerate(pieces):

        def widen(start, k=k, piece=piece):
            values = piece[pl.ds(start, chunk), :].astype(f32)
            wide[pl.ds(k * 2 * half + start, chunk), :] = values

        def widen_pair(start, k=k, piece=piece):
            values = piece[pl.ds(2 * half + start, chunk), :].astype(f32)
            pair[pl.ds(k * half + start, chunk), :] = values

        in_chunks(2 * half, chunk, widen)
        in_chunks(half, chunk, widen_pair)
    upper = lax.broadcasted_iota(i32, (1, 128), 1) >= 64
    for base, total, start in groups:
        for side, list_ref in enumerate((own_ref, their_ref)):
            own = upper if side else ~upper

            def go(i, carry, base=base, start=start, side=side, list_ref=list_ref, own=own):
                for u in range(8):
                    entry = list_ref[base + i * 8 + u]
                    row = entry >> 16
                    p = (entry & 0xFFFF) + start
                    q = (p // half) * half + p + side * half
                    acc[pl.ds(row, 1), :] += wide[pl.ds(q, 1), :]
                    tail[pl.ds(row, 1), :] += jnp.where(own, pair[pl.ds(p, 1), :], 0.0)
                return carry

            lax.fori_loop(0, (list_ref[base + total + 8] + 7) // 8, go, 0)


def scatter_first_kernel(count, groups, own_ref, their_ref, *refs):
    pieces = refs[:count]
    acc, tail, wide, pair = refs[count:]

    def clear(start):
        acc[pl.ds(start, 128), :] = jnp.zeros((128, 128), f32)
        tail[pl.ds(start, 128), :] = jnp.zeros((128, 128), f32)

    in_chunks(acc.shape[0], 128, clear)
    add_rows(own_ref, their_ref, groups, pieces, acc, tail, wide, pair)


def scatter_last_kernel(
    count, groups, rows_all, own_ref, their_ref, first_acc, first_tail, lex_ref, stack_ref, *refs
):
    pieces = [stack_ref.at[k] for k in range(stack_ref.shape[0])] + list(refs[:count])
    pieces = [pieces[k] for k in (1, 0, 2, 3)]
    out_ref, square_ref, acc, tail, wide, pair = refs[count:]

    def carry_over(start):
        acc[pl.ds(start, 128), :] = first_acc[pl.ds(start, 128), :]
        tail[pl.ds(start, 128), :] = first_tail[pl.ds(start, 128), :]

    in_chunks(acc.shape[0], 128, carry_over)
    add_rows(own_ref, their_ref, groups, pieces, acc, tail, wide, pair)
    chunks = rows_all // 128
    rest = rows_all - chunks * 128

    def turn(start, width):
        upright = acc[pl.ds(start, 128), :].T
        lower = tail[pl.ds(start, 128), :].T
        lower = lower[:64] + lower[64:]
        lanes = pl.ds(start, width)
        left = lex_ref[pl.ds(0, 128), lanes] + upright[:, :width]
        right = lex_ref[pl.ds(128, 64), lanes] + lower[:, :width]
        out_ref[pl.ds(0, 128), lanes] = left
        out_ref[pl.ds(128, 64), lanes] = right
        return jnp.sum(left * left, 0, keepdims=True), jnp.sum(right * right, 0, keepdims=True)

    def step(i, carry):
        left, right = turn(pl.multiple_of(i * 128, 128), 128)
        return carry + left + right

    squares = lax.fori_loop(0, chunks, step, jnp.zeros((1, 128), f32))
    total = jnp.sum(squares)
    if rest:
        left, right = turn(chunks * 128, rest)
        total = total + jnp.sum(left) + jnp.sum(right)
    square_ref[0, 0] = total


def scatter_first(own_list, their_list, groups, pieces, rows_all):
    half = pieces[0].shape[0] // 3
    count = len(pieces)
    padded = (rows_all // 128 + 1) * 128
    return pl.pallas_call(
        partial(scatter_first_kernel, count, groups),
        out_shape=[jax.ShapeDtypeStruct((padded, 128), f32)] * 2,
        in_specs=[pl.BlockSpec(memory_space=SMEM)] * 2
        + [pl.BlockSpec(memory_space=pltpu.VMEM)] * count,
        out_specs=[pl.BlockSpec(memory_space=pltpu.VMEM)] * 2,
        scratch_shapes=[
            pltpu.VMEM((count * 2 * half, 128), f32),
            pltpu.VMEM((count * half, 128), f32),
        ],
        name="scatter_first",
        cost_estimate=cost(1e10, rows_all * 128 * 8),
    )(own_list, their_list, *pieces)


def scatter_last(own_list, their_list, groups, before, lex, stacked, pieces, rows_all):
    width = lex.shape[0]
    half = stacked.shape[1] // 3
    count = len(pieces)
    used = count + stacked.shape[0]
    padded = (rows_all // 128 + 1) * 128
    return pl.pallas_call(
        partial(scatter_last_kernel, count, groups, rows_all),
        out_shape=[
            jax.ShapeDtypeStruct((width, rows_all), f32),
            jax.ShapeDtypeStruct((1, 1), f32),
        ],
        in_specs=[pl.BlockSpec(memory_space=SMEM)] * 2
        + [pl.BlockSpec(memory_space=pltpu.VMEM)] * (count + 4),
        out_specs=[
            pl.BlockSpec(memory_space=pltpu.VMEM),
            pl.BlockSpec(memory_space=SMEM),
        ],
        scratch_shapes=[
            pltpu.VMEM((padded, 128), f32),
            pltpu.VMEM((padded, 128), f32),
            pltpu.VMEM((used * 2 * half, 128), f32),
            pltpu.VMEM((used * half, 128), f32),
        ],
        name="scatter_last",
        cost_estimate=cost(1e10, rows_all * width * 8),
    )(own_list, their_list, *before, lex, stacked, *pieces)


def norm_parts(inputs):
    centered = inputs - jnp.mean(inputs, -1, keepdims=True)
    scale = lax.rsqrt(jnp.mean(centered * centered, -1, keepdims=True) + NORM_EPSILON)
    return centered, scale


def norm_pull(inputs, gain_row, grads):
    centered, scale = norm_parts(inputs)
    unit = centered * scale
    pulled = grads * gain_row
    lead = jnp.mean(pulled, -1, keepdims=True)
    along = jnp.mean(pulled * unit, -1, keepdims=True)
    grad_in = scale * (pulled - lead - unit * along)
    return (
        grad_in,
        jnp.sum(grads * unit, 0, keepdims=True),
        jnp.sum(grads, 0, keepdims=True),
    )


def qkv_kernel(x_ref, w_ref, vec_ref, h_ref, mixed_ref):
    j = pl.program_id(0)

    @pl.when(j == 0)
    def _():
        centered, scale = norm_parts(x_ref[...].astype(f32))
        h_ref[...] = (centered * scale * vec_ref[0:1, :] + vec_ref[1:2, :]).astype(bf16)

    mixed_ref[...] = (mm(h_ref[...], w_ref[...]) + vec_ref[pl.ds(8 + j, 1), :]).astype(bf16)


def qkv_forward(x0, wqkv, vectors):
    tokens = x0.shape[0]
    return pl.pallas_call(
        qkv_kernel,
        grid=(3,),
        out_shape=[
            jax.ShapeDtypeStruct((tokens, D), bf16),
            jax.ShapeDtypeStruct((tokens, 3 * D), bf16),
        ],
        in_specs=[
            full((tokens, D)),
            pl.BlockSpec((D, D), lambda j: (0, j)),
            full(vectors.shape),
        ],
        out_specs=[full((tokens, D)), pl.BlockSpec((tokens, D), lambda j: (0, j))],
        name="qkv_forward",
        cost_estimate=cost(2 * tokens * D * 3 * D, 8e6),
    )(x0, wqkv, vectors)


def feature_parts(values, lift, low_half):
    raw = mm(values, lift)
    top_a = jnp.max(jnp.where(low_half, raw, -jnp.inf), -1, keepdims=True)
    top_b = jnp.max(jnp.where(low_half, -jnp.inf, raw), -1, keepdims=True)
    grown = jnp.exp(raw - jnp.where(low_half, top_a, top_b))
    sum_a = jnp.sum(jnp.where(low_half, grown, 0.0), -1, keepdims=True)
    sum_b = jnp.sum(jnp.where(low_half, 0.0, grown), -1, keepdims=True)
    return grown / jnp.where(low_half, sum_a, sum_b)


def feature_pull(soft, grads, low_half):
    weighed = soft * grads
    sum_a = jnp.sum(jnp.where(low_half, weighed, 0.0), -1, keepdims=True)
    sum_b = jnp.sum(jnp.where(low_half, 0.0, weighed), -1, keepdims=True)
    pulled = soft * (grads - jnp.where(low_half, sum_a, sum_b))
    return (pulled - pltpu.roll(pulled, HD, 1)).astype(bf16)


def fill_allowed(len_ref, allow_ref):
    tokens = allow_ref.shape[0]
    first = len_ref[0, 0]
    second = first + len_ref[0, 1]
    third = second + len_ref[0, 2]

    def document(places):
        return (
            (places >= first).astype(i32)
            + (places >= second).astype(i32)
            + (places >= third).astype(i32)
        )

    rows = lax.broadcasted_iota(i32, (tokens, tokens), 0)
    cols = lax.broadcasted_iota(i32, (tokens, tokens), 1)
    allow_ref[...] = ((cols <= rows) & (document(rows) == document(cols))).astype(f32)


ROWS = 256


def attend_kernel(
    len_ref, q_ref, k_ref, v_ref, fq_ref, fk_ref, y_ref, distill_ref, allow_ref, lift_q, lift_k
):
    tokens = q_ref.shape[0]

    @pl.when(pl.program_id(0) == 0)
    def _():
        fill_allowed(len_ref, allow_ref)
        distill_ref[...] = jnp.zeros_like(distill_ref)

    low_half = lax.broadcasted_iota(i32, (1, 2 * HD), 1) < HD
    low_rows = lax.broadcasted_iota(i32, (ROWS, 2 * HD), 1) < HD
    total = jnp.zeros((1, 1), f32)
    for h in range(2):
        lift_q[h] = feature_parts(q_ref[...], fq_ref[h], low_half).astype(bf16)
        lift_k[h] = feature_parts(k_ref[...], fk_ref[h], low_half).astype(bf16)
    for begin in range(0, tokens, ROWS):
        width = begin + ROWS
        ok = allow_ref[pl.ds(begin, ROWS), pl.ds(0, width)] > 0.5
        queries = q_ref[pl.ds(begin, ROWS), :] * jnp.asarray(HD**-0.5, bf16)
        keys = k_ref[pl.ds(0, width), :]
        values = v_ref[pl.ds(0, width), :]
        parts = []
        for h in range(2):
            own = low_rows if h == 0 else ~low_rows
            scores = mm_t(jnp.where(own, queries, jnp.zeros_like(queries)), keys)
            scores = jnp.where(ok, scores, -1e30)
            grown = jnp.exp(scores - jnp.max(scores, -1, keepdims=True))
            inverse = 1.0 / jnp.sum(grown, -1, keepdims=True)
            similar = mm_t(lift_q[h, pl.ds(begin, ROWS), :], lift_k[h, pl.ds(0, width), :])
            kept = jnp.where(ok, similar, 0.0)
            sums = jnp.sum(kept, -1, keepdims=True)
            weights = (kept * (1.0 / sums)).astype(bf16)
            parts.append(mm(weights, values))
            logs = jnp.log(jnp.where(ok, similar, 1.0))
            row_terms = jnp.log(sums) - jnp.sum(grown * logs, -1, keepdims=True) * inverse
            total = total + jnp.sum(row_terms, 0, keepdims=True)
        y_ref[pl.ds(begin, ROWS), :] = jnp.where(low_rows, parts[0], parts[1]).astype(bf16)
    distill_ref[...] += jnp.broadcast_to(total, distill_ref.shape)


def attend(lengths, mixed, lift_maps):
    tokens = mixed.shape[0]
    column = lambda base: pl.BlockSpec((tokens, 2 * HD), lambda g: (0, base + g))
    maps = pl.BlockSpec((2, 2 * HD, 2 * HD), lambda g: (g, 0, 0))
    return pl.pallas_call(
        attend_kernel,
        grid=(PAIRS,),
        out_shape=[
            jax.ShapeDtypeStruct((tokens, D), bf16),
            jax.ShapeDtypeStruct((8, 128), f32),
        ],
        in_specs=[
            pl.BlockSpec(memory_space=SMEM),
            column(0),
            column(PAIRS),
            column(2 * PAIRS),
            maps,
            maps,
        ],
        out_specs=[column(0), full((8, 128))],
        scratch_shapes=[
            pltpu.VMEM((tokens, tokens), f32),
            pltpu.VMEM((2, tokens, 2 * HD), bf16),
            pltpu.VMEM((2, tokens, 2 * HD), bf16),
        ],
        name="attend",
        cost_estimate=cost(1.2e10, 4e6, 6e6),
    )(lengths, mixed, mixed, mixed, lift_maps[0], lift_maps[1])


def attend_back_kernel(
    coefficient,
    later,
    len_ref,
    q_ref,
    k_ref,
    v_ref,
    gy_ref,
    fq_ref,
    fk_ref,
    *refs,
):
    g_ref, gq_map_ref, gk_map_ref, allow_ref, soft_q, soft_k, grad_q, grad_k, grad_v = refs[later:]
    tokens = q_ref.shape[0]

    @pl.when(pl.program_id(0) == 0)
    def _():
        fill_allowed(len_ref, allow_ref)

    low_half = lax.broadcasted_iota(i32, (1, 2 * HD), 1) < HD
    low_rows = lax.broadcasted_iota(i32, (ROWS, 2 * HD), 1) < HD
    for h in range(2):
        soft_q[h] = feature_parts(q_ref[...], fq_ref[h], low_half)
        soft_k[h] = feature_parts(k_ref[...], fk_ref[h], low_half)
    for step, begin in enumerate(reversed(range(0, tokens, ROWS))):
        width = begin + ROWS
        ok = allow_ref[pl.ds(begin, ROWS), pl.ds(0, width)] > 0.5
        queries = q_ref[pl.ds(begin, ROWS), :] * jnp.asarray(HD**-0.5, bf16)
        keys = k_ref[pl.ds(0, width), :]
        values = v_ref[pl.ds(0, width), :]
        grads = gy_ref[pl.ds(begin, ROWS), :]
        value_sum = None
        for h in range(2):
            own = low_rows if h == 0 else ~low_rows
            scores = mm_t(jnp.where(own, queries, jnp.zeros_like(queries)), keys)
            scores = jnp.where(ok, scores, -1e30)
            grown = jnp.exp(scores - jnp.max(scores, -1, keepdims=True))
            teach = grown * (coefficient / jnp.sum(grown, -1, keepdims=True))
            phi_q = soft_q[h, pl.ds(begin, ROWS), :].astype(bf16)
            phi_k = soft_k[h, pl.ds(0, width), :].astype(bf16)
            similar = mm_t(phi_q, phi_k)
            kept = jnp.where(ok, similar, 0.0)
            inverse = 1.0 / jnp.sum(kept, -1, keepdims=True)
            weights = kept * inverse
            own_grads = jnp.where(own, grads, jnp.zeros_like(grads))
            grad_w = mm_t(own_grads, values)
            row_sum = jnp.sum(grad_w * weights, -1, keepdims=True)
            grad_sums = (coefficient - row_sum) * inverse
            grad_sim = jnp.where(
                ok,
                grad_w * inverse - teach / jnp.where(ok, similar, 1.0) + grad_sums,
                0.0,
            ).astype(bf16)
            grad_q[h, pl.ds(begin, ROWS), :] = mm(grad_sim, phi_k)
            part_k = mm_l(grad_sim, phi_q)
            part_v = mm_l(weights.astype(bf16), own_grads)
            value_sum = part_v if value_sum is None else value_sum + part_v
            if step == 0:
                grad_k[h] = part_k
            else:
                grad_k[h, pl.ds(0, width), :] += part_k
        if step == 0:
            grad_v[...] = value_sum
        else:
            grad_v[pl.ds(0, width), :] += value_sum
    for slot, own_ref, map_ref, soft, grad, out in (
        (0, q_ref, fq_ref, soft_q, grad_q, gq_map_ref),
        (1, k_ref, fk_ref, soft_k, grad_k, gk_map_ref),
    ):
        result = None
        for h in range(2):
            pulled = feature_pull(soft[h], grad[h], low_half)
            back = mm_t(pulled, map_ref[h]) * 0.5
            result = back if result is None else result + back
            out[h] = mm_l(own_ref[...], pulled)[h * HD : (h + 1) * HD, :HD]
        g_ref[slot] = result.astype(bf16)
    g_ref[2] = grad_v[...].astype(bf16)


def attend_back(lengths, mixed, grad_y, lift_maps, coefficient, start, pairs, before):
    tokens = mixed.shape[0]
    column = lambda base: pl.BlockSpec((tokens, 2 * HD), lambda g: (0, base + start + g))
    maps = pl.BlockSpec((2, 2 * HD, 2 * HD), lambda g: (start + g, 0, 0))
    small = pl.BlockSpec((2, HD, HD), lambda g: (g, 0, 0))
    wide = (2, tokens, 2 * HD)
    later = before is not None
    return pl.pallas_call(
        partial(attend_back_kernel, coefficient, int(later)),
        grid=(pairs,),
        out_shape=[
            jax.ShapeDtypeStruct((3, tokens, D), bf16),
            jax.ShapeDtypeStruct((2 * pairs, HD, HD), f32),
            jax.ShapeDtypeStruct((2 * pairs, HD, HD), f32),
        ],
        in_specs=[
            pl.BlockSpec(memory_space=SMEM),
            column(0),
            column(PAIRS),
            column(2 * PAIRS),
            column(0),
            maps,
            maps,
        ]
        + [pl.BlockSpec(memory_space=ANY)] * later,
        out_specs=[
            pl.BlockSpec((3, tokens, 2 * HD), lambda g: (0, 0, start + g)),
            small,
            small,
        ],
        scratch_shapes=[
            pltpu.VMEM((tokens, tokens), f32),
            pltpu.VMEM(wide, f32),
            pltpu.VMEM(wide, f32),
            pltpu.VMEM(wide, f32),
            pltpu.VMEM(wide, f32),
            pltpu.VMEM((tokens, 2 * HD), f32),
        ],
        input_output_aliases={7: 0} if later else {},
        name="attend_back",
        cost_estimate=cost(1.2e10, 4e6, 3e6),
    )(lengths, mixed, mixed, mixed, grad_y, lift_maps[0], lift_maps[1], *([before] * later))


FSTEPS = FF // D


def mlp_kernel(
    x_ref,
    y_ref,
    wo_ref,
    wup_ref,
    wdown_ref,
    vec_ref,
    pick_ref,
    x1_ref,
    h_ref,
    up_ref,
    act_ref,
    x2_ref,
    hp_ref,
):
    j = pl.program_id(0)

    @pl.when(j == 0)
    def _():
        x1 = x_ref[...].astype(f32) + mm(y_ref[...], wo_ref[...]) + vec_ref[6:7, :]
        x1_ref[...] = x1
        centered, scale = norm_parts(x1)
        h_ref[...] = (centered * scale * vec_ref[2:3, :] + vec_ref[3:4, :]).astype(bf16)
        x2_ref[...] = x1 + vec_ref[7:8, :]

    up = mm(h_ref[...], wup_ref[...]) + vec_ref[pl.ds(11 + j, 1), :]
    up_ref[...] = up
    act = (0.5 * up * (1.0 + jnp.tanh(0.7978845608 * (up + 0.044715 * up * up * up)))).astype(bf16)
    act_ref[...] = act
    x2_ref[...] += mm(act, wdown_ref[...])

    @pl.when(j == FSTEPS - 1)
    def _():
        centered, scale = norm_parts(x2_ref[...])
        last = (centered * scale * vec_ref[4:5, :] + vec_ref[5:6, :]).astype(bf16)
        tokens = last.shape[0]
        places = lax.broadcasted_iota(i32, (pick_ref.shape[0], tokens), 1)
        chosen = (places == pick_ref[...]).astype(bf16)
        hp_ref[...] = mm(chosen, last).astype(bf16)


def mlp_forward(x0, y, wo, wup, wdown, vectors, picks):
    tokens = x0.shape[0]
    count = picks.shape[0]
    wide = pl.BlockSpec((tokens, D), lambda j: (0, j))
    shape = lambda cols, kind: jax.ShapeDtypeStruct((tokens, cols), kind)
    return pl.pallas_call(
        mlp_kernel,
        grid=(FSTEPS,),
        out_shape=[
            shape(D, f32),
            shape(D, bf16),
            shape(FF, f32),
            shape(FF, bf16),
            shape(D, f32),
            jax.ShapeDtypeStruct((count, D), bf16),
        ],
        in_specs=[
            full((tokens, D)),
            full((tokens, D)),
            full((D, D)),
            pl.BlockSpec((D, D), lambda j: (0, j)),
            pl.BlockSpec((D, D), lambda j: (j, 0)),
            full(vectors.shape),
            full((count, 1)),
        ],
        out_specs=[
            full((tokens, D)),
            full((tokens, D)),
            wide,
            wide,
            full((tokens, D)),
            full((count, D)),
        ],
        name="mlp_forward",
        cost_estimate=cost(2 * tokens * D * (2 * FF + D), 3e7, tokens * FF),
    )(x0, y, wo, wup, wdown, vectors, picks.reshape(count, 1))


def keep_tiles(values, out, top, slot):
    for c in range(2):
        out[slot + c] = values[:, c * BS : (c + 1) * BS]
    high = jnp.max(jnp.abs(values), 0, keepdims=True)
    top[...] = jnp.maximum(top[...], jnp.maximum(high[:, :BS], high[:, BS:]))


def near_far(core):
    return pl.ds(pl.multiple_of(core * BS, BS), BS), pl.ds(pl.multiple_of((1 - core) * BS, BS), BS)


def mlp_back_kernel(
    core_ref,
    ghp_ref,
    pick_ref,
    x2_ref,
    act_ref,
    up_ref,
    h_ref,
    x1_ref,
    wdown_ref,
    wup_ref,
    wo_ref,
    vec_ref,
    mine_ref,
    theirs_ref,
    mine_top_ref,
    theirs_top_ref,
    gx1_ref,
    ga_ref,
    gy_ref,
    vg_ref,
    gx2,
    gm,
    gh,
):
    j = pl.program_id(0)
    core = core_ref[0]
    tokens = x2_ref.shape[0]

    @pl.when(j == 0)
    def _():
        mine_top_ref[...] = jnp.zeros_like(mine_top_ref)
        theirs_top_ref[...] = jnp.zeros_like(theirs_top_ref)
        vg_ref[...] = jnp.zeros_like(vg_ref)
        places = lax.broadcasted_iota(i32, (tokens, pick_ref.shape[1]), 0)
        chosen = (places == pick_ref[...]).astype(bf16)
        rest = ghp_ref[...]
        spread = jnp.zeros((tokens, D), f32)
        for _ in range(3):
            part = rest.astype(bf16)
            rest = rest - part.astype(f32)
            spread = spread + mm(chosen, part)
        grad, gain, bias = norm_pull(x2_ref[...], vec_ref[4:5, :], spread)
        gx2[...] = grad
        low = grad.astype(bf16)
        gm[...] = low
        vg_ref[4:5, :] = gain
        vg_ref[5:6, :] = bias
        vg_ref[7:8, :] = jnp.sum(low.astype(f32), 0, keepdims=True)

    grad_act = mm_t(gm[...], wdown_ref[...])
    up = up_ref[...]
    turn = jnp.tanh(0.7978845608 * (up + 0.044715 * up * up * up))
    slope = 0.5 * (1.0 + turn) + 0.5 * up * (1.0 - turn * turn) * (
        0.7978845608 * (1.0 + 3.0 * 0.044715 * up * up)
    )
    gup = (grad_act * slope).astype(bf16)
    vg_ref[pl.ds(11 + j, 1), :] = jnp.sum(gup.astype(f32), 0, keepdims=True)
    part = mm_t(gup, wup_ref[...])

    @pl.when(j == 0)
    def _():
        gh[...] = part

    @pl.when(j > 0)
    def _():
        gh[...] += part

    for cols, out, top in zip(
        near_far(core), (mine_ref, theirs_ref), (mine_top_ref, theirs_top_ref)
    ):
        keep_tiles(mm_l(h_ref[:, cols], gup), out, top, 0)
        keep_tiles(mm_l(act_ref[:, cols], gm[...]), out, top, 2)

    @pl.when(j == FSTEPS - 1)
    def _():
        grad, gain, bias = norm_pull(x1_ref[...], vec_ref[2:3, :], gh[...])
        vg_ref[2:3, :] = gain
        vg_ref[3:4, :] = bias
        grad = grad + gx2[...]
        gx1_ref[...] = grad
        low = grad.astype(bf16)
        ga_ref[...] = low
        vg_ref[6:7, :] = jnp.sum(low.astype(f32), 0, keepdims=True)
        gy_ref[...] = mm_t(low, wo_ref[...]).astype(bf16)


def mlp_back(core, ghp, picks, x2, act, up, h2, x1, wdown, wup, wo, vectors):
    tokens = x2.shape[0]
    count = picks.shape[0]
    wide = pl.BlockSpec((tokens, D), lambda j: (0, j))
    flat = full((tokens, D))
    tiles = pl.BlockSpec((4, BS, BS), lambda j: (j, 0, 0))
    tops = full((1, BS))
    halves = jax.ShapeDtypeStruct((4 * FSTEPS, BS, BS), f32)
    highs = jax.ShapeDtypeStruct((1, BS), f32)
    return pl.pallas_call(
        mlp_back_kernel,
        grid=(FSTEPS,),
        out_shape=[
            halves,
            halves,
            highs,
            highs,
            jax.ShapeDtypeStruct((tokens, D), f32),
            jax.ShapeDtypeStruct((tokens, D), bf16),
            jax.ShapeDtypeStruct((tokens, D), bf16),
            jax.ShapeDtypeStruct((16, D), f32),
        ],
        in_specs=[
            pl.BlockSpec(memory_space=SMEM),
            full((count, D)),
            full((1, count)),
            flat,
            wide,
            wide,
            flat,
            flat,
            pl.BlockSpec((D, D), lambda j: (j, 0)),
            pl.BlockSpec((D, D), lambda j: (0, j)),
            full((D, D)),
            full(vectors.shape),
        ],
        out_specs=[tiles, tiles, tops, tops, flat, flat, flat, full((16, D))],
        scratch_shapes=[
            pltpu.VMEM((tokens, D), f32),
            pltpu.VMEM((tokens, D), bf16),
            pltpu.VMEM((tokens, D), f32),
        ],
        name="mlp_back",
        cost_estimate=cost(8 * tokens * D * FF, 5e7, tokens * FF),
    )(core, ghp, picks.reshape(1, count), x2, act, up, h2, x1, wdown, wup, wo, vectors)


def qkv_back_kernel(g_ref, w_ref, x_ref, gx1_ref, vec_ref, gx0_ref, vg_ref, gh):
    j = pl.program_id(0)
    part = mm_t(g_ref[0], w_ref[...])

    @pl.when(j == 0)
    def _():
        vg_ref[...] = jnp.zeros_like(vg_ref)
        gh[...] = part

    @pl.when(j > 0)
    def _():
        gh[...] += part

    vg_ref[pl.ds(8 + j, 1), :] = jnp.sum(g_ref[0].astype(f32), 0, keepdims=True)

    @pl.when(j == 2)
    def _():
        grad, gain, bias = norm_pull(x_ref[...].astype(f32), vec_ref[0:1, :], gh[...])
        vg_ref[0:1, :] = gain
        vg_ref[1:2, :] = bias
        gx0_ref[...] = (gx1_ref[...] + grad).astype(bf16)


def qkv_back(grads, wqkv, x0, gx1, vectors):
    tokens = x0.shape[0]
    flat = full((tokens, D))
    return pl.pallas_call(
        qkv_back_kernel,
        grid=(3,),
        out_shape=[
            jax.ShapeDtypeStruct((tokens, D), bf16),
            jax.ShapeDtypeStruct((16, D), f32),
        ],
        in_specs=[
            pl.BlockSpec((1, tokens, D), lambda j: (j, 0, 0)),
            pl.BlockSpec((D, D), lambda j: (0, j)),
            flat,
            flat,
            full(vectors.shape),
        ],
        out_specs=[flat, full((16, D))],
        scratch_shapes=[pltpu.VMEM((tokens, D), f32)],
        name="qkv_back",
        cost_estimate=cost(2 * tokens * D * 3 * D, 1e7),
    )(grads, wqkv, x0, gx1, vectors)


def qkv_weights_kernel(
    core_ref, h_ref, g_ref, y_ref, ga_ref, small_ref, mine_ref, theirs_ref, mtop_ref, ttop_ref
):
    j = pl.program_id(0)
    core = core_ref[0]
    both = tuple(zip(near_far(core), (mine_ref, theirs_ref), (mtop_ref, ttop_ref)))

    @pl.when(j == 0)
    def _():
        for turn, (_, out, top) in enumerate(both):
            values = small_ref[core if turn == 0 else 1 - core]
            out[8] = values
            top[...] = jnp.max(jnp.abs(values), 0, keepdims=True)

    @pl.when(j < 3)
    def _():
        for cols, out, top in both:
            keep_tiles(mm_l(h_ref[:, cols], g_ref[0]), out, top, 2 * j)

    @pl.when(j == 3)
    def _():
        for cols, out, top in both:
            keep_tiles(mm_l(y_ref[:, cols], ga_ref[...]), out, top, 6)


def qkv_weights(core, h1, grads, y, ga, small):
    tokens = h1.shape[0]
    flat = full((tokens, D))
    halves = (9, BS, BS)
    highs = (1, BS)
    shapes = (halves, halves, highs, highs)
    return pl.pallas_call(
        qkv_weights_kernel,
        grid=(4,),
        out_shape=[jax.ShapeDtypeStruct(shape, f32) for shape in shapes],
        in_specs=[
            pl.BlockSpec(memory_space=SMEM),
            flat,
            pl.BlockSpec((1, tokens, D), lambda j: (jnp.minimum(j, 2), 0, 0)),
            flat,
            flat,
            full((2, BS, BS)),
        ],
        out_specs=[full(shape) for shape in shapes],
        name="qkv_weights",
        cost_estimate=cost(2 * tokens * D * 4 * D, 2e7),
    )(core, h1, grads, y, ga, small)


def comm_positions():
    side = np.zeros(48, np.int32)
    place = np.zeros(48, np.int32)
    for r in range(2):
        for c in range(2):
            for j in range(FSTEPS):
                place[16 + r * 8 + 2 * j + c] = 4 * j + c
                place[32 + (2 * j + r) * 2 + c] = 4 * j + 2 + c
                side[16 + r * 8 + 2 * j + c] = side[32 + (2 * j + r) * 2 + c] = r
            for j in range(3):
                place[r * 6 + 2 * j + c] = 16 + 2 * j + c
                side[r * 6 + 2 * j + c] = r
            place[12 + r * 2 + c] = 22 + c
            side[12 + r * 2 + c] = r
    return side, place


def lane_block(rows_all):
    return min(1280, (rows_all // 128 + 1) * 128)


def fill_table(places_ref, pieces, tab, valid):
    depth = pieces[0].shape[0]
    for p, piece in enumerate(pieces):
        start = pl.multiple_of(places_ref[p], depth)
        tab[pl.ds(start, depth), :] = jnp.where(valid, piece[...], jnp.zeros((), bf16))


def logits_kernel(rows_all, count, places_ref, group_ref, target_ref, *refs):
    pieces = refs[:count]
    logit_ref, stat_ref, tab, top, total, chosen = refs[count:]
    j = pl.program_id(0)
    wide = tab.shape[1]
    lane = lax.broadcasted_iota(i32, (1, wide), 1) + j * wide
    valid = lane < rows_all
    fill_table(places_ref, pieces, tab, valid)

    @pl.when(j == 0)
    def _():
        top[...] = jnp.full(top.shape, -jnp.inf, f32)
        total[...] = jnp.zeros(total.shape, f32)
        chosen[...] = jnp.zeros(chosen.shape, f32)

    logits = mm(group_ref[...], tab[...])
    logit_ref[...] = logits
    kept = jnp.where(valid, logits, -jnp.inf)
    before = top[...]
    after = jnp.maximum(before, jnp.max(kept, -1, keepdims=True))
    top[...] = after
    total[...] = total[...] * jnp.exp(before - after) + jnp.sum(
        jnp.exp(kept - after), -1, keepdims=True
    )
    hit = (lane == target_ref[...]) & valid
    chosen[...] += jnp.sum(jnp.where(hit, logits, 0.0), -1, keepdims=True)

    @pl.when(j == pl.num_programs(0) - 1)
    def _():
        spot = lax.broadcasted_iota(i32, (1, 128), 1)
        merged = jnp.where(
            spot == 0, top[...], jnp.where(spot == 1, total[...], chosen[...])
        )
        stat_ref[...] = merged.T[:8]


def table_specs(pieces, wide):
    return [pl.BlockSpec((pieces[0].shape[0], wide), lambda j: (0, j))] * len(pieces)


def vocabulary_logits(places, group, local_targets, pieces):
    count, rows_all = group.shape[0], pieces[0].shape[1]
    wide = lane_block(rows_all)
    return pl.pallas_call(
        partial(logits_kernel, rows_all, len(pieces)),
        grid=(pl.cdiv(rows_all, wide),),
        out_shape=[
            jax.ShapeDtypeStruct((count, rows_all), f32),
            jax.ShapeDtypeStruct((8, count), f32),
        ],
        in_specs=[pl.BlockSpec(memory_space=SMEM), full((count, D)), full((count, 1))]
        + table_specs(pieces, wide),
        out_specs=[pl.BlockSpec((count, wide), lambda j: (0, j)), full((8, count))],
        scratch_shapes=[pltpu.VMEM((D, wide), bf16)] + [pltpu.VMEM((count, 1), f32)] * 3,
        name="vocabulary_logits",
        cost_estimate=cost(2 * count * D * rows_all, 2e7, count * rows_all),
    )(places, group, local_targets.reshape(count, 1), *pieces)


def vocabulary_back_kernel(
    rows_all, count, scale, places_ref, logit_ref, stat_ref, target_ref, *refs
):
    pieces = refs[:count]
    grad_ref, ghp_ref, tab, stat = refs[count:]
    j = pl.program_id(0)
    wide = tab.shape[1]
    lane = lax.broadcasted_iota(i32, (1, wide), 1) + j * wide
    valid = lane < rows_all
    fill_table(places_ref, pieces, tab, valid)

    @pl.when(j == 0)
    def _():
        stat[...] = stat_ref[...].T
        ghp_ref[...] = jnp.zeros_like(ghp_ref)

    hit = (lane == target_ref[...]).astype(f32)
    soft = jnp.exp(logit_ref[...] - stat[:, 0:1]) * stat[:, 1:2]
    grads = jnp.where(valid, (soft - hit) * scale, 0.0).astype(bf16)
    grad_ref[...] = grads
    ghp_ref[...] += mm_t(grads, tab[...])


def vocabulary_back(places, logits, stats, local_targets, pieces, scale):
    count, rows_all = logits.shape
    wide = lane_block(rows_all)
    block = pl.BlockSpec((count, wide), lambda j: (0, j))
    return pl.pallas_call(
        partial(vocabulary_back_kernel, rows_all, len(pieces), scale),
        grid=(pl.cdiv(rows_all, wide),),
        out_shape=[
            jax.ShapeDtypeStruct((count, pl.cdiv(rows_all, wide) * wide), bf16),
            jax.ShapeDtypeStruct((count, D), f32),
        ],
        in_specs=[
            pl.BlockSpec(memory_space=SMEM),
            block,
            full(stats.shape),
            full((count, 1)),
        ]
        + table_specs(pieces, wide),
        out_specs=[block, full((count, D))],
        scratch_shapes=[pltpu.VMEM((D, wide), bf16), pltpu.VMEM((count, stats.shape[0]), f32)],
        name="vocabulary_back",
        cost_estimate=cost(2 * count * D * rows_all, 3e7, count * rows_all),
    )(places, logits, stats, local_targets.reshape(count, 1), *pieces)


def lexicon_kernel(
    depth, places_ref, turned_ref, grad_ref, mine_ref, theirs_ref, mtop_ref, ttop_ref, sel
):
    j = pl.program_id(0)
    half = mine_ref.shape[0]

    @pl.when(j == 0)
    def _():
        for p in range(sel.shape[0] // depth):
            start = pl.multiple_of(places_ref[p], depth)
            sel[pl.ds(p * depth, depth), :] = turned_ref[pl.ds(start, depth), :]
        mtop_ref[...] = jnp.zeros_like(mtop_ref)
        ttop_ref[...] = jnp.zeros_like(ttop_ref)

    for start, out, top in ((0, mine_ref, mtop_ref), (half, theirs_ref, ttop_ref)):
        part = mm(sel[pl.ds(start, half), :], grad_ref[...])
        out[...] = part
        top[...] = jnp.maximum(top[...], jnp.max(jnp.abs(part), 0, keepdims=True))


def lexicon(places, turned, grads, depth, rows_all):
    count, padded = grads.shape
    wide = lane_block(rows_all)
    half = D // 2
    block = pl.BlockSpec((half, wide), lambda j: (0, j))
    return pl.pallas_call(
        partial(lexicon_kernel, depth),
        grid=(padded // wide,),
        out_shape=[jax.ShapeDtypeStruct((half, padded), f32)] * 2
        + [jax.ShapeDtypeStruct((1, wide), f32)] * 2,
        in_specs=[
            pl.BlockSpec(memory_space=SMEM),
            full((D, count)),
            pl.BlockSpec((count, wide), lambda j: (0, j)),
        ],
        out_specs=[block, block, full((1, wide)), full((1, wide))],
        scratch_shapes=[pltpu.VMEM((D, count), bf16)],
        name="lexicon",
        cost_estimate=cost(2 * count * D * padded, 3e7),
    )(places, turned, grads)


def three(left, right, product):
    left_high, left_low = left
    right_high, right_low = right
    return (
        product(left_high, right_high)
        + product(left_high, right_low)
        + product(left_low, right_high)
    )


def shampoo_kernel(count, strip, places_ref, clip_ref, *refs):
    pieces, smalls, tails = refs[:count], refs[count : 2 * count], refs[2 * count : 3 * count]
    w_ref, ls_ref, rs_ref, lr_ref, rr_ref = refs[3 * count : 3 * count + 5]
    g_ref, nw_ref, nl_ref, nr_ref, small_ref = refs[3 * count + 5 :]
    clip = clip_ref[0]
    for k in range(count):
        place = pl.multiple_of(places_ref[k], strip)
        scale = jnp.exp2(tails[k][0:1, :] - 15.0) * clip
        g_ref[0, pl.ds(place, strip), :] = pieces[k][...] * scale

        @pl.when(pl.program_id(0) == 0)
        def _(k=k, place=place, scale=scale):
            for side in range(2):
                values = smalls[k][pl.ds(side * strip, strip), :] * scale
                small_ref[side, pl.ds(place, strip), :] = values

    grads = split_two(g_ref[0])
    for old, new, product in ((ls_ref, nl_ref, mm_t), (rs_ref, nr_ref, mm_l)):
        cross = product(grads[0], grads[1])
        outer = product(grads[0], grads[0]) + (cross + cross.T)
        new[0] = SHAMPOO_BETA * old[0] + (1.0 - SHAMPOO_BETA) * outer
    turned = split_two(three(grads, split_two(rr_ref[0]), mm))
    direction = three(split_two(lr_ref[0]), turned, mm)
    weights = w_ref[0]
    nw_ref[0] = weights - RATE_BLOCKS * (direction + DECAY_RATE * weights)


def shampoo(places, clip, pieces, strip, kept):
    slots = kept[0].shape[0]
    count = len(pieces)
    block = pl.BlockSpec((1, BS, BS), lambda s: (s, 0, 0))
    shape = jax.ShapeDtypeStruct((slots, BS, BS), f32)
    small_at, tail_at = slots // 2, (slots + 2) * strip // 16
    return pl.pallas_call(
        partial(shampoo_kernel, count, strip),
        grid=(slots,),
        out_shape=[shape] * 4 + [jax.ShapeDtypeStruct((2, BS, BS), f32)],
        in_specs=[pl.BlockSpec(memory_space=SMEM)] * 2
        + [pl.BlockSpec((strip, BS), lambda s: (s, 0))] * count
        + [pl.BlockSpec((2 * strip, BS), lambda s: (small_at, 0))] * count
        + [pl.BlockSpec((16, BS), lambda s: (tail_at, 0))] * count
        + [block] * 5,
        out_specs=[block] * 4 + [full((2, BS, BS))],
        name="shampoo",
        cost_estimate=cost(slots * 24 * BS**3, slots * BS * BS * 40),
    )(places, clip, *pieces, *pieces, *pieces, *kept)


def adam_update(weight, first, second, gradient, rate, step_value):
    first_new = BETA_FIRST * first + (1.0 - BETA_FIRST) * gradient
    second_new = BETA_SECOND * second + (1.0 - BETA_SECOND) * gradient * gradient
    first_hat = first_new / (1.0 - BETA_FIRST**step_value)
    second_hat = second_new / (1.0 - BETA_SECOND**step_value)
    return (
        weight - rate * (first_hat / (jnp.sqrt(second_hat) + ADAM_EPSILON) + DECAY_RATE * weight),
        first_new,
        second_new,
    )


def tie(values, *others):
    return lax.optimization_barrier((values,) + others)[0]


def exponent(bound):
    return jnp.floor(jnp.log2(jnp.maximum(bound, 1e-30))) + 1.0


def encode(values, bound):
    level = exponent(bound)
    coded = (values * jnp.exp2(15.0 - level)).astype(jnp.float16)
    return coded.reshape(-1, values.shape[-1]), level.astype(jnp.float16)


def pack(values, bound):
    coded, level = encode(values, bound)
    return jnp.concatenate([coded, jnp.broadcast_to(level, (16, coded.shape[1]))], 0)


def unpack(payload, shape):
    count = payload.shape[0] - 16
    wide = payload.astype(f32)
    level = wide[count : count + 1]
    values = wide[:count] * jnp.exp2(level - 15.0)
    return values.reshape(shape), jnp.exp2(payload[-1, 0].astype(f32))


def pack_lanes(values, bound):
    coded, level = encode(values, bound)
    lane = lax.broadcasted_iota(i32, coded.shape, 1)
    return jnp.where(lane == coded.shape[1] - 1, level, coded)


def unpack_lanes(payload):
    level = payload[0, -1].astype(f32)
    return payload.astype(f32) * jnp.exp2(level - 15.0)


def per_device(
    sizes,
    token_ids,
    seq_lengths,
    pick_rows,
    targets,
    step_count,
    block_order,
    slot_weights,
    left_stats,
    right_stats,
    left_roots,
    right_roots,
    embedding,
    embedding_first_moment,
    emb_second,
    vectors,
    vec_first,
    vec_second,
    feature_maps,
    map_first,
    map_second,
):
    ny, nc, n1, n0 = sizes
    n_dp, n_voc = ny * nc, n1 * n0
    dp_index, voc_index = lax.axis_index("dp"), lax.axis_index("vocab")
    y_at, c_at = dp_index // nc, dp_index % nc
    i1, i0 = voc_index // n0, voc_index % n0

    def over_dp(values, dy, dc):
        pairs = [
            (a * nc + b, ((a + dy) % ny) * nc + (b + dc) % nc) for a in range(ny) for b in range(nc)
        ]
        return lax.ppermute(values, "dp", pairs)

    def over_voc(values, d1, d0):
        pairs = [
            (a * n0 + b, ((a + d1) % n1) * n0 + (b + d0) % n0) for a in range(n1) for b in range(n0)
        ]
        return lax.ppermute(values, "vocab", pairs)

    def gather_voc(values):
        near = [values] + [over_voc(values, k, 0) for k in range(1, n1)]
        return [[part] + [over_voc(part, 0, k) for k in range(1, n0)] for part in near]

    def gather_stacked(values):
        near = jnp.stack([values] + [over_voc(values, 0, k) for k in range(1, n0)])
        return jnp.stack([near] + [over_voc(near, k, 0) for k in range(1, n1)])

    def flat_gather(values):
        return [part for line in gather_voc(values) for part in line]

    def gather_y(values):
        return [values] + [over_dp(values, k, 0) for k in range(1, ny)]

    def line_up(parts, at):
        size = len(parts)
        return jnp.take(jnp.stack(parts), (at - jnp.arange(size)) % size, axis=0)

    tokens = token_ids.shape[0]
    picks_own = pick_rows.shape[0]
    devices_all = n_dp * n_voc
    total_picks = picks_own * devices_all
    coefficient = DISTILL_WEIGHT / (tokens * devices_all * HEADS)
    shard_rows, cols_own = embedding.shape
    cols_y = cols_own * nc
    vocab_start = (voc_index * shard_rows).astype(i32)
    per_owner = slot_weights.shape[0]
    block_count = block_order.shape[0]
    table_own = embedding.T
    core = c_at.astype(i32).reshape(1)
    piece_places = jnp.stack(
        [
            (((y_at - ky) % ny) * nc + (c_at + kc) % nc) * cols_own
            for kc in range(nc)
            for ky in range(ny)
        ]
    ).astype(i32)

    low_own = table_own.astype(bf16)
    low_other = over_dp(low_own, 0, 1)
    upright = turn_table(core, low_own, low_other)

    ids_y = gather_y(token_ids)
    numbers = jnp.concatenate(ids_y + [targets])

    slots_y = gather_y(tie(slot_weights.astype(bf16), numbers))
    numbers = gather_stacked(numbers)
    targets_all = numbers[:, :, ny * tokens :].reshape(-1)
    lines = sorted(range(1, n1), key=lambda a: -min(a, n1 - a)) + [0]
    piece_order = [(a, b) for b in list(range(1, n0)) + [0] for a in lines]
    ids_order = [numbers[a, b, : ny * tokens] for a, b in piece_order]
    def near_piece(h, sums, *before):
        part = looked[n1 * (n0 - 1) + h]
        for b in range(1, n0):
            moved = over_voc(tie(looked[(b - 1) * n1 + h], *sums[: max(h - 1, 0)]), 0, -b)
            part = part + tie(moved, *sums, *before)
        return part.reshape(ny, tokens, cols_y)

    looked, hits, bases, by_one = [], [], [], []
    step = n1 // 2
    for first in range(0, n0 * n1, step):
        ids_rows = jnp.concatenate(ids_order[first : first + step])
        local_ids = ids_rows - vocab_start
        packed_ids = jnp.where(
            (local_ids >= 0) & (local_ids < shard_rows),
            (local_ids << 16) | jnp.arange(ids_rows.shape[0], dtype=i32),
            -1,
        )
        bases.append(sum(own.shape[0] for own in hits))
        if first == n0 * n1 - step:
            by_one.append(near_piece(0, by_one))
        hits.append(find_hits(tie(packed_ids, upright, *by_one), shard_rows))
        looked += lookup(hits[-1], upright, ids_rows.shape[0], step)
    hits = jnp.concatenate(hits)
    listed = step * ny * tokens
    early = (n0 - 1) * n1 // step

    for h in range(1, n1 - 1):
        by_one.append(near_piece(h, by_one))
    far_parts = [over_voc(by_one[h], -lines[h], 0) for h in range(n1 - 1)]
    slots_y = [tie(part, by_one[n1 - 2], far_parts[0]) for part in slots_y]
    slots_core = [over_dp(part, 0, 1) for part in slots_y]
    inverse = (
        jnp.zeros((block_count,), i32).at[block_order].set(jnp.arange(block_count, dtype=i32))
    )
    owner = inverse // per_owner
    src = ((c_at - owner % nc) % nc) * ny + (y_at - owner // nc) % ny
    wqkv, wo, wup, wdown = place_blocks(
        src.astype(i32), inverse % per_owner, slots_y + slots_core
    )

    by_one.append(near_piece(n1 - 1, by_one, wup))
    mine = by_one[-1]
    for part in far_parts:
        mine = mine + part

    row_parts = [mine[0]] + [over_dp(mine[k], -k, 0) for k in range(1, ny)]
    if ny == 2:
        first = y_at == 0
        x0 = jnp.concatenate(
            [
                jnp.where(first, row_parts[0], row_parts[1]),
                jnp.where(first, row_parts[1], row_parts[0]),
            ],
            1,
        )
    else:
        stacked = jnp.stack(row_parts)
        x0 = jnp.concatenate(
            [jnp.take(stacked, (j - y_at) % ny, axis=0) for j in range(ny)], axis=1
        )

    low_sent = tie(low_own, x0)
    low_y = [over_dp(low_sent, k, 0) for k in range(1, ny)]

    maps_low = feature_maps.astype(bf16)
    both = jnp.concatenate([maps_low, -maps_low], -1).reshape(2, PAIRS, 2, HD, 2 * HD)
    empty = jnp.zeros_like(both[:, :, 0])
    lift_maps = jnp.stack(
        [
            jnp.concatenate([both[:, :, 0], empty], -2),
            jnp.concatenate([empty, both[:, :, 1]], -2),
        ],
        2,
    ).reshape(2, HEADS, 2 * HD, 2 * HD)
    their_hits = over_dp(hits, 0, 1)
    h1, mixed = qkv_forward(tie(x0, their_hits), wqkv, vectors)
    y, distill = attend(seq_lengths, mixed, lift_maps)
    x1, h2, up, act, x2, picked = mlp_forward(x0, y, wo, wup, wdown, vectors, pick_rows)

    near_picked = [picked] + [over_voc(picked, 0, k) for k in range(1, n0)]
    low_y = [tie(part, *near_picked) for part in low_y]
    low_y_other = [over_dp(part, 0, 1) for part in low_y]
    pieces = [low_own] + low_y + [low_other] + low_y_other
    near_picked = jnp.concatenate(near_picked, 0)
    group = [near_picked] + [over_voc(near_picked, k, 0) for k in range(1, n1)]
    group = jnp.concatenate(group, 0)
    local_targets = targets_all - vocab_start
    logits, stats = vocabulary_logits(piece_places, group, local_targets, pieces)
    stats_all = gather_stacked(stats)
    lined = jnp.stack(
        [
            jnp.roll(stats_all[a, b, :3].reshape(3, n1, n0, picks_own), (a, b), (1, 2))
            for a in range(n1)
            for b in range(n0)
        ]
    ).reshape(n_voc, 3, n_voc * picks_own)
    top_all = jnp.max(lined[:, 0], 0)
    sum_all = jnp.sum(lined[:, 1] * jnp.exp(lined[:, 0] - top_all[None]), 0)
    losses = top_all + jnp.log(sum_all) - jnp.sum(lined[:, 2], 0)
    loss_part = jnp.sum(losses[:picks_own]) / total_picks + coefficient * distill[0, 0]
    shares = jnp.pad(jnp.stack([top_all, 1.0 / sum_all]), ((0, 126), (0, 0)))
    grad_logits, grad_group = vocabulary_back(
        piece_places, logits, shares, local_targets, pieces, 1.0 / total_picks
    )
    grad_group = grad_group.reshape(n1, n0, picks_own, D)
    by_one = []
    for a in list(range(1, n1)) + [0]:
        part = grad_group[a, 0]
        for b in range(1, n0):
            part = part + over_voc(grad_group[a, b], 0, -b)
        by_one.append(part)
    near_parts = [over_voc(by_one[a - 1], -a, 0) for a in range(1, n1)]

    lex_mine, lex_theirs, mine_high, theirs_high = lexicon(
        piece_places, group.T, tie(grad_logits, *by_one[:-1]), cols_own, shard_rows
    )
    lex_arrived = over_dp(lex_theirs, 0, 1)
    their_high = over_dp(theirs_high, 0, 1)
    lex_high = jnp.max(mine_high) + jnp.max(their_high)
    ghp = by_one[-1]
    for part in near_parts:
        ghp = ghp + tie(part, lex_theirs, their_high)

    def lex_lines(k):
        lines = slice(k * cols_own, (k + 1) * cols_own)
        return lex_mine[lines] + lex_arrived[lines]

    lex_sent = [pack_lanes(lex_lines(k), lex_high) for k in range(1, ny)]


    def core_parts(mine_part, their_part, mine_top, their_top, *later):
        arrived = tie(over_dp(their_part, 0, 1), *later)
        bound = jnp.max(mine_top) + jnp.max(over_dp(their_top, 0, 1))
        return coded_parts((mine_part, arrived), bound, 0) + (bound,)

    def coded_parts(parts, bound, axis):
        size = (n0, ny, n1)[axis]

        def lines(part, k):
            count = part.shape[0]
            if axis == 1:
                rows = part.reshape(count, n1, ny, -1, BS)
                rows = lax.dynamic_index_in_dim(rows, (y_at + k) % ny, 2, False)
                return rows.reshape(count, -1, BS)
            rows = part.shape[1] // size
            at = (i0 if axis == 0 else i1) + k
            return lax.dynamic_slice_in_dim(part, (at % size) * rows, rows, 1)

        def summed(k):
            cut = [lines(part, k) for part in parts]
            return sum(cut[1:], cut[0])

        return summed(0), [pack(summed(k), bound) for k in range(1, size)]

    def moved_parts(sent, axis):
        if axis == 1:
            return [over_dp(part, k, 0) for k, part in enumerate(sent, 1)]
        return [
            over_voc(part, k, 0) if axis == 2 else over_voc(part, 0, k)
            for k, part in enumerate(sent, 1)
        ]

    def collect(own, arrived, bound, *later):
        total, high = own, bound
        for part in arrived:
            values, top = unpack(tie(part, *later), own.shape)
            total = total + values
            high = high + top
        return total, high

    *halves_a, gx1, ga, gy, vg_a = mlp_back(
        core, ghp, pick_rows, x2, act, up, h2, x1, wdown, wup, wo, vectors
    )
    own_a, sent_a, bound_a = core_parts(*halves_a, *lex_sent)
    gy = tie(gy, *lex_sent, own_a, *sent_a)
    gqkv, map_q, map_k = attend_back(
        seq_lengths, mixed, gy, lift_maps, coefficient, 0, PAIRS, None
    )
    lex_parts = [over_dp(part, -k, 0) for k, part in enumerate(lex_sent, 1)]
    gx0, vg_b = qkv_back(gqkv, wqkv, x0, gx1, vectors)

    map_grads = jnp.concatenate([map_q, map_k], 0)
    vec_grads = (vg_a + vg_b)[:15]
    small_count = map_grads.size + vec_grads.size
    small = jnp.concatenate(
        [
            map_grads.reshape(-1),
            vec_grads.reshape(-1),
            jnp.zeros((2 * BS * BS - small_count,), f32),
        ]
    ).reshape(2, BS, BS)
    gx0_cols = gx0.reshape(tokens, ny, cols_y)
    cols_sent = [jnp.take(gx0_cols, (y_at + k) % ny, axis=1) for k in range(1, ny)]
    lex = lex_lines(0)
    for part in lex_parts:
        lex = lex + unpack_lanes(part)
    arrived = [jnp.take(gx0_cols, y_at, axis=1)] + [
        tie(over_dp(part, k, 0), lex) for k, part in enumerate(cols_sent, 1)
    ]
    arrived = jnp.concatenate(arrived, 0).reshape(ny * tokens, nc, cols_own)
    rows_mine = jnp.take(arrived, c_at, axis=1)
    moved_a = moved_parts(sent_a, 0)
    rows_sent = jnp.take(arrived, (c_at + 1) % nc, axis=1)
    rows_other = over_dp(rows_sent, 0, 1)
    if cols_own == 192 and n0 == 2 and n1 == 4:
        packed = jnp.concatenate(
            [
                rows_mine[:, :128],
                rows_other[:, :128],
                jnp.concatenate([rows_mine[:, 128:], rows_other[:, 128:]], 1),
            ],
            0,
        )
    else:
        packed = jnp.stack([rows_mine, rows_other])
    halves_b = qkv_weights(core, tie(h1, packed, *moved_a), gqkv, y, ga, small)
    total_a, high_a = collect(own_a, moved_a, bound_a, halves_b[0])
    near_raw = [over_voc(packed, k, 0) for k in range(1, n1)]
    own_b, sent_b, bound_b = core_parts(*halves_b, packed)
    total_b, high_b = collect(own_b, moved_parts(sent_b, 0), bound_b)
    own_a, sent_a = coded_parts((total_a,), high_a, 1)
    own_b, sent_b = coded_parts((total_b,), high_b, 1)
    near_rows = [packed] + [tie(part, *sent_b) for part in near_raw]
    total_a, high_a = collect(own_a, moved_parts(sent_a, 1), high_a, *sent_b)
    total_b, high_b = collect(own_b, moved_parts(sent_b, 1), high_b)
    total = jnp.concatenate([total_a, total_b], 0)
    own, sent = coded_parts((total,), jnp.maximum(high_a, high_b), 2)
    high = jnp.maximum(high_a, high_b)
    own_x = [over_voc(tie(packed, *sent_b, near_rows[-2]), 0, k) for k in range(1, n0)]
    sent = [tie(part, *near_rows) for part in sent]
    far_rows = jnp.stack([tie(part, *own_x) for part in near_rows[1:]])
    far_x = [over_voc(far_rows, 0, k) for k in range(1, n0)]
    moved_ab = moved_parts(sent, 2)

    if cols_own == 192 and n0 == 2 and n1 == 4:
        groups = [(base, listed, (g % early) * listed) for g, base in enumerate(bases)]
        before = scatter_first(
            hits,
            their_hits,
            groups[early:],
            [tie(near_rows[a], *sent) for a in lines],
            shard_rows,
        )
        lex = tie(lex, *before, moved_ab[0])
        emb_grads, emb_square = scatter_last(
            hits, their_hits, groups[:early], before, lex, far_x[0], own_x, shard_rows
        )
        emb_square = emb_square[0, 0]
    else:
        gathered = [[packed] + own_x]
        for a in range(1, n1):
            gathered.append([near_rows[a]] + [part[a - 1] for part in far_x])
        pieces = jnp.stack([gathered[a][b] for a, b in piece_order], 1).reshape(-1, cols_own)
        ids_rows = jnp.concatenate(ids_order)
        local = jnp.concatenate([ids_rows, over_dp(ids_rows, 0, 1)]) - vocab_start
        local = jnp.where((local >= 0) & (local < shard_rows), local, shard_rows)
        emb_grads = lex[:, :shard_rows].T.at[local].add(pieces.astype(f32), mode="drop").T
        emb_square = jnp.sum(emb_grads * emb_grads)

    blocks = collect(own, moved_ab, high, emb_grads)[0]

    square = emb_square + jnp.sum(blocks * blocks)
    sums = jnp.pad(jnp.stack([square, loss_part]).reshape(1, 2), ((0, 7), (0, 126)))
    sums = sums + over_dp(sums, 0, 1)
    sums = jnp.sum(line_up(gather_y(sums), y_at), 0)
    per_side = blocks.shape[0]
    both = jnp.concatenate([blocks, over_dp(blocks, 0, 1)], 0)
    side, place = comm_positions()
    side = jnp.concatenate([jnp.take(jnp.asarray(side), block_order), jnp.arange(2, dtype=i32)])
    place = jnp.concatenate(
        [jnp.take(jnp.asarray(place), block_order), jnp.full((2,), per_side - 1, i32)]
    )
    at_place = ((side - c_at) % nc) * per_side + place
    smalls = at_place[block_count:]
    at_place = at_place[:block_count].reshape(ny, nc, per_owner)

    def slots_of(k):
        mine = jnp.take(jnp.take(at_place, c_at, axis=1), (y_at + k) % ny, axis=0)
        return jnp.take(both, jnp.concatenate([mine, smalls]), axis=0)

    moved = [slots_of(k) for k in range(1, ny)]
    slots_sent = [pack(part, jnp.max(jnp.abs(both))) for part in moved]
    sums = tie(sums, *slots_sent)
    sums = jnp.sum(line_up([sums] + [over_voc(sums, 0, k) for k in range(1, n0)], i0), 0)

    small_own = unpack(slots_sent[0], moved[0].shape)[0][per_owner:]
    strip_parts = [jnp.concatenate([slots_of(0)[:per_owner], small_own], 0)]
    slots_moved = moved_parts(slots_sent, 1)
    sums = tie(sums, *slots_moved)
    for part in slots_moved:
        strip_parts.append(unpack(part, moved[0].shape)[0])
    sums = jnp.sum(line_up([sums] + [over_voc(sums, k, 0) for k in range(1, n1)], i1), 0)
    grad_norm = jnp.sqrt(sums[0, 0])
    loss_total = sums[0, 1]
    clip_scale = CLIP_NORM / jnp.maximum(grad_norm, CLIP_NORM)
    own_strips = line_up(strip_parts, y_at).transpose(1, 0, 2, 3)
    own_strips = own_strips.reshape(per_owner + 2, -1, BS)
    strip_rows = own_strips.shape[1]
    strip_half = BS // n0
    places = [
        ((i0 - b) % n0) * strip_half + ((i1 - a) % n1) * strip_rows
        for a in range(n1)
        for b in range(n0)
    ]
    places = jnp.stack(places).astype(i32)
    strip_sent = tie(pack(own_strips, jnp.max(jnp.abs(own_strips))), sums)
    strip_pieces = [part.astype(f32) for part in flat_gather(strip_sent)]
    clipped, new_slots, new_left, new_right, small_all = shampoo(
        places,
        clip_scale.reshape(1),
        strip_pieces,
        strip_rows,
        (slot_weights, left_stats, right_stats, left_roots, right_roots),
    )
    clip_late = tie(clip_scale, strip_sent)
    small_all = small_all.reshape(-1)
    map_grad = small_all[: map_grads.size].reshape(feature_maps.shape)
    vec_grad = small_all[map_grads.size : small_count].reshape(vectors.shape)

    step_value = step_count[0].astype(f32)
    emb_out = adam_update(
        table_own,
        embedding_first_moment.T,
        emb_second.T,
        emb_grads * clip_late,
        RATE_TABLE,
        step_value,
    )
    vec_out = adam_update(
        vectors, vec_first, vec_second, vec_grad, RATE_VECTORS, step_value
    )
    map_out = adam_update(
        feature_maps, map_first, map_second, map_grad, RATE_MAPS, step_value
    )
    return (
        loss_total,
        grad_norm,
        clipped,
        new_slots,
        new_left,
        new_right,
        emb_out[0].T,
        emb_out[1].T,
        emb_out[2].T,
        vec_out[0],
        vec_out[1],
        vec_out[2],
        map_out[0],
        map_out[1],
        map_out[2],
    )


def solution(mesh):
    n_dp, n_voc = mesh.shape["dp"], mesh.shape["vocab"]
    sizes = (n_dp // 2, 2, 4, n_voc // 4)
    rows = P(("dp", "vocab"))
    blocks = P("dp", None, None)
    table = P("vocab", "dp")
    placed = (
        (rows, P(("dp", "vocab"), None), rows, rows, P(), P())
        + (blocks,) * 5
        + (table,) * 3
        + (P(),) * 6
    )
    return jax.shard_map(
        partial(per_device, sizes),
        mesh=mesh,
        in_specs=placed,
        out_specs=(P(), P()) + (blocks,) * 4 + (table,) * 3 + (P(),) * 6,
        check_vma=False,
    )
```

```python
from functools import partial

import jax
import jax.numpy as jnp
import numpy as np
from jax import lax
from jax.experimental import pallas as pl
from jax.experimental.pallas import tpu as pltpu
from jax.sharding import PartitionSpec as P

D = 768
HEADS = 12
HD = 64
FF = 3072
BS = 384
PAIRS = HEADS // 2

NORM_EPSILON = 1e-05
CLIP_NORM = 0.01
DISTILL_WEIGHT = 0.5
BETA_FIRST = 0.9
BETA_SECOND = 0.95
ADAM_EPSILON = 1e-08
DECAY_RATE = 0.01
SHAMPOO_BETA = 0.95
RATE_BLOCKS = 0.1
RATE_TABLE = 0.05
RATE_VECTORS = 0.2
RATE_MAPS = 0.1

f32 = jnp.float32
bf16 = jnp.bfloat16
i32 = jnp.int32
SMEM = pltpu.SMEM
ANY = pl.ANY


def mm(left, right):
    return lax.dot_general(left, right, (((1,), (0,)), ((), ())), preferred_element_type=f32)


def mm_t(left, right):
    return lax.dot_general(left, right, (((1,), (1,)), ((), ())), preferred_element_type=f32)


def mm_l(left, right):
    return lax.dot_general(left, right, (((0,), (0,)), ((), ())), preferred_element_type=f32)


def split_two(values):
    high = values.astype(bf16)
    return high, (values - high.astype(f32)).astype(bf16)


def full(shape):
    return pl.BlockSpec(shape, lambda *_: (0,) * len(shape))


def cost(flops, bytes_moved, transcendentals=0):
    return pl.CostEstimate(
        flops=int(flops * 0.02),
        bytes_accessed=int(bytes_moved * 0.02),
        transcendentals=int(transcendentals * 0.02),
    )


def place_kernel(piece_count, src_ref, off_ref, *refs):
    pieces = refs[:piece_count]
    outs = refs[piece_count : piece_count + 4]
    sems = refs[piece_count + 4]
    base = 0
    for out, rows, cols in zip(outs, (D, D, D, FF), (3 * D, D, FF, D)):
        wide = cols // BS
        count = (rows // BS) * wide

        def go(t, carry, out=out, wide=wide, base=base):
            k = base + t
            r0 = pl.multiple_of((t // wide) * BS, BS)
            c0 = pl.multiple_of((t % wide) * BS, BS)
            for p in range(piece_count):

                @pl.when(src_ref[k] == p)
                def _(p=p):
                    pltpu.make_async_copy(
                        pieces[p].at[off_ref[k]],
                        out.at[pl.ds(r0, BS), pl.ds(c0, BS)],
                        sems.at[k],
                    ).start()

            return carry

        lax.fori_loop(0, count, go, 0)
        base += count
    base = 0
    for out, rows, cols in zip(outs, (D, D, D, FF), (3 * D, D, FF, D)):
        count = (rows // BS) * (cols // BS)

        def done(t, carry, out=out, base=base):
            pltpu.make_async_copy(
                pieces[0].at[0], out.at[pl.ds(0, BS), pl.ds(0, BS)], sems.at[base + t]
            ).wait()
            return carry

        lax.fori_loop(0, count, done, 0)
        base += count


def place_blocks(src, off, pieces):
    count = len(pieces)
    return pl.pallas_call(
        partial(place_kernel, count),
        out_shape=[
            jax.ShapeDtypeStruct(shape, bf16)
            for shape in ((D, 3 * D), (D, D), (D, FF), (FF, D))
        ],
        in_specs=[pl.BlockSpec(memory_space=SMEM)] * 2 + [pl.BlockSpec(memory_space=ANY)] * count,
        out_specs=[pl.BlockSpec(memory_space=pltpu.VMEM)] * 4,
        scratch_shapes=[pltpu.SemaphoreType.DMA((48,))],
        name="place_blocks",
        cost_estimate=cost(0, 2 * 48 * BS * BS * 2),
    )(src, off, *pieces)


def hits_kernel(empty_row, packed_ref, list_ref):
    total = packed_ref.shape[0]

    def go(i, n):
        for u in range(16):
            entry = packed_ref[i * 16 + u]
            list_ref[n] = entry
            n = n + 1 + (entry >> 31)
        return n

    n = lax.fori_loop(0, total // 16, go, jnp.int32(0))
    list_ref[total + 8] = n
    for u in range(8):
        list_ref[n + u] = empty_row << 16


def find_hits(packed, empty_row):
    total = packed.shape[0]
    return pl.pallas_call(
        partial(hits_kernel, empty_row),
        out_shape=jax.ShapeDtypeStruct((total + 16,), i32),
        in_specs=[pl.BlockSpec(memory_space=SMEM)],
        out_specs=pl.BlockSpec(memory_space=SMEM),
        name="find_hits",
        cost_estimate=cost(1e10, total * 8),
    )(packed)


def turn_kernel(core_ref, own_ref, other_ref, out_ref):
    first = core_ref[0] == 0
    own, other = own_ref[...].astype(f32), other_ref[...].astype(f32)
    depth = own.shape[0]
    both = jnp.concatenate([jnp.where(first, own, other), jnp.where(first, other, own)], 0)
    out_ref[...] = both.T


def turn_table(core, own, other):
    depth, rows_all = own.shape
    wide = lane_block(rows_all)
    block = pl.BlockSpec((depth, wide), lambda j: (0, j))
    return pl.pallas_call(
        turn_kernel,
        grid=(pl.cdiv(rows_all, wide),),
        out_shape=jax.ShapeDtypeStruct((rows_all, 2 * depth), f32),
        in_specs=[pl.BlockSpec(memory_space=SMEM), block, block],
        out_specs=pl.BlockSpec((wide, 2 * depth), lambda j: (j, 0)),
        name="turn_table",
        cost_estimate=cost(1e7, 1e7),
    )(core, own, other)


def in_chunks(count, size, body):
    def go(i, carry):
        body(pl.multiple_of(i * size, size))
        return carry

    lax.fori_loop(0, count // size, go, 0)


def lookup_kernel(rows_all, list_ref, table_ref, *refs):
    outs, acc = refs[:-1], refs[-1]
    total = acc.shape[0] - 8
    chunk = 128

    def clear(start):
        acc[pl.ds(start, chunk), :] = jnp.zeros((chunk, acc.shape[1]), f32)

    in_chunks(total, chunk, clear)

    def go(i, carry):
        for u in range(8):
            entry = list_ref[i * 8 + u]
            row = entry >> 16
            place = jnp.where(row < rows_all, entry & 0xFFFF, total)
            row = jnp.minimum(row, rows_all - 1)
            acc[pl.ds(place, 1), :] = table_ref[pl.ds(row, 1), :]
        return carry

    lax.fori_loop(0, (list_ref[total + 8] + 7) // 8, go, 0)
    each = outs[0].shape[0]
    for part, out in enumerate(outs):

        def keep(start, part=part, out=out):
            out[pl.ds(start, chunk), :] = acc[pl.ds(part * each + start, chunk), :].astype(bf16)

        in_chunks(each, chunk, keep)


def lookup(hit_list, table, count, parts):
    rows_all, width = table.shape
    return pl.pallas_call(
        partial(lookup_kernel, rows_all),
        out_shape=[jax.ShapeDtypeStruct((count // parts, width), bf16)] * parts,
        in_specs=[
            pl.BlockSpec(memory_space=SMEM),
            pl.BlockSpec(memory_space=pltpu.VMEM),
        ],
        out_specs=[pl.BlockSpec(memory_space=pltpu.VMEM)] * parts,
        scratch_shapes=[pltpu.VMEM((count + 8, width), f32)],
        name="lookup",
        cost_estimate=cost(1e10, rows_all * width * 2),
    )(hit_list, table)


def add_rows(own_ref, their_ref, groups, pieces, acc, tail, wide, pair):
    half = pieces[0].shape[0] // 3
    chunk = 128
    for k, piece in enumerate(pieces):

        def widen(start, k=k, piece=piece):
            values = piece[pl.ds(start, chunk), :].astype(f32)
            wide[pl.ds(k * 2 * half + start, chunk), :] = values

        def widen_pair(start, k=k, piece=piece):
            values = piece[pl.ds(2 * half + start, chunk), :].astype(f32)
            pair[pl.ds(k * half + start, chunk), :] = values

        in_chunks(2 * half, chunk, widen)
        in_chunks(half, chunk, widen_pair)
    upper = lax.broadcasted_iota(i32, (1, 128), 1) >= 64
    for base, total, start in groups:
        for side, list_ref in enumerate((own_ref, their_ref)):
            own = upper if side else ~upper

            def go(i, carry, base=base, start=start, side=side, list_ref=list_ref, own=own):
                for u in range(8):
                    entry = list_ref[base + i * 8 + u]
                    row = entry >> 16
                    p = (entry & 0xFFFF) + start
                    q = (p // half) * half + p + side * half
                    acc[pl.ds(row, 1), :] += wide[pl.ds(q, 1), :]
                    tail[pl.ds(row, 1), :] += jnp.where(own, pair[pl.ds(p, 1), :], 0.0)
                return carry

            lax.fori_loop(0, (list_ref[base + total + 8] + 7) // 8, go, 0)


def scatter_first_kernel(count, groups, own_ref, their_ref, *refs):
    pieces = refs[:count]
    acc, tail, wide, pair = refs[count:]

    def clear(start):
        acc[pl.ds(start, 128), :] = jnp.zeros((128, 128), f32)
        tail[pl.ds(start, 128), :] = jnp.zeros((128, 128), f32)

    in_chunks(acc.shape[0], 128, clear)
    add_rows(own_ref, their_ref, groups, pieces, acc, tail, wide, pair)


def scatter_last_kernel(
    count, groups, rows_all, own_ref, their_ref, first_acc, first_tail, lex_ref, stack_ref, *refs
):
    pieces = [stack_ref.at[k] for k in range(stack_ref.shape[0])] + list(refs[:count])
    pieces = [pieces[k] for k in (1, 0, 2, 3)]
    out_ref, square_ref, acc, tail, wide, pair = refs[count:]

    def carry_over(start):
        acc[pl.ds(start, 128), :] = first_acc[pl.ds(start, 128), :]
        tail[pl.ds(start, 128), :] = first_tail[pl.ds(start, 128), :]

    in_chunks(acc.shape[0], 128, carry_over)
    add_rows(own_ref, their_ref, groups, pieces, acc, tail, wide, pair)
    chunks = rows_all // 128
    rest = rows_all - chunks * 128

    def turn(start, width):
        upright = acc[pl.ds(start, 128), :].T
        lower = tail[pl.ds(start, 128), :].T
        lower = lower[:64] + lower[64:]
        lanes = pl.ds(start, width)
        left = lex_ref[pl.ds(0, 128), lanes] + upright[:, :width]
        right = lex_ref[pl.ds(128, 64), lanes] + lower[:, :width]
        out_ref[pl.ds(0, 128), lanes] = left
        out_ref[pl.ds(128, 64), lanes] = right
        return jnp.sum(left * left, 0, keepdims=True), jnp.sum(right * right, 0, keepdims=True)

    def step(i, carry):
        left, right = turn(pl.multiple_of(i * 128, 128), 128)
        return carry + left + right

    squares = lax.fori_loop(0, chunks, step, jnp.zeros((1, 128), f32))
    total = jnp.sum(squares)
    if rest:
        left, right = turn(chunks * 128, rest)
        total = total + jnp.sum(left) + jnp.sum(right)
    square_ref[0, 0] = total


def scatter_first(own_list, their_list, groups, pieces, rows_all):
    half = pieces[0].shape[0] // 3
    count = len(pieces)
    padded = (rows_all // 128 + 1) * 128
    return pl.pallas_call(
        partial(scatter_first_kernel, count, groups),
        out_shape=[jax.ShapeDtypeStruct((padded, 128), f32)] * 2,
        in_specs=[pl.BlockSpec(memory_space=SMEM)] * 2
        + [pl.BlockSpec(memory_space=pltpu.VMEM)] * count,
        out_specs=[pl.BlockSpec(memory_space=pltpu.VMEM)] * 2,
        scratch_shapes=[
            pltpu.VMEM((count * 2 * half, 128), f32),
            pltpu.VMEM((count * half, 128), f32),
        ],
        name="scatter_first",
        cost_estimate=cost(1e10, rows_all * 128 * 8),
    )(own_list, their_list, *pieces)


def scatter_last(own_list, their_list, groups, before, lex, stacked, pieces, rows_all):
    width = lex.shape[0]
    half = stacked.shape[1] // 3
    count = len(pieces)
    used = count + stacked.shape[0]
    padded = (rows_all // 128 + 1) * 128
    return pl.pallas_call(
        partial(scatter_last_kernel, count, groups, rows_all),
        out_shape=[
            jax.ShapeDtypeStruct((width, rows_all), f32),
            jax.ShapeDtypeStruct((1, 1), f32),
        ],
        in_specs=[pl.BlockSpec(memory_space=SMEM)] * 2
        + [pl.BlockSpec(memory_space=pltpu.VMEM)] * (count + 4),
        out_specs=[
            pl.BlockSpec(memory_space=pltpu.VMEM),
            pl.BlockSpec(memory_space=SMEM),
        ],
        scratch_shapes=[
            pltpu.VMEM((padded, 128), f32),
            pltpu.VMEM((padded, 128), f32),
            pltpu.VMEM((used * 2 * half, 128), f32),
            pltpu.VMEM((used * half, 128), f32),
        ],
        name="scatter_last",
        cost_estimate=cost(1e10, rows_all * width * 8),
    )(own_list, their_list, *before, lex, stacked, *pieces)


def norm_parts(inputs):
    centered = inputs - jnp.mean(inputs, -1, keepdims=True)
    scale = lax.rsqrt(jnp.mean(centered * centered, -1, keepdims=True) + NORM_EPSILON)
    return centered, scale


def norm_pull(inputs, gain_row, grads):
    centered, scale = norm_parts(inputs)
    unit = centered * scale
    pulled = grads * gain_row
    lead = jnp.mean(pulled, -1, keepdims=True)
    along = jnp.mean(pulled * unit, -1, keepdims=True)
    grad_in = scale * (pulled - lead - unit * along)
    return (
        grad_in,
        jnp.sum(grads * unit, 0, keepdims=True),
        jnp.sum(grads, 0, keepdims=True),
    )


def qkv_kernel(x_ref, w_ref, vec_ref, h_ref, mixed_ref):
    j = pl.program_id(0)

    @pl.when(j == 0)
    def _():
        centered, scale = norm_parts(x_ref[...].astype(f32))
        h_ref[...] = (centered * scale * vec_ref[0:1, :] + vec_ref[1:2, :]).astype(bf16)

    mixed_ref[...] = (mm(h_ref[...], w_ref[...]) + vec_ref[pl.ds(8 + j, 1), :]).astype(bf16)


def qkv_forward(x0, wqkv, vectors):
    tokens = x0.shape[0]
    return pl.pallas_call(
        qkv_kernel,
        grid=(3,),
        out_shape=[
            jax.ShapeDtypeStruct((tokens, D), bf16),
            jax.ShapeDtypeStruct((tokens, 3 * D), bf16),
        ],
        in_specs=[
            full((tokens, D)),
            pl.BlockSpec((D, D), lambda j: (0, j)),
            full(vectors.shape),
        ],
        out_specs=[full((tokens, D)), pl.BlockSpec((tokens, D), lambda j: (0, j))],
        name="qkv_forward",
        cost_estimate=cost(2 * tokens * D * 3 * D, 8e6),
    )(x0, wqkv, vectors)


def feature_parts(values, lift, low_half):
    raw = mm(values, lift)
    top_a = jnp.max(jnp.where(low_half, raw, -jnp.inf), -1, keepdims=True)
    top_b = jnp.max(jnp.where(low_half, -jnp.inf, raw), -1, keepdims=True)
    grown = jnp.exp(raw - jnp.where(low_half, top_a, top_b))
    sum_a = jnp.sum(jnp.where(low_half, grown, 0.0), -1, keepdims=True)
    sum_b = jnp.sum(jnp.where(low_half, 0.0, grown), -1, keepdims=True)
    return grown / jnp.where(low_half, sum_a, sum_b)


def feature_pull(soft, grads, low_half):
    weighed = soft * grads
    sum_a = jnp.sum(jnp.where(low_half, weighed, 0.0), -1, keepdims=True)
    sum_b = jnp.sum(jnp.where(low_half, 0.0, weighed), -1, keepdims=True)
    pulled = soft * (grads - jnp.where(low_half, sum_a, sum_b))
    return (pulled - pltpu.roll(pulled, HD, 1)).astype(bf16)


def fill_allowed(len_ref, allow_ref):
    tokens = allow_ref.shape[0]
    first = len_ref[0, 0]
    second = first + len_ref[0, 1]
    third = second + len_ref[0, 2]

    def document(places):
        return (
            (places >= first).astype(i32)
            + (places >= second).astype(i32)
            + (places >= third).astype(i32)
        )

    rows = lax.broadcasted_iota(i32, (tokens, tokens), 0)
    cols = lax.broadcasted_iota(i32, (tokens, tokens), 1)
    allow_ref[...] = ((cols <= rows) & (document(rows) == document(cols))).astype(f32)


ROWS = 256


def attend_kernel(
    len_ref, q_ref, k_ref, v_ref, fq_ref, fk_ref, y_ref, distill_ref, allow_ref, lift_q, lift_k
):
    tokens = q_ref.shape[0]

    @pl.when(pl.program_id(0) == 0)
    def _():
        fill_allowed(len_ref, allow_ref)
        distill_ref[...] = jnp.zeros_like(distill_ref)

    low_half = lax.broadcasted_iota(i32, (1, 2 * HD), 1) < HD
    low_rows = lax.broadcasted_iota(i32, (ROWS, 2 * HD), 1) < HD
    total = jnp.zeros((1, 1), f32)
    for h in range(2):
        lift_q[h] = feature_parts(q_ref[...], fq_ref[h], low_half).astype(bf16)
        lift_k[h] = feature_parts(k_ref[...], fk_ref[h], low_half).astype(bf16)
    for begin in range(0, tokens, ROWS):
        width = begin + ROWS
        ok = allow_ref[pl.ds(begin, ROWS), pl.ds(0, width)] > 0.5
        queries = q_ref[pl.ds(begin, ROWS), :] * jnp.asarray(HD**-0.5, bf16)
        keys = k_ref[pl.ds(0, width), :]
        values = v_ref[pl.ds(0, width), :]
        parts = []
        for h in range(2):
            own = low_rows if h == 0 else ~low_rows
            scores = mm_t(jnp.where(own, queries, jnp.zeros_like(queries)), keys)
            scores = jnp.where(ok, scores, -1e30)
            grown = jnp.exp(scores - jnp.max(scores, -1, keepdims=True))
            inverse = 1.0 / jnp.sum(grown, -1, keepdims=True)
            similar = mm_t(lift_q[h, pl.ds(begin, ROWS), :], lift_k[h, pl.ds(0, width), :])
            kept = jnp.where(ok, similar, 0.0)
            sums = jnp.sum(kept, -1, keepdims=True)
            weights = (kept * (1.0 / sums)).astype(bf16)
            parts.append(mm(weights, values))
            logs = jnp.log(jnp.where(ok, similar, 1.0))
            row_terms = jnp.log(sums) - jnp.sum(grown * logs, -1, keepdims=True) * inverse
            total = total + jnp.sum(row_terms, 0, keepdims=True)
        y_ref[pl.ds(begin, ROWS), :] = jnp.where(low_rows, parts[0], parts[1]).astype(bf16)
    distill_ref[...] += jnp.broadcast_to(total, distill_ref.shape)


def attend(lengths, mixed, lift_maps):
    tokens = mixed.shape[0]
    column = lambda base: pl.BlockSpec((tokens, 2 * HD), lambda g: (0, base + g))
    maps = pl.BlockSpec((2, 2 * HD, 2 * HD), lambda g: (g, 0, 0))
    return pl.pallas_call(
        attend_kernel,
        grid=(PAIRS,),
        out_shape=[
            jax.ShapeDtypeStruct((tokens, D), bf16),
            jax.ShapeDtypeStruct((8, 128), f32),
        ],
        in_specs=[
            pl.BlockSpec(memory_space=SMEM),
            column(0),
            column(PAIRS),
            column(2 * PAIRS),
            maps,
            maps,
        ],
        out_specs=[column(0), full((8, 128))],
        scratch_shapes=[
            pltpu.VMEM((tokens, tokens), f32),
            pltpu.VMEM((2, tokens, 2 * HD), bf16),
            pltpu.VMEM((2, tokens, 2 * HD), bf16),
        ],
        name="attend",
        cost_estimate=cost(1.2e10, 4e6, 6e6),
    )(lengths, mixed, mixed, mixed, lift_maps[0], lift_maps[1])


def attend_back_kernel(
    coefficient,
    later,
    len_ref,
    q_ref,
    k_ref,
    v_ref,
    gy_ref,
    fq_ref,
    fk_ref,
    *refs,
):
    g_ref, gq_map_ref, gk_map_ref, allow_ref, soft_q, soft_k, grad_q, grad_k, grad_v = refs[later:]
    tokens = q_ref.shape[0]

    @pl.when(pl.program_id(0) == 0)
    def _():
        fill_allowed(len_ref, allow_ref)

    low_half = lax.broadcasted_iota(i32, (1, 2 * HD), 1) < HD
    low_rows = lax.broadcasted_iota(i32, (ROWS, 2 * HD), 1) < HD
    for h in range(2):
        soft_q[h] = feature_parts(q_ref[...], fq_ref[h], low_half)
        soft_k[h] = feature_parts(k_ref[...], fk_ref[h], low_half)
    for step, begin in enumerate(reversed(range(0, tokens, ROWS))):
        width = begin + ROWS
        ok = allow_ref[pl.ds(begin, ROWS), pl.ds(0, width)] > 0.5
        queries = q_ref[pl.ds(begin, ROWS), :] * jnp.asarray(HD**-0.5, bf16)
        keys = k_ref[pl.ds(0, width), :]
        values = v_ref[pl.ds(0, width), :]
        grads = gy_ref[pl.ds(begin, ROWS), :]
        value_sum = None
        for h in range(2):
            own = low_rows if h == 0 else ~low_rows
            scores = mm_t(jnp.where(own, queries, jnp.zeros_like(queries)), keys)
            scores = jnp.where(ok, scores, -1e30)
            grown = jnp.exp(scores - jnp.max(scores, -1, keepdims=True))
            teach = grown * (coefficient / jnp.sum(grown, -1, keepdims=True))
            phi_q = soft_q[h, pl.ds(begin, ROWS), :].astype(bf16)
            phi_k = soft_k[h, pl.ds(0, width), :].astype(bf16)
            similar = mm_t(phi_q, phi_k)
            kept = jnp.where(ok, similar, 0.0)
            inverse = 1.0 / jnp.sum(kept, -1, keepdims=True)
            weights = kept * inverse
            own_grads = jnp.where(own, grads, jnp.zeros_like(grads))
            grad_w = mm_t(own_grads, values)
            row_sum = jnp.sum(grad_w * weights, -1, keepdims=True)
            grad_sums = (coefficient - row_sum) * inverse
            grad_sim = jnp.where(
                ok,
                grad_w * inverse - teach / jnp.where(ok, similar, 1.0) + grad_sums,
                0.0,
            ).astype(bf16)
            grad_q[h, pl.ds(begin, ROWS), :] = mm(grad_sim, phi_k)
            part_k = mm_l(grad_sim, phi_q)
            part_v = mm_l(weights.astype(bf16), own_grads)
            value_sum = part_v if value_sum is None else value_sum + part_v
            if step == 0:
                grad_k[h] = part_k
            else:
                grad_k[h, pl.ds(0, width), :] += part_k
        if step == 0:
            grad_v[...] = value_sum
        else:
            grad_v[pl.ds(0, width), :] += value_sum
    for slot, own_ref, map_ref, soft, grad, out in (
        (0, q_ref, fq_ref, soft_q, grad_q, gq_map_ref),
        (1, k_ref, fk_ref, soft_k, grad_k, gk_map_ref),
    ):
        result = None
        for h in range(2):
            pulled = feature_pull(soft[h], grad[h], low_half)
            back = mm_t(pulled, map_ref[h]) * 0.5
            result = back if result is None else result + back
            out[h] = mm_l(own_ref[...], pulled)[h * HD : (h + 1) * HD, :HD]
        g_ref[slot] = result.astype(bf16)
    g_ref[2] = grad_v[...].astype(bf16)


def attend_back(lengths, mixed, grad_y, lift_maps, coefficient, start, pairs, before):
    tokens = mixed.shape[0]
    column = lambda base: pl.BlockSpec((tokens, 2 * HD), lambda g: (0, base + start + g))
    maps = pl.BlockSpec((2, 2 * HD, 2 * HD), lambda g: (start + g, 0, 0))
    small = pl.BlockSpec((2, HD, HD), lambda g: (g, 0, 0))
    wide = (2, tokens, 2 * HD)
    later = before is not None
    return pl.pallas_call(
        partial(attend_back_kernel, coefficient, int(later)),
        grid=(pairs,),
        out_shape=[
            jax.ShapeDtypeStruct((3, tokens, D), bf16),
            jax.ShapeDtypeStruct((2 * pairs, HD, HD), f32),
            jax.ShapeDtypeStruct((2 * pairs, HD, HD), f32),
        ],
        in_specs=[
            pl.BlockSpec(memory_space=SMEM),
            column(0),
            column(PAIRS),
            column(2 * PAIRS),
            column(0),
            maps,
            maps,
        ]
        + [pl.BlockSpec(memory_space=ANY)] * later,
        out_specs=[
            pl.BlockSpec((3, tokens, 2 * HD), lambda g: (0, 0, start + g)),
            small,
            small,
        ],
        scratch_shapes=[
            pltpu.VMEM((tokens, tokens), f32),
            pltpu.VMEM(wide, f32),
            pltpu.VMEM(wide, f32),
            pltpu.VMEM(wide, f32),
            pltpu.VMEM(wide, f32),
            pltpu.VMEM((tokens, 2 * HD), f32),
        ],
        input_output_aliases={7: 0} if later else {},
        name="attend_back",
        cost_estimate=cost(1.2e10, 4e6, 3e6),
    )(lengths, mixed, mixed, mixed, grad_y, lift_maps[0], lift_maps[1], *([before] * later))


FSTEPS = FF // D


def mlp_kernel(
    x_ref,
    y_ref,
    wo_ref,
    wup_ref,
    wdown_ref,
    vec_ref,
    pick_ref,
    x1_ref,
    h_ref,
    up_ref,
    act_ref,
    x2_ref,
    hp_ref,
):
    j = pl.program_id(0)

    @pl.when(j == 0)
    def _():
        x1 = x_ref[...].astype(f32) + mm(y_ref[...], wo_ref[...]) + vec_ref[6:7, :]
        x1_ref[...] = x1
        centered, scale = norm_parts(x1)
        h_ref[...] = (centered * scale * vec_ref[2:3, :] + vec_ref[3:4, :]).astype(bf16)
        x2_ref[...] = x1 + vec_ref[7:8, :]

    up = mm(h_ref[...], wup_ref[...]) + vec_ref[pl.ds(11 + j, 1), :]
    up_ref[...] = up
    act = (0.5 * up * (1.0 + jnp.tanh(0.7978845608 * (up + 0.044715 * up * up * up)))).astype(bf16)
    act_ref[...] = act
    x2_ref[...] += mm(act, wdown_ref[...])

    @pl.when(j == FSTEPS - 1)
    def _():
        centered, scale = norm_parts(x2_ref[...])
        last = (centered * scale * vec_ref[4:5, :] + vec_ref[5:6, :]).astype(bf16)
        tokens = last.shape[0]
        places = lax.broadcasted_iota(i32, (pick_ref.shape[0], tokens), 1)
        chosen = (places == pick_ref[...]).astype(bf16)
        hp_ref[...] = mm(chosen, last).astype(bf16)


def mlp_forward(x0, y, wo, wup, wdown, vectors, picks):
    tokens = x0.shape[0]
    count = picks.shape[0]
    wide = pl.BlockSpec((tokens, D), lambda j: (0, j))
    shape = lambda cols, kind: jax.ShapeDtypeStruct((tokens, cols), kind)
    return pl.pallas_call(
        mlp_kernel,
        grid=(FSTEPS,),
        out_shape=[
            shape(D, f32),
            shape(D, bf16),
            shape(FF, f32),
            shape(FF, bf16),
            shape(D, f32),
            jax.ShapeDtypeStruct((count, D), bf16),
        ],
        in_specs=[
            full((tokens, D)),
            full((tokens, D)),
            full((D, D)),
            pl.BlockSpec((D, D), lambda j: (0, j)),
            pl.BlockSpec((D, D), lambda j: (j, 0)),
            full(vectors.shape),
            full((count, 1)),
        ],
        out_specs=[
            full((tokens, D)),
            full((tokens, D)),
            wide,
            wide,
            full((tokens, D)),
            full((count, D)),
        ],
        name="mlp_forward",
        cost_estimate=cost(2 * tokens * D * (2 * FF + D), 3e7, tokens * FF),
    )(x0, y, wo, wup, wdown, vectors, picks.reshape(count, 1))


def keep_tiles(values, out, top, slot):
    for c in range(2):
        out[slot + c] = values[:, c * BS : (c + 1) * BS]
    high = jnp.max(jnp.abs(values), 0, keepdims=True)
    top[...] = jnp.maximum(top[...], jnp.maximum(high[:, :BS], high[:, BS:]))


def near_far(core):
    return pl.ds(pl.multiple_of(core * BS, BS), BS), pl.ds(pl.multiple_of((1 - core) * BS, BS), BS)


def mlp_back_kernel(
    core_ref,
    ghp_ref,
    pick_ref,
    x2_ref,
    act_ref,
    up_ref,
    h_ref,
    x1_ref,
    wdown_ref,
    wup_ref,
    wo_ref,
    vec_ref,
    mine_ref,
    theirs_ref,
    mine_top_ref,
    theirs_top_ref,
    gx1_ref,
    ga_ref,
    gy_ref,
    vg_ref,
    gx2,
    gm,
    gh,
):
    j = pl.program_id(0)
    core = core_ref[0]
    tokens = x2_ref.shape[0]

    @pl.when(j == 0)
    def _():
        mine_top_ref[...] = jnp.zeros_like(mine_top_ref)
        theirs_top_ref[...] = jnp.zeros_like(theirs_top_ref)
        vg_ref[...] = jnp.zeros_like(vg_ref)
        places = lax.broadcasted_iota(i32, (tokens, pick_ref.shape[1]), 0)
        chosen = (places == pick_ref[...]).astype(bf16)
        rest = ghp_ref[...]
        spread = jnp.zeros((tokens, D), f32)
        for _ in range(3):
            part = rest.astype(bf16)
            rest = rest - part.astype(f32)
            spread = spread + mm(chosen, part)
        grad, gain, bias = norm_pull(x2_ref[...], vec_ref[4:5, :], spread)
        gx2[...] = grad
        low = grad.astype(bf16)
        gm[...] = low
        vg_ref[4:5, :] = gain
        vg_ref[5:6, :] = bias
        vg_ref[7:8, :] = jnp.sum(low.astype(f32), 0, keepdims=True)

    grad_act = mm_t(gm[...], wdown_ref[...])
    up = up_ref[...]
    turn = jnp.tanh(0.7978845608 * (up + 0.044715 * up * up * up))
    slope = 0.5 * (1.0 + turn) + 0.5 * up * (1.0 - turn * turn) * (
        0.7978845608 * (1.0 + 3.0 * 0.044715 * up * up)
    )
    gup = (grad_act * slope).astype(bf16)
    vg_ref[pl.ds(11 + j, 1), :] = jnp.sum(gup.astype(f32), 0, keepdims=True)
    part = mm_t(gup, wup_ref[...])

    @pl.when(j == 0)
    def _():
        gh[...] = part

    @pl.when(j > 0)
    def _():
        gh[...] += part

    for cols, out, top in zip(
        near_far(core), (mine_ref, theirs_ref), (mine_top_ref, theirs_top_ref)
    ):
        keep_tiles(mm_l(h_ref[:, cols], gup), out, top, 0)
        keep_tiles(mm_l(act_ref[:, cols], gm[...]), out, top, 2)

    @pl.when(j == FSTEPS - 1)
    def _():
        grad, gain, bias = norm_pull(x1_ref[...], vec_ref[2:3, :], gh[...])
        vg_ref[2:3, :] = gain
        vg_ref[3:4, :] = bias
        grad = grad + gx2[...]
        gx1_ref[...] = grad
        low = grad.astype(bf16)
        ga_ref[...] = low
        vg_ref[6:7, :] = jnp.sum(low.astype(f32), 0, keepdims=True)
        gy_ref[...] = mm_t(low, wo_ref[...]).astype(bf16)


def mlp_back(core, ghp, picks, x2, act, up, h2, x1, wdown, wup, wo, vectors):
    tokens = x2.shape[0]
    count = picks.shape[0]
    wide = pl.BlockSpec((tokens, D), lambda j: (0, j))
    flat = full((tokens, D))
    tiles = pl.BlockSpec((4, BS, BS), lambda j: (j, 0, 0))
    tops = full((1, BS))
    halves = jax.ShapeDtypeStruct((4 * FSTEPS, BS, BS), f32)
    highs = jax.ShapeDtypeStruct((1, BS), f32)
    return pl.pallas_call(
        mlp_back_kernel,
        grid=(FSTEPS,),
        out_shape=[
            halves,
            halves,
            highs,
            highs,
            jax.ShapeDtypeStruct((tokens, D), f32),
            jax.ShapeDtypeStruct((tokens, D), bf16),
            jax.ShapeDtypeStruct((tokens, D), bf16),
            jax.ShapeDtypeStruct((16, D), f32),
        ],
        in_specs=[
            pl.BlockSpec(memory_space=SMEM),
            full((count, D)),
            full((1, count)),
            flat,
            wide,
            wide,
            flat,
            flat,
            pl.BlockSpec((D, D), lambda j: (j, 0)),
            pl.BlockSpec((D, D), lambda j: (0, j)),
            full((D, D)),
            full(vectors.shape),
        ],
        out_specs=[tiles, tiles, tops, tops, flat, flat, flat, full((16, D))],
        scratch_shapes=[
            pltpu.VMEM((tokens, D), f32),
            pltpu.VMEM((tokens, D), bf16),
            pltpu.VMEM((tokens, D), f32),
        ],
        name="mlp_back",
        cost_estimate=cost(8 * tokens * D * FF, 5e7, tokens * FF),
    )(core, ghp, picks.reshape(1, count), x2, act, up, h2, x1, wdown, wup, wo, vectors)


def qkv_back_kernel(g_ref, w_ref, x_ref, gx1_ref, vec_ref, gx0_ref, vg_ref, gh):
    j = pl.program_id(0)
    part = mm_t(g_ref[0], w_ref[...])

    @pl.when(j == 0)
    def _():
        vg_ref[...] = jnp.zeros_like(vg_ref)
        gh[...] = part

    @pl.when(j > 0)
    def _():
        gh[...] += part

    vg_ref[pl.ds(8 + j, 1), :] = jnp.sum(g_ref[0].astype(f32), 0, keepdims=True)

    @pl.when(j == 2)
    def _():
        grad, gain, bias = norm_pull(x_ref[...].astype(f32), vec_ref[0:1, :], gh[...])
        vg_ref[0:1, :] = gain
        vg_ref[1:2, :] = bias
        gx0_ref[...] = (gx1_ref[...] + grad).astype(bf16)


def qkv_back(grads, wqkv, x0, gx1, vectors):
    tokens = x0.shape[0]
    flat = full((tokens, D))
    return pl.pallas_call(
        qkv_back_kernel,
        grid=(3,),
        out_shape=[
            jax.ShapeDtypeStruct((tokens, D), bf16),
            jax.ShapeDtypeStruct((16, D), f32),
        ],
        in_specs=[
            pl.BlockSpec((1, tokens, D), lambda j: (j, 0, 0)),
            pl.BlockSpec((D, D), lambda j: (0, j)),
            flat,
            flat,
            full(vectors.shape),
        ],
        out_specs=[flat, full((16, D))],
        scratch_shapes=[pltpu.VMEM((tokens, D), f32)],
        name="qkv_back",
        cost_estimate=cost(2 * tokens * D * 3 * D, 1e7),
    )(grads, wqkv, x0, gx1, vectors)


def qkv_weights_kernel(
    core_ref, h_ref, g_ref, y_ref, ga_ref, small_ref, mine_ref, theirs_ref, mtop_ref, ttop_ref
):
    j = pl.program_id(0)
    core = core_ref[0]
    both = tuple(zip(near_far(core), (mine_ref, theirs_ref), (mtop_ref, ttop_ref)))

    @pl.when(j == 0)
    def _():
        for turn, (_, out, top) in enumerate(both):
            values = small_ref[core if turn == 0 else 1 - core]
            out[8] = values
            top[...] = jnp.max(jnp.abs(values), 0, keepdims=True)

    @pl.when(j < 3)
    def _():
        for cols, out, top in both:
            keep_tiles(mm_l(h_ref[:, cols], g_ref[0]), out, top, 2 * j)

    @pl.when(j == 3)
    def _():
        for cols, out, top in both:
            keep_tiles(mm_l(y_ref[:, cols], ga_ref[...]), out, top, 6)


def qkv_weights(core, h1, grads, y, ga, small):
    tokens = h1.shape[0]
    flat = full((tokens, D))
    halves = (9, BS, BS)
    highs = (1, BS)
    shapes = (halves, halves, highs, highs)
    return pl.pallas_call(
        qkv_weights_kernel,
        grid=(4,),
        out_shape=[jax.ShapeDtypeStruct(shape, f32) for shape in shapes],
        in_specs=[
            pl.BlockSpec(memory_space=SMEM),
            flat,
            pl.BlockSpec((1, tokens, D), lambda j: (jnp.minimum(j, 2), 0, 0)),
            flat,
            flat,
            full((2, BS, BS)),
        ],
        out_specs=[full(shape) for shape in shapes],
        name="qkv_weights",
        cost_estimate=cost(2 * tokens * D * 4 * D, 2e7),
    )(core, h1, grads, y, ga, small)


def comm_positions():
    side = np.zeros(48, np.int32)
    place = np.zeros(48, np.int32)
    for r in range(2):
        for c in range(2):
            for j in range(FSTEPS):
                place[16 + r * 8 + 2 * j + c] = 4 * j + c
                place[32 + (2 * j + r) * 2 + c] = 4 * j + 2 + c
                side[16 + r * 8 + 2 * j + c] = side[32 + (2 * j + r) * 2 + c] = r
            for j in range(3):
                place[r * 6 + 2 * j + c] = 16 + 2 * j + c
                side[r * 6 + 2 * j + c] = r
            place[12 + r * 2 + c] = 22 + c
            side[12 + r * 2 + c] = r
    return side, place


def lane_block(rows_all):
    return min(1280, (rows_all // 128 + 1) * 128)


def fill_table(places_ref, pieces, tab, valid):
    depth = pieces[0].shape[0]
    for p, piece in enumerate(pieces):
        start = pl.multiple_of(places_ref[p], depth)
        tab[pl.ds(start, depth), :] = jnp.where(valid, piece[...], jnp.zeros((), bf16))


def logits_kernel(rows_all, count, places_ref, group_ref, target_ref, *refs):
    pieces = refs[:count]
    logit_ref, stat_ref, tab, top, total, chosen = refs[count:]
    j = pl.program_id(0)
    wide = tab.shape[1]
    lane = lax.broadcasted_iota(i32, (1, wide), 1) + j * wide
    valid = lane < rows_all
    fill_table(places_ref, pieces, tab, valid)

    @pl.when(j == 0)
    def _():
        top[...] = jnp.full(top.shape, -jnp.inf, f32)
        total[...] = jnp.zeros(total.shape, f32)
        chosen[...] = jnp.zeros(chosen.shape, f32)

    logits = mm(group_ref[...], tab[...])
    logit_ref[...] = logits
    kept = jnp.where(valid, logits, -jnp.inf)
    before = top[...]
    after = jnp.maximum(before, jnp.max(kept, -1, keepdims=True))
    top[...] = after
    total[...] = total[...] * jnp.exp(before - after) + jnp.sum(
        jnp.exp(kept - after), -1, keepdims=True
    )
    hit = (lane == target_ref[...]) & valid
    chosen[...] += jnp.sum(jnp.where(hit, logits, 0.0), -1, keepdims=True)

    @pl.when(j == pl.num_programs(0) - 1)
    def _():
        spot = lax.broadcasted_iota(i32, (1, 128), 1)
        merged = jnp.where(
            spot == 0, top[...], jnp.where(spot == 1, total[...], chosen[...])
        )
        stat_ref[...] = merged.T[:8]


def table_specs(pieces, wide):
    return [pl.BlockSpec((pieces[0].shape[0], wide), lambda j: (0, j))] * len(pieces)


def vocabulary_logits(places, group, local_targets, pieces):
    count, rows_all = group.shape[0], pieces[0].shape[1]
    wide = lane_block(rows_all)
    return pl.pallas_call(
        partial(logits_kernel, rows_all, len(pieces)),
        grid=(pl.cdiv(rows_all, wide),),
        out_shape=[
            jax.ShapeDtypeStruct((count, rows_all), f32),
            jax.ShapeDtypeStruct((8, count), f32),
        ],
        in_specs=[pl.BlockSpec(memory_space=SMEM), full((count, D)), full((count, 1))]
        + table_specs(pieces, wide),
        out_specs=[pl.BlockSpec((count, wide), lambda j: (0, j)), full((8, count))],
        scratch_shapes=[pltpu.VMEM((D, wide), bf16)] + [pltpu.VMEM((count, 1), f32)] * 3,
        name="vocabulary_logits",
        cost_estimate=cost(2 * count * D * rows_all, 2e7, count * rows_all),
    )(places, group, local_targets.reshape(count, 1), *pieces)


def vocabulary_back_kernel(
    rows_all, count, scale, places_ref, logit_ref, stat_ref, target_ref, *refs
):
    pieces = refs[:count]
    grad_ref, ghp_ref, tab, stat = refs[count:]
    j = pl.program_id(0)
    wide = tab.shape[1]
    lane = lax.broadcasted_iota(i32, (1, wide), 1) + j * wide
    valid = lane < rows_all
    fill_table(places_ref, pieces, tab, valid)

    @pl.when(j == 0)
    def _():
        stat[...] = stat_ref[...].T
        ghp_ref[...] = jnp.zeros_like(ghp_ref)

    hit = (lane == target_ref[...]).astype(f32)
    soft = jnp.exp(logit_ref[...] - stat[:, 0:1]) * stat[:, 1:2]
    grads = jnp.where(valid, (soft - hit) * scale, 0.0).astype(bf16)
    grad_ref[...] = grads
    ghp_ref[...] += mm_t(grads, tab[...])


def vocabulary_back(places, logits, stats, local_targets, pieces, scale):
    count, rows_all = logits.shape
    wide = lane_block(rows_all)
    block = pl.BlockSpec((count, wide), lambda j: (0, j))
    return pl.pallas_call(
        partial(vocabulary_back_kernel, rows_all, len(pieces), scale),
        grid=(pl.cdiv(rows_all, wide),),
        out_shape=[
            jax.ShapeDtypeStruct((count, pl.cdiv(rows_all, wide) * wide), bf16),
            jax.ShapeDtypeStruct((count, D), f32),
        ],
        in_specs=[
            pl.BlockSpec(memory_space=SMEM),
            block,
            full(stats.shape),
            full((count, 1)),
        ]
        + table_specs(pieces, wide),
        out_specs=[block, full((count, D))],
        scratch_shapes=[pltpu.VMEM((D, wide), bf16), pltpu.VMEM((count, stats.shape[0]), f32)],
        name="vocabulary_back",
        cost_estimate=cost(2 * count * D * rows_all, 3e7, count * rows_all),
    )(places, logits, stats, local_targets.reshape(count, 1), *pieces)


def lexicon_kernel(
    depth, places_ref, turned_ref, grad_ref, mine_ref, theirs_ref, mtop_ref, ttop_ref, sel
):
    j = pl.program_id(0)
    half = mine_ref.shape[0]

    @pl.when(j == 0)
    def _():
        for p in range(sel.shape[0] // depth):
            start = pl.multiple_of(places_ref[p], depth)
            sel[pl.ds(p * depth, depth), :] = turned_ref[pl.ds(start, depth), :]
        mtop_ref[...] = jnp.zeros_like(mtop_ref)
        ttop_ref[...] = jnp.zeros_like(ttop_ref)

    for start, out, top in ((0, mine_ref, mtop_ref), (half, theirs_ref, ttop_ref)):
        part = mm(sel[pl.ds(start, half), :], grad_ref[...])
        out[...] = part
        top[...] = jnp.maximum(top[...], jnp.max(jnp.abs(part), 0, keepdims=True))


def lexicon(places, turned, grads, depth, rows_all):
    count, padded = grads.shape
    wide = lane_block(rows_all)
    half = D // 2
    block = pl.BlockSpec((half, wide), lambda j: (0, j))
    return pl.pallas_call(
        partial(lexicon_kernel, depth),
        grid=(padded // wide,),
        out_shape=[jax.ShapeDtypeStruct((half, padded), f32)] * 2
        + [jax.ShapeDtypeStruct((1, wide), f32)] * 2,
        in_specs=[
            pl.BlockSpec(memory_space=SMEM),
            full((D, count)),
            pl.BlockSpec((count, wide), lambda j: (0, j)),
        ],
        out_specs=[block, block, full((1, wide)), full((1, wide))],
        scratch_shapes=[pltpu.VMEM((D, count), bf16)],
        name="lexicon",
        cost_estimate=cost(2 * count * D * padded, 3e7),
    )(places, turned, grads)


def three(left, right, product):
    left_high, left_low = left
    right_high, right_low = right
    return (
        product(left_high, right_high)
        + product(left_high, right_low)
        + product(left_low, right_high)
    )


def shampoo_kernel(count, strip, places_ref, clip_ref, *refs):
    pieces, smalls, tails = refs[:count], refs[count : 2 * count], refs[2 * count : 3 * count]
    w_ref, ls_ref, rs_ref, lr_ref, rr_ref = refs[3 * count : 3 * count + 5]
    g_ref, nw_ref, nl_ref, nr_ref, small_ref = refs[3 * count + 5 :]
    clip = clip_ref[0]
    for k in range(count):
        place = pl.multiple_of(places_ref[k], strip)
        scale = jnp.exp2(tails[k][0:1, :] - 15.0) * clip
        for slot in range(2):
            values = pieces[k][pl.ds(slot * strip, strip), :] * scale
            g_ref[slot, pl.ds(place, strip), :] = values

        @pl.when(pl.program_id(0) == 0)
        def _(k=k, place=place, scale=scale):
            for side in range(2):
                values = smalls[k][pl.ds(side * strip, strip), :] * scale
                small_ref[side, pl.ds(place, strip), :] = values

    for slot in range(2):
        grads = split_two(g_ref[slot])
        for old, new, product in ((ls_ref, nl_ref, mm_t), (rs_ref, nr_ref, mm_l)):
            cross = product(grads[0], grads[1])
            outer = product(grads[0], grads[0]) + (cross + cross.T)
            new[slot] = SHAMPOO_BETA * old[slot] + (1.0 - SHAMPOO_BETA) * outer
        turned = split_two(three(grads, split_two(rr_ref[slot]), mm))
        direction = three(split_two(lr_ref[slot]), turned, mm)
        weights = w_ref[slot]
        nw_ref[slot] = weights - RATE_BLOCKS * (direction + DECAY_RATE * weights)


def shampoo(places, clip, pieces, strip, kept):
    slots = kept[0].shape[0]
    count = len(pieces)
    block = pl.BlockSpec((2, BS, BS), lambda s: (s, 0, 0))
    shape = jax.ShapeDtypeStruct((slots, BS, BS), f32)
    small_at, tail_at = slots // 2, (slots + 2) * strip // 16
    return pl.pallas_call(
        partial(shampoo_kernel, count, strip),
        grid=(slots // 2,),
        out_shape=[shape] * 4 + [jax.ShapeDtypeStruct((2, BS, BS), f32)],
        in_specs=[pl.BlockSpec(memory_space=SMEM)] * 2
        + [pl.BlockSpec((2 * strip, BS), lambda s: (s, 0))] * count
        + [pl.BlockSpec((2 * strip, BS), lambda s: (small_at, 0))] * count
        + [pl.BlockSpec((16, BS), lambda s: (tail_at, 0))] * count
        + [block] * 5,
        out_specs=[block] * 4 + [full((2, BS, BS))],
        name="shampoo",
        cost_estimate=cost(slots * 24 * BS**3, slots * BS * BS * 40),
    )(places, clip, *pieces, *pieces, *pieces, *kept)


def adam_update(weight, first, second, gradient, rate, step_value):
    first_new = BETA_FIRST * first + (1.0 - BETA_FIRST) * gradient
    second_new = BETA_SECOND * second + (1.0 - BETA_SECOND) * gradient * gradient
    first_hat = first_new / (1.0 - BETA_FIRST**step_value)
    second_hat = second_new / (1.0 - BETA_SECOND**step_value)
    return (
        weight - rate * (first_hat / (jnp.sqrt(second_hat) + ADAM_EPSILON) + DECAY_RATE * weight),
        first_new,
        second_new,
    )


def tie(values, *others):
    return lax.optimization_barrier((values,) + others)[0]


def exponent(bound):
    return jnp.floor(jnp.log2(jnp.maximum(bound, 1e-30))) + 1.0


def encode(values, bound):
    level = exponent(bound)
    coded = (values * jnp.exp2(15.0 - level)).astype(jnp.float16)
    return coded.reshape(-1, values.shape[-1]), level.astype(jnp.float16)


def pack(values, bound):
    coded, level = encode(values, bound)
    return jnp.concatenate([coded, jnp.broadcast_to(level, (16, coded.shape[1]))], 0)


def unpack(payload, shape):
    count = payload.shape[0] - 16
    wide = payload.astype(f32)
    level = wide[count : count + 1]
    values = wide[:count] * jnp.exp2(level - 15.0)
    return values.reshape(shape), jnp.exp2(payload[-1, 0].astype(f32))


def pack_lanes(values, bound):
    coded, level = encode(values, bound)
    lane = lax.broadcasted_iota(i32, coded.shape, 1)
    return jnp.where(lane == coded.shape[1] - 1, level, coded)


def unpack_lanes(payload):
    level = payload[0, -1].astype(f32)
    return payload.astype(f32) * jnp.exp2(level - 15.0)


def per_device(
    sizes,
    token_ids,
    seq_lengths,
    pick_rows,
    targets,
    step_count,
    block_order,
    slot_weights,
    left_stats,
    right_stats,
    left_roots,
    right_roots,
    embedding,
    embedding_first_moment,
    emb_second,
    vectors,
    vec_first,
    vec_second,
    feature_maps,
    map_first,
    map_second,
):
    ny, nc, n1, n0 = sizes
    n_dp, n_voc = ny * nc, n1 * n0
    dp_index, voc_index = lax.axis_index("dp"), lax.axis_index("vocab")
    y_at, c_at = dp_index // nc, dp_index % nc
    i1, i0 = voc_index // n0, voc_index % n0

    def over_dp(values, dy, dc):
        pairs = [
            (a * nc + b, ((a + dy) % ny) * nc + (b + dc) % nc) for a in range(ny) for b in range(nc)
        ]
        return lax.ppermute(values, "dp", pairs)

    def over_voc(values, d1, d0):
        pairs = [
            (a * n0 + b, ((a + d1) % n1) * n0 + (b + d0) % n0) for a in range(n1) for b in range(n0)
        ]
        return lax.ppermute(values, "vocab", pairs)

    def gather_voc(values):
        near = [values] + [over_voc(values, k, 0) for k in range(1, n1)]
        return [[part] + [over_voc(part, 0, k) for k in range(1, n0)] for part in near]

    def gather_stacked(values):
        near = jnp.stack([values] + [over_voc(values, 0, k) for k in range(1, n0)])
        return jnp.stack([near] + [over_voc(near, k, 0) for k in range(1, n1)])

    def flat_gather(values):
        return [part for line in gather_voc(values) for part in line]

    def gather_y(values):
        return [values] + [over_dp(values, k, 0) for k in range(1, ny)]

    def line_up(parts, at):
        size = len(parts)
        return jnp.take(jnp.stack(parts), (at - jnp.arange(size)) % size, axis=0)

    tokens = token_ids.shape[0]
    picks_own = pick_rows.shape[0]
    devices_all = n_dp * n_voc
    total_picks = picks_own * devices_all
    coefficient = DISTILL_WEIGHT / (tokens * devices_all * HEADS)
    shard_rows, cols_own = embedding.shape
    cols_y = cols_own * nc
    vocab_start = (voc_index * shard_rows).astype(i32)
    per_owner = slot_weights.shape[0]
    block_count = block_order.shape[0]
    table_own = embedding.T
    core = c_at.astype(i32).reshape(1)
    piece_places = jnp.stack(
        [
            (((y_at - ky) % ny) * nc + (c_at + kc) % nc) * cols_own
            for kc in range(nc)
            for ky in range(ny)
        ]
    ).astype(i32)

    low_own = table_own.astype(bf16)
    low_other = over_dp(low_own, 0, 1)
    upright = turn_table(core, low_own, low_other)

    ids_y = gather_y(token_ids)
    numbers = jnp.concatenate(ids_y + [targets])

    slots_y = gather_y(tie(slot_weights.astype(bf16), numbers))
    numbers = gather_stacked(numbers)
    targets_all = numbers[:, :, ny * tokens :].reshape(-1)
    lines = sorted(range(1, n1), key=lambda a: -min(a, n1 - a)) + [0]
    piece_order = [(a, b) for b in list(range(1, n0)) + [0] for a in lines]
    ids_order = [numbers[a, b, : ny * tokens] for a, b in piece_order]
    def near_piece(h, sums, *before):
        part = looked[n1 * (n0 - 1) + h]
        for b in range(1, n0):
            moved = over_voc(tie(looked[(b - 1) * n1 + h], *sums[: max(h - 1, 0)]), 0, -b)
            part = part + tie(moved, *sums, *before)
        return part.reshape(ny, tokens, cols_y)

    looked, hits, bases, by_one = [], [], [], []
    step = n1 // 2
    for first in range(0, n0 * n1, step):
        ids_rows = jnp.concatenate(ids_order[first : first + step])
        local_ids = ids_rows - vocab_start
        packed_ids = jnp.where(
            (local_ids >= 0) & (local_ids < shard_rows),
            (local_ids << 16) | jnp.arange(ids_rows.shape[0], dtype=i32),
            -1,
        )
        bases.append(sum(own.shape[0] for own in hits))
        if first == n0 * n1 - step:
            by_one.append(near_piece(0, by_one))
        hits.append(find_hits(tie(packed_ids, upright, *by_one), shard_rows))
        looked += lookup(hits[-1], upright, ids_rows.shape[0], step)
    hits = jnp.concatenate(hits)
    listed = step * ny * tokens
    early = (n0 - 1) * n1 // step

    for h in range(1, n1 - 1):
        by_one.append(near_piece(h, by_one))
    far_parts = [over_voc(by_one[h], -lines[h], 0) for h in range(n1 - 1)]
    slots_y = [tie(part, by_one[n1 - 2], far_parts[0]) for part in slots_y]
    slots_core = [over_dp(part, 0, 1) for part in slots_y]
    inverse = (
        jnp.zeros((block_count,), i32).at[block_order].set(jnp.arange(block_count, dtype=i32))
    )
    owner = inverse // per_owner
    src = ((c_at - owner % nc) % nc) * ny + (y_at - owner // nc) % ny
    wqkv, wo, wup, wdown = place_blocks(
        src.astype(i32), inverse % per_owner, slots_y + slots_core
    )

    by_one.append(near_piece(n1 - 1, by_one, wup))
    mine = by_one[-1]
    for part in far_parts:
        mine = mine + part

    row_parts = [mine[0]] + [over_dp(mine[k], -k, 0) for k in range(1, ny)]
    if ny == 2:
        first = y_at == 0
        x0 = jnp.concatenate(
            [
                jnp.where(first, row_parts[0], row_parts[1]),
                jnp.where(first, row_parts[1], row_parts[0]),
            ],
            1,
        )
    else:
        stacked = jnp.stack(row_parts)
        x0 = jnp.concatenate(
            [jnp.take(stacked, (j - y_at) % ny, axis=0) for j in range(ny)], axis=1
        )

    low_sent = tie(low_own, x0)
    low_y = [over_dp(low_sent, k, 0) for k in range(1, ny)]

    maps_low = feature_maps.astype(bf16)
    both = jnp.concatenate([maps_low, -maps_low], -1).reshape(2, PAIRS, 2, HD, 2 * HD)
    empty = jnp.zeros_like(both[:, :, 0])
    lift_maps = jnp.stack(
        [
            jnp.concatenate([both[:, :, 0], empty], -2),
            jnp.concatenate([empty, both[:, :, 1]], -2),
        ],
        2,
    ).reshape(2, HEADS, 2 * HD, 2 * HD)
    their_hits = over_dp(hits, 0, 1)
    h1, mixed = qkv_forward(tie(x0, their_hits), wqkv, vectors)
    y, distill = attend(seq_lengths, mixed, lift_maps)
    x1, h2, up, act, x2, picked = mlp_forward(x0, y, wo, wup, wdown, vectors, pick_rows)

    near_picked = [picked] + [over_voc(picked, 0, k) for k in range(1, n0)]
    low_y = [tie(part, *near_picked) for part in low_y]
    low_y_other = [over_dp(part, 0, 1) for part in low_y]
    pieces = [low_own] + low_y + [low_other] + low_y_other
    near_picked = jnp.concatenate(near_picked, 0)
    group = [near_picked] + [over_voc(near_picked, k, 0) for k in range(1, n1)]
    group = jnp.concatenate(group, 0)
    local_targets = targets_all - vocab_start
    logits, stats = vocabulary_logits(piece_places, group, local_targets, pieces)
    stats_all = gather_stacked(stats)
    lined = jnp.stack(
        [
            jnp.roll(stats_all[a, b, :3].reshape(3, n1, n0, picks_own), (a, b), (1, 2))
            for a in range(n1)
            for b in range(n0)
        ]
    ).reshape(n_voc, 3, n_voc * picks_own)
    top_all = jnp.max(lined[:, 0], 0)
    sum_all = jnp.sum(lined[:, 1] * jnp.exp(lined[:, 0] - top_all[None]), 0)
    losses = top_all + jnp.log(sum_all) - jnp.sum(lined[:, 2], 0)
    loss_part = jnp.sum(losses[:picks_own]) / total_picks + coefficient * distill[0, 0]
    shares = jnp.pad(jnp.stack([top_all, 1.0 / sum_all]), ((0, 126), (0, 0)))
    grad_logits, grad_group = vocabulary_back(
        piece_places, logits, shares, local_targets, pieces, 1.0 / total_picks
    )
    grad_group = grad_group.reshape(n1, n0, picks_own, D)
    by_one = []
    for a in list(range(1, n1)) + [0]:
        part = grad_group[a, 0]
        for b in range(1, n0):
            part = part + over_voc(grad_group[a, b], 0, -b)
        by_one.append(part)
    near_parts = [over_voc(by_one[a - 1], -a, 0) for a in range(1, n1)]

    lex_mine, lex_theirs, mine_high, theirs_high = lexicon(
        piece_places, group.T, tie(grad_logits, *by_one[:-1]), cols_own, shard_rows
    )
    lex_arrived = over_dp(lex_theirs, 0, 1)
    their_high = over_dp(theirs_high, 0, 1)
    lex_high = jnp.max(mine_high) + jnp.max(their_high)
    ghp = by_one[-1]
    for part in near_parts:
        ghp = ghp + tie(part, lex_theirs, their_high)

    def lex_lines(k):
        lines = slice(k * cols_own, (k + 1) * cols_own)
        return lex_mine[lines] + lex_arrived[lines]

    lex_sent = [pack_lanes(lex_lines(k), lex_high) for k in range(1, ny)]


    def core_parts(mine_part, their_part, mine_top, their_top, *later):
        arrived = tie(over_dp(their_part, 0, 1), *later)
        bound = jnp.max(mine_top) + jnp.max(over_dp(their_top, 0, 1))
        return coded_parts((mine_part, arrived), bound, 0) + (bound,)

    def coded_parts(parts, bound, axis):
        size = (n0, ny, n1)[axis]

        def lines(part, k):
            count = part.shape[0]
            if axis == 1:
                rows = part.reshape(count, n1, ny, -1, BS)
                rows = lax.dynamic_index_in_dim(rows, (y_at + k) % ny, 2, False)
                return rows.reshape(count, -1, BS)
            rows = part.shape[1] // size
            at = (i0 if axis == 0 else i1) + k
            return lax.dynamic_slice_in_dim(part, (at % size) * rows, rows, 1)

        def summed(k):
            cut = [lines(part, k) for part in parts]
            return sum(cut[1:], cut[0])

        return summed(0), [pack(summed(k), bound) for k in range(1, size)]

    def moved_parts(sent, axis):
        if axis == 1:
            return [over_dp(part, k, 0) for k, part in enumerate(sent, 1)]
        return [
            over_voc(part, k, 0) if axis == 2 else over_voc(part, 0, k)
            for k, part in enumerate(sent, 1)
        ]

    def collect(own, arrived, bound, *later):
        total, high = own, bound
        for part in arrived:
            values, top = unpack(tie(part, *later), own.shape)
            total = total + values
            high = high + top
        return total, high

    *halves_a, gx1, ga, gy, vg_a = mlp_back(
        core, ghp, pick_rows, x2, act, up, h2, x1, wdown, wup, wo, vectors
    )
    own_a, sent_a, bound_a = core_parts(*halves_a, *lex_sent)
    gy = tie(gy, *lex_sent, own_a, *sent_a)
    gqkv, map_q, map_k = attend_back(
        seq_lengths, mixed, gy, lift_maps, coefficient, 0, PAIRS, None
    )
    lex_parts = [over_dp(part, -k, 0) for k, part in enumerate(lex_sent, 1)]
    gx0, vg_b = qkv_back(gqkv, wqkv, x0, gx1, vectors)

    map_grads = jnp.concatenate([map_q, map_k], 0)
    vec_grads = (vg_a + vg_b)[:15]
    small_count = map_grads.size + vec_grads.size
    small = jnp.concatenate(
        [
            map_grads.reshape(-1),
            vec_grads.reshape(-1),
            jnp.zeros((2 * BS * BS - small_count,), f32),
        ]
    ).reshape(2, BS, BS)
    gx0_cols = gx0.reshape(tokens, ny, cols_y)
    cols_sent = [jnp.take(gx0_cols, (y_at + k) % ny, axis=1) for k in range(1, ny)]
    lex = lex_lines(0)
    for part in lex_parts:
        lex = lex + unpack_lanes(part)
    arrived = [jnp.take(gx0_cols, y_at, axis=1)] + [
        tie(over_dp(part, k, 0), lex) for k, part in enumerate(cols_sent, 1)
    ]
    arrived = jnp.concatenate(arrived, 0).reshape(ny * tokens, nc, cols_own)
    rows_mine = jnp.take(arrived, c_at, axis=1)
    moved_a = moved_parts(sent_a, 0)
    rows_sent = jnp.take(arrived, (c_at + 1) % nc, axis=1)
    rows_other = over_dp(rows_sent, 0, 1)
    if cols_own == 192 and n0 == 2 and n1 == 4:
        packed = jnp.concatenate(
            [
                rows_mine[:, :128],
                rows_other[:, :128],
                jnp.concatenate([rows_mine[:, 128:], rows_other[:, 128:]], 1),
            ],
            0,
        )
    else:
        packed = jnp.stack([rows_mine, rows_other])
    halves_b = qkv_weights(core, tie(h1, packed, *moved_a), gqkv, y, ga, small)
    total_a, high_a = collect(own_a, moved_a, bound_a, halves_b[0])
    near_raw = [over_voc(packed, k, 0) for k in range(1, n1)]
    own_b, sent_b, bound_b = core_parts(*halves_b, packed)
    total_b, high_b = collect(own_b, moved_parts(sent_b, 0), bound_b)
    own_a, sent_a = coded_parts((total_a,), high_a, 1)
    own_b, sent_b = coded_parts((total_b,), high_b, 1)
    near_rows = [packed] + [tie(part, *sent_b) for part in near_raw]
    total_a, high_a = collect(own_a, moved_parts(sent_a, 1), high_a, *sent_b)
    total_b, high_b = collect(own_b, moved_parts(sent_b, 1), high_b)
    total = jnp.concatenate([total_a, total_b], 0)
    own, sent = coded_parts((total,), jnp.maximum(high_a, high_b), 2)
    high = jnp.maximum(high_a, high_b)
    own_x = [over_voc(tie(packed, *sent_b, near_rows[-2]), 0, k) for k in range(1, n0)]
    sent = [tie(part, *near_rows) for part in sent]
    far_rows = jnp.stack([tie(part, *own_x) for part in near_rows[1:]])
    far_x = [over_voc(far_rows, 0, k) for k in range(1, n0)]
    moved_ab = moved_parts(sent, 2)

    if cols_own == 192 and n0 == 2 and n1 == 4:
        groups = [(base, listed, (g % early) * listed) for g, base in enumerate(bases)]
        before = scatter_first(
            hits,
            their_hits,
            groups[early:],
            [tie(near_rows[a], *sent) for a in lines],
            shard_rows,
        )
        lex = tie(lex, *before, moved_ab[0])
        emb_grads, emb_square = scatter_last(
            hits, their_hits, groups[:early], before, lex, far_x[0], own_x, shard_rows
        )
        emb_square = emb_square[0, 0]
    else:
        gathered = [[packed] + own_x]
        for a in range(1, n1):
            gathered.append([near_rows[a]] + [part[a - 1] for part in far_x])
        pieces = jnp.stack([gathered[a][b] for a, b in piece_order], 1).reshape(-1, cols_own)
        ids_rows = jnp.concatenate(ids_order)
        local = jnp.concatenate([ids_rows, over_dp(ids_rows, 0, 1)]) - vocab_start
        local = jnp.where((local >= 0) & (local < shard_rows), local, shard_rows)
        emb_grads = lex[:, :shard_rows].T.at[local].add(pieces.astype(f32), mode="drop").T
        emb_square = jnp.sum(emb_grads * emb_grads)

    blocks = collect(own, moved_ab, high, emb_grads)[0]

    square = emb_square + jnp.sum(blocks * blocks)
    sums = jnp.pad(jnp.stack([square, loss_part]).reshape(1, 2), ((0, 7), (0, 126)))
    sums = sums + over_dp(sums, 0, 1)
    sums = jnp.sum(line_up(gather_y(sums), y_at), 0)
    per_side = blocks.shape[0]
    both = jnp.concatenate([blocks, over_dp(blocks, 0, 1)], 0)
    side, place = comm_positions()
    side = jnp.concatenate([jnp.take(jnp.asarray(side), block_order), jnp.arange(2, dtype=i32)])
    place = jnp.concatenate(
        [jnp.take(jnp.asarray(place), block_order), jnp.full((2,), per_side - 1, i32)]
    )
    at_place = ((side - c_at) % nc) * per_side + place
    smalls = at_place[block_count:]
    at_place = at_place[:block_count].reshape(ny, nc, per_owner)

    def slots_of(k):
        mine = jnp.take(jnp.take(at_place, c_at, axis=1), (y_at + k) % ny, axis=0)
        return jnp.take(both, jnp.concatenate([mine, smalls]), axis=0)

    moved = [slots_of(k) for k in range(1, ny)]
    slots_sent = [pack(part, jnp.max(jnp.abs(both))) for part in moved]
    sums = tie(sums, *slots_sent)
    sums = jnp.sum(line_up([sums] + [over_voc(sums, 0, k) for k in range(1, n0)], i0), 0)

    small_own = unpack(slots_sent[0], moved[0].shape)[0][per_owner:]
    strip_parts = [jnp.concatenate([slots_of(0)[:per_owner], small_own], 0)]
    slots_moved = moved_parts(slots_sent, 1)
    sums = tie(sums, *slots_moved)
    for part in slots_moved:
        strip_parts.append(unpack(part, moved[0].shape)[0])
    sums = jnp.sum(line_up([sums] + [over_voc(sums, k, 0) for k in range(1, n1)], i1), 0)
    grad_norm = jnp.sqrt(sums[0, 0])
    loss_total = sums[0, 1]
    clip_scale = CLIP_NORM / jnp.maximum(grad_norm, CLIP_NORM)
    own_strips = line_up(strip_parts, y_at).transpose(1, 0, 2, 3)
    own_strips = own_strips.reshape(per_owner + 2, -1, BS)
    strip_rows = own_strips.shape[1]
    strip_half = BS // n0
    places = [
        ((i0 - b) % n0) * strip_half + ((i1 - a) % n1) * strip_rows
        for a in range(n1)
        for b in range(n0)
    ]
    places = jnp.stack(places).astype(i32)
    strip_sent = tie(pack(own_strips, jnp.max(jnp.abs(own_strips))), sums)
    strip_pieces = [part.astype(f32) for part in flat_gather(strip_sent)]
    clipped, new_slots, new_left, new_right, small_all = shampoo(
        places,
        clip_scale.reshape(1),
        strip_pieces,
        strip_rows,
        (slot_weights, left_stats, right_stats, left_roots, right_roots),
    )
    clip_late = tie(clip_scale, strip_sent)
    small_all = small_all.reshape(-1)
    map_grad = small_all[: map_grads.size].reshape(feature_maps.shape)
    vec_grad = small_all[map_grads.size : small_count].reshape(vectors.shape)

    step_value = step_count[0].astype(f32)
    emb_out = adam_update(
        table_own,
        embedding_first_moment.T,
        emb_second.T,
        emb_grads * clip_late,
        RATE_TABLE,
        step_value,
    )
    vec_out = adam_update(
        vectors, vec_first, vec_second, vec_grad, RATE_VECTORS, step_value
    )
    map_out = adam_update(
        feature_maps, map_first, map_second, map_grad, RATE_MAPS, step_value
    )
    return (
        loss_total,
        grad_norm,
        clipped,
        new_slots,
        new_left,
        new_right,
        emb_out[0].T,
        emb_out[1].T,
        emb_out[2].T,
        vec_out[0],
        vec_out[1],
        vec_out[2],
        map_out[0],
        map_out[1],
        map_out[2],
    )


def solution(mesh):
    n_dp, n_voc = mesh.shape["dp"], mesh.shape["vocab"]
    sizes = (n_dp // 2, 2, 4, n_voc // 4)
    rows = P(("dp", "vocab"))
    blocks = P("dp", None, None)
    table = P("vocab", "dp")
    placed = (
        (rows, P(("dp", "vocab"), None), rows, rows, P(), P())
        + (blocks,) * 5
        + (table,) * 3
        + (P(),) * 6
    )
    return jax.shard_map(
        partial(per_device, sizes),
        mesh=mesh,
        in_specs=placed,
        out_specs=(P(), P()) + (blocks,) * 4 + (table,) * 3 + (P(),) * 6,
        check_vma=False,
    )
```

```python
from functools import partial

import jax
import jax.numpy as jnp
import numpy as np
from jax import lax
from jax.experimental import pallas as pl
from jax.experimental.pallas import tpu as pltpu
from jax.sharding import PartitionSpec as P

D = 768
HEADS = 12
HD = 64
FF = 3072
BS = 384
PAIRS = HEADS // 2

NORM_EPSILON = 1e-05
CLIP_NORM = 0.01
DISTILL_WEIGHT = 0.5
BETA_FIRST = 0.9
BETA_SECOND = 0.95
ADAM_EPSILON = 1e-08
DECAY_RATE = 0.01
SHAMPOO_BETA = 0.95
RATE_BLOCKS = 0.1
RATE_TABLE = 0.05
RATE_VECTORS = 0.2
RATE_MAPS = 0.1

f32 = jnp.float32
bf16 = jnp.bfloat16
i32 = jnp.int32
SMEM = pltpu.SMEM
ANY = pl.ANY


def mm(left, right):
    return lax.dot_general(left, right, (((1,), (0,)), ((), ())), preferred_element_type=f32)


def mm_t(left, right):
    return lax.dot_general(left, right, (((1,), (1,)), ((), ())), preferred_element_type=f32)


def mm_l(left, right):
    return lax.dot_general(left, right, (((0,), (0,)), ((), ())), preferred_element_type=f32)


def split_two(values):
    high = values.astype(bf16)
    return high, (values - high.astype(f32)).astype(bf16)


def full(shape):
    return pl.BlockSpec(shape, lambda *_: (0,) * len(shape))


def cost(flops, bytes_moved, transcendentals=0):
    return pl.CostEstimate(
        flops=int(flops * 0.02),
        bytes_accessed=int(bytes_moved * 0.02),
        transcendentals=int(transcendentals * 0.02),
    )


def place_kernel(piece_count, src_ref, off_ref, *refs):
    pieces = refs[:piece_count]
    outs = refs[piece_count : piece_count + 4]
    sems = refs[piece_count + 4]
    base = 0
    for out, rows, cols in zip(outs, (D, D, D, FF), (3 * D, D, FF, D)):
        wide = cols // BS
        count = (rows // BS) * wide

        def go(t, carry, out=out, wide=wide, base=base):
            k = base + t
            r0 = pl.multiple_of((t // wide) * BS, BS)
            c0 = pl.multiple_of((t % wide) * BS, BS)
            for p in range(piece_count):

                @pl.when(src_ref[k] == p)
                def _(p=p):
                    pltpu.make_async_copy(
                        pieces[p].at[off_ref[k]],
                        out.at[pl.ds(r0, BS), pl.ds(c0, BS)],
                        sems.at[k],
                    ).start()

            return carry

        lax.fori_loop(0, count, go, 0)
        base += count
    base = 0
    for out, rows, cols in zip(outs, (D, D, D, FF), (3 * D, D, FF, D)):
        count = (rows // BS) * (cols // BS)

        def done(t, carry, out=out, base=base):
            pltpu.make_async_copy(
                pieces[0].at[0], out.at[pl.ds(0, BS), pl.ds(0, BS)], sems.at[base + t]
            ).wait()
            return carry

        lax.fori_loop(0, count, done, 0)
        base += count


def place_blocks(src, off, pieces):
    count = len(pieces)
    return pl.pallas_call(
        partial(place_kernel, count),
        out_shape=[
            jax.ShapeDtypeStruct(shape, bf16)
            for shape in ((D, 3 * D), (D, D), (D, FF), (FF, D))
        ],
        in_specs=[pl.BlockSpec(memory_space=SMEM)] * 2 + [pl.BlockSpec(memory_space=ANY)] * count,
        out_specs=[pl.BlockSpec(memory_space=pltpu.VMEM)] * 4,
        scratch_shapes=[pltpu.SemaphoreType.DMA((48,))],
        name="place_blocks",
        cost_estimate=cost(0, 2 * 48 * BS * BS * 2),
    )(src, off, *pieces)


def hits_kernel(empty_row, packed_ref, list_ref):
    total = packed_ref.shape[0]

    def go(i, n):
        for u in range(16):
            entry = packed_ref[i * 16 + u]
            list_ref[n] = entry
            n = n + 1 + (entry >> 31)
        return n

    n = lax.fori_loop(0, total // 16, go, jnp.int32(0))
    list_ref[total + 8] = n
    for u in range(8):
        list_ref[n + u] = empty_row << 16


def find_hits(packed, empty_row):
    total = packed.shape[0]
    return pl.pallas_call(
        partial(hits_kernel, empty_row),
        out_shape=jax.ShapeDtypeStruct((total + 16,), i32),
        in_specs=[pl.BlockSpec(memory_space=SMEM)],
        out_specs=pl.BlockSpec(memory_space=SMEM),
        name="find_hits",
        cost_estimate=cost(1e10, total * 8),
    )(packed)


def turn_kernel(core_ref, own_ref, other_ref, out_ref):
    first = core_ref[0] == 0
    own, other = own_ref[...].astype(f32), other_ref[...].astype(f32)
    depth = own.shape[0]
    both = jnp.concatenate([jnp.where(first, own, other), jnp.where(first, other, own)], 0)
    out_ref[...] = both.T


def turn_table(core, own, other):
    depth, rows_all = own.shape
    wide = lane_block(rows_all)
    block = pl.BlockSpec((depth, wide), lambda j: (0, j))
    return pl.pallas_call(
        turn_kernel,
        grid=(pl.cdiv(rows_all, wide),),
        out_shape=jax.ShapeDtypeStruct((rows_all, 2 * depth), f32),
        in_specs=[pl.BlockSpec(memory_space=SMEM), block, block],
        out_specs=pl.BlockSpec((wide, 2 * depth), lambda j: (j, 0)),
        name="turn_table",
        cost_estimate=cost(1e7, 1e7),
    )(core, own, other)


def in_chunks(count, size, body):
    def go(i, carry):
        body(pl.multiple_of(i * size, size))
        return carry

    lax.fori_loop(0, count // size, go, 0)


def lookup_kernel(rows_all, list_ref, table_ref, *refs):
    outs, acc = refs[:-1], refs[-1]
    total = acc.shape[0] - 8
    chunk = 128

    def clear(start):
        acc[pl.ds(start, chunk), :] = jnp.zeros((chunk, acc.shape[1]), f32)

    in_chunks(total, chunk, clear)

    def go(i, carry):
        for u in range(8):
            entry = list_ref[i * 8 + u]
            row = entry >> 16
            place = jnp.where(row < rows_all, entry & 0xFFFF, total)
            row = jnp.minimum(row, rows_all - 1)
            acc[pl.ds(place, 1), :] = table_ref[pl.ds(row, 1), :]
        return carry

    lax.fori_loop(0, (list_ref[total + 8] + 7) // 8, go, 0)
    each = outs[0].shape[0]
    for part, out in enumerate(outs):

        def keep(start, part=part, out=out):
            out[pl.ds(start, chunk), :] = acc[pl.ds(part * each + start, chunk), :].astype(bf16)

        in_chunks(each, chunk, keep)


def lookup(hit_list, table, count, parts):
    rows_all, width = table.shape
    return pl.pallas_call(
        partial(lookup_kernel, rows_all),
        out_shape=[jax.ShapeDtypeStruct((count // parts, width), bf16)] * parts,
        in_specs=[
            pl.BlockSpec(memory_space=SMEM),
            pl.BlockSpec(memory_space=pltpu.VMEM),
        ],
        out_specs=[pl.BlockSpec(memory_space=pltpu.VMEM)] * parts,
        scratch_shapes=[pltpu.VMEM((count + 8, width), f32)],
        name="lookup",
        cost_estimate=cost(1e10, rows_all * width * 2),
    )(hit_list, table)


def add_rows(own_ref, their_ref, groups, pieces, acc, tail, wide, pair):
    half = pieces[0].shape[0] // 3
    chunk = 128
    for k, piece in enumerate(pieces):

        def widen(start, k=k, piece=piece):
            values = piece[pl.ds(start, chunk), :].astype(f32)
            wide[pl.ds(k * 2 * half + start, chunk), :] = values

        def widen_pair(start, k=k, piece=piece):
            values = piece[pl.ds(2 * half + start, chunk), :].astype(f32)
            pair[pl.ds(k * half + start, chunk), :] = values

        in_chunks(2 * half, chunk, widen)
        in_chunks(half, chunk, widen_pair)
    upper = lax.broadcasted_iota(i32, (1, 128), 1) >= 64
    for base, total, start in groups:
        for side, list_ref in enumerate((own_ref, their_ref)):
            own = upper if side else ~upper

            def go(i, carry, base=base, start=start, side=side, list_ref=list_ref, own=own):
                for u in range(8):
                    entry = list_ref[base + i * 8 + u]
                    row = entry >> 16
                    p = (entry & 0xFFFF) + start
                    q = (p // half) * half + p + side * half
                    acc[pl.ds(row, 1), :] += wide[pl.ds(q, 1), :]
                    tail[pl.ds(row, 1), :] += jnp.where(own, pair[pl.ds(p, 1), :], 0.0)
                return carry

            lax.fori_loop(0, (list_ref[base + total + 8] + 7) // 8, go, 0)


def scatter_first_kernel(count, groups, own_ref, their_ref, *refs):
    pieces = refs[:count]
    acc, tail, wide, pair = refs[count:]

    def clear(start):
        acc[pl.ds(start, 128), :] = jnp.zeros((128, 128), f32)
        tail[pl.ds(start, 128), :] = jnp.zeros((128, 128), f32)

    in_chunks(acc.shape[0], 128, clear)
    add_rows(own_ref, their_ref, groups, pieces, acc, tail, wide, pair)


def scatter_last_kernel(
    count, groups, rows_all, own_ref, their_ref, first_acc, first_tail, lex_ref, stack_ref, *refs
):
    pieces = [stack_ref.at[k] for k in range(stack_ref.shape[0])] + list(refs[:count])
    pieces = [pieces[k] for k in (1, 0, 2, 3)]
    out_ref, square_ref, acc, tail, wide, pair = refs[count:]

    def carry_over(start):
        acc[pl.ds(start, 128), :] = first_acc[pl.ds(start, 128), :]
        tail[pl.ds(start, 128), :] = first_tail[pl.ds(start, 128), :]

    in_chunks(acc.shape[0], 128, carry_over)
    add_rows(own_ref, their_ref, groups, pieces, acc, tail, wide, pair)
    chunks = rows_all // 128
    rest = rows_all - chunks * 128

    def turn(start, width):
        upright = acc[pl.ds(start, 128), :].T
        lower = tail[pl.ds(start, 128), :].T
        lower = lower[:64] + lower[64:]
        lanes = pl.ds(start, width)
        left = lex_ref[pl.ds(0, 128), lanes] + upright[:, :width]
        right = lex_ref[pl.ds(128, 64), lanes] + lower[:, :width]
        out_ref[pl.ds(0, 128), lanes] = left
        out_ref[pl.ds(128, 64), lanes] = right
        return jnp.sum(left * left, 0, keepdims=True), jnp.sum(right * right, 0, keepdims=True)

    def step(i, carry):
        left, right = turn(pl.multiple_of(i * 128, 128), 128)
        return carry + left + right

    squares = lax.fori_loop(0, chunks, step, jnp.zeros((1, 128), f32))
    total = jnp.sum(squares)
    if rest:
        left, right = turn(chunks * 128, rest)
        total = total + jnp.sum(left) + jnp.sum(right)
    square_ref[0, 0] = total


def scatter_first(own_list, their_list, groups, pieces, rows_all):
    half = pieces[0].shape[0] // 3
    count = len(pieces)
    padded = (rows_all // 128 + 1) * 128
    return pl.pallas_call(
        partial(scatter_first_kernel, count, groups),
        out_shape=[jax.ShapeDtypeStruct((padded, 128), f32)] * 2,
        in_specs=[pl.BlockSpec(memory_space=SMEM)] * 2
        + [pl.BlockSpec(memory_space=pltpu.VMEM)] * count,
        out_specs=[pl.BlockSpec(memory_space=pltpu.VMEM)] * 2,
        scratch_shapes=[
            pltpu.VMEM((count * 2 * half, 128), f32),
            pltpu.VMEM((count * half, 128), f32),
        ],
        name="scatter_first",
        cost_estimate=cost(1e10, rows_all * 128 * 8),
    )(own_list, their_list, *pieces)


def scatter_last(own_list, their_list, groups, before, lex, stacked, pieces, rows_all):
    width = lex.shape[0]
    half = stacked.shape[1] // 3
    count = len(pieces)
    used = count + stacked.shape[0]
    padded = (rows_all // 128 + 1) * 128
    return pl.pallas_call(
        partial(scatter_last_kernel, count, groups, rows_all),
        out_shape=[
            jax.ShapeDtypeStruct((width, rows_all), f32),
            jax.ShapeDtypeStruct((1, 1), f32),
        ],
        in_specs=[pl.BlockSpec(memory_space=SMEM)] * 2
        + [pl.BlockSpec(memory_space=pltpu.VMEM)] * (count + 4),
        out_specs=[
            pl.BlockSpec(memory_space=pltpu.VMEM),
            pl.BlockSpec(memory_space=SMEM),
        ],
        scratch_shapes=[
            pltpu.VMEM((padded, 128), f32),
            pltpu.VMEM((padded, 128), f32),
            pltpu.VMEM((used * 2 * half, 128), f32),
            pltpu.VMEM((used * half, 128), f32),
        ],
        name="scatter_last",
        cost_estimate=cost(1e10, rows_all * width * 8),
    )(own_list, their_list, *before, lex, stacked, *pieces)


def norm_parts(inputs):
    centered = inputs - jnp.mean(inputs, -1, keepdims=True)
    scale = lax.rsqrt(jnp.mean(centered * centered, -1, keepdims=True) + NORM_EPSILON)
    return centered, scale


def norm_pull(inputs, gain_row, grads):
    centered, scale = norm_parts(inputs)
    unit = centered * scale
    pulled = grads * gain_row
    lead = jnp.mean(pulled, -1, keepdims=True)
    along = jnp.mean(pulled * unit, -1, keepdims=True)
    grad_in = scale * (pulled - lead - unit * along)
    return (
        grad_in,
        jnp.sum(grads * unit, 0, keepdims=True),
        jnp.sum(grads, 0, keepdims=True),
    )


def qkv_kernel(x_ref, w_ref, vec_ref, h_ref, mixed_ref):
    j = pl.program_id(0)

    @pl.when(j == 0)
    def _():
        centered, scale = norm_parts(x_ref[...].astype(f32))
        h_ref[...] = (centered * scale * vec_ref[0:1, :] + vec_ref[1:2, :]).astype(bf16)

    mixed_ref[...] = (mm(h_ref[...], w_ref[...]) + vec_ref[pl.ds(8 + j, 1), :]).astype(bf16)


def qkv_forward(x0, wqkv, vectors):
    tokens = x0.shape[0]
    return pl.pallas_call(
        qkv_kernel,
        grid=(3,),
        out_shape=[
            jax.ShapeDtypeStruct((tokens, D), bf16),
            jax.ShapeDtypeStruct((tokens, 3 * D), bf16),
        ],
        in_specs=[
            full((tokens, D)),
            pl.BlockSpec((D, D), lambda j: (0, j)),
            full(vectors.shape),
        ],
        out_specs=[full((tokens, D)), pl.BlockSpec((tokens, D), lambda j: (0, j))],
        name="qkv_forward",
        cost_estimate=cost(2 * tokens * D * 3 * D, 8e6),
    )(x0, wqkv, vectors)


def feature_parts(values, lift, low_half):
    raw = mm(values, lift)
    top_a = jnp.max(jnp.where(low_half, raw, -jnp.inf), -1, keepdims=True)
    top_b = jnp.max(jnp.where(low_half, -jnp.inf, raw), -1, keepdims=True)
    grown = jnp.exp(raw - jnp.where(low_half, top_a, top_b))
    sum_a = jnp.sum(jnp.where(low_half, grown, 0.0), -1, keepdims=True)
    sum_b = jnp.sum(jnp.where(low_half, 0.0, grown), -1, keepdims=True)
    return grown / jnp.where(low_half, sum_a, sum_b)


def feature_pull(soft, grads, low_half):
    weighed = soft * grads
    sum_a = jnp.sum(jnp.where(low_half, weighed, 0.0), -1, keepdims=True)
    sum_b = jnp.sum(jnp.where(low_half, 0.0, weighed), -1, keepdims=True)
    pulled = soft * (grads - jnp.where(low_half, sum_a, sum_b))
    return (pulled - pltpu.roll(pulled, HD, 1)).astype(bf16)


def fill_allowed(len_ref, allow_ref):
    tokens = allow_ref.shape[0]
    first = len_ref[0, 0]
    second = first + len_ref[0, 1]
    third = second + len_ref[0, 2]

    def document(places):
        return (
            (places >= first).astype(i32)
            + (places >= second).astype(i32)
            + (places >= third).astype(i32)
        )

    rows = lax.broadcasted_iota(i32, (tokens, tokens), 0)
    cols = lax.broadcasted_iota(i32, (tokens, tokens), 1)
    allow_ref[...] = ((cols <= rows) & (document(rows) == document(cols))).astype(f32)


ROWS = 128


def attend_kernel(
    len_ref, q_ref, k_ref, v_ref, fq_ref, fk_ref, y_ref, distill_ref, allow_ref, lift_q, lift_k
):
    tokens = q_ref.shape[0]

    @pl.when(pl.program_id(0) == 0)
    def _():
        fill_allowed(len_ref, allow_ref)
        distill_ref[...] = jnp.zeros_like(distill_ref)

    low_half = lax.broadcasted_iota(i32, (1, 2 * HD), 1) < HD
    low_rows = lax.broadcasted_iota(i32, (ROWS, 2 * HD), 1) < HD
    total = jnp.zeros((1, 1), f32)
    for h in range(2):
        lift_q[h] = feature_parts(q_ref[...], fq_ref[h], low_half).astype(bf16)
        lift_k[h] = feature_parts(k_ref[...], fk_ref[h], low_half).astype(bf16)
    for begin in range(0, tokens, ROWS):
        width = begin + ROWS
        ok = allow_ref[pl.ds(begin, ROWS), pl.ds(0, width)] > 0.5
        queries = q_ref[pl.ds(begin, ROWS), :] * jnp.asarray(HD**-0.5, bf16)
        keys = k_ref[pl.ds(0, width), :]
        values = v_ref[pl.ds(0, width), :]
        parts = []
        for h in range(2):
            own = low_rows if h == 0 else ~low_rows
            scores = mm_t(jnp.where(own, queries, jnp.zeros_like(queries)), keys)
            scores = jnp.where(ok, scores, -1e30)
            grown = jnp.exp(scores - jnp.max(scores, -1, keepdims=True))
            inverse = 1.0 / jnp.sum(grown, -1, keepdims=True)
            similar = mm_t(lift_q[h, pl.ds(begin, ROWS), :], lift_k[h, pl.ds(0, width), :])
            kept = jnp.where(ok, similar, 0.0)
            sums = jnp.sum(kept, -1, keepdims=True)
            weights = (kept * (1.0 / sums)).astype(bf16)
            parts.append(mm(weights, values))
            logs = jnp.log(jnp.where(ok, similar, 1.0))
            row_terms = jnp.log(sums) - jnp.sum(grown * logs, -1, keepdims=True) * inverse
            total = total + jnp.sum(row_terms, 0, keepdims=True)
        y_ref[pl.ds(begin, ROWS), :] = jnp.where(low_rows, parts[0], parts[1]).astype(bf16)
    distill_ref[...] += jnp.broadcast_to(total, distill_ref.shape)


def attend(lengths, mixed, lift_maps):
    tokens = mixed.shape[0]
    column = lambda base: pl.BlockSpec((tokens, 2 * HD), lambda g: (0, base + g))
    maps = pl.BlockSpec((2, 2 * HD, 2 * HD), lambda g: (g, 0, 0))
    return pl.pallas_call(
        attend_kernel,
        grid=(PAIRS,),
        out_shape=[
            jax.ShapeDtypeStruct((tokens, D), bf16),
            jax.ShapeDtypeStruct((8, 128), f32),
        ],
        in_specs=[
            pl.BlockSpec(memory_space=SMEM),
            column(0),
            column(PAIRS),
            column(2 * PAIRS),
            maps,
            maps,
        ],
        out_specs=[column(0), full((8, 128))],
        scratch_shapes=[
            pltpu.VMEM((tokens, tokens), f32),
            pltpu.VMEM((2, tokens, 2 * HD), bf16),
            pltpu.VMEM((2, tokens, 2 * HD), bf16),
        ],
        name="attend",
        cost_estimate=cost(1.2e10, 4e6, 6e6),
    )(lengths, mixed, mixed, mixed, lift_maps[0], lift_maps[1])


def attend_back_kernel(
    coefficient,
    later,
    len_ref,
    q_ref,
    k_ref,
    v_ref,
    gy_ref,
    fq_ref,
    fk_ref,
    *refs,
):
    g_ref, gq_map_ref, gk_map_ref, allow_ref, soft_q, soft_k, grad_q, grad_k, grad_v = refs[later:]
    tokens = q_ref.shape[0]

    @pl.when(pl.program_id(0) == 0)
    def _():
        fill_allowed(len_ref, allow_ref)

    low_half = lax.broadcasted_iota(i32, (1, 2 * HD), 1) < HD
    low_rows = lax.broadcasted_iota(i32, (ROWS, 2 * HD), 1) < HD
    for h in range(2):
        soft_q[h] = feature_parts(q_ref[...], fq_ref[h], low_half)
        soft_k[h] = feature_parts(k_ref[...], fk_ref[h], low_half)
    for step, begin in enumerate(reversed(range(0, tokens, ROWS))):
        width = begin + ROWS
        ok = allow_ref[pl.ds(begin, ROWS), pl.ds(0, width)] > 0.5
        queries = q_ref[pl.ds(begin, ROWS), :] * jnp.asarray(HD**-0.5, bf16)
        keys = k_ref[pl.ds(0, width), :]
        values = v_ref[pl.ds(0, width), :]
        grads = gy_ref[pl.ds(begin, ROWS), :]
        value_sum = None
        for h in range(2):
            own = low_rows if h == 0 else ~low_rows
            scores = mm_t(jnp.where(own, queries, jnp.zeros_like(queries)), keys)
            scores = jnp.where(ok, scores, -1e30)
            grown = jnp.exp(scores - jnp.max(scores, -1, keepdims=True))
            teach = grown * (coefficient / jnp.sum(grown, -1, keepdims=True))
            phi_q = soft_q[h, pl.ds(begin, ROWS), :].astype(bf16)
            phi_k = soft_k[h, pl.ds(0, width), :].astype(bf16)
            similar = mm_t(phi_q, phi_k)
            kept = jnp.where(ok, similar, 0.0)
            inverse = 1.0 / jnp.sum(kept, -1, keepdims=True)
            weights = kept * inverse
            own_grads = jnp.where(own, grads, jnp.zeros_like(grads))
            grad_w = mm_t(own_grads, values)
            row_sum = jnp.sum(grad_w * weights, -1, keepdims=True)
            grad_sums = (coefficient - row_sum) * inverse
            grad_sim = jnp.where(
                ok,
                grad_w * inverse - teach / jnp.where(ok, similar, 1.0) + grad_sums,
                0.0,
            ).astype(bf16)
            grad_q[h, pl.ds(begin, ROWS), :] = mm(grad_sim, phi_k)
            part_k = mm_l(grad_sim, phi_q)
            part_v = mm_l(weights.astype(bf16), own_grads)
            value_sum = part_v if value_sum is None else value_sum + part_v
            if step == 0:
                grad_k[h] = part_k
            else:
                grad_k[h, pl.ds(0, width), :] += part_k
        if step == 0:
            grad_v[...] = value_sum
        else:
            grad_v[pl.ds(0, width), :] += value_sum
    for slot, own_ref, map_ref, soft, grad, out in (
        (0, q_ref, fq_ref, soft_q, grad_q, gq_map_ref),
        (1, k_ref, fk_ref, soft_k, grad_k, gk_map_ref),
    ):
        result = None
        for h in range(2):
            pulled = feature_pull(soft[h], grad[h], low_half)
            back = mm_t(pulled, map_ref[h]) * 0.5
            result = back if result is None else result + back
            out[h] = mm_l(own_ref[...], pulled)[h * HD : (h + 1) * HD, :HD]
        g_ref[slot] = result.astype(bf16)
    g_ref[2] = grad_v[...].astype(bf16)


def attend_back(lengths, mixed, grad_y, lift_maps, coefficient, start, pairs, before):
    tokens = mixed.shape[0]
    column = lambda base: pl.BlockSpec((tokens, 2 * HD), lambda g: (0, base + start + g))
    maps = pl.BlockSpec((2, 2 * HD, 2 * HD), lambda g: (start + g, 0, 0))
    small = pl.BlockSpec((2, HD, HD), lambda g: (g, 0, 0))
    wide = (2, tokens, 2 * HD)
    later = before is not None
    return pl.pallas_call(
        partial(attend_back_kernel, coefficient, int(later)),
        grid=(pairs,),
        out_shape=[
            jax.ShapeDtypeStruct((3, tokens, D), bf16),
            jax.ShapeDtypeStruct((2 * pairs, HD, HD), f32),
            jax.ShapeDtypeStruct((2 * pairs, HD, HD), f32),
        ],
        in_specs=[
            pl.BlockSpec(memory_space=SMEM),
            column(0),
            column(PAIRS),
            column(2 * PAIRS),
            column(0),
            maps,
            maps,
        ]
        + [pl.BlockSpec(memory_space=ANY)] * later,
        out_specs=[
            pl.BlockSpec((3, tokens, 2 * HD), lambda g: (0, 0, start + g)),
            small,
            small,
        ],
        scratch_shapes=[
            pltpu.VMEM((tokens, tokens), f32),
            pltpu.VMEM(wide, f32),
            pltpu.VMEM(wide, f32),
            pltpu.VMEM(wide, f32),
            pltpu.VMEM(wide, f32),
            pltpu.VMEM((tokens, 2 * HD), f32),
        ],
        input_output_aliases={7: 0} if later else {},
        name="attend_back",
        cost_estimate=cost(1.2e10, 4e6, 3e6),
    )(lengths, mixed, mixed, mixed, grad_y, lift_maps[0], lift_maps[1], *([before] * later))


FSTEPS = FF // D


def mlp_kernel(
    x_ref,
    y_ref,
    wo_ref,
    wup_ref,
    wdown_ref,
    vec_ref,
    pick_ref,
    x1_ref,
    h_ref,
    up_ref,
    act_ref,
    x2_ref,
    hp_ref,
):
    j = pl.program_id(0)

    @pl.when(j == 0)
    def _():
        x1 = x_ref[...].astype(f32) + mm(y_ref[...], wo_ref[...]) + vec_ref[6:7, :]
        x1_ref[...] = x1
        centered, scale = norm_parts(x1)
        h_ref[...] = (centered * scale * vec_ref[2:3, :] + vec_ref[3:4, :]).astype(bf16)
        x2_ref[...] = x1 + vec_ref[7:8, :]

    up = mm(h_ref[...], wup_ref[...]) + vec_ref[pl.ds(11 + j, 1), :]
    up_ref[...] = up
    act = (0.5 * up * (1.0 + jnp.tanh(0.7978845608 * (up + 0.044715 * up * up * up)))).astype(bf16)
    act_ref[...] = act
    x2_ref[...] += mm(act, wdown_ref[...])

    @pl.when(j == FSTEPS - 1)
    def _():
        centered, scale = norm_parts(x2_ref[...])
        last = (centered * scale * vec_ref[4:5, :] + vec_ref[5:6, :]).astype(bf16)
        tokens = last.shape[0]
        places = lax.broadcasted_iota(i32, (pick_ref.shape[0], tokens), 1)
        chosen = (places == pick_ref[...]).astype(bf16)
        hp_ref[...] = mm(chosen, last).astype(bf16)


def mlp_forward(x0, y, wo, wup, wdown, vectors, picks):
    tokens = x0.shape[0]
    count = picks.shape[0]
    wide = pl.BlockSpec((tokens, D), lambda j: (0, j))
    shape = lambda cols, kind: jax.ShapeDtypeStruct((tokens, cols), kind)
    return pl.pallas_call(
        mlp_kernel,
        grid=(FSTEPS,),
        out_shape=[
            shape(D, f32),
            shape(D, bf16),
            shape(FF, f32),
            shape(FF, bf16),
            shape(D, f32),
            jax.ShapeDtypeStruct((count, D), bf16),
        ],
        in_specs=[
            full((tokens, D)),
            full((tokens, D)),
            full((D, D)),
            pl.BlockSpec((D, D), lambda j: (0, j)),
            pl.BlockSpec((D, D), lambda j: (j, 0)),
            full(vectors.shape),
            full((count, 1)),
        ],
        out_specs=[
            full((tokens, D)),
            full((tokens, D)),
            wide,
            wide,
            full((tokens, D)),
            full((count, D)),
        ],
        name="mlp_forward",
        cost_estimate=cost(2 * tokens * D * (2 * FF + D), 3e7, tokens * FF),
    )(x0, y, wo, wup, wdown, vectors, picks.reshape(count, 1))


def keep_tiles(values, out, top, slot):
    for c in range(2):
        out[slot + c] = values[:, c * BS : (c + 1) * BS]
    high = jnp.max(jnp.abs(values), 0, keepdims=True)
    top[...] = jnp.maximum(top[...], jnp.maximum(high[:, :BS], high[:, BS:]))


def near_far(core):
    return pl.ds(pl.multiple_of(core * BS, BS), BS), pl.ds(pl.multiple_of((1 - core) * BS, BS), BS)


def mlp_back_kernel(
    core_ref,
    ghp_ref,
    pick_ref,
    x2_ref,
    act_ref,
    up_ref,
    h_ref,
    x1_ref,
    wdown_ref,
    wup_ref,
    wo_ref,
    vec_ref,
    mine_ref,
    theirs_ref,
    mine_top_ref,
    theirs_top_ref,
    gx1_ref,
    ga_ref,
    gy_ref,
    vg_ref,
    gx2,
    gm,
    gh,
):
    j = pl.program_id(0)
    core = core_ref[0]
    tokens = x2_ref.shape[0]

    @pl.when(j == 0)
    def _():
        mine_top_ref[...] = jnp.zeros_like(mine_top_ref)
        theirs_top_ref[...] = jnp.zeros_like(theirs_top_ref)
        vg_ref[...] = jnp.zeros_like(vg_ref)
        places = lax.broadcasted_iota(i32, (tokens, pick_ref.shape[1]), 0)
        chosen = (places == pick_ref[...]).astype(bf16)
        rest = ghp_ref[...]
        spread = jnp.zeros((tokens, D), f32)
        for _ in range(3):
            part = rest.astype(bf16)
            rest = rest - part.astype(f32)
            spread = spread + mm(chosen, part)
        grad, gain, bias = norm_pull(x2_ref[...], vec_ref[4:5, :], spread)
        gx2[...] = grad
        low = grad.astype(bf16)
        gm[...] = low
        vg_ref[4:5, :] = gain
        vg_ref[5:6, :] = bias
        vg_ref[7:8, :] = jnp.sum(low.astype(f32), 0, keepdims=True)

    grad_act = mm_t(gm[...], wdown_ref[...])
    up = up_ref[...]
    turn = jnp.tanh(0.7978845608 * (up + 0.044715 * up * up * up))
    slope = 0.5 * (1.0 + turn) + 0.5 * up * (1.0 - turn * turn) * (
        0.7978845608 * (1.0 + 3.0 * 0.044715 * up * up)
    )
    gup = (grad_act * slope).astype(bf16)
    vg_ref[pl.ds(11 + j, 1), :] = jnp.sum(gup.astype(f32), 0, keepdims=True)
    part = mm_t(gup, wup_ref[...])

    @pl.when(j == 0)
    def _():
        gh[...] = part

    @pl.when(j > 0)
    def _():
        gh[...] += part

    for cols, out, top in zip(
        near_far(core), (mine_ref, theirs_ref), (mine_top_ref, theirs_top_ref)
    ):
        keep_tiles(mm_l(h_ref[:, cols], gup), out, top, 0)
        keep_tiles(mm_l(act_ref[:, cols], gm[...]), out, top, 2)

    @pl.when(j == FSTEPS - 1)
    def _():
        grad, gain, bias = norm_pull(x1_ref[...], vec_ref[2:3, :], gh[...])
        vg_ref[2:3, :] = gain
        vg_ref[3:4, :] = bias
        grad = grad + gx2[...]
        gx1_ref[...] = grad
        low = grad.astype(bf16)
        ga_ref[...] = low
        vg_ref[6:7, :] = jnp.sum(low.astype(f32), 0, keepdims=True)
        gy_ref[...] = mm_t(low, wo_ref[...]).astype(bf16)


def mlp_back(core, ghp, picks, x2, act, up, h2, x1, wdown, wup, wo, vectors):
    tokens = x2.shape[0]
    count = picks.shape[0]
    wide = pl.BlockSpec((tokens, D), lambda j: (0, j))
    flat = full((tokens, D))
    tiles = pl.BlockSpec((4, BS, BS), lambda j: (j, 0, 0))
    tops = full((1, BS))
    halves = jax.ShapeDtypeStruct((4 * FSTEPS, BS, BS), f32)
    highs = jax.ShapeDtypeStruct((1, BS), f32)
    return pl.pallas_call(
        mlp_back_kernel,
        grid=(FSTEPS,),
        out_shape=[
            halves,
            halves,
            highs,
            highs,
            jax.ShapeDtypeStruct((tokens, D), f32),
            jax.ShapeDtypeStruct((tokens, D), bf16),
            jax.ShapeDtypeStruct((tokens, D), bf16),
            jax.ShapeDtypeStruct((16, D), f32),
        ],
        in_specs=[
            pl.BlockSpec(memory_space=SMEM),
            full((count, D)),
            full((1, count)),
            flat,
            wide,
            wide,
            flat,
            flat,
            pl.BlockSpec((D, D), lambda j: (j, 0)),
            pl.BlockSpec((D, D), lambda j: (0, j)),
            full((D, D)),
            full(vectors.shape),
        ],
        out_specs=[tiles, tiles, tops, tops, flat, flat, flat, full((16, D))],
        scratch_shapes=[
            pltpu.VMEM((tokens, D), f32),
            pltpu.VMEM((tokens, D), bf16),
            pltpu.VMEM((tokens, D), f32),
        ],
        name="mlp_back",
        cost_estimate=cost(8 * tokens * D * FF, 5e7, tokens * FF),
    )(core, ghp, picks.reshape(1, count), x2, act, up, h2, x1, wdown, wup, wo, vectors)


def qkv_back_kernel(g_ref, w_ref, x_ref, gx1_ref, vec_ref, gx0_ref, vg_ref, gh):
    j = pl.program_id(0)
    part = mm_t(g_ref[0], w_ref[...])

    @pl.when(j == 0)
    def _():
        vg_ref[...] = jnp.zeros_like(vg_ref)
        gh[...] = part

    @pl.when(j > 0)
    def _():
        gh[...] += part

    vg_ref[pl.ds(8 + j, 1), :] = jnp.sum(g_ref[0].astype(f32), 0, keepdims=True)

    @pl.when(j == 2)
    def _():
        grad, gain, bias = norm_pull(x_ref[...].astype(f32), vec_ref[0:1, :], gh[...])
        vg_ref[0:1, :] = gain
        vg_ref[1:2, :] = bias
        gx0_ref[...] = (gx1_ref[...] + grad).astype(bf16)


def qkv_back(grads, wqkv, x0, gx1, vectors):
    tokens = x0.shape[0]
    flat = full((tokens, D))
    return pl.pallas_call(
        qkv_back_kernel,
        grid=(3,),
        out_shape=[
            jax.ShapeDtypeStruct((tokens, D), bf16),
            jax.ShapeDtypeStruct((16, D), f32),
        ],
        in_specs=[
            pl.BlockSpec((1, tokens, D), lambda j: (j, 0, 0)),
            pl.BlockSpec((D, D), lambda j: (0, j)),
            flat,
            flat,
            full(vectors.shape),
        ],
        out_specs=[flat, full((16, D))],
        scratch_shapes=[pltpu.VMEM((tokens, D), f32)],
        name="qkv_back",
        cost_estimate=cost(2 * tokens * D * 3 * D, 1e7),
    )(grads, wqkv, x0, gx1, vectors)


def qkv_weights_kernel(
    core_ref, h_ref, g_ref, y_ref, ga_ref, small_ref, mine_ref, theirs_ref, mtop_ref, ttop_ref
):
    j = pl.program_id(0)
    core = core_ref[0]
    both = tuple(zip(near_far(core), (mine_ref, theirs_ref), (mtop_ref, ttop_ref)))

    @pl.when(j == 0)
    def _():
        for turn, (_, out, top) in enumerate(both):
            values = small_ref[core if turn == 0 else 1 - core]
            out[8] = values
            top[...] = jnp.max(jnp.abs(values), 0, keepdims=True)

    @pl.when(j < 3)
    def _():
        for cols, out, top in both:
            keep_tiles(mm_l(h_ref[:, cols], g_ref[0]), out, top, 2 * j)

    @pl.when(j == 3)
    def _():
        for cols, out, top in both:
            keep_tiles(mm_l(y_ref[:, cols], ga_ref[...]), out, top, 6)


def qkv_weights(core, h1, grads, y, ga, small):
    tokens = h1.shape[0]
    flat = full((tokens, D))
    halves = (9, BS, BS)
    highs = (1, BS)
    shapes = (halves, halves, highs, highs)
    return pl.pallas_call(
        qkv_weights_kernel,
        grid=(4,),
        out_shape=[jax.ShapeDtypeStruct(shape, f32) for shape in shapes],
        in_specs=[
            pl.BlockSpec(memory_space=SMEM),
            flat,
            pl.BlockSpec((1, tokens, D), lambda j: (jnp.minimum(j, 2), 0, 0)),
            flat,
            flat,
            full((2, BS, BS)),
        ],
        out_specs=[full(shape) for shape in shapes],
        name="qkv_weights",
        cost_estimate=cost(2 * tokens * D * 4 * D, 2e7),
    )(core, h1, grads, y, ga, small)


def comm_positions():
    side = np.zeros(48, np.int32)
    place = np.zeros(48, np.int32)
    for r in range(2):
        for c in range(2):
            for j in range(FSTEPS):
                place[16 + r * 8 + 2 * j + c] = 4 * j + c
                place[32 + (2 * j + r) * 2 + c] = 4 * j + 2 + c
                side[16 + r * 8 + 2 * j + c] = side[32 + (2 * j + r) * 2 + c] = r
            for j in range(3):
                place[r * 6 + 2 * j + c] = 16 + 2 * j + c
                side[r * 6 + 2 * j + c] = r
            place[12 + r * 2 + c] = 22 + c
            side[12 + r * 2 + c] = r
    return side, place


def lane_block(rows_all):
    return min(1280, (rows_all // 128 + 1) * 128)


def fill_table(places_ref, pieces, tab, valid):
    depth = pieces[0].shape[0]
    for p, piece in enumerate(pieces):
        start = pl.multiple_of(places_ref[p], depth)
        tab[pl.ds(start, depth), :] = jnp.where(valid, piece[...], jnp.zeros((), bf16))


def logits_kernel(rows_all, count, places_ref, group_ref, target_ref, *refs):
    pieces = refs[:count]
    logit_ref, stat_ref, tab, top, total, chosen = refs[count:]
    j = pl.program_id(0)
    wide = tab.shape[1]
    lane = lax.broadcasted_iota(i32, (1, wide), 1) + j * wide
    valid = lane < rows_all
    fill_table(places_ref, pieces, tab, valid)

    @pl.when(j == 0)
    def _():
        top[...] = jnp.full(top.shape, -jnp.inf, f32)
        total[...] = jnp.zeros(total.shape, f32)
        chosen[...] = jnp.zeros(chosen.shape, f32)

    logits = mm(group_ref[...], tab[...])
    logit_ref[...] = logits
    kept = jnp.where(valid, logits, -jnp.inf)
    before = top[...]
    after = jnp.maximum(before, jnp.max(kept, -1, keepdims=True))
    top[...] = after
    total[...] = total[...] * jnp.exp(before - after) + jnp.sum(
        jnp.exp(kept - after), -1, keepdims=True
    )
    hit = (lane == target_ref[...]) & valid
    chosen[...] += jnp.sum(jnp.where(hit, logits, 0.0), -1, keepdims=True)

    @pl.when(j == pl.num_programs(0) - 1)
    def _():
        spot = lax.broadcasted_iota(i32, (1, 128), 1)
        merged = jnp.where(
            spot == 0, top[...], jnp.where(spot == 1, total[...], chosen[...])
        )
        stat_ref[...] = merged.T[:8]


def table_specs(pieces, wide):
    return [pl.BlockSpec((pieces[0].shape[0], wide), lambda j: (0, j))] * len(pieces)


def vocabulary_logits(places, group, local_targets, pieces):
    count, rows_all = group.shape[0], pieces[0].shape[1]
    wide = lane_block(rows_all)
    return pl.pallas_call(
        partial(logits_kernel, rows_all, len(pieces)),
        grid=(pl.cdiv(rows_all, wide),),
        out_shape=[
            jax.ShapeDtypeStruct((count, rows_all), f32),
            jax.ShapeDtypeStruct((8, count), f32),
        ],
        in_specs=[pl.BlockSpec(memory_space=SMEM), full((count, D)), full((count, 1))]
        + table_specs(pieces, wide),
        out_specs=[pl.BlockSpec((count, wide), lambda j: (0, j)), full((8, count))],
        scratch_shapes=[pltpu.VMEM((D, wide), bf16)] + [pltpu.VMEM((count, 1), f32)] * 3,
        name="vocabulary_logits",
        cost_estimate=cost(2 * count * D * rows_all, 2e7, count * rows_all),
    )(places, group, local_targets.reshape(count, 1), *pieces)


def vocabulary_back_kernel(
    rows_all, count, scale, places_ref, logit_ref, stat_ref, target_ref, *refs
):
    pieces = refs[:count]
    grad_ref, ghp_ref, tab, stat = refs[count:]
    j = pl.program_id(0)
    wide = tab.shape[1]
    lane = lax.broadcasted_iota(i32, (1, wide), 1) + j * wide
    valid = lane < rows_all
    fill_table(places_ref, pieces, tab, valid)

    @pl.when(j == 0)
    def _():
        stat[...] = stat_ref[...].T
        ghp_ref[...] = jnp.zeros_like(ghp_ref)

    hit = (lane == target_ref[...]).astype(f32)
    soft = jnp.exp(logit_ref[...] - stat[:, 0:1]) * stat[:, 1:2]
    grads = jnp.where(valid, (soft - hit) * scale, 0.0).astype(bf16)
    grad_ref[...] = grads
    ghp_ref[...] += mm_t(grads, tab[...])


def vocabulary_back(places, logits, stats, local_targets, pieces, scale):
    count, rows_all = logits.shape
    wide = lane_block(rows_all)
    block = pl.BlockSpec((count, wide), lambda j: (0, j))
    return pl.pallas_call(
        partial(vocabulary_back_kernel, rows_all, len(pieces), scale),
        grid=(pl.cdiv(rows_all, wide),),
        out_shape=[
            jax.ShapeDtypeStruct((count, pl.cdiv(rows_all, wide) * wide), bf16),
            jax.ShapeDtypeStruct((count, D), f32),
        ],
        in_specs=[
            pl.BlockSpec(memory_space=SMEM),
            block,
            full(stats.shape),
            full((count, 1)),
        ]
        + table_specs(pieces, wide),
        out_specs=[block, full((count, D))],
        scratch_shapes=[pltpu.VMEM((D, wide), bf16), pltpu.VMEM((count, stats.shape[0]), f32)],
        name="vocabulary_back",
        cost_estimate=cost(2 * count * D * rows_all, 3e7, count * rows_all),
    )(places, logits, stats, local_targets.reshape(count, 1), *pieces)


def lexicon_kernel(
    depth, places_ref, turned_ref, grad_ref, mine_ref, theirs_ref, mtop_ref, ttop_ref, sel
):
    j = pl.program_id(0)
    half = mine_ref.shape[0]

    @pl.when(j == 0)
    def _():
        for p in range(sel.shape[0] // depth):
            start = pl.multiple_of(places_ref[p], depth)
            sel[pl.ds(p * depth, depth), :] = turned_ref[pl.ds(start, depth), :]
        mtop_ref[...] = jnp.zeros_like(mtop_ref)
        ttop_ref[...] = jnp.zeros_like(ttop_ref)

    for start, out, top in ((0, mine_ref, mtop_ref), (half, theirs_ref, ttop_ref)):
        part = mm(sel[pl.ds(start, half), :], grad_ref[...])
        out[...] = part
        top[...] = jnp.maximum(top[...], jnp.max(jnp.abs(part), 0, keepdims=True))


def lexicon(places, turned, grads, depth, rows_all):
    count, padded = grads.shape
    wide = lane_block(rows_all)
    half = D // 2
    block = pl.BlockSpec((half, wide), lambda j: (0, j))
    return pl.pallas_call(
        partial(lexicon_kernel, depth),
        grid=(padded // wide,),
        out_shape=[jax.ShapeDtypeStruct((half, padded), f32)] * 2
        + [jax.ShapeDtypeStruct((1, wide), f32)] * 2,
        in_specs=[
            pl.BlockSpec(memory_space=SMEM),
            full((D, count)),
            pl.BlockSpec((count, wide), lambda j: (0, j)),
        ],
        out_specs=[block, block, full((1, wide)), full((1, wide))],
        scratch_shapes=[pltpu.VMEM((D, count), bf16)],
        name="lexicon",
        cost_estimate=cost(2 * count * D * padded, 3e7),
    )(places, turned, grads)


def three(left, right, product):
    left_high, left_low = left
    right_high, right_low = right
    return (
        product(left_high, right_high)
        + product(left_high, right_low)
        + product(left_low, right_high)
    )


def shampoo_kernel(count, strip, places_ref, clip_ref, *refs):
    pieces, smalls, tails = refs[:count], refs[count : 2 * count], refs[2 * count : 3 * count]
    w_ref, ls_ref, rs_ref, lr_ref, rr_ref = refs[3 * count : 3 * count + 5]
    g_ref, nw_ref, nl_ref, nr_ref, small_ref = refs[3 * count + 5 :]
    clip = clip_ref[0]
    for k in range(count):
        place = pl.multiple_of(places_ref[k], strip)
        scale = jnp.exp2(tails[k][0:1, :] - 15.0) * clip
        for slot in range(2):
            values = pieces[k][pl.ds(slot * strip, strip), :] * scale
            g_ref[slot, pl.ds(place, strip), :] = values

        @pl.when(pl.program_id(0) == 0)
        def _(k=k, place=place, scale=scale):
            for side in range(2):
                values = smalls[k][pl.ds(side * strip, strip), :] * scale
                small_ref[side, pl.ds(place, strip), :] = values

    for slot in range(2):
        grads = split_two(g_ref[slot])
        for old, new, product in ((ls_ref, nl_ref, mm_t), (rs_ref, nr_ref, mm_l)):
            cross = product(grads[0], grads[1])
            outer = product(grads[0], grads[0]) + (cross + cross.T)
            new[slot] = SHAMPOO_BETA * old[slot] + (1.0 - SHAMPOO_BETA) * outer
        turned = split_two(three(grads, split_two(rr_ref[slot]), mm))
        direction = three(split_two(lr_ref[slot]), turned, mm)
        weights = w_ref[slot]
        nw_ref[slot] = weights - RATE_BLOCKS * (direction + DECAY_RATE * weights)


def shampoo(places, clip, pieces, strip, kept):
    slots = kept[0].shape[0]
    count = len(pieces)
    block = pl.BlockSpec((2, BS, BS), lambda s: (s, 0, 0))
    shape = jax.ShapeDtypeStruct((slots, BS, BS), f32)
    small_at, tail_at = slots // 2, (slots + 2) * strip // 16
    return pl.pallas_call(
        partial(shampoo_kernel, count, strip),
        grid=(slots // 2,),
        out_shape=[shape] * 4 + [jax.ShapeDtypeStruct((2, BS, BS), f32)],
        in_specs=[pl.BlockSpec(memory_space=SMEM)] * 2
        + [pl.BlockSpec((2 * strip, BS), lambda s: (s, 0))] * count
        + [pl.BlockSpec((2 * strip, BS), lambda s: (small_at, 0))] * count
        + [pl.BlockSpec((16, BS), lambda s: (tail_at, 0))] * count
        + [block] * 5,
        out_specs=[block] * 4 + [full((2, BS, BS))],
        name="shampoo",
        cost_estimate=cost(slots * 24 * BS**3, slots * BS * BS * 40),
    )(places, clip, *pieces, *pieces, *pieces, *kept)


def adam_update(weight, first, second, gradient, rate, step_value):
    first_new = BETA_FIRST * first + (1.0 - BETA_FIRST) * gradient
    second_new = BETA_SECOND * second + (1.0 - BETA_SECOND) * gradient * gradient
    first_hat = first_new / (1.0 - BETA_FIRST**step_value)
    second_hat = second_new / (1.0 - BETA_SECOND**step_value)
    return (
        weight - rate * (first_hat / (jnp.sqrt(second_hat) + ADAM_EPSILON) + DECAY_RATE * weight),
        first_new,
        second_new,
    )


def tie(values, *others):
    return lax.optimization_barrier((values,) + others)[0]


def exponent(bound):
    return jnp.floor(jnp.log2(jnp.maximum(bound, 1e-30))) + 1.0


def encode(values, bound):
    level = exponent(bound)
    coded = (values * jnp.exp2(15.0 - level)).astype(jnp.float16)
    return coded.reshape(-1, values.shape[-1]), level.astype(jnp.float16)


def pack(values, bound):
    coded, level = encode(values, bound)
    return jnp.concatenate([coded, jnp.broadcast_to(level, (16, coded.shape[1]))], 0)


def unpack(payload, shape):
    count = payload.shape[0] - 16
    wide = payload.astype(f32)
    level = wide[count : count + 1]
    values = wide[:count] * jnp.exp2(level - 15.0)
    return values.reshape(shape), jnp.exp2(payload[-1, 0].astype(f32))


def pack_lanes(values, bound):
    coded, level = encode(values, bound)
    lane = lax.broadcasted_iota(i32, coded.shape, 1)
    return jnp.where(lane == coded.shape[1] - 1, level, coded)


def unpack_lanes(payload):
    level = payload[0, -1].astype(f32)
    return payload.astype(f32) * jnp.exp2(level - 15.0)


def per_device(
    sizes,
    token_ids,
    seq_lengths,
    pick_rows,
    targets,
    step_count,
    block_order,
    slot_weights,
    left_stats,
    right_stats,
    left_roots,
    right_roots,
    embedding,
    embedding_first_moment,
    emb_second,
    vectors,
    vec_first,
    vec_second,
    feature_maps,
    map_first,
    map_second,
):
    ny, nc, n1, n0 = sizes
    n_dp, n_voc = ny * nc, n1 * n0
    dp_index, voc_index = lax.axis_index("dp"), lax.axis_index("vocab")
    y_at, c_at = dp_index // nc, dp_index % nc
    i1, i0 = voc_index // n0, voc_index % n0

    def over_dp(values, dy, dc):
        pairs = [
            (a * nc + b, ((a + dy) % ny) * nc + (b + dc) % nc) for a in range(ny) for b in range(nc)
        ]
        return lax.ppermute(values, "dp", pairs)

    def over_voc(values, d1, d0):
        pairs = [
            (a * n0 + b, ((a + d1) % n1) * n0 + (b + d0) % n0) for a in range(n1) for b in range(n0)
        ]
        return lax.ppermute(values, "vocab", pairs)

    def gather_voc(values):
        near = [values] + [over_voc(values, k, 0) for k in range(1, n1)]
        return [[part] + [over_voc(part, 0, k) for k in range(1, n0)] for part in near]

    def gather_stacked(values):
        near = jnp.stack([values] + [over_voc(values, 0, k) for k in range(1, n0)])
        return jnp.stack([near] + [over_voc(near, k, 0) for k in range(1, n1)])

    def flat_gather(values):
        return [part for line in gather_voc(values) for part in line]

    def gather_y(values):
        return [values] + [over_dp(values, k, 0) for k in range(1, ny)]

    def line_up(parts, at):
        size = len(parts)
        return jnp.take(jnp.stack(parts), (at - jnp.arange(size)) % size, axis=0)

    tokens = token_ids.shape[0]
    picks_own = pick_rows.shape[0]
    devices_all = n_dp * n_voc
    total_picks = picks_own * devices_all
    coefficient = DISTILL_WEIGHT / (tokens * devices_all * HEADS)
    shard_rows, cols_own = embedding.shape
    cols_y = cols_own * nc
    vocab_start = (voc_index * shard_rows).astype(i32)
    per_owner = slot_weights.shape[0]
    block_count = block_order.shape[0]
    table_own = embedding.T
    core = c_at.astype(i32).reshape(1)
    piece_places = jnp.stack(
        [
            (((y_at - ky) % ny) * nc + (c_at + kc) % nc) * cols_own
            for kc in range(nc)
            for ky in range(ny)
        ]
    ).astype(i32)

    low_own = table_own.astype(bf16)
    low_other = over_dp(low_own, 0, 1)
    upright = turn_table(core, low_own, low_other)

    ids_y = gather_y(token_ids)
    numbers = jnp.concatenate(ids_y + [targets])

    slots_y = gather_y(tie(slot_weights.astype(bf16), numbers))
    numbers = gather_stacked(numbers)
    targets_all = numbers[:, :, ny * tokens :].reshape(-1)
    lines = sorted(range(1, n1), key=lambda a: -min(a, n1 - a)) + [0]
    piece_order = [(a, b) for b in list(range(1, n0)) + [0] for a in lines]
    ids_order = [numbers[a, b, : ny * tokens] for a, b in piece_order]
    def near_piece(h, sums, *before):
        part = looked[n1 * (n0 - 1) + h]
        for b in range(1, n0):
            moved = over_voc(tie(looked[(b - 1) * n1 + h], *sums[: max(h - 1, 0)]), 0, -b)
            part = part + tie(moved, *sums, *before)
        return part.reshape(ny, tokens, cols_y)

    looked, hits, bases, by_one = [], [], [], []
    step = n1 // 2
    for first in range(0, n0 * n1, step):
        ids_rows = jnp.concatenate(ids_order[first : first + step])
        local_ids = ids_rows - vocab_start
        packed_ids = jnp.where(
            (local_ids >= 0) & (local_ids < shard_rows),
            (local_ids << 16) | jnp.arange(ids_rows.shape[0], dtype=i32),
            -1,
        )
        bases.append(sum(own.shape[0] for own in hits))
        if first == n0 * n1 - step:
            by_one.append(near_piece(0, by_one))
        hits.append(find_hits(tie(packed_ids, upright, *by_one), shard_rows))
        looked += lookup(hits[-1], upright, ids_rows.shape[0], step)
    hits = jnp.concatenate(hits)
    listed = step * ny * tokens
    early = (n0 - 1) * n1 // step

    for h in range(1, n1 - 1):
        by_one.append(near_piece(h, by_one))
    far_parts = [over_voc(by_one[h], -lines[h], 0) for h in range(n1 - 1)]
    slots_y = [tie(part, by_one[n1 - 2], far_parts[0]) for part in slots_y]
    slots_core = [over_dp(part, 0, 1) for part in slots_y]
    inverse = (
        jnp.zeros((block_count,), i32).at[block_order].set(jnp.arange(block_count, dtype=i32))
    )
    owner = inverse // per_owner
    src = ((c_at - owner % nc) % nc) * ny + (y_at - owner // nc) % ny
    wqkv, wo, wup, wdown = place_blocks(
        src.astype(i32), inverse % per_owner, slots_y + slots_core
    )

    by_one.append(near_piece(n1 - 1, by_one, wup))
    mine = by_one[-1]
    for part in far_parts:
        mine = mine + part

    row_parts = [mine[0]] + [over_dp(mine[k], -k, 0) for k in range(1, ny)]
    if ny == 2:
        first = y_at == 0
        x0 = jnp.concatenate(
            [
                jnp.where(first, row_parts[0], row_parts[1]),
                jnp.where(first, row_parts[1], row_parts[0]),
            ],
            1,
        )
    else:
        stacked = jnp.stack(row_parts)
        x0 = jnp.concatenate(
            [jnp.take(stacked, (j - y_at) % ny, axis=0) for j in range(ny)], axis=1
        )

    low_sent = tie(low_own, x0)
    low_y = [over_dp(low_sent, k, 0) for k in range(1, ny)]

    maps_low = feature_maps.astype(bf16)
    both = jnp.concatenate([maps_low, -maps_low], -1).reshape(2, PAIRS, 2, HD, 2 * HD)
    empty = jnp.zeros_like(both[:, :, 0])
    lift_maps = jnp.stack(
        [
            jnp.concatenate([both[:, :, 0], empty], -2),
            jnp.concatenate([empty, both[:, :, 1]], -2),
        ],
        2,
    ).reshape(2, HEADS, 2 * HD, 2 * HD)
    their_hits = over_dp(hits, 0, 1)
    h1, mixed = qkv_forward(tie(x0, their_hits), wqkv, vectors)
    y, distill = attend(seq_lengths, mixed, lift_maps)
    x1, h2, up, act, x2, picked = mlp_forward(x0, y, wo, wup, wdown, vectors, pick_rows)

    near_picked = [picked] + [over_voc(picked, 0, k) for k in range(1, n0)]
    low_y = [tie(part, *near_picked) for part in low_y]
    low_y_other = [over_dp(part, 0, 1) for part in low_y]
    pieces = [low_own] + low_y + [low_other] + low_y_other
    near_picked = jnp.concatenate(near_picked, 0)
    group = [near_picked] + [over_voc(near_picked, k, 0) for k in range(1, n1)]
    group = jnp.concatenate(group, 0)
    local_targets = targets_all - vocab_start
    logits, stats = vocabulary_logits(piece_places, group, local_targets, pieces)
    stats_all = gather_stacked(stats)
    lined = jnp.stack(
        [
            jnp.roll(stats_all[a, b, :3].reshape(3, n1, n0, picks_own), (a, b), (1, 2))
            for a in range(n1)
            for b in range(n0)
        ]
    ).reshape(n_voc, 3, n_voc * picks_own)
    top_all = jnp.max(lined[:, 0], 0)
    sum_all = jnp.sum(lined[:, 1] * jnp.exp(lined[:, 0] - top_all[None]), 0)
    losses = top_all + jnp.log(sum_all) - jnp.sum(lined[:, 2], 0)
    loss_part = jnp.sum(losses[:picks_own]) / total_picks + coefficient * distill[0, 0]
    shares = jnp.pad(jnp.stack([top_all, 1.0 / sum_all]), ((0, 126), (0, 0)))
    grad_logits, grad_group = vocabulary_back(
        piece_places, logits, shares, local_targets, pieces, 1.0 / total_picks
    )
    grad_group = grad_group.reshape(n1, n0, picks_own, D)
    by_one = []
    for a in list(range(1, n1)) + [0]:
        part = grad_group[a, 0]
        for b in range(1, n0):
            part = part + over_voc(grad_group[a, b], 0, -b)
        by_one.append(part)
    near_parts = [over_voc(by_one[a - 1], -a, 0) for a in range(1, n1)]

    lex_mine, lex_theirs, mine_high, theirs_high = lexicon(
        piece_places, group.T, tie(grad_logits, *by_one[:-1]), cols_own, shard_rows
    )
    lex_arrived = over_dp(lex_theirs, 0, 1)
    their_high = over_dp(theirs_high, 0, 1)
    lex_high = jnp.max(mine_high) + jnp.max(their_high)
    ghp = by_one[-1]
    for part in near_parts:
        ghp = ghp + tie(part, lex_theirs, their_high)

    def lex_lines(k):
        lines = slice(k * cols_own, (k + 1) * cols_own)
        return lex_mine[lines] + lex_arrived[lines]

    lex_sent = [pack_lanes(lex_lines(k), lex_high) for k in range(1, ny)]


    def core_parts(mine_part, their_part, mine_top, their_top, *later):
        arrived = tie(over_dp(their_part, 0, 1), *later)
        bound = jnp.max(mine_top) + jnp.max(over_dp(their_top, 0, 1))
        return coded_parts((mine_part, arrived), bound, 0) + (bound,)

    def coded_parts(parts, bound, axis):
        size = (n0, ny, n1)[axis]

        def lines(part, k):
            count = part.shape[0]
            if axis == 1:
                rows = part.reshape(count, n1, ny, -1, BS)
                rows = lax.dynamic_index_in_dim(rows, (y_at + k) % ny, 2, False)
                return rows.reshape(count, -1, BS)
            rows = part.shape[1] // size
            at = (i0 if axis == 0 else i1) + k
            return lax.dynamic_slice_in_dim(part, (at % size) * rows, rows, 1)

        def summed(k):
            cut = [lines(part, k) for part in parts]
            return sum(cut[1:], cut[0])

        return summed(0), [pack(summed(k), bound) for k in range(1, size)]

    def moved_parts(sent, axis):
        if axis == 1:
            return [over_dp(part, k, 0) for k, part in enumerate(sent, 1)]
        return [
            over_voc(part, k, 0) if axis == 2 else over_voc(part, 0, k)
            for k, part in enumerate(sent, 1)
        ]

    def collect(own, arrived, bound, *later):
        total, high = own, bound
        for part in arrived:
            values, top = unpack(tie(part, *later), own.shape)
            total = total + values
            high = high + top
        return total, high

    *halves_a, gx1, ga, gy, vg_a = mlp_back(
        core, ghp, pick_rows, x2, act, up, h2, x1, wdown, wup, wo, vectors
    )
    own_a, sent_a, bound_a = core_parts(*halves_a, *lex_sent)
    gy = tie(gy, *lex_sent, own_a, *sent_a)
    gqkv, map_q, map_k = attend_back(
        seq_lengths, mixed, gy, lift_maps, coefficient, 0, PAIRS, None
    )
    lex_parts = [over_dp(part, -k, 0) for k, part in enumerate(lex_sent, 1)]
    gx0, vg_b = qkv_back(gqkv, wqkv, x0, gx1, vectors)

    map_grads = jnp.concatenate([map_q, map_k], 0)
    vec_grads = (vg_a + vg_b)[:15]
    small_count = map_grads.size + vec_grads.size
    small = jnp.concatenate(
        [
            map_grads.reshape(-1),
            vec_grads.reshape(-1),
            jnp.zeros((2 * BS * BS - small_count,), f32),
        ]
    ).reshape(2, BS, BS)
    gx0_cols = gx0.reshape(tokens, ny, cols_y)
    cols_sent = [jnp.take(gx0_cols, (y_at + k) % ny, axis=1) for k in range(1, ny)]
    lex = lex_lines(0)
    for part in lex_parts:
        lex = lex + unpack_lanes(part)
    arrived = [jnp.take(gx0_cols, y_at, axis=1)] + [
        tie(over_dp(part, k, 0), lex) for k, part in enumerate(cols_sent, 1)
    ]
    arrived = jnp.concatenate(arrived, 0).reshape(ny * tokens, nc, cols_own)
    rows_mine = jnp.take(arrived, c_at, axis=1)
    moved_a = moved_parts(sent_a, 0)
    rows_sent = jnp.take(arrived, (c_at + 1) % nc, axis=1)
    rows_other = over_dp(rows_sent, 0, 1)
    if cols_own == 192 and n0 == 2 and n1 == 4:
        packed = jnp.concatenate(
            [
                rows_mine[:, :128],
                rows_other[:, :128],
                jnp.concatenate([rows_mine[:, 128:], rows_other[:, 128:]], 1),
            ],
            0,
        )
    else:
        packed = jnp.stack([rows_mine, rows_other])
    halves_b = qkv_weights(core, tie(h1, packed, *moved_a), gqkv, y, ga, small)
    total_a, high_a = collect(own_a, moved_a, bound_a, halves_b[0])
    near_raw = [over_voc(packed, k, 0) for k in range(1, n1)]
    own_b, sent_b, bound_b = core_parts(*halves_b, packed)
    total_b, high_b = collect(own_b, moved_parts(sent_b, 0), bound_b)
    own_a, sent_a = coded_parts((total_a,), high_a, 1)
    own_b, sent_b = coded_parts((total_b,), high_b, 1)
    near_rows = [packed] + [tie(part, *sent_b) for part in near_raw]
    total_a, high_a = collect(own_a, moved_parts(sent_a, 1), high_a, *sent_b)
    total_b, high_b = collect(own_b, moved_parts(sent_b, 1), high_b)
    total = jnp.concatenate([total_a, total_b], 0)
    own, sent = coded_parts((total,), jnp.maximum(high_a, high_b), 2)
    high = jnp.maximum(high_a, high_b)
    own_x = [over_voc(tie(packed, *sent_b, near_rows[-2]), 0, k) for k in range(1, n0)]
    sent = [tie(part, *near_rows) for part in sent]
    far_rows = jnp.stack([tie(part, *own_x) for part in near_rows[1:]])
    far_x = [over_voc(far_rows, 0, k) for k in range(1, n0)]
    moved_ab = moved_parts(sent, 2)

    if cols_own == 192 and n0 == 2 and n1 == 4:
        groups = [(base, listed, (g % early) * listed) for g, base in enumerate(bases)]
        before = scatter_first(
            hits,
            their_hits,
            groups[early:],
            [tie(near_rows[a], *sent) for a in lines],
            shard_rows,
        )
        lex = tie(lex, *before, moved_ab[0])
        emb_grads, emb_square = scatter_last(
            hits, their_hits, groups[:early], before, lex, far_x[0], own_x, shard_rows
        )
        emb_square = emb_square[0, 0]
    else:
        gathered = [[packed] + own_x]
        for a in range(1, n1):
            gathered.append([near_rows[a]] + [part[a - 1] for part in far_x])
        pieces = jnp.stack([gathered[a][b] for a, b in piece_order], 1).reshape(-1, cols_own)
        ids_rows = jnp.concatenate(ids_order)
        local = jnp.concatenate([ids_rows, over_dp(ids_rows, 0, 1)]) - vocab_start
        local = jnp.where((local >= 0) & (local < shard_rows), local, shard_rows)
        emb_grads = lex[:, :shard_rows].T.at[local].add(pieces.astype(f32), mode="drop").T
        emb_square = jnp.sum(emb_grads * emb_grads)

    blocks = collect(own, moved_ab, high, emb_grads)[0]

    square = emb_square + jnp.sum(blocks * blocks)
    sums = jnp.pad(jnp.stack([square, loss_part]).reshape(1, 2), ((0, 7), (0, 126)))
    sums = sums + over_dp(sums, 0, 1)
    sums = jnp.sum(line_up(gather_y(sums), y_at), 0)
    per_side = blocks.shape[0]
    both = jnp.concatenate([blocks, over_dp(blocks, 0, 1)], 0)
    side, place = comm_positions()
    side = jnp.concatenate([jnp.take(jnp.asarray(side), block_order), jnp.arange(2, dtype=i32)])
    place = jnp.concatenate(
        [jnp.take(jnp.asarray(place), block_order), jnp.full((2,), per_side - 1, i32)]
    )
    at_place = ((side - c_at) % nc) * per_side + place
    smalls = at_place[block_count:]
    at_place = at_place[:block_count].reshape(ny, nc, per_owner)

    def slots_of(k):
        mine = jnp.take(jnp.take(at_place, c_at, axis=1), (y_at + k) % ny, axis=0)
        return jnp.take(both, jnp.concatenate([mine, smalls]), axis=0)

    moved = [slots_of(k) for k in range(1, ny)]
    slots_sent = [pack(part, jnp.max(jnp.abs(both))) for part in moved]
    sums = tie(sums, *slots_sent)
    sums = jnp.sum(line_up([sums] + [over_voc(sums, 0, k) for k in range(1, n0)], i0), 0)

    small_own = unpack(slots_sent[0], moved[0].shape)[0][per_owner:]
    strip_parts = [jnp.concatenate([slots_of(0)[:per_owner], small_own], 0)]
    slots_moved = moved_parts(slots_sent, 1)
    sums = tie(sums, *slots_moved)
    for part in slots_moved:
        strip_parts.append(unpack(part, moved[0].shape)[0])
    sums = jnp.sum(line_up([sums] + [over_voc(sums, k, 0) for k in range(1, n1)], i1), 0)
    grad_norm = jnp.sqrt(sums[0, 0])
    loss_total = sums[0, 1]
    clip_scale = CLIP_NORM / jnp.maximum(grad_norm, CLIP_NORM)
    own_strips = line_up(strip_parts, y_at).transpose(1, 0, 2, 3)
    own_strips = own_strips.reshape(per_owner + 2, -1, BS)
    strip_rows = own_strips.shape[1]
    strip_half = BS // n0
    places = [
        ((i0 - b) % n0) * strip_half + ((i1 - a) % n1) * strip_rows
        for a in range(n1)
        for b in range(n0)
    ]
    places = jnp.stack(places).astype(i32)
    strip_sent = tie(pack(own_strips, jnp.max(jnp.abs(own_strips))), sums)
    strip_pieces = [part.astype(f32) for part in flat_gather(strip_sent)]
    clipped, new_slots, new_left, new_right, small_all = shampoo(
        places,
        clip_scale.reshape(1),
        strip_pieces,
        strip_rows,
        (slot_weights, left_stats, right_stats, left_roots, right_roots),
    )
    clip_late = tie(clip_scale, strip_sent)
    small_all = small_all.reshape(-1)
    map_grad = small_all[: map_grads.size].reshape(feature_maps.shape)
    vec_grad = small_all[map_grads.size : small_count].reshape(vectors.shape)

    step_value = step_count[0].astype(f32)
    emb_out = adam_update(
        table_own,
        embedding_first_moment.T,
        emb_second.T,
        emb_grads * clip_late,
        RATE_TABLE,
        step_value,
    )
    vec_out = adam_update(
        vectors, vec_first, vec_second, vec_grad, RATE_VECTORS, step_value
    )
    map_out = adam_update(
        feature_maps, map_first, map_second, map_grad, RATE_MAPS, step_value
    )
    return (
        loss_total,
        grad_norm,
        clipped,
        new_slots,
        new_left,
        new_right,
        emb_out[0].T,
        emb_out[1].T,
        emb_out[2].T,
        vec_out[0],
        vec_out[1],
        vec_out[2],
        map_out[0],
        map_out[1],
        map_out[2],
    )


def solution(mesh):
    n_dp, n_voc = mesh.shape["dp"], mesh.shape["vocab"]
    sizes = (n_dp // 2, 2, 4, n_voc // 4)
    rows = P(("dp", "vocab"))
    blocks = P("dp", None, None)
    table = P("vocab", "dp")
    placed = (
        (rows, P(("dp", "vocab"), None), rows, rows, P(), P())
        + (blocks,) * 5
        + (table,) * 3
        + (P(),) * 6
    )
    return jax.shard_map(
        partial(per_device, sizes),
        mesh=mesh,
        in_specs=placed,
        out_specs=(P(), P()) + (blocks,) * 4 + (table,) * 3 + (P(),) * 6,
        check_vma=False,
    )
```
